32 devices in a mesh: dp: 8 (over y, x, core), tp: 4 (over z).
Axes of the slice: x: 2, y: 2, z: 4, core: 2. Of those that a mesh axis runs over, the one named last changes fastest.
Arguments:
- layer_in: bfloat16 [32768, 768], P(('dp', 'tp')), may hold values from -6 to 6
- out_grad: bfloat16 [32768, 768], P(('dp', 'tp')), may hold values from -6 to 6
- lengths: int32 [8], P('dp'), may hold values from 2049 to 4096, as said below
- w_query: bfloat16 [768, 768], replicated, may hold values from -0.875 to 0.875
- b_query: bfloat16 [768], replicated, may hold values from -6 to 6
- w_key: bfloat16 [768, 768], replicated, may hold values from -0.21875 to 0.21875
- b_key: bfloat16 [768], replicated, may hold values from -3 to 3
- w_value: bfloat16 [768, 768], replicated, may hold values from -0.21875 to 0.21875
- b_value: bfloat16 [768], replicated, may hold values from -3 to 3
- w_out: bfloat16 [768, 768], replicated, may hold values from -0.875 to 0.875
- b_out: bfloat16 [768], replicated, may hold values from -3 to 3
- seq_proj: bfloat16 [256, 4096], replicated, may hold values from -0.09375 to 0.09375
- attn_gain: bfloat16 [768], replicated, may hold values from 0.5 to 1.5
- attn_shift: bfloat16 [768], replicated, may hold values from -3 to 3
- w_up: bfloat16 [768, 3072], P(None, 'tp'), may hold values from -0.21875 to 0.21875
- b_up: bfloat16 [3072], P('tp'), may hold values from -3 to 3
- w_down: bfloat16 [3072, 768], P('tp'), may hold values from -0.109375 to 0.109375
- b_down: bfloat16 [768], replicated, may hold values from -3 to 3
- ffn_gain: bfloat16 [768], replicated, may hold values from 0.5 to 1.5
- ffn_shift: bfloat16 [768], replicated, may hold values from -3 to 3
Outputs:
- layer_out: bfloat16 [32768, 768], P(('dp', 'tp'))
- grad_in: bfloat16 [32768, 768], P(('dp', 'tp'))
- grad_w_query: float32 [768, 768], replicated
- grad_b_query: float32 [768], replicated
- grad_w_key: float32 [768, 768], replicated
- grad_b_key: float32 [768], replicated
- grad_w_value: float32 [768, 768], replicated
- grad_b_value: float32 [768], replicated
- grad_w_out: float32 [768, 768], replicated
- grad_b_out: float32 [768], replicated
- grad_seq_proj: float32 [256, 4096], replicated
- grad_attn_gain: float32 [768], replicated
- grad_attn_shift: float32 [768], replicated
- grad_w_up: float32 [768, 3072], P(None, 'tp')
- grad_b_up: float32 [3072], P('tp')
- grad_w_down: float32 [3072, 768], P('tp')
- grad_b_down: float32 [768], replicated
- grad_ffn_gain: float32 [768], replicated
- grad_ffn_shift: float32 [768], replicated
The draws below stay inside these ranges and needn't reach their ends.
Inputs may be any that keep to these rules, and one draw needn't show every extreme that they name: `lengths`: rows from a sequence's length on are padding; some sequence has exactly 4096 rows.
All inputs are finite; a program needn't handle non-finite values.
Results may differ from the reference program's by a relative error of at most 0.022.
The reference program's roundings to bfloat16 on the way count: a program that leaves them out, or rounds other values in their place, can miss the bound.
Values may be sent and summed in bfloat16 or wider, within the bound.
A program may use at most 192 MiB of HBM per device.

```python
import jax
import jax.numpy as jnp
from jax import lax

D = 768
HEADS = 12
HEAD = 64
FF = 3072
KP = 256
LPAD = 4096
SEQS = 8
TOKENS = 32768


def draw_lengths(key, part):
    shortest = LPAD // 2 + 1
    raw_lengths = jax.random.randint(key, (SEQS,), shortest, LPAD + 1, dtype=jnp.int32)
    longest_at = jax.random.randint(jax.random.fold_in(key, 7), (), 0, SEQS, dtype=jnp.int32)
    return jnp.where(jnp.arange(SEQS, dtype=jnp.int32) == longest_at, jnp.int32(LPAD), raw_lengths)


def block_levels(key, extent, cuts, smallest, top_value):
    def one(dim, shards_of):
        heights = jax.random.uniform(jax.random.fold_in(jax.random.fold_in(key, 6), dim), (shards_of,), jnp.float32, smallest / len(cuts), top_value / len(cuts))
        return jnp.repeat(jnp.exp(heights), extent[dim] // shards_of).reshape((-1,) + (1,) * (len(extent) - dim - 1))

    loudness = one(*cuts[0])
    for cut in cuts[1:]:
        loudness = loudness * one(*cut)
    return loudness


def bell_draw(stream_key, dims, deviation, most, shards=(), held_as=jnp.bfloat16):
    array = deviation * jax.random.normal(stream_key, dims, jnp.float32)
    if shards:
        array = array * block_levels(stream_key, dims, shards, -0.22, 0.18)
    return jnp.clip(array, -most, most).astype(held_as)


def setup_inputs(seed: int = 0) -> dict:
    seeds = jax.random.split(jax.random.key(seed), 21)
    return {
        "layer_in": bell_draw(seeds[0], (TOKENS, D), 1.0, 6.0, ((0, 32),)),
        "out_grad": bell_draw(seeds[1], (TOKENS, D), 1.0, 6.0, ((0, 32),)),
        "lengths": draw_lengths(jax.random.fold_in(seeds[20], 71), 0),
        "w_query": bell_draw(seeds[3], (D, D), (D // 16) ** -0.5, 0.875),
        "b_query": bell_draw(seeds[4], (D,), 1.0, 6.0),
        "w_key": bell_draw(seeds[5], (D, D), D ** -0.5, 0.21875),
        "b_key": bell_draw(seeds[6], (D,), 0.5, 3.0),
        "w_value": bell_draw(seeds[7], (D, D), D ** -0.5, 0.21875),
        "b_value": bell_draw(seeds[8], (D,), 0.5, 3.0),
        "w_out": bell_draw(seeds[9], (D, D), (D // 16) ** -0.5, 0.875),
        "b_out": bell_draw(seeds[10], (D,), 0.5, 3.0),
        "seq_proj": bell_draw(seeds[11], (KP, LPAD), LPAD ** -0.5, 0.09375),
        "attn_gain": jnp.clip(1.0 + 0.1 * jax.random.normal(seeds[12], (D,), jnp.float32), 0.5, 1.5).astype(jnp.bfloat16),
        "attn_shift": bell_draw(seeds[13], (D,), 0.5, 3.0),
        "w_up": bell_draw(seeds[14], (D, FF), D ** -0.5, 0.21875, ((1, 4),)),
        "b_up": bell_draw(seeds[15], (FF,), 0.5, 3.0, ((0, 4),)),
        "w_down": bell_draw(seeds[16], (FF, D), FF ** -0.5, 0.109375, ((0, 4),)),
        "b_down": bell_draw(seeds[17], (D,), 0.5, 3.0),
        "ffn_gain": jnp.clip(1.0 + 0.1 * jax.random.normal(seeds[18], (D,), jnp.float32), 0.5, 1.5).astype(jnp.bfloat16),
        "ffn_shift": bell_draw(seeds[19], (D,), 0.5, 3.0),
    }


@jax.custom_vjp
def low(v):
    return lax.optimization_barrier(v.astype(jnp.bfloat16)).astype(jnp.float32)

@jax.custom_vjp
def low_back(v):
    return v

def low_keep(v):
    return (low(v), None)

def low_pass(kept, grad):
    return (grad,)

def back_keep(v):
    return (v, None)

def back_low(kept, grad):
    return (low(grad),)
low.defvjp(low_keep, low_pass)
low_back.defvjp(back_keep, back_low)

def matmul_high(left, right):
    return jnp.dot(left, right, precision=lax.Precision.HIGHEST)

def both_ways(value):
    return low(low_back(value))

def layer_norm(hidden, gain, shift):
    center = hidden - lax.optimization_barrier(jnp.mean(hidden, axis=-1, keepdims=True))
    spread = lax.optimization_barrier(jnp.mean(center * center, axis=-1, keepdims=True))
    return center * lax.rsqrt(spread + 1e-05) * gain + shift

def one_sequence(weights_all, inputs, length):
    w_query, b_query, w_key, b_key, w_value, b_value, w_out, b_out, seq_proj, attn_gain, attn_shift, w_up, b_up, w_down, b_down, ffn_gain, ffn_shift = weights_all
    live_rows = (jnp.arange(LPAD) < length).astype(jnp.float32)
    queries = both_ways(matmul_high(inputs, w_query) + b_query)
    keys_full = both_ways(matmul_high(inputs, w_key) + b_key)
    values_full = both_ways(matmul_high(inputs, w_value) + b_value)
    masked_proj = seq_proj * live_rows[None, :]
    proj_keys = both_ways(matmul_high(masked_proj, keys_full)).reshape(KP, HEADS, HEAD)
    proj_values = both_ways(matmul_high(masked_proj, values_full)).reshape(KP, HEADS, HEAD)
    query_heads = queries.reshape(LPAD, HEADS, HEAD)
    logits = low_back(jnp.einsum('rhd,khd->rhk', query_heads, proj_keys, precision=lax.Precision.HIGHEST) * 0.125)
    probs = low(jax.nn.softmax(logits, axis=-1))
    mixed_heads = both_ways(jnp.einsum('rhk,khd->rhd', probs, proj_values, precision=lax.Precision.HIGHEST).reshape(LPAD, D))
    attn_branch = low_back(matmul_high(mixed_heads, w_out) + b_out)
    normed = layer_norm(inputs + attn_branch, attn_gain, attn_shift)
    pre_act = low_back(matmul_high(low(normed), w_up) + b_up)
    hidden_act = low(jax.nn.gelu(pre_act, approximate=False))
    ffn_branch = low_back(matmul_high(hidden_act, w_down) + b_down)
    return layer_norm(normed + ffn_branch, ffn_gain, ffn_shift)

def reference(layer_in, out_grad, lengths, w_query, b_query, w_key, b_key, w_value, b_value, w_out, b_out, seq_proj, attn_gain, attn_shift, w_up, b_up, w_down, b_down, ffn_gain, ffn_shift):
    weights_all = tuple((param_value.astype(jnp.float32) for param_value in (w_query, b_query, w_key, b_key, w_value, b_value, w_out, b_out, seq_proj, attn_gain, attn_shift, w_up, b_up, w_down, b_down, ffn_gain, ffn_shift)))
    inputs_all = layer_in.astype(jnp.float32).reshape(SEQS, LPAD, D)

    def forward(inputs_all, weights_all):

        def per_sequence(running, element):
            inputs, length = element
            return (running, jax.checkpoint(one_sequence)(weights_all, inputs, length))
        running, outputs = lax.scan(per_sequence, jnp.zeros((), jnp.float32), (inputs_all, lengths))
        return outputs
    outputs, pull = jax.vjp(forward, inputs_all, weights_all)
    grad_inputs, grads = pull(out_grad.astype(jnp.float32).reshape(SEQS, LPAD, D))
    g_wq, g_bq, g_wk, g_bk, g_wv, g_bv, g_wo, g_bo, g_proj, g_again, g_ashift, g_wup, g_bup, g_wdown, g_bdown, g_fgain, g_fshift = grads
    return (outputs.reshape(TOKENS, D).astype(jnp.bfloat16), grad_inputs.reshape(TOKENS, D).astype(jnp.bfloat16), g_wq, g_bq, g_wk, g_bk, g_wv, g_bv, g_wo, g_bo, g_proj, g_again, g_ashift, g_wup, g_bup, g_wdown, g_bdown, g_fgain, g_fshift)
```

```python
import jax
import jax.numpy as jnp
from jax import lax
from jax.sharding import PartitionSpec as P

HEADS = 12
HEAD = 64
BF = jnp.bfloat16
F32 = jnp.float32


def layer_norm(hidden, gain, shift):
    center = hidden - jnp.mean(hidden, axis=-1, keepdims=True)
    spread = jnp.mean(center * center, axis=-1, keepdims=True)
    return center * lax.rsqrt(spread + 1e-05) * gain + shift


def dot(left, right, left_dim, right_dim):
    return lax.dot_general(
        left, right, (((left_dim,), (right_dim,)), ((), ())), preferred_element_type=F32
    )


def exact_gelu(value):
    return jax.nn.gelu(value, approximate=False)


def on_device(
    layer_in,
    out_grad,
    lengths,
    w_query,
    b_query,
    w_key,
    b_key,
    w_value,
    b_value,
    w_out,
    b_out,
    seq_proj,
    attn_gain,
    attn_shift,
    w_up,
    b_up,
    w_down,
    b_down,
    ffn_gain,
    ffn_shift,
):
    row_count, width = layer_in.shape
    slots = seq_proj.shape[0]
    tp_index = lax.axis_index("tp")
    own_first = tp_index * row_count
    own_positions = own_first + jnp.arange(row_count, dtype=jnp.int32)
    own_live = (own_positions < lengths[0]).astype(F32)
    own_cols = lax.dynamic_slice_in_dim(seq_proj, own_first, row_count, 1)
    own_proj = (own_cols.astype(F32) * own_live[None, :]).astype(BF)
    total_rows = seq_proj.shape[1]
    live = (jnp.arange(total_rows, dtype=jnp.int32) < lengths[0]).astype(F32)
    slot_sum = jnp.sum(seq_proj.astype(F32) * live[None, :], axis=1)[:, None]

    folded = lax.psum(dot(own_proj, layer_in, 1, 0), "tp")
    up_all = lax.all_gather(w_up.T, "tp", axis=0, tiled=True)
    down_all = lax.all_gather(w_down, "tp", axis=0, tiled=True)
    bias_up = lax.all_gather(b_up, "tp", axis=0, tiled=True)
    folded_b = folded.astype(BF)
    folded_low = (folded - folded_b.astype(F32)).astype(BF)

    def project(weight, bias):
        full = dot(folded_b, weight, 1, 0) + dot(folded_low, weight, 1, 0)
        return (full + slot_sum * bias.astype(F32)[None, :]).astype(BF)

    proj_keys = project(w_key, b_key)
    proj_values = project(w_value, b_value)
    queries = (dot(layer_in, w_query, 1, 0) + b_query.astype(F32)).astype(BF)
    mixed_parts, prob_parts = [], []
    for h in range(HEADS):
        cols = slice(h * HEAD, (h + 1) * HEAD)
        logits = dot(queries[:, cols], proj_keys[:, cols], 1, 1) * 0.125
        peak = jnp.max(logits, axis=-1, keepdims=True)
        raised = jnp.exp(logits - peak)
        probs = raised / jnp.sum(raised, axis=-1, keepdims=True)
        prob_parts.append(probs)
        mixed_parts.append(dot(probs.astype(BF), proj_values[:, cols], 1, 0).astype(BF))
    mixed = jnp.concatenate(mixed_parts, axis=1)
    attn = dot(mixed, w_out, 1, 0) + b_out.astype(F32)
    res_one = layer_in.astype(F32) + attn
    normed, norm_one_pull = jax.vjp(
        layer_norm, res_one, attn_gain.astype(F32), attn_shift.astype(F32)
    )
    normed_b = normed.astype(BF)
    pre_act = dot(normed_b, up_all, 1, 1) + bias_up.astype(F32)
    hidden_act, gelu_pull = jax.vjp(exact_gelu, pre_act)
    hidden_b = hidden_act.astype(BF)
    branch = dot(hidden_b, down_all, 1, 0) + b_down.astype(F32)
    res_two = normed + branch
    final, norm_two_pull = jax.vjp(
        layer_norm, res_two, ffn_gain.astype(F32), ffn_shift.astype(F32)
    )
    layer_out = final.astype(BF)
    d_res_two, g_ffn_gain, g_ffn_shift = norm_two_pull(out_grad.astype(F32))
    d_branch = d_res_two.astype(BF)
    g_b_down = jnp.sum(d_branch.astype(F32), axis=0)
    g_w_down = dot(hidden_b, d_branch, 0, 0).astype(BF)
    (d_hidden,) = gelu_pull(dot(d_branch, down_all, 1, 1))
    d_pre = d_hidden.astype(BF)
    g_b_up = jnp.sum(d_pre.astype(F32), axis=0)
    g_w_up = dot(d_pre, normed_b, 0, 0).astype(BF)
    d_normed = d_res_two + dot(d_pre, up_all, 1, 0)
    d_res_one, g_attn_gain, g_attn_shift = norm_one_pull(d_normed)
    d_attn = d_res_one.astype(BF)
    g_b_out = jnp.sum(d_attn.astype(F32), axis=0)
    g_w_out = dot(mixed, d_attn, 0, 0).astype(BF)
    d_mixed = dot(d_attn, w_out, 1, 1).astype(BF)
    d_query_parts, d_key_parts, d_value_parts = [], [], []
    for h in range(HEADS):
        cols = slice(h * HEAD, (h + 1) * HEAD)
        probs = prob_parts[h]
        d_probs = dot(d_mixed[:, cols], proj_values[:, cols], 1, 1)
        d_logits = (probs * (d_probs - jnp.sum(probs * d_probs, axis=-1, keepdims=True))).astype(BF)
        d_query_parts.append((dot(d_logits, proj_keys[:, cols], 1, 0) * 0.125).astype(BF))
        d_key_parts.append((dot(queries[:, cols], d_logits, 0, 0) * 0.125).astype(BF))
        d_value_parts.append(dot(d_mixed[:, cols], probs.astype(BF), 0, 0).astype(BF))
    d_queries = jnp.concatenate(d_query_parts, axis=1)
    part_keys = jnp.concatenate(d_key_parts, axis=0)
    part_values = jnp.concatenate(d_value_parts, axis=0)
    own_dk = lax.psum_scatter(part_keys, "tp", scatter_dimension=0, tiled=True)
    own_dv = lax.psum_scatter(part_values, "tp", scatter_dimension=0, tiled=True)
    d_proj_keys = lax.all_gather(own_dk, "tp", axis=0, tiled=True)
    d_proj_values = lax.all_gather(own_dv, "tp", axis=0, tiled=True)
    g_w_key = dot(own_dk, folded_b, 1, 0)
    g_w_value = dot(own_dv, folded_b, 1, 0)
    g_b_key = dot(d_proj_keys.astype(F32), slot_sum, 1, 0)[:, 0]
    g_b_value = dot(d_proj_values.astype(F32), slot_sum, 1, 0)[:, 0]
    back = dot(d_proj_keys, w_key, 0, 1) + dot(d_proj_values, w_value, 0, 1)
    back_b = back.astype(BF)
    bias_back = dot(d_proj_keys.astype(F32), b_key.astype(F32)[:, None], 0, 0) + dot(
        d_proj_values.astype(F32), b_value.astype(F32)[:, None], 0, 0
    )
    own_proj_grad = (dot(back_b, layer_in, 1, 1) + bias_back) * own_live[None, :]
    g_w_query = dot(layer_in, d_queries, 0, 0)
    g_b_query = jnp.sum(d_queries.astype(F32), axis=0)
    grad_in = (
        d_res_one + dot(d_queries, w_query, 1, 1) + dot(own_proj, back_b, 0, 0)
    ).astype(BF)
    g_w_query, g_w_out = lax.psum((g_w_query.astype(BF), g_w_out), ("dp", "tp"))
    g_w_key, g_w_value, own_proj_grad = lax.psum(
        (g_w_key.astype(BF), g_w_value.astype(BF), own_proj_grad.astype(BF)), "dp"
    )
    g_w_key = lax.all_gather(g_w_key, "tp", axis=0, tiled=True).T
    g_w_value = lax.all_gather(g_w_value, "tp", axis=0, tiled=True).T
    g_seq_proj = lax.all_gather(own_proj_grad, "tp", axis=1, tiled=True)
    g_b_key, g_b_value = g_b_key / lax.axis_size("tp"), g_b_value / lax.axis_size("tp")
    (
        g_b_query,
        g_b_key,
        g_b_value,
        g_b_out,
        g_attn_gain,
        g_attn_shift,
        g_ffn_gain,
        g_ffn_shift,
        g_b_down,
        g_b_up,
    ) = lax.psum(
        (
            g_b_query,
            g_b_key,
            g_b_value,
            g_b_out,
            g_attn_gain,
            g_attn_shift,
            g_ffn_gain,
            g_ffn_shift,
            g_b_down,
            g_b_up,
        ),
        ("dp", "tp"),
    )
    own_ff = b_up.shape[0]
    g_b_up = lax.dynamic_slice_in_dim(g_b_up, tp_index * own_ff, own_ff, 0)
    g_w_up, g_w_down = (
        lax.psum_scatter(g_w_up, "tp", scatter_dimension=0, tiled=True),
        lax.psum_scatter(g_w_down, "tp", scatter_dimension=0, tiled=True),
    )
    g_w_up, g_w_down = lax.psum((g_w_up, g_w_down), "dp")
    up = lambda v: v.astype(F32)
    return (
        layer_out,
        grad_in,
        up(g_w_query),
        g_b_query,
        up(g_w_key),
        g_b_key,
        up(g_w_value),
        g_b_value,
        up(g_w_out),
        g_b_out,
        up(g_seq_proj),
        g_attn_gain,
        g_attn_shift,
        up(g_w_up.T),
        g_b_up,
        up(g_w_down),
        g_b_down,
        g_ffn_gain,
        g_ffn_shift,
    )


def solution(mesh):
    in_specs = (
        P(("dp", "tp"), None),
        P(("dp", "tp"), None),
        P("dp"),
        *([P()] * 11),
        P(None, "tp"),
        P("tp"),
        P("tp", None),
        P(),
        P(),
        P(),
    )
    out_specs = (
        P(("dp", "tp"), None),
        P(("dp", "tp"), None),
        *([P()] * 11),
        P(None, "tp"),
        P("tp"),
        P("tp", None),
        P(),
        P(),
        P(),
    )
    return jax.shard_map(
        on_device, mesh=mesh, in_specs=in_specs, out_specs=out_specs, check_vma=False
    )
```

```python
import functools

import jax
import jax.numpy as jnp
from jax import lax
from jax.experimental import pallas as pl
from jax.experimental.pallas import tpu as pltpu
from jax.sharding import PartitionSpec as P

HEADS = 12
HEAD = 64
PAIRS = HEADS // 2
PAIR = 2 * HEAD
BF = jnp.bfloat16
F32 = jnp.float32
MESH = pl.DeviceIdType.MESH
VMEM_LIMIT = 67_043_328


def dot(left, right, left_dim, right_dim):
    return lax.dot_general(
        left, right, (((left_dim,), (right_dim,)), ((), ())), preferred_element_type=F32
    )


def place(index, size):
    return pl.ds(pl.multiple_of(index * size, size), size)


def rows_at(first, size, multiple):
    return pl.ds(pl.multiple_of(first, multiple), size)


class Link:
    def __init__(self, dp_size, tp_size, send_sems, recv_sems):
        self.dp_size, self.tp_size = dp_size, tp_size
        self.dp, self.tp = lax.axis_index("dp"), lax.axis_index("tp")
        self.bits = dp_size.bit_length() - 1
        self.low = min(3, self.bits)
        self.send_sems, self.recv_sems = send_sems, recv_sems
        self.used = 0

    def bit(self, b):
        return lax.rem(lax.div(self.dp, 1 << b), 2)

    def partner(self, b):
        return (self.dp + (1 - 2 * self.bit(b)) * (1 << b), self.tp)

    def ahead(self, k):
        return lax.rem(self.tp + k, self.tp_size)

    def behind(self, k):
        return lax.rem(self.tp + self.tp_size - k, self.tp_size)

    def greet(self, dp_bits):
        barrier = pltpu.get_barrier_semaphore()
        peers = [(self.dp, self.ahead(k)) for k in range(1, self.tp_size)]
        peers += [self.partner(b) for b in range(dp_bits)]
        for peer in peers:
            pl.semaphore_signal(barrier, inc=1, device_id=peer, device_id_type=MESH)
        pl.semaphore_wait(barrier, len(peers))

    def send(self, source, target, device):
        copy = pltpu.make_async_remote_copy(
            src_ref=source,
            dst_ref=target,
            send_sem=self.send_sems.at[self.used],
            recv_sem=self.recv_sems.at[self.used],
            device_id=device,
            device_id_type=MESH,
        )
        self.used += 1
        copy.start()
        return copy


def layer_norm(hidden, gain, shift):
    center = hidden - jnp.mean(hidden, axis=-1, keepdims=True)
    spread = jnp.mean(center * center, axis=-1, keepdims=True)
    return center * lax.rsqrt(spread + 1e-05) * gain + shift


def exact_gelu(value):
    return jax.nn.gelu(value, approximate=False)


FRONT_SEMS = 64


def gather_order(name):
    return (1, 2, 0) if name == "up" else (2, 1, 0)


class WeightGather:
    def __init__(self, link, name, shard, whole):
        self.link, self.shard, self.whole = link, shard, whole
        self.rows = shard.shape[0]
        self.order = [b for b in gather_order(name) if b < link.low]
        self.piece = self.rows >> len(self.order)
        offset, size = 0, self.piece
        for b in self.order:
            offset = offset + link.bit(b) * size
            size *= 2
        self.offset = offset
        self.step = {}
        self.waiting = {}

    def across(self, k):
        link = self.link
        rows = rows_at(self.offset, self.piece, self.piece)
        self.waiting[k] = link.send(
            self.shard.at[rows, :], self.whole.at[link.tp, rows, :], (link.dp, link.ahead(k))
        )
        self.step[k] = 0

    def advance(self, k):
        link, done = self.link, self.step[k]
        if done > len(self.order):
            return
        self.waiting[k].wait()
        self.step[k] = done + 1
        if done == len(self.order):
            return
        size = self.piece << done
        first = self.offset - lax.rem(self.offset, size)
        rows = rows_at(first, size, self.piece)
        region = self.whole.at[link.behind(k), rows, :]
        self.waiting[k] = link.send(region, region, link.partner(self.order[done]))


def front_kernel(
    dp_size,
    tp_size,
    len_ref,
    vec,
    bup,
    x,
    wq,
    wk,
    wv,
    wo,
    wup,
    wdn,
    e,
    xhat,
    rstd,
    mixed,
    q,
    probs,
    kb,
    vb,
    yb,
    ssum,
    em,
    bup_all,
    wup_all,
    wdn_all,
    ysend,
    yrecv,
    send_sems,
    recv_sems,
    local_sems,
):
    link = Link(dp_size, tp_size, send_sems, recv_sems)
    rows, width = x.shape
    slots, total = e.shape
    quarter = slots // tp_size
    others = range(1, tp_size)
    link.greet(link.low)

    own_up = pltpu.make_async_copy(wup, wup_all.at[link.tp], local_sems.at[0])
    own_dn = pltpu.make_async_copy(wdn, wdn_all.at[link.tp], local_sems.at[1])
    own_up.start()
    own_dn.start()
    bup_all[link.tp] = bup[...]
    length = len_ref[0]
    own_first = link.tp * rows
    position = lax.broadcasted_iota(jnp.int32, (1, rows), 1) + own_first
    live = (position < length).astype(F32)
    em[...] = (e[:, rows_at(own_first, rows, rows)].astype(F32) * live).astype(BF)
    ysend[...] = dot(em[...], x[...], 1, 0).astype(ysend.dtype)
    reduce = [
        link.send(ysend.at[place(link.ahead(k), quarter), :], yrecv.at[k - 1], (link.dp, link.ahead(k)))
        for k in others
    ]
    biases = [link.send(bup, bup_all.at[link.tp], (link.dp, link.ahead(k))) for k in others]
    q[...] = (dot(x[...], wq[...], 1, 0) + vec[0:1, :]).astype(BF)
    own_slots = place(link.tp, quarter)
    for copy in reduce:
        copy.wait()
    own_y = ysend[own_slots, :].astype(F32)
    for k in others:
        own_y = own_y + yrecv[k - 1].astype(F32)
    yb[own_slots, :] = own_y.astype(BF)
    share = [
        link.send(yb.at[own_slots, :], yb.at[own_slots, :], (link.dp, link.ahead(k))) for k in others
    ]
    gathers = [WeightGather(link, "up", wup, wup_all), WeightGather(link, "down", wdn, wdn_all)]
    for k in others:
        for gather in gathers:
            gather.across(k)
    row_live = (lax.broadcasted_iota(jnp.int32, (total, 128), 0) < length).astype(F32).astype(BF)
    ssum[...] = dot(e[...], row_live, 1, 0)
    for copy in share:
        copy.wait()
    for copy in biases:
        copy.wait()

    lane = lax.broadcasted_iota(jnp.int32, (1, PAIR), 1)
    first_half = (lane < HEAD).astype(F32)

    def project(weight, bias_row, blocks):
        full = dot(yb[...], weight[...], 1, 0)
        for p in range(PAIRS):
            cols = slice(p * PAIR, (p + 1) * PAIR)
            part = full[:, cols] + ssum[...] * vec[bias_row : bias_row + 1, cols]
            blocks[p, 0:slots, :] = (part * first_half).astype(BF)
            blocks[p, slots : 2 * slots, :] = (part * (1.0 - first_half)).astype(BF)

    project(wk, 1, kb)
    project(wv, 2, vb)

    block = min(256, rows)

    def attend(step, carry):
        p = lax.div(step, rows // block)
        here = place(lax.rem(step, rows // block), block)
        cols = place(p, PAIR)
        logits = dot(q[here, cols], kb[p], 1, 1) * 0.125
        halves = []
        for half in range(2):
            part = logits[:, half * slots : (half + 1) * slots]
            peak = jnp.max(part, axis=-1, keepdims=True)
            raised = jnp.exp(part - peak)
            halves.append((raised * (1.0 / jnp.sum(raised, axis=-1, keepdims=True))).astype(BF))
        both = jnp.concatenate(halves, axis=1)
        probs[p, here, :] = both
        mixed[here, cols] = dot(both, vb[p], 1, 0).astype(BF)
        return carry

    def advance(*ks):
        for k in ks:
            for gather in gathers:
                gather.advance(k)

    per_pair = rows // block
    lax.fori_loop(0, 2 * per_pair, attend, 0)
    advance(1)
    lax.fori_loop(2 * per_pair, 4 * per_pair, attend, 0)
    advance(2, 1)
    lax.fori_loop(4 * per_pair, 6 * per_pair, attend, 0)
    advance(3, 2, 1)

    def finish(step, carry):
        here = place(step, block)
        res = x[here, :].astype(F32) + dot(mixed[here, :], wo[...], 1, 0) + vec[3:4, :]
        center = res - jnp.mean(res, axis=-1, keepdims=True)
        inverse = lax.rsqrt(jnp.mean(center * center, axis=-1, keepdims=True) + 1e-05)
        xhat[here, :] = center * inverse
        rstd[here, :] = jnp.broadcast_to(inverse, (block, 128))
        return carry

    lax.fori_loop(0, rows // block, finish, 0)
    advance(3, 2, 3, 1, 2, 3)
    own_up.wait()
    own_dn.wait()


def front(mesh, lengths, vec, bup, x, wq, wk, wv, wo, wup, wdn, e):
    dp_size, tp_size = mesh.shape["dp"], mesh.shape["tp"]
    rows, width = x.shape
    slots = e.shape[0]
    vmem = pl.BlockSpec(memory_space=pltpu.VMEM)
    hbm = pl.BlockSpec(memory_space=pltpu.HBM)
    shape = jax.ShapeDtypeStruct
    return pl.pallas_call(
        functools.partial(front_kernel, dp_size, tp_size),
        out_shape=(
            shape((rows, width), F32),
            shape((rows, 128), F32),
            shape((rows, width), BF),
            shape((rows, width), BF),
            shape((PAIRS, rows, 2 * slots), BF),
            shape((PAIRS, 2 * slots, PAIR), BF),
            shape((PAIRS, 2 * slots, PAIR), BF),
            shape((slots, width), BF),
            shape((slots, 128), F32),
            shape((slots, rows), BF),
            shape((tp_size, 8, width), F32),
            shape((tp_size, *wup.shape), BF),
            shape((tp_size, *wdn.shape), BF),
        ),
        in_specs=[pl.BlockSpec(memory_space=pltpu.SMEM)] + [vmem] * 10,
        out_specs=tuple([vmem] * 11 + [hbm] * 2),
        scratch_shapes=[
            pltpu.VMEM((slots, width), BF),
            pltpu.VMEM((tp_size - 1, slots // tp_size, width), BF),
            pltpu.SemaphoreType.DMA((FRONT_SEMS,)),
            pltpu.SemaphoreType.DMA((FRONT_SEMS,)),
            pltpu.SemaphoreType.DMA((2,)),
        ],
        compiler_params=pltpu.CompilerParams(
            collective_id=0, has_side_effects=True, vmem_limit_bytes=VMEM_LIMIT
        ),
        name="front",
    )(lengths, vec, bup, x, wq, wk, wv, wo, wup, wdn, e)


BACK_SEMS = 160
VECTORS = 16


def add_rows(target, first, left, left_first, right, count):
    block = 96 if count % 96 == 0 else (48 if count % 48 == 0 else (32 if count % 32 == 0 else count))

    def step(i, carry):
        at = i * block
        total = (
            left[rows_at(left_first + at, block, 16), :].astype(F32)
            + right[rows_at(at, block, 16), :].astype(F32)
        )
        target[rows_at(first + at, block, 16), :] = total.astype(target.dtype)
        return carry

    lax.fori_loop(0, count // block, step, 0)


class Spread:
    def __init__(self, link, order, rows, acc, landing):
        self.link, self.acc, self.landing, self.rows = link, acc, landing, rows
        self.order = [b for b in order if b < link.low]
        self.inside = 0
        self.copy = None

    def _landing(self, i):
        first = sum(self.rows >> (j + 1) for j in range(i))
        return self.landing.at[pl.ds(first, self.rows >> (i + 1)), :]

    def start(self, i, source=None, loaded=False):
        if i == 0:
            self.source = None if loaded else source
        link, size = self.link, self.rows >> (i + 1)
        mine = link.bit(self.order[i])
        where, base = (source, 0) if i == 0 else (self.acc, self.inside)
        other = base + (1 - mine) * size
        self.copy = link.send(
            where.at[rows_at(other, size, 16), :], self._landing(i), link.partner(self.order[i])
        )
        if i > 0:
            self.inside = self.inside + mine * size

    def finish(self, i):
        source = self.source
        link, size = self.link, self.rows >> (i + 1)
        self.copy.wait()
        if i == 0:
            if source is None:
                add_rows(self.acc, 0, self.acc, 0, self._landing(0), size)
            else:
                add_rows(self.acc, 0, source, link.bit(self.order[0]) * size, self._landing(0), size)
        else:
            add_rows(self.acc, self.inside, self.acc, self.inside, self._landing(i), size)

    @property
    def piece(self):
        return self.rows >> len(self.order)

    @property
    def offset(self):
        return self.link.bit(self.order[0]) * (self.rows >> 1) + self.inside


class Collect:
    def __init__(self, link, order, offset, piece, region):
        self.link, self.offset, self.piece, self.region = link, offset, piece, region
        self.order = [b for b in order if b < link.low][::-1]
        self.copies = []
        self.stage = 0

    def start(self):
        size = self.piece << self.stage
        first = self.offset - lax.rem(self.offset, size)
        refs = self.region(first, size)
        peer = self.link.partner(self.order[self.stage])
        self.copies = [self.link.send(ref, ref, peer) for ref in refs]

    def finish(self):
        for copy in self.copies:
            copy.wait()
        self.stage += 1


def double_up(link, piece, landing):
    for i, b in enumerate(range(link.low, link.bits)):
        copy = link.send(piece, landing.at[i], link.partner(b))
        copy.wait()
        piece[...] = (piece[...].astype(F32) + landing[i].astype(F32)).astype(piece.dtype)


def back_kernel(
    dp_size,
    tp_size,
    len_ref,
    vec,
    part_vec,
    dnorm,
    xhat,
    rstd,
    x,
    q,
    mixed,
    probs,
    kb,
    vb,
    yb,
    ssum,
    em,
    wq,
    wk,
    wv,
    wo,
    gup,
    gdn,
    grad_in,
    gup_out,
    gdn_out,
    gq_out,
    go_out,
    gkv_out,
    seq_out,
    vec_out,
    dres,
    dmix,
    dq,
    dl,
    prob_slots,
    dpart,
    dland,
    dfull,
    up_acc,
    up_land,
    dn_acc,
    dn_land,
    up_zland,
    dn_zland,
    o_acc,
    o_land,
    q_acc,
    q_land,
    o_zland,
    q_zland,
    kv_send,
    kv_acc,
    kv_land,
    s_send,
    s_acc,
    s_land,
    vec_acc,
    vec_land,
    vec_z,
    wide_ff,
    wide_q,
    wide_kv,
    wide_s,
    wide_vec,
    send_sems,
    recv_sems,
    local_sems,
):
    link = Link(dp_size, tp_size, send_sems, recv_sems)
    rows, width = x.shape
    slots = yb.shape[0]
    others = range(1, tp_size)
    low = link.low
    first_load = pltpu.make_async_copy(dnorm, dres, local_sems.at[2 * tp_size])
    first_load.start()
    link.greet(link.bits)
    chunks = range(tp_size)
    up_order, dn_order = (0, 1, 2), (0, 2, 1)

    ups = [Spread(link, up_order, width, up_acc.at[c], up_land.at[c]) for c in chunks]
    dns = [Spread(link, dn_order, width, dn_acc.at[c], dn_land.at[c]) for c in chunks]
    half = width >> 1
    keep = rows_at(link.bit(0) * half, half, half)
    loads = []
    for c in chunks:
        ups[c].start(0, gup.at[c], loaded=True)
        dns[c].start(0, gdn.at[c], loaded=True)
        for n, (source, acc) in enumerate(((gup, up_acc), (gdn, dn_acc))):
            load = pltpu.make_async_copy(source.at[c, keep, :], acc.at[c], local_sems.at[2 * c + n])
            load.start()
            loads.append(load)

    block = min(256, rows)
    count = rows // block
    gain = vec[4:5, :]

    def norm_back(step, carry):
        g_gain, g_shift, g_out = carry
        here = place(step, block)
        grad, hat = dres[here, :], xhat[here, :]
        g_gain = g_gain + jnp.sum(grad * hat, axis=0, keepdims=True)
        g_shift = g_shift + jnp.sum(grad, axis=0, keepdims=True)
        scaled = grad * gain
        d_res = rstd[here, 0:1] * (
            scaled
            - jnp.mean(scaled, axis=-1, keepdims=True)
            - hat * jnp.mean(scaled * hat, axis=-1, keepdims=True)
        )
        dres[here, :] = d_res
        d_attn = d_res.astype(BF)
        dq[here, :] = d_attn
        g_out = g_out + jnp.sum(d_attn.astype(F32), axis=0, keepdims=True)
        return g_gain, g_shift, g_out

    zero = jnp.zeros((1, width), F32)
    first_load.wait()
    g_gain, g_shift, g_out = lax.fori_loop(0, count, norm_back, (zero, zero, zero))
    vec_acc[...] = part_vec[...]
    vec_acc[3:4, :] = g_out
    vec_acc[4:5, :] = g_gain
    vec_acc[5:6, :] = g_shift
    d_attn = dq

    def weight_grad(left, right, target):
        for m in range(3):
            cols = slice(m * (width // 3), (m + 1) * (width // 3))
            target[cols, :] = dot(left[:, cols], right[...], 0, 0).astype(BF)

    weight_grad(mixed, d_attn, go_out)
    spread_o = Spread(link, (0, 1, 2), width, o_acc, o_land)
    spread_o.start(0, go_out)
    dmix[...] = dot(d_attn[...], wo[...], 1, 1).astype(BF)

    for load in loads:
        load.wait()

    def spread_all(objs, i):
        for s in objs:
            s.finish(i)
        if i + 1 < low:
            for s in objs:
                s.start(i + 1)

    spread_all((ups[0], dns[0]), 0)

    own_half = lax.div(link.tp, 2)
    parity = lax.rem(link.tp, 2)
    lane_half = slots

    three = PAIRS // 2

    def pair_at(n):
        second = lax.div(n, three)
        which = (1 - own_half) * (1 - second) + own_half * second
        return which * three + lax.rem(n, three)

    def fetch(n):
        slot = lax.rem(n, 2)
        return pltpu.make_async_copy(
            probs.at[pair_at(n)], prob_slots.at[slot], local_sems.at[2 * tp_size + 1 + slot]
        )

    fetch(0).start()

    def attend_back(n):
        p = pair_at(n)
        cols = place(p, PAIR)

        @pl.when(n + 1 < PAIRS)
        def _():
            fetch(n + 1).start()

        fetch(n).wait()
        held = prob_slots.at[lax.rem(n, 2)]

        def part(step, carry):
            here = place(step, block)
            d_probs = dot(dmix[here, cols], vb[p], 1, 1)
            weights = held[here, :].astype(F32)
            halves = []
            for h in range(2):
                w = weights[:, h * slots : (h + 1) * slots]
                d = d_probs[:, h * slots : (h + 1) * slots]
                halves.append((w * (d - jnp.sum(w * d, axis=-1, keepdims=True))).astype(BF))
            both = jnp.concatenate(halves, axis=1)
            dl[here, :] = both
            dq[here, cols] = (dot(both, kb[p], 1, 0) * 0.125).astype(BF)
            return carry

        lax.fori_loop(0, count, part, 0)
        top, low_rows = rows_at(p * PAIR, HEAD, HEAD), rows_at(p * PAIR + HEAD, HEAD, HEAD)
        for n, total in enumerate(
            (dot(q[:, cols], dl[...], 0, 0) * 0.125, dot(dmix[:, cols], held[...], 0, 0))
        ):
            dpart[n, top, :] = total[:HEAD, :lane_half].astype(BF)
            dpart[n, low_rows, :] = total[HEAD:, lane_half:].astype(BF)

    def attend_half(first):
        def one(n, carry):
            attend_back(n)
            return carry

        lax.fori_loop(first, first + three, one, 0)

    attend_half(0)
    owned = width // tp_size

    def block_of(peer):
        return dpart.at[:, rows_at(peer * owned, owned, 64), :]

    d_copies = []
    for j in range(2):
        peer = 2 * (1 - own_half) + lax.rem(parity + j, 2)
        d_copies.append(link.send(block_of(peer), dland.at[j], (link.dp, peer)))
    spread_o.finish(0)
    if low > 1:
        spread_o.start(1)
    spread_all((ups[1], dns[1]), 0)
    spread_all((ups[0], dns[0]), 1)
    attend_half(three)
    peer = 2 * own_half + (1 - parity)
    d_copies.append(link.send(block_of(peer), dland.at[2], (link.dp, peer)))
    spread_all((ups[2], dns[2]), 0)
    spread_all((ups[1], dns[1]), 1)

    weight_grad(x, dq, gq_out)
    spread_q = Spread(link, (0, 2, 1), width, q_acc, q_land)
    spread_q.start(0, gq_out)

    for copy in d_copies:
        copy.wait()
    own_block = rows_at(link.tp * owned, owned, 64)
    for n in range(2):
        total = dpart[n, own_block, :].astype(F32)
        for j in range(tp_size - 1):
            total = total + dland[j, n].astype(F32)
        dfull[n, own_block, :] = total.astype(BF)
    d_share = [
        link.send(dfull.at[:, own_block, :], dfull.at[:, own_block, :], (link.dp, link.ahead(k)))
        for k in others
    ]
    for n in range(2):
        kv_send[n * owned : (n + 1) * owned, :] = dot(dfull[n, own_block, :], yb[...], 1, 0).astype(BF)
    spread_kv = Spread(link, (0, 1, 2), 2 * owned, kv_acc, kv_land)
    spread_kv.start(0, kv_send)
    spread_all((ups[3], dns[3]), 0)
    spread_all((ups[2], dns[2]), 1)
    vec_acc[0:1, :] = jnp.sum(dq[...].astype(F32), axis=0, keepdims=True)

    def input_grad(step, carry):
        here = place(step, block)
        dres[here, :] += dot(dq[here, :], wq[...], 1, 1)
        return carry

    lax.fori_loop(0, count, input_grad, 0)
    spread_o.finish(1) if low > 1 else None
    if low > 2:
        spread_o.start(2)
    spread_q.finish(0)
    if low > 1:
        spread_q.start(1)
    for copy in d_share:
        copy.wait()
    backs = dot(wk[...], dfull[0], 1, 0) + dot(wv[...], dfull[1], 1, 0)
    back = backs.T.astype(BF)
    small = vec[0:8, :].astype(BF)
    bias_row = dot(small, dfull[0], 1, 0)[1:2, :] + dot(small, dfull[1], 1, 0)[2:3, :]
    bias_column = jnp.broadcast_to(bias_row, (128, slots)).T[:, 0:1]
    position = lax.broadcasted_iota(jnp.int32, (1, rows), 1) + link.tp * rows
    live = (position < len_ref[0]).astype(F32)
    s_send[...] = ((dot(back, x[...], 1, 1) + bias_column) * live).astype(BF)
    spread_s = Spread(link, (0, 2, 1), slots, s_acc, s_land)
    spread_s.start(0, s_send)
    column = ssum[...].T[0:8, :]
    column_b = column.astype(BF)
    column_low = (column - column_b.astype(F32)).astype(BF)
    for n in range(2):
        total = dot(column_b, dfull[n], 1, 1) + dot(column_low, dfull[n], 1, 1)
        vec_acc[1 + n : 2 + n, :] = total[0:1, :] * (1.0 / tp_size)
    spread_all((ups[3], dns[3]), 1)

    def input_grad_last(step, carry):
        here = place(step, block)
        grad_in[here, :] = (dres[here, :] + dot(em[:, here], back, 0, 0)).astype(BF)
        return carry

    lax.fori_loop(0, count, input_grad_last, 0)

    def vec_step(b):
        copy = link.send(vec_acc, vec_land.at[b], link.partner(b))
        return copy

    tail = [spread_kv, spread_s]
    for i in range(low):
        copy = vec_step(i)
        for s in tail:
            s.finish(i)
            if i + 1 < low:
                s.start(i + 1)
        if i == 0:
            spread_all((ups[0], dns[0], ups[1], dns[1]), 2) if low > 2 else None
            if low > 1:
                spread_q.finish(1)
            if low > 2:
                spread_q.start(2)
                spread_o.finish(2)
        if i == 1:
            spread_all((ups[2], dns[2], ups[3], dns[3]), 2) if low > 2 else None
            if low > 2:
                spread_q.finish(2)
        copy.wait()
        vec_acc[...] = vec_acc[...] + vec_land[i]
    for b in range(low, link.bits):
        copy = vec_step(b)
        copy.wait()
        vec_acc[...] = vec_acc[...] + vec_land[b]

    vec_z[link.tp] = vec_acc[...]
    vec_copies = [link.send(vec_acc, vec_z.at[link.tp], (link.dp, link.ahead(k))) for k in others]

    ff_piece = ups[0].piece
    ff = []
    for accs, spreads, zland in ((up_acc, ups, up_zland), (dn_acc, dns, dn_zland)):
        inside = spreads[0].inside
        for k in others:
            source = accs.at[link.ahead(k), rows_at(inside, ff_piece, 16), :]
            ff.append(link.send(source, zland.at[k - 1], (link.dp, link.ahead(k))))
    lanes = 2
    deep = tp_size // lanes
    q_rows, q_cols = spread_q.piece // deep, width // lanes

    def quarter(first, t):
        return (
            rows_at(first + lax.div(t, lanes) * q_rows, q_rows, 16),
            pl.ds(pl.multiple_of(lax.rem(t, lanes) * q_cols, 128), q_cols),
        )

    quarters = []
    for spread, zland in ((spread_q, q_zland), (spread_o, o_zland)):
        for k in others:
            r, c = quarter(spread.inside, link.ahead(k))
            quarters.append(link.send(spread.acc.at[r, c], zland.at[k - 1], (link.dp, link.ahead(k))))

    kv_rows = rows_at(spread_kv.offset, spread_kv.piece, 16)
    s_rows = rows_at(spread_s.offset, spread_s.piece, 16)
    z_copies = []
    for spread, at, out, wide in (
        (spread_kv, kv_rows, gkv_out, wide_kv),
        (spread_s, s_rows, seq_out, wide_s),
    ):
        out[link.tp, at, :] = spread.acc[rows_at(spread.inside, spread.piece, 16), :]
        double_up(link, out.at[link.tp, at, :], wide)
        for k in others:
            z_copies.append(
                link.send(out.at[link.tp, at, :], out.at[link.tp, at, :], (link.dp, link.ahead(k)))
            )

    for copy in quarters:
        copy.wait()
    back_quarters = []
    for n, (spread, zland, out) in enumerate(((spread_q, q_zland, gq_out), (spread_o, o_zland, go_out))):
        r, c = quarter(spread.inside, link.tp)
        total = spread.acc[r, c].astype(F32)
        for k in others:
            total = total + zland[k - 1].astype(F32)
        r_out, _ = quarter(spread.offset, link.tp)
        out[r_out, c] = total.astype(BF)
        region = out.at[r_out, c]
        double_up(link, region, wide_q.at[n])
        for k in others:
            back_quarters.append(link.send(region, region, (link.dp, link.ahead(k))))

    for copy in ff:
        copy.wait()
    collects = []
    for n, (accs, spreads, zland, out, order) in enumerate(
        ((up_acc, ups, up_zland, gup_out, up_order), (dn_acc, dns, dn_zland, gdn_out, dn_order))
    ):
        inside, offset = spreads[0].inside, spreads[0].offset
        total = accs[link.tp, rows_at(inside, ff_piece, 16), :].astype(F32)
        for k in others:
            total = total + zland[k - 1].astype(F32)
        own = rows_at(offset, ff_piece, 16)
        out[own, :] = total.astype(BF)
        double_up(link, out.at[own, :], wide_ff.at[n])
        collects.append(
            Collect(
                link, order, offset, ff_piece,
                lambda first, size, out=out: [out.at[rows_at(first, size, 16), :]],
            )
        )
        collects[-1].start()
    for copy in z_copies:
        copy.wait()
    for spread, out, order in ((spread_kv, gkv_out, (0, 1, 2)), (spread_s, seq_out, (0, 2, 1))):
        collects.append(
            Collect(
                link, order, spread.offset, spread.piece,
                lambda first, size, out=out: [out.at[:, rows_at(first, size, 16), :]],
            )
        )
        collects[-1].start()
    for copy in back_quarters:
        copy.wait()
    for spread, out, order in ((spread_q, gq_out, (0, 2, 1)), (spread_o, go_out, (0, 1, 2))):
        collects.append(
            Collect(
                link, order, spread.offset, spread.piece,
                lambda first, size, out=out: [out.at[rows_at(first, size, 16), :]],
            )
        )
        collects[-1].start()
    for i in range(low):
        for collect in collects:
            collect.finish()
            if i + 1 < low:
                collect.start()
    for copy in vec_copies:
        copy.wait()
    total = vec_z[0]
    for t in range(1, tp_size):
        total = total + vec_z[t]
    vec_out[...] = total


def back(mesh, lengths, vec, part_vec, dnorm, xhat, rstd, x, q, mixed, probs, kb, vb, yb, ssum, em, wq, wk, wv, wo, gup, gdn):
    dp_size, tp_size = mesh.shape["dp"], mesh.shape["tp"]
    bits = dp_size.bit_length() - 1
    low = min(3, bits)
    wide = max(1, bits - low)
    rows, width = x.shape
    slots = yb.shape[0]
    owned = width // tp_size
    others = tp_size - 1
    vmem = pl.BlockSpec(memory_space=pltpu.VMEM)
    hbm = pl.BlockSpec(memory_space=pltpu.HBM)
    shape = jax.ShapeDtypeStruct

    def landing(total):
        return sum(total >> (i + 1) for i in range(low))

    def buf(*dims, dtype=BF):
        return pltpu.VMEM(dims, dtype)

    ff_piece, kv_piece, s_piece = width >> low, 2 * owned >> low, slots >> low
    return pl.pallas_call(
        functools.partial(back_kernel, dp_size, tp_size),
        out_shape=(
            shape((rows, width), BF),
            shape((width, width), BF),
            shape((width, width), BF),
            shape((width, width), BF),
            shape((width, width), BF),
            shape((tp_size, 2 * owned, width), BF),
            shape((tp_size, slots, rows), BF),
            shape((VECTORS, width), F32),
        ),
        in_specs=[pl.BlockSpec(memory_space=pltpu.SMEM)] + [vmem] * 2 + [hbm] + [vmem] * 5 + [hbm] + [vmem] * 9 + [hbm] * 2,
        out_specs=tuple([vmem] * 8),
        scratch_shapes=[
            buf(rows, width, dtype=F32),
            buf(rows, width),
            buf(rows, width),
            buf(rows, 2 * slots),
            buf(2, rows, 2 * slots),
            buf(2, width, slots),
            buf(others, 2, owned, slots),
            buf(2, width, slots),
            buf(tp_size, width // 2, width),
            buf(tp_size, landing(width), width),
            buf(tp_size, width // 2, width),
            buf(tp_size, landing(width), width),
            buf(others, ff_piece, width),
            buf(others, ff_piece, width),
            buf(width // 2, width),
            buf(landing(width), width),
            buf(width // 2, width),
            buf(landing(width), width),
            buf(others, ff_piece // (tp_size // 2), width // 2),
            buf(others, ff_piece // (tp_size // 2), width // 2),
            buf(2 * owned, width),
            buf(owned, width),
            buf(landing(2 * owned), width),
            buf(slots, rows),
            buf(slots // 2, rows),
            buf(landing(slots), rows),
            buf(VECTORS, width, dtype=F32),
            buf(max(1, bits), VECTORS, width, dtype=F32),
            buf(tp_size, VECTORS, width, dtype=F32),
            buf(2, wide, ff_piece, width),
            buf(2, wide, ff_piece // (tp_size // 2), width // 2),
            buf(wide, kv_piece, width),
            buf(wide, s_piece, rows),
            buf(wide, VECTORS, width, dtype=F32),
            pltpu.SemaphoreType.DMA((BACK_SEMS,)),
            pltpu.SemaphoreType.DMA((BACK_SEMS,)),
            pltpu.SemaphoreType.DMA((2 * tp_size + 3,)),
        ],
        compiler_params=pltpu.CompilerParams(
            collective_id=1, has_side_effects=True, vmem_limit_bytes=VMEM_LIMIT
        ),
        name="back",
    )(lengths, vec, part_vec, dnorm, xhat, rstd, x, q, mixed, probs, kb, vb, yb, ssum, em, wq, wk, wv, wo, gup, gdn)


def finish_kernel(
    tp_size, gup, gdn, gq, go, gkv, seq, vec,
    o_up, o_dn, o_q, o_o, o_k, o_v, o_seq, *rest,
):
    vectors, (in_up, in_dn, in_q, in_o, in_kv, in_seq, f_up, f_dn, f_q, f_o, f_k, f_v, f_seq, turn, in_sems, out_sems) = rest[:10], rest[10:]
    pairs = [(gq, in_q), (go, in_o), (gup, in_up), (gdn, in_dn), (gkv, in_kv), (seq, in_seq)]
    loads = []
    for n, (source, target) in enumerate(pairs):
        loads.append(pltpu.make_async_copy(source, target, in_sems.at[n]))
        loads[-1].start()
    stores = []

    def put(staged, out):
        copy = pltpu.make_async_copy(staged, out, out_sems.at[len(stores)])
        copy.start()
        stores.append(copy)

    for n, row in enumerate((0, 1, 2, 3, 4, 5, 6, 7, 8)):
        vectors[n][...] = vec[row, :]
    vectors[9][...] = vec[pl.ds(9 + lax.axis_index("tp"), 1), :][0]
    width = gq.shape[0]
    for n, (narrow, wide, out) in enumerate(
        ((in_q, f_q, o_q), (in_o, f_o, o_o), (in_up, f_up, o_up), (in_dn, f_dn, o_dn))
    ):
        loads[n].wait()
        wide[...] = narrow[...].astype(F32)
        put(wide, out)
    loads[4].wait()
    owned = width // tp_size
    for n, (wide, out) in enumerate(((f_k, o_k), (f_v, o_v))):
        for c in range(tp_size):
            turn[c * owned : (c + 1) * owned, :] = in_kv[c, n * owned : (n + 1) * owned, :]
        for c in range(3):
            cols = slice(c * (width // 3), (c + 1) * (width // 3))
            wide[:, cols] = turn[cols, :].astype(F32).T
        put(wide, out)
    loads[5].wait()
    rows = in_seq.shape[2]
    for c in range(tp_size):
        f_seq[:, c * rows : (c + 1) * rows] = in_seq[c].astype(F32)
    put(f_seq, o_seq)
    for copy in stores:
        copy.wait()


def finish(tp_size, gup, gdn, gq, go, gkv, seq, vec):
    width = gq.shape[0]
    _, slots, rows = seq.shape
    square, flat = (width, width), (slots, tp_size * rows)
    vmem = pl.BlockSpec(memory_space=pltpu.VMEM)
    hbm = pl.BlockSpec(memory_space=pltpu.HBM)
    shape = jax.ShapeDtypeStruct
    return pl.pallas_call(
        functools.partial(finish_kernel, tp_size),
        out_shape=tuple([shape(square, F32)] * 6 + [shape(flat, F32)] + [shape((width,), F32)] * 10),
        in_specs=[hbm] * 6 + [vmem],
        out_specs=tuple([hbm] * 7 + [vmem] * 10),
        scratch_shapes=[pltpu.VMEM(square, BF)] * 4
        + [pltpu.VMEM(gkv.shape, BF), pltpu.VMEM(seq.shape, BF)]
        + [pltpu.VMEM(square, F32)] * 6
        + [pltpu.VMEM(flat, F32), pltpu.VMEM(square, BF)]
        + [pltpu.SemaphoreType.DMA((6,)), pltpu.SemaphoreType.DMA((7,))],
        compiler_params=pltpu.CompilerParams(vmem_limit_bytes=VMEM_LIMIT),
        name="finish",
    )(gup, gdn, gq, go, gkv, seq, vec)


def on_device(
    mesh,
    layer_in,
    out_grad,
    lengths,
    w_query,
    b_query,
    w_key,
    b_key,
    w_value,
    b_value,
    w_out,
    b_out,
    seq_proj,
    attn_gain,
    attn_shift,
    w_up,
    b_up,
    w_down,
    b_down,
    ffn_gain,
    ffn_shift,
):
    row_count, width = layer_in.shape
    tp_size = mesh.shape["tp"]
    vec = jnp.stack(
        [b_query, b_key, b_value, b_out, attn_gain, attn_shift, b_down, ffn_gain, ffn_shift] + [b_query] * 7
    ).astype(F32)
    bup = jnp.broadcast_to(b_up.astype(F32)[None, :], (8, width))
    xhat, rstd, mixed, queries, probs, kb, vb, folded, ssum, own_proj, bup_all, up_all, down_all = front(
        mesh, lengths, vec, bup, layer_in, w_query, w_key, w_value, w_out, w_up, w_down, seq_proj
    )
    normed = xhat * attn_gain.astype(F32) + attn_shift.astype(F32)
    normed_b = normed.astype(BF)
    pre_act = jnp.concatenate([dot(normed_b, up_all[c], 1, 0) + bup_all[c, 0:1] for c in range(tp_size)], axis=1)
    down_flat = down_all.reshape(-1, width)
    hidden_act, gelu_pull = jax.vjp(exact_gelu, pre_act)
    hidden_b = hidden_act.astype(BF)
    branch = dot(hidden_b, down_flat, 1, 0) + b_down.astype(F32)
    res_two = normed + branch
    final, norm_two_pull = jax.vjp(
        layer_norm, res_two, ffn_gain.astype(F32), ffn_shift.astype(F32)
    )
    layer_out = final.astype(BF)
    d_res_two, g_ffn_gain, g_ffn_shift = norm_two_pull(out_grad.astype(F32))
    d_branch = d_res_two.astype(BF)
    g_b_down = jnp.sum(d_branch.astype(F32), axis=0)
    g_down = dot(hidden_b, d_branch, 0, 0).astype(BF).reshape(tp_size, width, width)
    (d_hidden,) = gelu_pull(dot(d_branch, down_flat, 1, 1))
    d_pre = d_hidden.astype(BF)
    g_b_up = jnp.sum(d_pre.astype(F32), axis=0)
    parts = [d_pre[:, c * width : (c + 1) * width] for c in range(tp_size)]
    g_up = jnp.stack([dot(normed_b, part, 0, 0).astype(BF) for part in parts])
    d_normed = d_res_two + sum(dot(part, up_all[c], 1, 1) for c, part in enumerate(parts))
    none = jnp.zeros((width,), F32)
    part_vec = jnp.stack(
        [none] * 6 + [g_ffn_gain, g_ffn_shift, g_b_down, *g_b_up.reshape(tp_size, width)] + [none] * (7 - tp_size)
    )
    grad_in, g_up, g_down, g_q, g_o, g_kv, g_seq, vec_sum = back(
        mesh, lengths, vec, part_vec, d_normed, xhat, rstd, layer_in, queries, mixed, probs, kb, vb, folded, ssum,
        own_proj, w_query, w_key, w_value, w_out, g_up, g_down
    )
    (
        g_w_up, g_w_down, g_w_query, g_w_out, g_w_key, g_w_value, g_seq_proj,
        g_b_query, g_b_key, g_b_value, g_b_out, g_attn_gain, g_attn_shift, g_ffn_gain, g_ffn_shift, g_b_down, g_b_up,
    ) = finish(tp_size, g_up, g_down, g_q, g_o, g_kv, g_seq, vec_sum)
    return (
        layer_out,
        grad_in,
        g_w_query,
        g_b_query,
        g_w_key,
        g_b_key,
        g_w_value,
        g_b_value,
        g_w_out,
        g_b_out,
        g_seq_proj,
        g_attn_gain,
        g_attn_shift,
        g_w_up,
        g_b_up,
        g_w_down,
        g_b_down,
        g_ffn_gain,
        g_ffn_shift,
    )


def solution(mesh):
    in_specs = (
        P(("dp", "tp"), None),
        P(("dp", "tp"), None),
        P("dp"),
        *([P()] * 11),
        P(None, "tp"),
        P("tp"),
        P("tp", None),
        P(),
        P(),
        P(),
    )
    out_specs = (
        P(("dp", "tp"), None),
        P(("dp", "tp"), None),
        *([P()] * 11),
        P(None, "tp"),
        P("tp"),
        P("tp", None),
        P(),
        P(),
        P(),
    )
    return jax.shard_map(
        functools.partial(on_device, mesh), mesh=mesh, in_specs=in_specs, out_specs=out_specs, check_vma=False
    )
```

```python
import functools

import jax
import jax.numpy as jnp
from jax import lax
from jax.experimental import pallas as pl
from jax.experimental.pallas import tpu as pltpu
from jax.sharding import PartitionSpec as P

HEADS = 12
HEAD = 64
PAIRS = HEADS // 2
PAIR = 2 * HEAD
BF = jnp.bfloat16
F32 = jnp.float32
MESH = pl.DeviceIdType.MESH
VMEM_LIMIT = 67_043_328


def dot(left, right, left_dim, right_dim):
    return lax.dot_general(
        left, right, (((left_dim,), (right_dim,)), ((), ())), preferred_element_type=F32
    )


def place(index, size):
    return pl.ds(pl.multiple_of(index * size, size), size)


def rows_at(first, size, multiple):
    return pl.ds(pl.multiple_of(first, multiple), size)


class Link:
    def __init__(self, dp_size, tp_size, send_sems, recv_sems):
        self.dp_size, self.tp_size = dp_size, tp_size
        self.dp, self.tp = lax.axis_index("dp"), lax.axis_index("tp")
        self.bits = dp_size.bit_length() - 1
        self.low = min(3, self.bits)
        self.send_sems, self.recv_sems = send_sems, recv_sems
        self.used = 0

    def bit(self, b):
        return lax.rem(lax.div(self.dp, 1 << b), 2)

    def partner(self, b):
        return (self.dp + (1 - 2 * self.bit(b)) * (1 << b), self.tp)

    def ahead(self, k):
        return lax.rem(self.tp + k, self.tp_size)

    def behind(self, k):
        return lax.rem(self.tp + self.tp_size - k, self.tp_size)

    def greet(self, dp_bits):
        barrier = pltpu.get_barrier_semaphore()
        peers = [(self.dp, self.ahead(k)) for k in range(1, self.tp_size)]
        peers += [self.partner(b) for b in range(dp_bits)]
        for peer in peers:
            pl.semaphore_signal(barrier, inc=1, device_id=peer, device_id_type=MESH)
        pl.semaphore_wait(barrier, len(peers))

    def take(self, count):
        first = self.used
        self.used += count
        assert self.used <= self.send_sems.shape[0]
        return first

    def remote(self, slot, source, target, device):
        return pltpu.make_async_remote_copy(
            src_ref=source,
            dst_ref=target,
            send_sem=self.send_sems.at[slot],
            recv_sem=self.recv_sems.at[slot],
            device_id=device,
            device_id_type=MESH,
        )

    def send(self, source, target, device):
        copy = self.remote(self.take(1), source, target, device)
        copy.start()
        return copy


FRONT_SEMS = 64
VECTORS = 16


def gather_order(name):
    return (1, 2, 0) if name == "up" else (2, 1, 0)


class WeightGather:
    def __init__(self, link, name, shard, whole):
        self.link, self.shard, self.whole = link, shard, whole
        self.rows = shard.shape[0]
        self.order = [b for b in gather_order(name) if b < link.low]
        self.piece = self.rows >> len(self.order)
        offset, size = 0, self.piece
        for b in self.order:
            offset = offset + link.bit(b) * size
            size *= 2
        self.offset = offset
        self.step = {}
        self.waiting = {}

    def across(self, k):
        link = self.link
        rows = rows_at(self.offset, self.piece, self.piece)
        self.waiting[k] = link.send(
            self.shard.at[rows, :], self.whole.at[link.tp, rows, :], (link.dp, link.ahead(k))
        )
        self.step[k] = 0

    def advance(self, k):
        link, done = self.link, self.step[k]
        if done > len(self.order):
            return
        self.waiting[k].wait()
        self.step[k] = done + 1
        if done == len(self.order):
            return
        size = self.piece << done
        first = self.offset - lax.rem(self.offset, size)
        rows = rows_at(first, size, self.piece)
        region = self.whole.at[link.behind(k), rows, :]
        self.waiting[k] = link.send(region, region, link.partner(self.order[done]))


def front_kernel(
    dp_size,
    tp_size,
    len_ref,
    x,
    wq,
    wk,
    wv,
    wo,
    wup,
    wdn,
    e,
    *rest,
):
    names, b_up, rest = rest[:9], rest[9], rest[10:]
    front_body(dp_size, tp_size, len_ref, x, wq, wk, wv, wo, wup, wdn, e, names, b_up, *rest)


def front_body(
    dp_size,
    tp_size,
    len_ref,
    x,
    wq,
    wk,
    wv,
    wo,
    wup,
    wdn,
    e,
    vectors,
    b_up,
    vec,
    xhat,
    rstd,
    mixed,
    q,
    probs,
    kb,
    vb,
    yb,
    ssum,
    em,
    bup_all,
    wup_all,
    wdn_all,
    bup,
    ysend,
    yrecv,
    send_sems,
    recv_sems,
    local_sems,
):
    link = Link(dp_size, tp_size, send_sems, recv_sems)
    rows, width = x.shape
    slots, total = e.shape
    quarter = slots // tp_size
    others = range(1, tp_size)
    link.greet(link.low)

    own_up = pltpu.make_async_copy(wup, wup_all.at[link.tp], local_sems.at[0])
    own_dn = pltpu.make_async_copy(wdn, wdn_all.at[link.tp], local_sems.at[1])
    own_up.start()
    own_dn.start()
    vec[...] = jnp.zeros_like(vec)
    for n, vector in enumerate(vectors):
        vec[n : n + 1, :] = vector[...].astype(F32).reshape(1, width)
    bup[...] = jnp.broadcast_to(b_up[...].astype(F32).reshape(1, width), bup.shape)
    bup_all[link.tp] = bup[...]
    length = len_ref[0]
    own_first = link.tp * rows
    position = lax.broadcasted_iota(jnp.int32, (1, rows), 1) + own_first
    live = (position < length).astype(F32)
    em[...] = (e[:, rows_at(own_first, rows, rows)].astype(F32) * live).astype(BF)
    ysend[...] = dot(em[...], x[...], 1, 0).astype(ysend.dtype)
    reduce = [
        link.send(ysend.at[place(link.ahead(k), quarter), :], yrecv.at[k - 1], (link.dp, link.ahead(k)))
        for k in others
    ]
    biases = [link.send(bup, bup_all.at[link.tp], (link.dp, link.ahead(k))) for k in others]
    q[...] = (dot(x[...], wq[...], 1, 0) + vec[0:1, :]).astype(BF)
    own_slots = place(link.tp, quarter)
    for copy in reduce:
        copy.wait()
    own_y = ysend[own_slots, :].astype(F32)
    for k in others:
        own_y = own_y + yrecv[k - 1].astype(F32)
    yb[own_slots, :] = own_y.astype(BF)
    share = [
        link.send(yb.at[own_slots, :], yb.at[own_slots, :], (link.dp, link.ahead(k))) for k in others
    ]
    gathers = [WeightGather(link, "up", wup, wup_all), WeightGather(link, "down", wdn, wdn_all)]
    for k in others:
        for gather in gathers:
            gather.across(k)
    row_live = (lax.broadcasted_iota(jnp.int32, (total, 128), 0) < length).astype(F32).astype(BF)
    ssum[...] = dot(e[...], row_live, 1, 0)
    for copy in share:
        copy.wait()
    for copy in biases:
        copy.wait()

    lane = lax.broadcasted_iota(jnp.int32, (1, PAIR), 1)
    first_half = (lane < HEAD).astype(F32)

    def project(weight, bias_row, blocks):
        full = dot(yb[...], weight[...], 1, 0)
        for p in range(PAIRS):
            cols = slice(p * PAIR, (p + 1) * PAIR)
            part = full[:, cols] + ssum[...] * vec[bias_row : bias_row + 1, cols]
            blocks[p, 0:slots, :] = (part * first_half).astype(BF)
            blocks[p, slots : 2 * slots, :] = (part * (1.0 - first_half)).astype(BF)

    project(wk, 1, kb)
    project(wv, 2, vb)

    block = min(256, rows)

    def attend(step, carry):
        p = lax.div(step, rows // block)
        here = place(lax.rem(step, rows // block), block)
        cols = place(p, PAIR)
        logits = dot(q[here, cols], kb[p], 1, 1) * 0.125
        halves = []
        for half in range(2):
            part = logits[:, half * slots : (half + 1) * slots]
            peak = jnp.max(part, axis=-1, keepdims=True)
            raised = jnp.exp(part - peak)
            halves.append((raised * (1.0 / jnp.sum(raised, axis=-1, keepdims=True))).astype(BF))
        both = jnp.concatenate(halves, axis=1)
        probs[p, here, :] = both
        mixed[here, cols] = dot(both, vb[p], 1, 0).astype(BF)
        return carry

    def advance(*ks):
        for k in ks:
            for gather in gathers:
                gather.advance(k)

    per_pair = rows // block
    lax.fori_loop(0, 2 * per_pair, attend, 0)
    advance(1)
    lax.fori_loop(2 * per_pair, 4 * per_pair, attend, 0)
    advance(2, 1)
    lax.fori_loop(4 * per_pair, 6 * per_pair, attend, 0)
    advance(3, 2, 1)

    def finish(step, carry):
        here = place(step, block)
        res = x[here, :].astype(F32) + dot(mixed[here, :], wo[...], 1, 0) + vec[3:4, :]
        center = res - jnp.mean(res, axis=-1, keepdims=True)
        inverse = lax.rsqrt(jnp.mean(center * center, axis=-1, keepdims=True) + 1e-05)
        xhat[here, :] = center * inverse
        rstd[here, :] = jnp.broadcast_to(inverse, (block, 128))
        return carry

    lax.fori_loop(0, rows // block, finish, 0)
    advance(3, 2, 3, 1, 2, 3)
    own_up.wait()
    own_dn.wait()


def front(mesh, lengths, x, wq, wk, wv, wo, wup, wdn, e, vectors, b_up):
    dp_size, tp_size = mesh.shape["dp"], mesh.shape["tp"]
    rows, width = x.shape
    slots = e.shape[0]
    vmem = pl.BlockSpec(memory_space=pltpu.VMEM)
    hbm = pl.BlockSpec(memory_space=pltpu.HBM)
    shape = jax.ShapeDtypeStruct
    return pl.pallas_call(
        functools.partial(front_kernel, dp_size, tp_size),
        out_shape=(
            shape((VECTORS, width), F32),
            shape((rows, width), F32),
            shape((rows, 128), F32),
            shape((rows, width), BF),
            shape((rows, width), BF),
            shape((PAIRS, rows, 2 * slots), BF),
            shape((PAIRS, 2 * slots, PAIR), BF),
            shape((PAIRS, 2 * slots, PAIR), BF),
            shape((slots, width), BF),
            shape((slots, 128), F32),
            shape((slots, rows), BF),
            shape((tp_size, 8, width), F32),
            shape((tp_size, *wup.shape), BF),
            shape((tp_size, *wdn.shape), BF),
        ),
        in_specs=[pl.BlockSpec(memory_space=pltpu.SMEM)] + [vmem] * (9 + len(vectors)),
        out_specs=tuple([vmem] * 12 + [hbm] * 2),
        scratch_shapes=[
            pltpu.VMEM((8, width), F32),
            pltpu.VMEM((slots, width), BF),
            pltpu.VMEM((tp_size - 1, slots // tp_size, width), BF),
            pltpu.SemaphoreType.DMA((FRONT_SEMS,)),
            pltpu.SemaphoreType.DMA((FRONT_SEMS,)),
            pltpu.SemaphoreType.DMA((2,)),
        ],
        compiler_params=pltpu.CompilerParams(
            collective_id=0, has_side_effects=True, vmem_limit_bytes=VMEM_LIMIT
        ),
        name="front",
    )(lengths, x, wq, wk, wv, wo, wup, wdn, e, *vectors, b_up)


BACK_SEMS = 128
VECTORS = 16


def add_rows(target, first, left, left_first, right, count):
    block = 96 if count % 96 == 0 else (48 if count % 48 == 0 else (32 if count % 32 == 0 else count))

    def step(i, carry):
        at = i * block
        total = (
            left[rows_at(left_first + at, block, 16), :].astype(F32)
            + right[rows_at(at, block, 16), :].astype(F32)
        )
        target[rows_at(first + at, block, 16), :] = total.astype(target.dtype)
        return carry

    lax.fori_loop(0, count // block, step, 0)


class Spread:
    def __init__(self, link, order, rows, source, acc, landing):
        self.link, self.rows, self.source, self.acc, self.landing = link, rows, source, acc, landing
        self.order = [b for b in order if b < link.low]
        self.stages = len(self.order)
        self.slot = link.take(self.stages)
        self.piece = rows >> self.stages

    def inside(self, i):
        first = 0
        for j in range(1, i + 1):
            first = first + self.link.bit(self.order[j]) * (self.rows >> (j + 1))
        return first

    def kept(self):
        return rows_at(self.inside(self.stages - 1), self.piece, 16)

    def offset(self):
        return self.link.bit(self.order[0]) * (self.rows >> 1) + self.inside(self.stages - 1)

    def landed(self, i):
        first = sum(self.rows >> (j + 1) for j in range(i))
        return self.landing.at[pl.ds(first, self.rows >> (i + 1)), :]

    def copy(self, i):
        link, size = self.link, self.rows >> (i + 1)
        where, base = (self.source, 0) if i == 0 else (self.acc, self.inside(i - 1))
        other = base + (1 - link.bit(self.order[i])) * size
        return link.remote(
            self.slot + i, where.at[rows_at(other, size, 16), :], self.landed(i), link.partner(self.order[i])
        )

    def start(self, i):
        self.copy(i).start()

    def finish(self, i):
        size = self.rows >> (i + 1)
        self.copy(i).wait()
        if i == 0:
            add_rows(self.acc, 0, self.source, self.link.bit(self.order[0]) * size, self.landed(0), size)
        else:
            at = self.inside(i)
            add_rows(self.acc, at, self.acc, at, self.landed(i), size)

    def steps(self):
        yield lambda: self.start(0)
        for i in range(1, self.stages):

            def step(i=i):
                self.finish(i - 1)
                self.start(i)

            yield step


class Collect:
    def __init__(self, link, order, offset, piece, region):
        self.link, self.offset, self.piece, self.region = link, offset, piece, region
        self.order = [b for b in order if b < link.low][::-1]
        self.slot = link.take(len(self.order))

    def copy(self, i):
        size = self.piece << i
        first = self.offset()
        first = first - lax.rem(first, size)
        ref = self.region(first, size)
        return self.link.remote(self.slot + i, ref, ref, self.link.partner(self.order[i]))

    def steps(self):
        yield lambda: self.copy(0).start()
        for i in range(1, len(self.order)):

            def step(i=i):
                self.copy(i - 1).wait()
                self.copy(i).start()

            yield step
        yield lambda: self.copy(len(self.order) - 1).wait()


class Widen:
    def __init__(self, link, landing):
        self.link, self.landing = link, landing
        self.slot = link.take(max(0, link.bits - link.low))

    def run(self, piece):
        link = self.link
        for i, b in enumerate(range(link.low, link.bits)):
            copy = link.remote(self.slot + i, piece, self.landing.at[i], link.partner(b))
            copy.start()
            copy.wait()
            piece[...] = (piece[...].astype(F32) + self.landing[i].astype(F32)).astype(piece.dtype)


class Fan:
    def __init__(self, link, ends):
        self.link, self.ends = link, ends
        self.slot = link.take(link.tp_size - 1)

    def copy(self, k):
        source, target = self.ends(k)
        return self.link.remote(self.slot + k - 1, source, target, (self.link.dp, self.link.ahead(k)))

    def start(self):
        for k in range(1, self.link.tp_size):
            self.copy(k).start()

    def wait(self):
        for k in range(1, self.link.tp_size):
            self.copy(k).wait()


def then(*actions):
    def both():
        for action in actions:
            action()

    return both


class Track:
    def __init__(self):
        self.todo = []

    def add(self, steps, join=False):
        steps = list(steps)
        if join and self.todo:
            steps[0] = then(self.todo.pop(), steps[0])
        self.todo += steps

    def advance(self):
        if self.todo:
            self.todo.pop(0)()


def back_kernel(
    dp_size,
    tp_size,
    len_ref,
    vec,
    part_vec,
    xhat,
    rstd,
    mixed,
    wo,
    ff_pieces,
    dnorm,
    probs,
    x_hbm,
    q_hbm,
    kb_hbm,
    vb_hbm,
    yb_hbm,
    ssum_hbm,
    em_hbm,
    wq_hbm,
    wk_hbm,
    wv_hbm,
    grad_in,
    ff_out,
    gq_out,
    go_out,
    gkv_out,
    seq_out,
    vec_out,
    x,
    q,
    kb,
    vb,
    yb,
    ssum,
    em,
    wq,
    wk,
    wv,
    dres,
    dmix,
    dq,
    dl,
    prob_slots,
    dpart,
    dland,
    dfull,
    ff_zland,
    o_acc,
    o_land,
    q_acc,
    q_land,
    o_zland,
    q_zland,
    kv_send,
    kv_acc,
    kv_land,
    s_send,
    s_acc,
    s_land,
    vec_acc,
    vec_land,
    vec_z,
    wide_ff,
    wide_q,
    wide_kv,
    wide_s,
    send_sems,
    recv_sems,
    local_sems,
):
    link = Link(dp_size, tp_size, send_sems, recv_sems)
    rows, width = x.shape
    slots = yb.shape[0]
    low = link.low
    others = range(1, tp_size)
    first_load = pltpu.make_async_copy(dnorm, dres, local_sems.at[0])
    first_load.start()
    late = []
    for n, (source, target) in enumerate(
        (
            (q_hbm, q), (kb_hbm, kb), (vb_hbm, vb), (x_hbm, x), (yb_hbm, yb),
            (wq_hbm, wq), (wk_hbm, wk), (wv_hbm, wv), (ssum_hbm, ssum), (em_hbm, em),
        )
    ):
        late.append(pltpu.make_async_copy(source, target, local_sems.at[3 + n]))
        late[-1].start()
    link.greet(link.bits)

    lanes = 2
    deep = tp_size // lanes
    third = width // 3
    owned = width // tp_size

    ff_track, ff_orders = Track(), ((0, 1, 2), (0, 2, 1))
    ff_rows = ff_pieces.shape[2]
    ff_fans, ff_joins = [], []
    for m in range(2):

        def ends(k, m=m):
            return ff_pieces.at[m, link.ahead(k)], ff_zland.at[m, k - 1]

        def offset(m=m):
            first, size = 0, width >> 1
            for b in ff_orders[m]:
                if b < low:
                    first = first + link.bit(b) * size
                    size = size >> 1
            return first

        fan = Fan(link, ends)
        widen = Widen(link, wide_ff.at[m])

        def join(m=m, fan=fan, widen=widen, offset=offset):
            fan.wait()
            total = ff_pieces[m, link.tp].astype(F32)
            for k in others:
                total = total + ff_zland[m, k - 1].astype(F32)
            own = rows_at(offset(), ff_rows, 16)
            ff_out[m, own, :] = total.astype(BF)
            widen.run(ff_out.at[m, own, :])

        collect = Collect(
            link, ff_orders[m], offset, ff_rows,
            lambda first, size, m=m: ff_out.at[m, rows_at(first, size, 16), :],
        )
        ff_fans.append(fan)
        ff_joins.append((join, collect))
    for fan in ff_fans:
        fan.start()
    steps = [list(collect.steps()) for _, collect in ff_joins]
    ff_track.add([then(ff_joins[0][0], steps[0][0], ff_joins[1][0], steps[1][0])])
    ff_track.add([then(*pair) for pair in zip(steps[0][1:], steps[1][1:])])

    def square_track(order, out, acc, landing, zland, wide):
        track, spread = Track(), Spread(link, order, width, out, acc, landing)
        q_rows, q_cols = spread.piece // deep, width // lanes

        def quarter(first, t):
            return (
                rows_at(first + lax.div(t, lanes) * q_rows, q_rows, 16),
                pl.ds(pl.multiple_of(lax.rem(t, lanes) * q_cols, 128), q_cols),
            )

        def there(k):
            return acc.at[quarter(spread.inside(spread.stages - 1), link.ahead(k))], zland.at[k - 1]

        def again(k):
            region = out.at[quarter(spread.offset(), link.tp)]
            return region, region

        fan, share, widen = Fan(link, there), Fan(link, again), Widen(link, wide)

        def join():
            fan.wait()
            total = acc[quarter(spread.inside(spread.stages - 1), link.tp)].astype(F32)
            for k in others:
                total = total + zland[k - 1].astype(F32)
            mine = quarter(spread.offset(), link.tp)
            out[mine] = total.astype(BF)
            widen.run(out.at[mine])
            share.start()

        collect = Collect(
            link, order, spread.offset, spread.piece, lambda first, size: out.at[rows_at(first, size, 16), :]
        )
        track.add(spread.steps())
        track.add([then(lambda: spread.finish(spread.stages - 1), fan.start), join, share.wait])
        track.add(collect.steps(), join=True)
        return track

    def owned_track(order, total_rows, source, acc, landing, out, wide):
        track, spread = Track(), Spread(link, order, total_rows, source, acc, landing)

        def region(k):
            ref = out.at[link.tp, rows_at(spread.offset(), spread.piece, 16), :]
            return ref, ref

        share, widen = Fan(link, region), Widen(link, wide)

        def last():
            spread.finish(spread.stages - 1)
            ref = region(0)[0]
            ref[...] = acc[spread.kept(), :]
            widen.run(ref)
            share.start()

        collect = Collect(
            link, order, spread.offset, spread.piece, lambda first, size: out.at[:, rows_at(first, size, 16), :]
        )
        track.add(spread.steps())
        track.add([last, share.wait])
        track.add(collect.steps(), join=True)
        return track

    o_track = square_track((0, 1, 2), go_out, o_acc, o_land, o_zland, wide_q.at[0])
    q_track = square_track((0, 2, 1), gq_out, q_acc, q_land, q_zland, wide_q.at[1])
    kv_track = owned_track((0, 1, 2), 2 * owned, kv_send, kv_acc, kv_land, gkv_out, wide_kv)
    s_track = owned_track((0, 2, 1), slots, s_send, s_acc, s_land, seq_out, wide_s)

    vec_track, vec_slot = Track(), link.take(link.bits)
    vec_fan = Fan(link, lambda k: (vec_z.at[link.tp], vec_z.at[link.tp]))

    def vec_copy(b):
        return link.remote(vec_slot + b, vec_acc.at[b], vec_land.at[b], link.partner(b))

    vec_track.add([lambda: vec_copy(0).start()])
    for b in range(link.bits):

        def vec_step(b=b):
            vec_copy(b).wait()
            total = vec_acc[b] + vec_land[b]
            if b + 1 < link.bits:
                vec_acc[b + 1] = total
                vec_copy(b + 1).start()
            else:
                vec_z[link.tp] = total
                vec_fan.start()

        vec_track.add([vec_step])

    def vec_last():
        vec_fan.wait()
        total = vec_z[0]
        for t in range(1, tp_size):
            total = total + vec_z[t]
        vec_out[...] = total

    vec_track.add([vec_last])

    block = min(256, rows)
    count = rows // block
    gain = vec[4:5, :]

    def norm_back(step, carry):
        g_gain, g_shift, g_out = carry
        here = place(step, block)
        grad, hat = dres[here, :], xhat[here, :]
        g_gain = g_gain + jnp.sum(grad * hat, axis=0, keepdims=True)
        g_shift = g_shift + jnp.sum(grad, axis=0, keepdims=True)
        scaled = grad * gain
        d_res = rstd[here, 0:1] * (
            scaled
            - jnp.mean(scaled, axis=-1, keepdims=True)
            - hat * jnp.mean(scaled * hat, axis=-1, keepdims=True)
        )
        dres[here, :] = d_res
        d_attn = d_res.astype(BF)
        dq[here, :] = d_attn
        g_out = g_out + jnp.sum(d_attn.astype(F32), axis=0, keepdims=True)
        return g_gain, g_shift, g_out

    zero = jnp.zeros((1, width), F32)
    first_load.wait()
    g_gain, g_shift, g_out = lax.fori_loop(0, count, norm_back, (zero, zero, zero))
    vec_acc[0] = part_vec[...]
    vec_acc[0, 3:4, :] = g_out
    vec_acc[0, 4:5, :] = g_gain
    vec_acc[0, 5:6, :] = g_shift
    d_attn = dq

    def weight_grad(left, right, target):
        for m in range(3):
            cols = slice(m * third, (m + 1) * third)
            target[cols, :] = dot(left[:, cols], right[...], 0, 0).astype(BF)

    weight_grad(mixed, d_attn, go_out)
    o_track.advance()
    dmix[...] = dot(d_attn[...], wo[...], 1, 1).astype(BF)
    o_track.advance()
    for load in late:
        load.wait()

    own_half = lax.div(link.tp, 2)
    parity = lax.rem(link.tp, 2)
    three = PAIRS // 2

    def pair_at(n):
        second = lax.div(n, three)
        which = (1 - own_half) * (1 - second) + own_half * second
        return which * three + lax.rem(n, three)

    def fetch(n):
        slot = lax.rem(n, 2)
        return pltpu.make_async_copy(probs.at[pair_at(n)], prob_slots.at[slot], local_sems.at[1 + slot])

    fetch(0).start()

    def attend_back(n):
        p = pair_at(n)
        cols = place(p, PAIR)

        @pl.when(n + 1 < PAIRS)
        def _():
            fetch(n + 1).start()

        fetch(n).wait()
        held = prob_slots.at[lax.rem(n, 2)]

        def part(step, carry):
            here = place(step, block)
            d_probs = dot(dmix[here, cols], vb[p], 1, 1)
            weights = held[here, :].astype(F32)
            halves = []
            for h in range(2):
                w = weights[:, h * slots : (h + 1) * slots]
                d = d_probs[:, h * slots : (h + 1) * slots]
                halves.append((w * (d - jnp.sum(w * d, axis=-1, keepdims=True))).astype(BF))
            both = jnp.concatenate(halves, axis=1)
            dl[here, :] = both
            dq[here, cols] = (dot(both, kb[p], 1, 0) * 0.125).astype(BF)
            return carry

        lax.fori_loop(0, count, part, 0)
        top, under = rows_at(p * PAIR, HEAD, HEAD), rows_at(p * PAIR + HEAD, HEAD, HEAD)
        for n, total in enumerate(
            (dot(q[:, cols], dl[...], 0, 0) * 0.125, dot(dmix[:, cols], held[...], 0, 0))
        ):
            dpart[n, top, :] = total[:HEAD, :slots].astype(BF)
            dpart[n, under, :] = total[HEAD:, slots:].astype(BF)

    d_slot = link.take(tp_size - 1)

    def d_copy(j):
        near = 2 * own_half + (1 - parity)
        peer = near if j == 2 else 2 * (1 - own_half) + lax.rem(parity + j, 2)
        block_of = dpart.at[:, rows_at(peer * owned, owned, 64), :]
        return link.remote(d_slot + j, block_of, dland.at[j], (link.dp, peer))

    def far_blocks():
        d_copy(0).start()
        d_copy(1).start()

    events = [
        lambda: o_track.advance(),
        lambda: o_track.advance(),
        then(far_blocks, ff_track.advance, o_track.advance),
        then(ff_track.advance, o_track.advance),
        then(ff_track.advance, o_track.advance),
        then(lambda: d_copy(2).start(), ff_track.advance, o_track.advance),
    ]

    def one(n, carry):
        attend_back(n)
        for i, event in enumerate(events):
            pl.when(n == i)(event)
        return carry

    lax.fori_loop(0, PAIRS, one, 0)

    weight_grad(x, dq, gq_out)
    q_track.advance()

    for j in range(tp_size - 1):
        d_copy(j).wait()
    own_block = rows_at(link.tp * owned, owned, 64)
    for n in range(2):
        total = dpart[n, own_block, :].astype(F32)
        for j in range(tp_size - 1):
            total = total + dland[j, n].astype(F32)
        dfull[n, own_block, :] = total.astype(BF)
    d_share = Fan(link, lambda k: (dfull.at[:, own_block, :], dfull.at[:, own_block, :]))
    d_share.start()
    q_track.advance()
    for n in range(2):
        kv_send[n * owned : (n + 1) * owned, :] = dot(dfull[n, own_block, :], yb[...], 1, 0).astype(BF)
    kv_track.advance()
    vec_acc[0, 0:1, :] = jnp.sum(dq[...].astype(F32), axis=0, keepdims=True)

    def input_grad(step, carry):
        here = place(step, block)
        dres[here, :] += dot(dq[here, :], wq[...], 1, 1)
        return carry

    lax.fori_loop(0, count, input_grad, 0)
    kv_track.advance()
    q_track.advance()
    o_track.advance()
    kv_track.advance()
    d_share.wait()
    backs = dot(wk[...], dfull[0], 1, 0) + dot(wv[...], dfull[1], 1, 0)
    back = backs.T.astype(BF)
    small = vec[0:8, :].astype(BF)
    bias_row = dot(small, dfull[0], 1, 0)[1:2, :] + dot(small, dfull[1], 1, 0)[2:3, :]
    bias_column = jnp.broadcast_to(bias_row, (128, slots)).T[:, 0:1]
    position = lax.broadcasted_iota(jnp.int32, (1, rows), 1) + link.tp * rows
    live = (position < len_ref[0]).astype(F32)
    s_send[...] = ((dot(back, x[...], 1, 1) + bias_column) * live).astype(BF)
    s_track.advance()
    column = ssum[...].T[0:8, :]
    column_b = column.astype(BF)
    column_low = (column - column_b.astype(F32)).astype(BF)
    for n in range(2):
        total = dot(column_b, dfull[n], 1, 1) + dot(column_low, dfull[n], 1, 1)
        vec_acc[0, 1 + n : 2 + n, :] = total[0:1, :] * (1.0 / tp_size)
    vec_track.advance()
    s_track.advance()
    kv_track.advance()

    def input_grad_last(step, carry):
        here = place(step, block)
        grad_in[here, :] = (dres[here, :] + dot(em[:, here], back, 0, 0)).astype(BF)
        return carry

    lax.fori_loop(0, count, input_grad_last, 0)
    tracks = [s_track, kv_track, q_track, vec_track, ff_track, o_track]
    while any(track.todo for track in tracks):
        for track in tracks:
            track.advance()


def back(mesh, lengths, vec, part_vec, xhat, rstd, mixed, wo, ff_pieces, dnorm, probs, *late):
    dp_size, tp_size = mesh.shape["dp"], mesh.shape["tp"]
    bits = dp_size.bit_length() - 1
    low = min(3, bits)
    wide = max(1, bits - low)
    rows, width = xhat.shape
    slots = late[4].shape[0]
    owned = width // tp_size
    others = tp_size - 1
    vmem = pl.BlockSpec(memory_space=pltpu.VMEM)
    hbm = pl.BlockSpec(memory_space=pltpu.HBM)
    shape = jax.ShapeDtypeStruct

    def landing(total):
        return sum(total >> (i + 1) for i in range(low))

    def buf(*dims, dtype=BF):
        return pltpu.VMEM(dims, dtype)

    ff_piece, kv_piece, s_piece = width >> low, 2 * owned >> low, slots >> low
    quarter = (ff_piece // (tp_size // 2), width // 2)
    return pl.pallas_call(
        functools.partial(back_kernel, dp_size, tp_size),
        out_shape=(
            shape((rows, width), BF),
            shape((2, width, width), BF),
            shape((width, width), BF),
            shape((width, width), BF),
            shape((tp_size, 2 * owned, width), BF),
            shape((tp_size, slots, rows), BF),
            shape((VECTORS, width), F32),
        ),
        in_specs=[pl.BlockSpec(memory_space=pltpu.SMEM)] + [vmem] * 7 + [hbm] * (2 + len(late)),
        out_specs=tuple([vmem] * 7),
        scratch_shapes=[pltpu.VMEM(array.shape, array.dtype) for array in late]
        + [
            buf(rows, width, dtype=F32),
            buf(rows, width),
            buf(rows, width),
            buf(rows, 2 * slots),
            buf(2, rows, 2 * slots),
            buf(2, width, slots),
            buf(others, 2, owned, slots),
            buf(2, width, slots),
            buf(2, others, ff_piece, width),
            buf(width // 2, width),
            buf(landing(width), width),
            buf(width // 2, width),
            buf(landing(width), width),
            buf(others, *quarter),
            buf(others, *quarter),
            buf(2 * owned, width),
            buf(owned, width),
            buf(landing(2 * owned), width),
            buf(slots, rows),
            buf(slots // 2, rows),
            buf(landing(slots), rows),
            buf(bits, VECTORS, width, dtype=F32),
            buf(bits, VECTORS, width, dtype=F32),
            buf(tp_size, VECTORS, width, dtype=F32),
            buf(2, wide, ff_piece, width),
            buf(2, wide, *quarter),
            buf(wide, kv_piece, width),
            buf(wide, s_piece, rows),
            pltpu.SemaphoreType.DMA((BACK_SEMS,)),
            pltpu.SemaphoreType.DMA((BACK_SEMS,)),
            pltpu.SemaphoreType.DMA((3 + len(late),)),
        ],
        compiler_params=pltpu.CompilerParams(
            collective_id=1, has_side_effects=True, vmem_limit_bytes=VMEM_LIMIT
        ),
        name="back",
    )(lengths, vec, part_vec, xhat, rstd, mixed, wo, ff_pieces, dnorm, probs, *late)


class ChunkSpread:
    def __init__(self, link, rows, sent, acc, landing):
        self.link, self.rows, self.sent, self.acc, self.landing = link, rows, sent, acc, landing
        self.orders = [[b for b in order if b < link.low] for order in ((0, 1, 2), (0, 2, 1))]
        self.stages = link.low

    def inside(self, m, i):
        first = 0
        for j in range(1, i + 1):
            first = first + self.link.bit(self.orders[m][j]) * (self.rows >> (j + 1))
        return first

    def copy(self, c, m, i):
        link, size = self.link, self.rows >> (i + 1)
        bit = self.orders[m][i]
        if i == 0:
            source = self.sent.at[m, lax.rem(c, 2), rows_at((1 - link.bit(bit)) * size, size, 16), :]
        else:
            source = self.acc.at[m, c, rows_at(self.inside(m, i - 1) + (1 - link.bit(bit)) * size, size, 16), :]
        first = sum(self.rows >> (j + 1) for j in range(i))
        slot = (i * 2 + m) * self.acc.shape[1] + c
        return link.remote(slot, source, self.landing.at[m, c, pl.ds(first, size), :], link.partner(bit))

    def start(self, c, m, i):
        self.copy(c, m, i).start()

    def finish(self, c, m, i):
        size = self.rows >> (i + 1)
        self.copy(c, m, i).wait()
        first = sum(self.rows >> (j + 1) for j in range(i))
        landed = self.landing.at[m, c, pl.ds(first, size), :]
        acc = self.acc.at[m, c]
        if i == 0:
            mine = self.link.bit(self.orders[m][0]) * size
            add_rows(acc, 0, self.sent.at[m, lax.rem(c, 2)], mine, landed, size)
        else:
            at = self.inside(m, i)
            add_rows(acc, at, acc, at, landed, size)
        if i + 1 < self.stages:
            self.start(c, m, i + 1)


def middle_kernel(
    dp_size,
    tp_size,
    vec,
    bup_all,
    xhat,
    out_grad,
    wup_all,
    wdn_all,
    layer_out,
    dnorm,
    part_vec,
    ff_pieces,
    wup,
    wdn,
    nb,
    act,
    slope,
    d_branch,
    d_acc,
    sent,
    acc,
    landing,
    send_sems,
    recv_sems,
    local_sems,
):
    link = Link(dp_size, tp_size, send_sems, recv_sems)
    rows, width = xhat.shape
    loads = []
    for c in range(tp_size):
        for n, (source, target) in enumerate(((wup_all, wup), (wdn_all, wdn))):
            loads.append(pltpu.make_async_copy(source.at[c], target.at[c], local_sems.at[n * tp_size + c]))
            loads[-1].start()
    barrier = pltpu.get_barrier_semaphore()
    for b in range(link.low):
        pl.semaphore_signal(barrier, inc=1, device_id=link.partner(b), device_id_type=MESH)
    pl.semaphore_wait(barrier, link.low)
    gain, shift, b_down, f_gain, f_shift = (vec[n : n + 1, :] for n in (4, 5, 6, 7, 8))
    block = min(256, rows)
    count = rows // block
    big = min(512, rows)

    def norm(step, carry):
        here = place(step, block)
        nb[here, :] = (xhat[here, :] * gain + shift).astype(BF)
        return carry

    lax.fori_loop(0, count, norm, 0)
    for load in loads:
        load.wait()

    per_chunk = rows // big

    def forward(step, carry):
        c = lax.div(step, per_chunk)
        here, cols = place(lax.rem(step, per_chunk), big), place(c, width)
        pre = dot(nb[here, :], wup[c], 1, 0) + bup_all[c, 0:1, :]
        cdf = 0.5 * (1.0 + lax.erf(pre * 0.7071067811865476))
        act[here, cols] = (pre * cdf).astype(BF)
        slope[here, cols] = (cdf + pre * (jnp.exp(pre * pre * -0.5) * 0.3989422804014327)).astype(BF)
        return carry

    lax.fori_loop(0, tp_size * per_chunk, forward, 0)

    def second_norm(step, carry):
        g_gain, g_shift, g_down = carry
        here = place(step, block)
        branch = dot(act[here, 0:width], wdn[0], 1, 0)
        for c in range(1, tp_size):
            branch = branch + dot(act[here, c * width : (c + 1) * width], wdn[c], 1, 0)
        res = xhat[here, :] * gain + shift + (branch + b_down)
        center = res - jnp.mean(res, axis=-1, keepdims=True)
        inverse = lax.rsqrt(jnp.mean(center * center, axis=-1, keepdims=True) + 1e-05)
        hat = center * inverse
        layer_out[here, :] = (hat * f_gain + f_shift).astype(BF)
        grad = out_grad[here, :].astype(F32)
        g_gain = g_gain + jnp.sum(grad * hat, axis=0, keepdims=True)
        g_shift = g_shift + jnp.sum(grad, axis=0, keepdims=True)
        scaled = grad * f_gain
        d_res = inverse * (
            scaled
            - jnp.mean(scaled, axis=-1, keepdims=True)
            - hat * jnp.mean(scaled * hat, axis=-1, keepdims=True)
        )
        d_acc[here, :] = d_res
        rounded = d_res.astype(BF)
        d_branch[here, :] = rounded
        g_down = g_down + jnp.sum(rounded.astype(F32), axis=0, keepdims=True)
        return g_gain, g_shift, g_down

    zero = jnp.zeros((1, width), F32)
    g_gain, g_shift, g_down = lax.fori_loop(0, count, second_norm, (zero, zero, zero))
    part_vec[...] = jnp.zeros_like(part_vec)
    part_vec[6:7, :] = g_gain
    part_vec[7:8, :] = g_shift
    part_vec[8:9, :] = g_down

    spread = ChunkSpread(link, width, sent, acc, landing)
    third = width // 3

    def weight_grad(left, first, right, cols, target):
        for m in range(3):
            mine = pl.ds(pl.multiple_of(first + m * third, third), third)
            target[m * third : (m + 1) * third, :] = dot(left[:, mine], right[:, cols], 0, 0).astype(BF)

    def backward(c, carry):
        cols = place(c, width)
        slot = lax.rem(c, 2)
        weight_grad(act, c * width, d_branch, slice(0, width), sent.at[1, slot])
        spread.start(c, 1, 0)

        def through(step, total):
            here = place(step, big)
            grad = (dot(d_branch[here, :], wdn[c], 1, 1) * slope[here, cols].astype(F32)).astype(BF)
            slope[here, cols] = grad
            return total + jnp.sum(grad.astype(F32), axis=0, keepdims=True)

        part_vec[pl.ds(9 + c, 1), :] = lax.fori_loop(0, rows // big, through, zero)
        weight_grad(nb, 0, slope, cols, sent.at[0, slot])
        spread.start(c, 0, 0)
        for back_by in range(1, spread.stages + 1):

            @pl.when(c >= back_by)
            def _():
                for m in (1, 0):
                    spread.finish(c - back_by, m, back_by - 1)

        return carry

    lax.fori_loop(0, tp_size, backward, 0)

    def input_grad(step, carry):
        here = place(step, big)
        total = d_acc[here, :]
        for c in range(tp_size):
            total = total + dot(slope[here, c * width : (c + 1) * width], wup[c], 1, 1)
        d_acc[here, :] = total
        return carry

    half = rows // big // 2
    lax.fori_loop(0, half, input_grad, 0)
    for c in range(max(0, tp_size - spread.stages), tp_size):
        stage = tp_size - 1 - c
        for m in (1, 0):
            spread.finish(c, m, stage)
    lax.fori_loop(half, rows // big, input_grad, 0)
    store = pltpu.make_async_copy(d_acc, dnorm, local_sems.at[2 * tp_size])
    store.start()
    for late in range(1, spread.stages):
        for c in range(max(0, tp_size - spread.stages) + late, tp_size):
            stage = tp_size - 1 - c + late
            for m in (1, 0):
                spread.finish(c, m, stage)
    piece = width >> spread.stages
    for m in range(2):
        at = spread.inside(m, spread.stages - 1)
        for c in range(tp_size):
            ff_pieces[m, c] = acc[m, c, rows_at(at, piece, 16), :]
    store.wait()


def middle(mesh, vec, bup_all, xhat, out_grad, wup_all, wdn_all):
    dp_size, tp_size = mesh.shape["dp"], mesh.shape["tp"]
    low = min(3, dp_size.bit_length() - 1)
    rows, width = xhat.shape
    hidden = tp_size * width
    vmem = pl.BlockSpec(memory_space=pltpu.VMEM)
    hbm = pl.BlockSpec(memory_space=pltpu.HBM)
    shape = jax.ShapeDtypeStruct

    def buf(*dims, dtype=BF):
        return pltpu.VMEM(dims, dtype)

    sems = 2 * low * tp_size
    return pl.pallas_call(
        functools.partial(middle_kernel, dp_size, tp_size),
        out_shape=(
            shape((rows, width), BF),
            shape((rows, width), F32),
            shape((VECTORS, width), F32),
            shape((2, tp_size, width >> low, width), BF),
        ),
        in_specs=[vmem] * 4 + [hbm] * 2,
        out_specs=(vmem, hbm, vmem, vmem),
        scratch_shapes=[
            buf(tp_size, width, width),
            buf(tp_size, width, width),
            buf(rows, width),
            buf(rows, hidden),
            buf(rows, hidden),
            buf(rows, width),
            buf(rows, width, dtype=F32),
            buf(2, 2, width, width),
            buf(2, tp_size, width // 2, width),
            buf(2, tp_size, sum(width >> (i + 1) for i in range(low)), width),
            pltpu.SemaphoreType.DMA((sems,)),
            pltpu.SemaphoreType.DMA((sems,)),
            pltpu.SemaphoreType.DMA((2 * tp_size + 1,)),
        ],
        compiler_params=pltpu.CompilerParams(
            collective_id=2, has_side_effects=True, vmem_limit_bytes=VMEM_LIMIT
        ),
        name="middle",
    )(vec, bup_all, xhat, out_grad, wup_all, wdn_all)


def finish_kernel(
    tp_size, ff, gq, go, gkv, seq, vec, layer_out, grad_in,
    o_up, o_dn, o_q, o_o, o_k, o_v, o_seq, o_layer, o_grad, *rest,
):
    vectors, (in_up, in_dn, in_q, in_o, in_kv, in_seq, f_up, f_dn, f_q, f_o, f_k, f_v, f_seq, turn, pass_a, pass_b, in_sems, out_sems) = rest[:10], rest[10:]
    pairs = [(gq, in_q), (go, in_o), (ff.at[0], in_up), (ff.at[1], in_dn), (gkv, in_kv), (seq, in_seq), (layer_out, pass_a), (grad_in, pass_b)]
    loads = []
    for n, (source, target) in enumerate(pairs):
        loads.append(pltpu.make_async_copy(source, target, in_sems.at[n]))
        loads[-1].start()
    stores = []

    def put(staged, out):
        copy = pltpu.make_async_copy(staged, out, out_sems.at[len(stores)])
        copy.start()
        stores.append(copy)

    for n, (held, out) in enumerate(((pass_a, o_layer), (pass_b, o_grad))):
        loads[6 + n].wait()
        put(held, out)
    for n, row in enumerate((0, 1, 2, 3, 4, 5, 6, 7, 8)):
        vectors[n][...] = vec[row, :]
    vectors[9][...] = vec[pl.ds(9 + lax.axis_index("tp"), 1), :][0]
    width = gq.shape[0]
    for n, (narrow, wide, out) in enumerate(
        ((in_q, f_q, o_q), (in_o, f_o, o_o), (in_up, f_up, o_up), (in_dn, f_dn, o_dn))
    ):
        loads[n].wait()
        wide[...] = narrow[...].astype(F32)
        put(wide, out)
    loads[4].wait()
    owned = width // tp_size
    for n, (wide, out) in enumerate(((f_k, o_k), (f_v, o_v))):
        for c in range(tp_size):
            turn[c * owned : (c + 1) * owned, :] = in_kv[c, n * owned : (n + 1) * owned, :]
        for c in range(3):
            cols = slice(c * (width // 3), (c + 1) * (width // 3))
            wide[:, cols] = turn[cols, :].astype(F32).T
        put(wide, out)
    loads[5].wait()
    rows = in_seq.shape[2]
    for c in range(tp_size):
        f_seq[:, c * rows : (c + 1) * rows] = in_seq[c].astype(F32)
    put(f_seq, o_seq)
    for copy in stores:
        copy.wait()


def finish(tp_size, ff, gq, go, gkv, seq, vec, layer_out, grad_in):
    width = gq.shape[0]
    _, slots, rows = seq.shape
    square, flat = (width, width), (slots, tp_size * rows)
    vmem = pl.BlockSpec(memory_space=pltpu.VMEM)
    hbm = pl.BlockSpec(memory_space=pltpu.HBM)
    shape = jax.ShapeDtypeStruct
    return pl.pallas_call(
        functools.partial(finish_kernel, tp_size),
        out_shape=tuple([shape(square, F32)] * 6 + [shape(flat, F32)] + [shape(layer_out.shape, BF)] * 2 + [shape((width,), F32)] * 10),
        in_specs=[hbm] * 5 + [vmem] + [hbm] * 2,
        out_specs=tuple([hbm] * 9 + [vmem] * 10),
        scratch_shapes=[pltpu.VMEM(square, BF)] * 4
        + [pltpu.VMEM(gkv.shape, BF), pltpu.VMEM(seq.shape, BF)]
        + [pltpu.VMEM(square, F32)] * 6
        + [pltpu.VMEM(flat, F32), pltpu.VMEM(square, BF)]
        + [pltpu.VMEM(layer_out.shape, BF)] * 2
        + [pltpu.SemaphoreType.DMA((8,)), pltpu.SemaphoreType.DMA((9,))],
        compiler_params=pltpu.CompilerParams(vmem_limit_bytes=VMEM_LIMIT),
        name="finish",
    )(ff, gq, go, gkv, seq, vec, layer_out, grad_in)


def on_device(
    mesh,
    layer_in,
    out_grad,
    lengths,
    w_query,
    b_query,
    w_key,
    b_key,
    w_value,
    b_value,
    w_out,
    b_out,
    seq_proj,
    attn_gain,
    attn_shift,
    w_up,
    b_up,
    w_down,
    b_down,
    ffn_gain,
    ffn_shift,
):
    row_count, width = layer_in.shape
    tp_size = mesh.shape["tp"]
    vectors = (b_query, b_key, b_value, b_out, attn_gain, attn_shift, b_down, ffn_gain, ffn_shift)
    vec, xhat, rstd, mixed, queries, probs, kb, vb, folded, ssum, own_proj, bup_all, up_all, down_all = front(
        mesh, lengths, layer_in, w_query, w_key, w_value, w_out, w_up, w_down, seq_proj, vectors, b_up
    )
    layer_out, d_normed, part_vec, ff_pieces = middle(mesh, vec, bup_all, xhat, out_grad, up_all, down_all)
    grad_in, g_ff, g_q, g_o, g_kv, g_seq, vec_sum = back(
        mesh, lengths, vec, part_vec, xhat, rstd, mixed, w_out, ff_pieces, d_normed, probs,
        layer_in, queries, kb, vb, folded, ssum, own_proj, w_query, w_key, w_value
    )
    (
        g_w_up, g_w_down, g_w_query, g_w_out, g_w_key, g_w_value, g_seq_proj, layer_out, grad_in,
        g_b_query, g_b_key, g_b_value, g_b_out, g_attn_gain, g_attn_shift, g_ffn_gain, g_ffn_shift, g_b_down, g_b_up,
    ) = finish(tp_size, g_ff, g_q, g_o, g_kv, g_seq, vec_sum, layer_out, grad_in)
    return (
        layer_out,
        grad_in,
        g_w_query,
        g_b_query,
        g_w_key,
        g_b_key,
        g_w_value,
        g_b_value,
        g_w_out,
        g_b_out,
        g_seq_proj,
        g_attn_gain,
        g_attn_shift,
        g_w_up,
        g_b_up,
        g_w_down,
        g_b_down,
        g_ffn_gain,
        g_ffn_shift,
    )


def solution(mesh):
    in_specs = (
        P(("dp", "tp"), None),
        P(("dp", "tp"), None),
        P("dp"),
        *([P()] * 11),
        P(None, "tp"),
        P("tp"),
        P("tp", None),
        P(),
        P(),
        P(),
    )
    out_specs = (
        P(("dp", "tp"), None),
        P(("dp", "tp"), None),
        *([P()] * 11),
        P(None, "tp"),
        P("tp"),
        P("tp", None),
        P(),
        P(),
        P(),
    )
    return jax.shard_map(
        functools.partial(on_device, mesh), mesh=mesh, in_specs=in_specs, out_specs=out_specs, check_vma=False
    )
```

```python
import functools

import jax
import jax.numpy as jnp
from jax import lax
from jax.experimental import pallas as pl
from jax.experimental.pallas import tpu as pltpu
from jax.sharding import PartitionSpec as P

HEADS = 12
HEAD = 64
PAIRS = HEADS // 2
PAIR = 2 * HEAD
BF = jnp.bfloat16
F32 = jnp.float32
MESH = pl.DeviceIdType.MESH
VMEM_LIMIT = 67_043_328


def dot(left, right, left_dim, right_dim):
    return lax.dot_general(
        left, right, (((left_dim,), (right_dim,)), ((), ())), preferred_element_type=F32
    )


def place(index, size):
    return pl.ds(pl.multiple_of(index * size, size), size)


def rows_at(first, size, multiple):
    return pl.ds(pl.multiple_of(first, multiple), size)


class Link:
    def __init__(self, dp_size, tp_size, send_sems, recv_sems):
        self.dp_size, self.tp_size = dp_size, tp_size
        self.dp, self.tp = lax.axis_index("dp"), lax.axis_index("tp")
        self.bits = dp_size.bit_length() - 1
        self.low = min(3, self.bits)
        self.send_sems, self.recv_sems = send_sems, recv_sems
        self.used = 0

    def bit(self, b):
        return lax.rem(lax.div(self.dp, 1 << b), 2)

    def partner(self, b):
        return (self.dp + (1 - 2 * self.bit(b)) * (1 << b), self.tp)

    def ahead(self, k):
        return lax.rem(self.tp + k, self.tp_size)

    def behind(self, k):
        return lax.rem(self.tp + self.tp_size - k, self.tp_size)

    def greet(self, dp_bits):
        barrier = pltpu.get_barrier_semaphore()
        peers = [(self.dp, self.ahead(k)) for k in range(1, self.tp_size)]
        peers += [self.partner(b) for b in range(dp_bits)]
        for peer in peers:
            pl.semaphore_signal(barrier, inc=1, device_id=peer, device_id_type=MESH)
        pl.semaphore_wait(barrier, len(peers))

    def take(self, count):
        first = self.used
        self.used += count
        assert self.used <= self.send_sems.shape[0]
        return first

    def remote(self, slot, source, target, device):
        return pltpu.make_async_remote_copy(
            src_ref=source,
            dst_ref=target,
            send_sem=self.send_sems.at[slot],
            recv_sem=self.recv_sems.at[slot],
            device_id=device,
            device_id_type=MESH,
        )

    def send(self, source, target, device):
        copy = self.remote(self.take(1), source, target, device)
        copy.start()
        return copy


FRONT_SEMS = 64
VECTORS = 16


def half_orders(low):
    return [[b for b in order if b < low] for order in ((1, 2, 0), (2, 1, 0))]


def half_offset(link, order, piece):
    first, size = 0, piece
    for b in order:
        first = first + link.bit(b) * size
        size *= 2
    return first


class WeightCollect:
    def __init__(self, link, part, whole):
        self.link, self.whole, self.part = link, whole, part
        self.orders = half_orders(link.low)
        self.piece = self.part >> link.low
        self.stages = link.low
        self.slot = link.take(2 * (link.tp_size - 1) * link.low)

    def rows(self, h, i):
        size = self.piece << i
        first = half_offset(self.link, self.orders[h], self.piece)
        return rows_at(h * self.part + first - lax.rem(first, size), size, 16)

    def copies(self, k, i):
        for h in range(2):
            region = self.whole(k).at[self.rows(h, i), :]
            slot = self.slot + ((k - 1) * self.stages + i) * 2 + h
            yield self.link.remote(slot, region, region, self.link.partner(self.orders[h][i]))

    def step(self, k, j):
        if j > 0:
            for copy in self.copies(k, j - 1):
                copy.wait()
        if j < self.stages:
            for copy in self.copies(k, j):
                copy.start()


class Cross:
    def __init__(self, link, collect, shard):
        self.link, self.collect, self.shard = link, collect, shard
        self.slot = link.take(2 * (link.tp_size - 1))

    def copies(self, k):
        for h in range(2):
            rows = self.collect.rows(h, 0)
            yield self.link.remote(
                self.slot + 2 * (k - 1) + h,
                self.shard.at[rows, :],
                self.collect.whole(k).at[rows, :],
                (self.link.dp, self.link.ahead(k)),
            )

    def start(self, k):
        for copy in self.copies(k):
            copy.start()

    def wait(self, k):
        for copy in self.copies(k):
            copy.wait()


FRONT_TICKS = (
    ((3, 0),),
    (),
    ((3, 1),),
    (),
    ((3, 2),),
    (),
    ((3, 3),),
)


def front_kernel(dp_size, tp_size, n_vectors, len_ref, x, wq, e, wk_hbm, wv_hbm, wo_hbm, wup, *rest):
    vectors, b_up, rest = rest[:n_vectors], rest[n_vectors], rest[n_vectors + 1 :]
    outs, scratch = rest[:13], rest[13:]
    (vec, xhat, rstd, bup_all, mixed_out, q_out, probs_out, kb_out, vb_out, yb_out, ssum_out, em_out, ups) = outs
    (wk, wv, wo, e_all, mixed, q, probs, kb, vb, yb, ssum, em, bup, ysend, yrecv, send_sems, recv_sems, local_sems) = scratch
    link = Link(dp_size, tp_size, send_sems, recv_sems)
    rows, width = x.shape
    slots, total = e_all.shape
    quarter = slots // tp_size
    others = range(1, tp_size)
    used = [0]

    def local(source, target):
        copy = pltpu.make_async_copy(source, target, local_sems.at[used[0]])
        used[0] += 1
        copy.start()
        return copy

    own_first = link.tp * rows
    e_own = local(e.at[:, rows_at(own_first, rows, rows)], em)
    late = [local(e, e_all), local(wk_hbm, wk), local(wv_hbm, wv), local(wo_hbm, wo)]
    link.greet(link.low)

    collect = WeightCollect(link, wup.shape[0] // 2, lambda k: ups.at[k - 1])
    cross = Cross(link, collect, wup)
    cross.start(1)
    vec[...] = jnp.zeros_like(vec)
    for n, vector in enumerate(vectors):
        vec[n : n + 1, :] = vector[...].astype(F32).reshape(1, width)
    bup[...] = jnp.broadcast_to(b_up[...].astype(F32).reshape(1, width), bup.shape)
    bup_all[link.tp] = bup[...]
    length = len_ref[0]
    position = lax.broadcasted_iota(jnp.int32, (1, rows), 1) + own_first
    live = (position < length).astype(F32)
    e_own.wait()
    em[...] = (em[...].astype(F32) * live).astype(BF)
    ysend[...] = dot(em[...], x[...], 1, 0).astype(ysend.dtype)
    reduce = [
        link.send(ysend.at[place(link.ahead(k), quarter), :], yrecv.at[k - 1], (link.dp, link.ahead(k)))
        for k in others
    ]
    biases = [link.send(bup, bup_all.at[link.tp], (link.dp, link.ahead(k))) for k in others]
    cross.wait(1)
    collect.step(1, 0)
    q[...] = (dot(x[...], wq[...], 1, 0) + vec[0:1, :]).astype(BF)
    collect.step(1, 1)
    own_slots = place(link.tp, quarter)
    for copy in reduce:
        copy.wait()
    own_y = ysend[own_slots, :].astype(F32)
    for k in others:
        own_y = own_y + yrecv[k - 1].astype(F32)
    yb[own_slots, :] = own_y.astype(BF)
    share = [
        link.send(yb.at[own_slots, :], yb.at[own_slots, :], (link.dp, link.ahead(k))) for k in others
    ]
    for k in (3, 2):
        cross.start(k)
    collect.step(1, 2)
    stores = [local(q, q_out), local(em, em_out)]
    row_live = (lax.broadcasted_iota(jnp.int32, (total, 128), 0) < length).astype(F32).astype(BF)
    for load in late:
        load.wait()
    ssum[...] = dot(e_all[...], row_live, 1, 0)
    for copy in share:
        copy.wait()
    for copy in biases:
        copy.wait()
    collect.step(1, 3)
    stores += [local(yb, yb_out), local(ssum, ssum_out)]

    lane = lax.broadcasted_iota(jnp.int32, (1, PAIR), 1)
    first_half = (lane < HEAD).astype(F32)

    def project(weight, bias_row, blocks):
        full = dot(yb[...], weight[...], 1, 0)
        for p in range(PAIRS):
            cols = slice(p * PAIR, (p + 1) * PAIR)
            both = full[:, cols] + ssum[...] * vec[bias_row : bias_row + 1, cols]
            blocks[p, 0:slots, :] = (both * first_half).astype(BF)
            blocks[p, slots : 2 * slots, :] = (both * (1.0 - first_half)).astype(BF)

    project(wk, 1, kb)
    project(wv, 2, vb)
    stores += [local(kb, kb_out), local(vb, vb_out)]

    block = min(256, rows)
    per_pair = rows // block
    probs_sem = used[0]

    def tick(ticks):
        for k, j in ticks:
            if j == 0:
                cross.wait(k)
            collect.step(k, j)

    def attend(p, carry):
        cols = place(p, PAIR)

        def one(step, carry):
            here = place(step, block)
            logits = dot(q[here, cols], kb[p], 1, 1) * 0.125
            halves = []
            for half in range(2):
                part = logits[:, half * slots : (half + 1) * slots]
                peak = jnp.max(part, axis=-1, keepdims=True)
                raised = jnp.exp(part - peak)
                halves.append((raised * (1.0 / jnp.sum(raised, axis=-1, keepdims=True))).astype(BF))
            both = jnp.concatenate(halves, axis=1)
            probs[p, here, :] = both
            mixed[here, cols] = dot(both, vb[p], 1, 0).astype(BF)
            return carry

        lax.fori_loop(0, per_pair, one, 0)
        pltpu.make_async_copy(probs.at[p], probs_out.at[p], local_sems.at[probs_sem + p]).start()
        for n, ticks in enumerate(FRONT_TICKS[:-1]):

            @pl.when(p == n)
            def _():
                tick(ticks)

        return carry

    lax.fori_loop(0, PAIRS, attend, 0)
    used[0] += PAIRS
    stores.append(local(mixed, mixed_out))

    def finish(step, carry):
        here = place(step, block)
        res = x[here, :].astype(F32) + dot(mixed[here, :], wo[...], 1, 0) + vec[3:4, :]
        center = res - jnp.mean(res, axis=-1, keepdims=True)
        inverse = lax.rsqrt(jnp.mean(center * center, axis=-1, keepdims=True) + 1e-05)
        xhat[here, :] = center * inverse
        rstd[here, :] = jnp.broadcast_to(inverse, (block, 128))
        return carry

    lax.fori_loop(0, per_pair, finish, 0)
    tick(FRONT_TICKS[-1])
    cross.wait(2)
    for copy in stores:
        copy.wait()
    for p in range(PAIRS):
        pltpu.make_async_copy(probs.at[p], probs_out.at[p], local_sems.at[probs_sem + p]).wait()


def front(mesh, lengths, x, wq, e, wk, wv, wo, wup, vectors, b_up):
    dp_size, tp_size = mesh.shape["dp"], mesh.shape["tp"]
    low = min(3, dp_size.bit_length() - 1)
    rows, width = x.shape
    slots = e.shape[0]
    vmem = pl.BlockSpec(memory_space=pltpu.VMEM)
    hbm = pl.BlockSpec(memory_space=pltpu.HBM)
    shape = jax.ShapeDtypeStruct
    moved = (
        ((rows, width), BF),
        ((rows, width), BF),
        ((PAIRS, rows, 2 * slots), BF),
        ((PAIRS, 2 * slots, PAIR), BF),
        ((PAIRS, 2 * slots, PAIR), BF),
        ((slots, width), BF),
        ((slots, 128), F32),
        ((slots, rows), BF),
    )
    kept = (
        ((VECTORS, width), F32),
        ((rows, width), F32),
        ((rows, 128), F32),
        ((tp_size, 8, width), F32),
    )
    return pl.pallas_call(
        functools.partial(front_kernel, dp_size, tp_size, len(vectors)),
        out_shape=tuple(shape(*s) for s in kept + moved)
        + (shape((tp_size - 1, *wup.shape), BF),),
        in_specs=[pl.BlockSpec(memory_space=pltpu.SMEM)]
        + [vmem] * 2
        + [hbm] * 5
        + [vmem] * (len(vectors) + 1),
        out_specs=tuple([vmem] * len(kept) + [hbm] * (len(moved) + 1)),
        scratch_shapes=[pltpu.VMEM(w.shape, BF) for w in (wk, wv, wo, e)]
        + [pltpu.VMEM(*s) for s in moved]
        + [
            pltpu.VMEM((8, width), F32),
            pltpu.VMEM((slots, width), BF),
            pltpu.VMEM((tp_size - 1, slots // tp_size, width), BF),
            pltpu.SemaphoreType.DMA((FRONT_SEMS,)),
            pltpu.SemaphoreType.DMA((FRONT_SEMS,)),
            pltpu.SemaphoreType.DMA((24,)),
        ],
        compiler_params=pltpu.CompilerParams(
            collective_id=0, has_side_effects=True, vmem_limit_bytes=VMEM_LIMIT
        ),
        name="front",
    )(lengths, x, wq, e, wk, wv, wo, wup, *vectors, b_up)


BACK_SEMS = 128
VECTORS = 16


def add_rows(target, first, left, left_first, right, count):
    block = 96 if count % 96 == 0 else (48 if count % 48 == 0 else (32 if count % 32 == 0 else count))

    def step(i, carry):
        at = i * block
        total = (
            left[rows_at(left_first + at, block, 16), :].astype(F32)
            + right[rows_at(at, block, 16), :].astype(F32)
        )
        target[rows_at(first + at, block, 16), :] = total.astype(target.dtype)
        return carry

    lax.fori_loop(0, count // block, step, 0)


class Spread:
    def __init__(self, link, order, rows, source, acc, landing):
        self.link, self.rows, self.source, self.acc, self.landing = link, rows, source, acc, landing
        self.order = [b for b in order if b < link.low]
        self.stages = len(self.order)
        self.slot = link.take(self.stages)
        self.piece = rows >> self.stages

    def inside(self, i):
        first = 0
        for j in range(1, i + 1):
            first = first + self.link.bit(self.order[j]) * (self.rows >> (j + 1))
        return first

    def kept(self):
        return rows_at(self.inside(self.stages - 1), self.piece, 16)

    def offset(self):
        return self.link.bit(self.order[0]) * (self.rows >> 1) + self.inside(self.stages - 1)

    def landed(self, i):
        first = sum(self.rows >> (j + 1) for j in range(i))
        return self.landing.at[pl.ds(first, self.rows >> (i + 1)), :]

    def copy(self, i):
        link, size = self.link, self.rows >> (i + 1)
        where, base = (self.source, 0) if i == 0 else (self.acc, self.inside(i - 1))
        other = base + (1 - link.bit(self.order[i])) * size
        return link.remote(
            self.slot + i, where.at[rows_at(other, size, 16), :], self.landed(i), link.partner(self.order[i])
        )

    def start(self, i):
        self.copy(i).start()

    def finish(self, i):
        size = self.rows >> (i + 1)
        self.copy(i).wait()
        if i == 0:
            add_rows(self.acc, 0, self.source, self.link.bit(self.order[0]) * size, self.landed(0), size)
        else:
            at = self.inside(i)
            add_rows(self.acc, at, self.acc, at, self.landed(i), size)

    def steps(self):
        yield lambda: self.start(0)
        for i in range(1, self.stages):

            def step(i=i):
                self.finish(i - 1)
                self.start(i)

            yield step


class Collect:
    def __init__(self, link, order, offset, piece, region):
        self.link, self.offset, self.piece, self.region = link, offset, piece, region
        self.order = [b for b in order if b < link.low][::-1]
        self.slot = link.take(len(self.order))

    def copy(self, i):
        size = self.piece << i
        first = self.offset()
        first = first - lax.rem(first, size)
        ref = self.region(first, size)
        return self.link.remote(self.slot + i, ref, ref, self.link.partner(self.order[i]))

    def steps(self):
        yield lambda: self.copy(0).start()
        for i in range(1, len(self.order)):

            def step(i=i):
                self.copy(i - 1).wait()
                self.copy(i).start()

            yield step
        yield lambda: self.copy(len(self.order) - 1).wait()


class Widen:
    def __init__(self, link, landing):
        self.link, self.landing = link, landing
        self.slot = link.take(max(0, link.bits - link.low))

    def run(self, piece):
        link = self.link
        for i, b in enumerate(range(link.low, link.bits)):
            copy = link.remote(self.slot + i, piece, self.landing.at[i], link.partner(b))
            copy.start()
            copy.wait()
            piece[...] = (piece[...].astype(F32) + self.landing[i].astype(F32)).astype(piece.dtype)


class Fan:
    def __init__(self, link, ends):
        self.link, self.ends = link, ends
        self.slot = link.take(link.tp_size - 1)

    def copy(self, k):
        source, target = self.ends(k)
        return self.link.remote(self.slot + k - 1, source, target, (self.link.dp, self.link.ahead(k)))

    def start(self):
        for k in range(1, self.link.tp_size):
            self.copy(k).start()

    def wait(self):
        for k in range(1, self.link.tp_size):
            self.copy(k).wait()


def then(*actions):
    def both():
        for action in actions:
            action()

    return both


class Track:
    def __init__(self):
        self.todo = []

    def add(self, steps, join=False):
        steps = list(steps)
        if join and self.todo:
            steps[0] = then(self.todo.pop(), steps[0])
        self.todo += steps

    def advance(self):
        if self.todo:
            self.todo.pop(0)()


def back_kernel(
    dp_size,
    tp_size,
    len_ref,
    vec,
    part_vec,
    xhat,
    rstd,
    mixed,
    wo,
    ff_far,
    ff_own,
    ff_landed,
    ff_near,
    dnorm,
    probs,
    x_hbm,
    q_hbm,
    kb_hbm,
    vb_hbm,
    yb_hbm,
    ssum_hbm,
    em_hbm,
    wq_hbm,
    wk_hbm,
    wv_hbm,
    grad_hbm,
    ff_hbm,
    go_hbm,
    gq_out,
    gkv_out,
    seq_out,
    vec_out,
    grad_in,
    ff_out,
    go_out,
    x,
    q,
    kb,
    vb,
    yb,
    ssum,
    em,
    wq,
    wk,
    wv,
    dres,
    dmix,
    dq,
    dl,
    prob_slots,
    dpart,
    dland,
    dfull,
    ff_zland,
    far_acc,
    far_land,
    own_acc,
    own_land,
    o_acc,
    o_land,
    q_acc,
    q_land,
    o_zland,
    q_zland,
    kv_send,
    kv_acc,
    kv_land,
    s_send,
    s_acc,
    s_land,
    vec_acc,
    vec_land,
    vec_z,
    wide_ff,
    wide_q,
    wide_kv,
    wide_s,
    send_sems,
    recv_sems,
    local_sems,
):
    link = Link(dp_size, tp_size, send_sems, recv_sems)
    rows, width = x.shape
    slots = yb.shape[0]
    low = link.low
    others = range(1, tp_size)
    first_load = pltpu.make_async_copy(dnorm, dres, local_sems.at[0])
    first_load.start()
    late = []
    for n, (source, target) in enumerate(
        (
            (q_hbm, q), (kb_hbm, kb), (vb_hbm, vb), (x_hbm, x), (yb_hbm, yb),
            (wq_hbm, wq), (wk_hbm, wk), (wv_hbm, wv), (ssum_hbm, ssum), (em_hbm, em),
        )
    ):
        late.append(pltpu.make_async_copy(source, target, local_sems.at[3 + n]))
        late[-1].start()
    link.greet(link.bits)

    lanes = 2
    deep = tp_size // lanes
    third = width // 3
    owned = width // tp_size

    ff_track, ff_orders = Track(), ((0, 1, 2), (0, 2, 1))
    ff_rows = width >> 3
    ff_parts = []
    for m in range(2):
        first, second, third_bit = ff_orders[m]
        far = Spread(link, (third_bit,), width >> 2, ff_far.at[m], far_acc.at[m], far_land.at[m])
        own = Spread(link, (second, third_bit), width >> 1, ff_own.at[m], own_acc.at[m], own_land.at[m])
        slot = link.take(2)

        def piece_copy(n, m=m, slot=slot):
            source, k = ((far_acc, 3), (ff_near, 2))[n]
            return link.remote(slot + n, source.at[m], ff_zland.at[m, n], (link.dp, link.behind(k)))

        def offset(m=m, own=own):
            return link.bit(ff_orders[m][0]) * (width >> 1) + own.offset()

        widen = Widen(link, wide_ff.at[m])

        def join(m=m, own=own, piece_copy=piece_copy, offset=offset, widen=widen):
            total = own_acc[m, own.kept(), :].astype(F32) + ff_landed[m].astype(F32)
            for n in range(2):
                piece_copy(n).wait()
                total = total + ff_zland[m, n].astype(F32)
            mine = rows_at(offset(), ff_rows, 16)
            ff_out[m, mine, :] = total.astype(BF)
            widen.run(ff_out.at[m, mine, :])

        collect = Collect(
            link, ff_orders[m], offset, ff_rows,
            lambda first, size, m=m: ff_out.at[m, rows_at(first, size, 16), :],
        )
        ff_parts.append((far, own, piece_copy, join, list(collect.steps())))

    def ff_begin():
        for far, own, piece_copy, _, _ in ff_parts:
            far.start(0)
            own.start(0)
            piece_copy(1).start()

    def ff_second():
        for far, own, piece_copy, _, _ in ff_parts:
            far.finish(0)
            piece_copy(0).start()

    def ff_second_own():
        for far, own, piece_copy, _, _ in ff_parts:
            own.finish(0)
            own.start(1)

    def ff_third():
        for _, own, _, join, collects in ff_parts:
            own.finish(1)

    def ff_join():
        for _, _, _, join, collects in ff_parts:
            join()
            collects[0]()

    stores = []

    def store(n, source, target):
        copy = pltpu.make_async_copy(source, target, local_sems.at[13 + n])
        stores.append(copy)
        return copy

    ff_store, go_store, grad_store = store(0, ff_out, ff_hbm), store(1, go_out, go_hbm), store(2, grad_in, grad_hbm)
    ff_begin()
    ff_track.add([ff_second, ff_second_own, then(ff_third, ff_join)])
    ff_track.add([then(*pair) for pair in zip(ff_parts[0][4][1:], ff_parts[1][4][1:])])
    ff_track.add([ff_store.start], join=True)

    def square_track(order, out, acc, landing, zland, wide):
        track, spread = Track(), Spread(link, order, width, out, acc, landing)
        q_rows, q_cols = spread.piece // deep, width // lanes

        def quarter(first, t):
            return (
                rows_at(first + lax.div(t, lanes) * q_rows, q_rows, 16),
                pl.ds(pl.multiple_of(lax.rem(t, lanes) * q_cols, 128), q_cols),
            )

        def there(k):
            return acc.at[quarter(spread.inside(spread.stages - 1), link.ahead(k))], zland.at[k - 1]

        def again(k):
            region = out.at[quarter(spread.offset(), link.tp)]
            return region, region

        fan, share, widen = Fan(link, there), Fan(link, again), Widen(link, wide)

        def join():
            fan.wait()
            total = acc[quarter(spread.inside(spread.stages - 1), link.tp)].astype(F32)
            for k in others:
                total = total + zland[k - 1].astype(F32)
            mine = quarter(spread.offset(), link.tp)
            out[mine] = total.astype(BF)
            widen.run(out.at[mine])
            share.start()

        collect = Collect(
            link, order, spread.offset, spread.piece, lambda first, size: out.at[rows_at(first, size, 16), :]
        )
        track.add(spread.steps())
        track.add([then(lambda: spread.finish(spread.stages - 1), fan.start), join, share.wait])
        track.add(collect.steps(), join=True)
        return track

    def owned_track(order, total_rows, cols, source, acc, landing, out, wide):
        source, acc, landing = source.at[:, cols], acc.at[:, cols], landing.at[:, cols]
        track, spread = Track(), Spread(link, order, total_rows, source, acc, landing)

        def region(k):
            ref = out.at[link.tp, rows_at(spread.offset(), spread.piece, 16), cols]
            return ref, ref

        share, widen = Fan(link, region), Widen(link, wide)

        def last():
            spread.finish(spread.stages - 1)
            ref = region(0)[0]
            ref[...] = acc[spread.kept(), :]
            widen.run(ref)
            share.start()

        collect = Collect(
            link, order, spread.offset, spread.piece, lambda first, size: out.at[:, rows_at(first, size, 16), cols]
        )
        track.add(spread.steps())
        track.add([last, share.wait])
        track.add(collect.steps(), join=True)
        return track

    o_track = square_track((0, 1, 2), go_out, o_acc, o_land, o_zland, wide_q.at[0])
    o_track.add([go_store.start], join=True)
    q_track = square_track((0, 2, 1), gq_out, q_acc, q_land, q_zland, wide_q.at[1])
    def halves(total_rows, source, acc, landing, out, wide):
        tracks = []
        for h, order in enumerate(((0, 1, 2), (0, 2, 1))):
            cols = slice(h * source.shape[1] // 2, (h + 1) * source.shape[1] // 2)
            tracks.append(owned_track(order, total_rows, cols, source, acc, landing, out, wide.at[h]))
        both = Track()
        both.add([then(*pair) for pair in zip(tracks[0].todo, tracks[1].todo)])
        return both

    kv_track = halves(2 * owned, kv_send, kv_acc, kv_land, gkv_out, wide_kv)
    s_track = halves(slots, s_send, s_acc, s_land, seq_out, wide_s)

    vec_track, vec_slot = Track(), link.take(link.bits)
    vec_fan = Fan(link, lambda k: (vec_z.at[link.tp], vec_z.at[link.tp]))

    def vec_copy(b):
        return link.remote(vec_slot + b, vec_acc.at[b], vec_land.at[b], link.partner(b))

    vec_track.add([lambda: vec_copy(0).start()])
    for b in range(link.bits):

        def vec_step(b=b):
            vec_copy(b).wait()
            total = vec_acc[b] + vec_land[b]
            if b + 1 < link.bits:
                vec_acc[b + 1] = total
                vec_copy(b + 1).start()
            else:
                vec_z[link.tp] = total
                vec_fan.start()

        vec_track.add([vec_step])

    def vec_last():
        vec_fan.wait()
        total = vec_z[0]
        for t in range(1, tp_size):
            total = total + vec_z[t]
        vec_out[...] = total

    vec_track.add([vec_last])

    block = min(256, rows)
    count = rows // block
    gain = vec[4:5, :]

    def norm_back(step, carry):
        g_gain, g_shift, g_out = carry
        here = place(step, block)
        grad, hat = dres[here, :], xhat[here, :]
        g_gain = g_gain + jnp.sum(grad * hat, axis=0, keepdims=True)
        g_shift = g_shift + jnp.sum(grad, axis=0, keepdims=True)
        scaled = grad * gain
        d_res = rstd[here, 0:1] * (
            scaled
            - jnp.mean(scaled, axis=-1, keepdims=True)
            - hat * jnp.mean(scaled * hat, axis=-1, keepdims=True)
        )
        dres[here, :] = d_res
        d_attn = d_res.astype(BF)
        dq[here, :] = d_attn
        g_out = g_out + jnp.sum(d_attn.astype(F32), axis=0, keepdims=True)
        return g_gain, g_shift, g_out

    zero = jnp.zeros((1, width), F32)
    first_load.wait()
    g_gain, g_shift, g_out = lax.fori_loop(0, count, norm_back, (zero, zero, zero))
    vec_acc[0] = part_vec[...]
    vec_acc[0, 3:4, :] = g_out
    vec_acc[0, 4:5, :] = g_gain
    vec_acc[0, 5:6, :] = g_shift
    d_attn = dq

    def weight_grad(left, right, target):
        for m in range(3):
            cols = slice(m * third, (m + 1) * third)
            target[cols, :] = dot(left[:, cols], right[...], 0, 0).astype(BF)

    weight_grad(mixed, d_attn, go_out)
    o_track.advance()
    ff_track.advance()
    dmix[...] = dot(d_attn[...], wo[...], 1, 1).astype(BF)
    o_track.advance()
    for load in late:
        load.wait()

    own_half = lax.div(link.tp, 2)
    parity = lax.rem(link.tp, 2)
    three = PAIRS // 2

    def pair_at(n):
        second = lax.div(n, three)
        which = (1 - own_half) * (1 - second) + own_half * second
        along = lax.rem(n, three)
        return which * three + along * parity + (three - 1 - along) * (1 - parity)

    def fetch(n):
        slot = lax.rem(n, 2)
        return pltpu.make_async_copy(probs.at[pair_at(n)], prob_slots.at[slot], local_sems.at[1 + slot])

    fetch(0).start()

    def attend_back(n):
        p = pair_at(n)
        cols = place(p, PAIR)

        @pl.when(n + 1 < PAIRS)
        def _():
            fetch(n + 1).start()

        fetch(n).wait()
        held = prob_slots.at[lax.rem(n, 2)]

        def part(step, carry):
            here = place(step, block)
            d_probs = dot(dmix[here, cols], vb[p], 1, 1)
            weights = held[here, :].astype(F32)
            halves = []
            for h in range(2):
                w = weights[:, h * slots : (h + 1) * slots]
                d = d_probs[:, h * slots : (h + 1) * slots]
                halves.append((w * (d - jnp.sum(w * d, axis=-1, keepdims=True))).astype(BF))
            both = jnp.concatenate(halves, axis=1)
            dl[here, :] = both
            dq[here, cols] = (dot(both, kb[p], 1, 0) * 0.125).astype(BF)
            return carry

        lax.fori_loop(0, count, part, 0)
        top, under = rows_at(p * PAIR, HEAD, HEAD), rows_at(p * PAIR + HEAD, HEAD, HEAD)
        for n, total in enumerate(
            (dot(q[:, cols], dl[...], 0, 0) * 0.125, dot(dmix[:, cols], held[...], 0, 0))
        ):
            dpart[n, top, :] = total[:HEAD, :slots].astype(BF)
            dpart[n, under, :] = total[HEAD:, slots:].astype(BF)

    d_slot = link.take(tp_size - 1)

    def d_copy(j):
        near = 2 * own_half + (1 - parity)
        peer = near if j == 2 else 2 * (1 - own_half) + lax.rem(parity + j, 2)
        block_of = dpart.at[:, rows_at(peer * owned, owned, 64), :]
        return link.remote(d_slot + j, block_of, dland.at[j], (link.dp, peer))

    events = [
        then(),
        then(lambda: d_copy(1).start(), ff_track.advance),
        lambda: d_copy(0).start(),
        o_track.advance,
        then(lambda: d_copy(2).start(), ff_track.advance),
        then(),
    ]

    def one(n, carry):
        attend_back(n)
        for i, event in enumerate(events):
            pl.when(n == i)(event)
        return carry

    lax.fori_loop(0, PAIRS, one, 0)

    weight_grad(x, dq, gq_out)
    q_track.advance()
    ff_track.advance()

    def input_grad(step, carry):
        here = place(step, block)
        dres[here, :] += dot(dq[here, :], wq[...], 1, 1)
        return carry

    lax.fori_loop(0, count, input_grad, 0)
    q_track.advance()
    vec_acc[0, 0:1, :] = jnp.sum(dq[...].astype(F32), axis=0, keepdims=True)

    for j in range(tp_size - 1):
        d_copy(j).wait()
    own_block = rows_at(link.tp * owned, owned, 64)
    for n in range(2):
        total = dpart[n, own_block, :].astype(F32)
        for j in range(tp_size - 1):
            total = total + dland[j, n].astype(F32)
        dfull[n, own_block, :] = total.astype(BF)
    d_share = Fan(link, lambda k: (dfull.at[:, own_block, :], dfull.at[:, own_block, :]))
    d_share.start()
    ff_track.advance()
    for n in range(2):
        kv_send[n * owned : (n + 1) * owned, :] = dot(dfull[n, own_block, :], yb[...], 1, 0).astype(BF)
    kv_track.advance()
    q_track.advance()
    ff_track.advance()
    kv_track.advance()
    o_track.advance()
    kv_track.advance()
    q_track.advance()
    kv_track.advance()
    o_track.advance()
    d_share.wait()
    backs = dot(wk[...], dfull[0], 1, 0) + dot(wv[...], dfull[1], 1, 0)
    back = backs.T.astype(BF)
    small = vec[0:8, :].astype(BF)
    bias_row = dot(small, dfull[0], 1, 0)[1:2, :] + dot(small, dfull[1], 1, 0)[2:3, :]
    bias_column = jnp.broadcast_to(bias_row, (128, slots)).T[:, 0:1]
    position = lax.broadcasted_iota(jnp.int32, (1, rows), 1) + link.tp * rows
    live = (position < len_ref[0]).astype(F32)
    s_send[...] = ((dot(back, x[...], 1, 1) + bias_column) * live).astype(BF)
    s_track.advance()
    column = ssum[...].T[0:8, :]
    column_b = column.astype(BF)
    column_low = (column - column_b.astype(F32)).astype(BF)
    for n in range(2):
        total = dot(column_b, dfull[n], 1, 1) + dot(column_low, dfull[n], 1, 1)
        vec_acc[0, 1 + n : 2 + n, :] = total[0:1, :] * (1.0 / tp_size)
    vec_track.advance()
    s_track.advance()

    def input_grad_last(step, carry):
        here = place(step, block)
        grad_in[here, :] = (dres[here, :] + dot(em[:, here], back, 0, 0)).astype(BF)
        return carry

    lax.fori_loop(0, count, input_grad_last, 0)
    grad_store.start()
    tracks = [s_track, kv_track, q_track, o_track, vec_track, ff_track]
    while any(track.todo for track in tracks):
        for track in tracks:
            track.advance()
    for copy in stores:
        copy.wait()


def back(mesh, lengths, vec, part_vec, xhat, rstd, mixed, wo, ff_far, ff_own, ff_landed, ff_near, dnorm, probs, *late):
    dp_size, tp_size = mesh.shape["dp"], mesh.shape["tp"]
    bits = dp_size.bit_length() - 1
    low = min(3, bits)
    wide = max(1, bits - low)
    rows, width = xhat.shape
    slots = late[4].shape[0]
    owned = width // tp_size
    others = tp_size - 1
    vmem = pl.BlockSpec(memory_space=pltpu.VMEM)
    hbm = pl.BlockSpec(memory_space=pltpu.HBM)
    shape = jax.ShapeDtypeStruct

    def landing(total):
        return sum(total >> (i + 1) for i in range(low))

    def buf(*dims, dtype=BF):
        return pltpu.VMEM(dims, dtype)

    ff_piece, kv_piece, s_piece = width >> low, 2 * owned >> low, slots >> low
    quarter = (ff_piece // (tp_size // 2), width // 2)
    return pl.pallas_call(
        functools.partial(back_kernel, dp_size, tp_size),
        out_shape=(
            shape((rows, width), BF),
            shape((2, width, width), BF),
            shape((width, width), BF),
            shape((width, width), BF),
            shape((tp_size, 2 * owned, width), BF),
            shape((tp_size, slots, rows), BF),
            shape((VECTORS, width), F32),
        ),
        in_specs=[pl.BlockSpec(memory_space=pltpu.SMEM)] + [vmem] * 9 + [hbm] * (3 + len(late)),
        out_specs=tuple([hbm] * 3 + [vmem] * 4),
        scratch_shapes=[buf(rows, width), buf(2, width, width), buf(width, width)]
        + [pltpu.VMEM(array.shape, array.dtype) for array in late]
        + [
            buf(rows, width, dtype=F32),
            buf(rows, width),
            buf(rows, width),
            buf(rows, 2 * slots),
            buf(2, rows, 2 * slots),
            buf(2, width, slots),
            buf(others, 2, owned, slots),
            buf(2, width, slots),
            buf(2, 2, ff_piece, width),
            buf(2, width >> 3, width),
            buf(2, width >> 3, width),
            buf(2, width >> 2, width),
            buf(2, (width >> 2) + (width >> 3), width),
            buf(width // 2, width),
            buf(landing(width), width),
            buf(width // 2, width),
            buf(landing(width), width),
            buf(others, *quarter),
            buf(others, *quarter),
            buf(2 * owned, width),
            buf(owned, width),
            buf(landing(2 * owned), width),
            buf(slots, rows),
            buf(slots // 2, rows),
            buf(landing(slots), rows),
            buf(bits, VECTORS, width, dtype=F32),
            buf(bits, VECTORS, width, dtype=F32),
            buf(tp_size, VECTORS, width, dtype=F32),
            buf(2, wide, ff_piece, width),
            buf(2, wide, *quarter),
            buf(2, wide, kv_piece, width // 2),
            buf(2, wide, s_piece, rows // 2),
            pltpu.SemaphoreType.DMA((BACK_SEMS,)),
            pltpu.SemaphoreType.DMA((BACK_SEMS,)),
            pltpu.SemaphoreType.DMA((6 + len(late),)),
        ],
        compiler_params=pltpu.CompilerParams(
            collective_id=1, has_side_effects=True, vmem_limit_bytes=VMEM_LIMIT
        ),
        name="back",
    )(lengths, vec, part_vec, xhat, rstd, mixed, wo, ff_far, ff_own, ff_landed, ff_near, dnorm, probs, *late)


class ChunkSpread:
    def __init__(self, link, rows, sent, acc, landing):
        self.link, self.rows, self.sent, self.acc, self.landing = link, rows, sent, acc, landing
        self.orders = [[b for b in order if b < link.low] for order in ((0, 1, 2), (0, 2, 1))]
        self.stages = link.low
        self.slot = link.take(2 * link.low * acc.shape[1])

    def inside(self, m, i):
        first = 0
        for j in range(1, i + 1):
            first = first + self.link.bit(self.orders[m][j]) * (self.rows >> (j + 1))
        return first

    def copy(self, c, m, i):
        link, size = self.link, self.rows >> (i + 1)
        bit = self.orders[m][i]
        if i == 0:
            source = self.sent.at[m, lax.rem(c, 2), rows_at((1 - link.bit(bit)) * size, size, 16), :]
        else:
            source = self.acc.at[m, c, rows_at(self.inside(m, i - 1) + (1 - link.bit(bit)) * size, size, 16), :]
        first = sum(self.rows >> (j + 1) for j in range(i))
        slot = self.slot + (i * 2 + m) * self.acc.shape[1] + c
        return link.remote(slot, source, self.landing.at[m, c, pl.ds(first, size), :], link.partner(bit))

    def start(self, c, m, i):
        self.copy(c, m, i).start()

    def finish(self, c, m, i):
        size = self.rows >> (i + 1)
        self.copy(c, m, i).wait()
        first = sum(self.rows >> (j + 1) for j in range(i))
        landed = self.landing.at[m, c, pl.ds(first, size), :]
        acc = self.acc.at[m, c]
        if i == 0:
            mine = self.link.bit(self.orders[m][0]) * size
            add_rows(acc, 0, self.sent.at[m, lax.rem(c, 2)], mine, landed, size)
        else:
            at = self.inside(m, i)
            add_rows(acc, at, acc, at, landed, size)


MIDDLE_SEMS = 96
MIDDLE_TICKS = (
    (),
    ((0, 2, 1), (1, 1, 0), (1, 3, 0)),
    ((1, 1, 1),),
    ((0, 2, 2), (1, 3, 1), (1, 2, 0)),
    ((1, 1, 2),),
    ((0, 2, 3), (1, 3, 2), (1, 2, 1)),
    ((1, 1, 3),),
    ((1, 2, 2), (1, 3, 3), (1, 2, 3)),
)


def middle_kernel(
    dp_size,
    tp_size,
    vec,
    bup_all,
    xhat,
    out_grad_hbm,
    own_up,
    own_dn,
    ups,
    layer_out,
    dnorm,
    part_vec,
    ff_landed,
    ff_near,
    ff_far,
    ff_own,
    whole,
    out_grad,
    nb,
    act,
    slope,
    d_branch,
    d_acc,
    sent,
    acc,
    landing,
    send_sems,
    recv_sems,
    local_sems,
):
    link = Link(dp_size, tp_size, send_sems, recv_sems)
    rows, width = xhat.shape
    used = [0]

    def local(source, target):
        copy = pltpu.make_async_copy(source, target, local_sems.at[used[0]])
        used[0] += 1
        copy.start()
        return copy

    collect = WeightCollect(link, width // 2, lambda k: whole.at[1, k])
    cross = Cross(link, collect, own_dn)
    up_last = WeightCollect(link, width // 2, lambda k: whole.at[0, 2])
    placed = [
        local(ups.at[1, up_last.rows(h, 0), :], whole.at[0, 2, up_last.rows(h, 0), :]) for h in range(2)
    ]
    owns = [local(own_up, whole.at[0, 0])]
    owns += [local(ups.at[k - 1], whole.at[0, k]) for k in (1, 3)]
    owns += [local(own_dn, whole.at[1, 0]), local(out_grad_hbm, out_grad)]
    link.greet(link.low)
    for k in (1, 3, 2):
        cross.start(k)
    for copy in placed:
        copy.wait()
    up_last.step(2, 0)
    gain, shift, b_down, f_gain, f_shift = (vec[n : n + 1, :] for n in (4, 5, 6, 7, 8))
    block = min(256, rows)
    count = rows // block
    big = rows // 2

    def norm(step, carry):
        here = place(step, block)
        nb[here, :] = (xhat[here, :] * gain + shift).astype(BF)
        return carry

    lax.fori_loop(0, count, norm, 0)
    for copy in owns[:3]:
        copy.wait()

    def forward(step, carry):
        n = lax.div(step, 2)
        k = n + lax.div(n, 2) * (7 - 2 * n - 2)
        here, cols = place(lax.rem(step, 2), big), place(k, width)
        pre = dot(nb[here, :], whole[0, k], 1, 0) + bup_all[link.behind(k), 0:1, :]
        cdf = 0.5 * (1.0 + lax.erf(pre * 0.7071067811865476))
        act[here, cols] = (pre * cdf).astype(BF)
        slope[here, cols] = (cdf + pre * (jnp.exp(pre * pre * -0.5) * 0.3989422804014327)).astype(BF)
        for n, ticks in enumerate(MIDDLE_TICKS):

            @pl.when(step == n)
            def _():
                for m, shard, j in ticks:
                    if m == 1 and j == 0:
                        cross.wait(shard)
                    (up_last, collect)[m].step(shard, j)

        return carry

    lax.fori_loop(0, 2 * tp_size, forward, 0)
    for copy in owns[3:]:
        copy.wait()

    def second_norm(step, carry):
        g_gain, g_shift, g_down = carry
        here = place(step, block)
        branch = dot(act[here, 0:width], whole[1, 0], 1, 0)
        for k in range(1, tp_size):
            branch = branch + dot(act[here, k * width : (k + 1) * width], whole[1, k], 1, 0)
        res = xhat[here, :] * gain + shift + (branch + b_down)
        center = res - jnp.mean(res, axis=-1, keepdims=True)
        inverse = lax.rsqrt(jnp.mean(center * center, axis=-1, keepdims=True) + 1e-05)
        hat = center * inverse
        layer_out[here, :] = (hat * f_gain + f_shift).astype(BF)
        grad = out_grad[here, :].astype(F32)
        g_gain = g_gain + jnp.sum(grad * hat, axis=0, keepdims=True)
        g_shift = g_shift + jnp.sum(grad, axis=0, keepdims=True)
        scaled = grad * f_gain
        d_res = inverse * (
            scaled
            - jnp.mean(scaled, axis=-1, keepdims=True)
            - hat * jnp.mean(scaled * hat, axis=-1, keepdims=True)
        )
        d_acc[here, :] = d_res
        rounded = d_res.astype(BF)
        d_branch[here, :] = rounded
        g_down = g_down + jnp.sum(rounded.astype(F32), axis=0, keepdims=True)
        return g_gain, g_shift, g_down

    zero = jnp.zeros((1, width), F32)
    g_gain, g_shift, g_down = lax.fori_loop(0, count, second_norm, (zero, zero, zero))
    part_vec[...] = jnp.zeros_like(part_vec)
    part_vec[6:7, :] = g_gain
    part_vec[7:8, :] = g_shift
    part_vec[8:9, :] = g_down

    spread = ChunkSpread(link, width, sent, acc, landing)
    third = width // 3

    def weight_grad(left, first, right, cols, target):
        for m in range(3):
            mine = pl.ds(pl.multiple_of(first + m * third, third), third)
            target[m * third : (m + 1) * third, :] = dot(left[:, mine], right[:, cols], 0, 0).astype(BF)

    def settle(n, steps):
        for m, late, stage in steps:

            @pl.when(n >= late)
            def _():
                spread.finish(n - late, m, stage)

            if stage < 2:

                @pl.when(jnp.logical_and(n >= late, n - late < 3 - stage))
                def _():
                    spread.start(n - late, m, stage + 1)

    def backward(n, carry):
        k = lax.rem(n + 1, tp_size)
        cols = place(k, width)
        slot = lax.rem(n, 2)
        weight_grad(act, k * width, d_branch, slice(0, width), sent.at[1, slot])
        spread.start(n, 1, 0)
        settle(n, ((0, 1, 0), (1, 2, 1)))

        def through(step, total):
            here = place(step, big)
            grad = (dot(d_branch[here, :], whole[1, k], 1, 1) * slope[here, cols].astype(F32)).astype(BF)
            slope[here, cols] = grad
            return total + jnp.sum(grad.astype(F32), axis=0, keepdims=True)

        part_vec[pl.ds(9 + link.behind(k), 1), :] = lax.fori_loop(0, 2, through, zero)
        settle(n, ((1, 0, 0), (0, 2, 1)))
        weight_grad(nb, 0, slope, cols, sent.at[0, slot])
        spread.start(n, 0, 0)
        return carry

    lax.fori_loop(0, tp_size, backward, 0)

    def input_grad(step, carry):
        here = place(step, big)
        total = d_acc[here, :]
        for k in range(tp_size):
            total = total + dot(slope[here, k * width : (k + 1) * width], whole[0, k], 1, 1)
        d_acc[here, :] = total
        return carry

    slot = link.take(2)
    crossing = []
    lax.fori_loop(0, 1, input_grad, 0)
    for m in (1, 0):
        spread.finish(0, m, 2)
        at = rows_at(spread.inside(m, 2), width >> 3, 16)
        crossing.append(
            link.remote(slot + m, acc.at[m, 0, at, :], ff_landed.at[m], (link.dp, link.behind(1)))
        )
        crossing[-1].start()
    spread.finish(3, 0, 0)
    spread.finish(2, 1, 1)
    stores = [local(acc.at[m, 3], ff_own.at[m]) for m in range(2)]
    lax.fori_loop(1, 2, input_grad, 0)
    stores.append(local(d_acc, dnorm))
    spread.finish(2, 0, 1)
    for m in (1, 0):
        spread.finish(1, m, 2)
    for m in range(2):
        at = rows_at(spread.inside(m, 2), width >> 3, 16)
        stores.append(local(acc.at[m, 1, at, :], ff_near.at[m]))
        at = rows_at(spread.inside(m, 1), width >> 2, 16)
        stores.append(local(acc.at[m, 2, at, :], ff_far.at[m]))
    for copy in crossing + stores:
        copy.wait()


def middle(mesh, vec, bup_all, xhat, out_grad, w_up, w_dn, ups):
    dp_size, tp_size = mesh.shape["dp"], mesh.shape["tp"]
    low = min(3, dp_size.bit_length() - 1)
    assert low == 3 and tp_size == 4
    rows, width = xhat.shape
    hidden = tp_size * width
    vmem = pl.BlockSpec(memory_space=pltpu.VMEM)
    hbm = pl.BlockSpec(memory_space=pltpu.HBM)
    shape = jax.ShapeDtypeStruct

    def buf(*dims, dtype=BF):
        return pltpu.VMEM(dims, dtype)

    return pl.pallas_call(
        functools.partial(middle_kernel, dp_size, tp_size),
        out_shape=(
            shape((rows, width), BF),
            shape((rows, width), F32),
            shape((VECTORS, width), F32),
            shape((2, width >> 3, width), BF),
            shape((2, width >> 3, width), BF),
            shape((2, width >> 2, width), BF),
            shape((2, width >> 1, width), BF),
        ),
        in_specs=[vmem] * 3 + [hbm] * 4,
        out_specs=(vmem, hbm, vmem, hbm, hbm, hbm, hbm),
        scratch_shapes=[
            buf(2, tp_size, width, width),
            buf(rows, width),
            buf(rows, width),
            buf(rows, hidden),
            buf(rows, hidden),
            buf(rows, width),
            buf(rows, width, dtype=F32),
            buf(2, 2, width, width),
            buf(2, tp_size, width // 2, width),
            buf(2, tp_size, sum(width >> (i + 1) for i in range(low)), width),
            pltpu.SemaphoreType.DMA((MIDDLE_SEMS,)),
            pltpu.SemaphoreType.DMA((MIDDLE_SEMS,)),
            pltpu.SemaphoreType.DMA((24,)),
        ],
        compiler_params=pltpu.CompilerParams(
            collective_id=2, has_side_effects=True, vmem_limit_bytes=VMEM_LIMIT
        ),
        name="middle",
    )(vec, bup_all, xhat, out_grad, w_up, w_dn, ups)


def finish_kernel(
    tp_size, ff, gq, go, gkv, seq, vec, layer_out, grad_in,
    o_up, o_dn, o_q, o_o, o_k, o_v, o_seq, o_layer, o_grad, *rest,
):
    vectors, (in_up, in_dn, in_q, in_o, in_kv, in_seq, f_up, f_dn, f_q, f_o, f_k, f_v, f_seq, turn, pass_a, pass_b, in_sems, out_sems) = rest[:10], rest[10:]
    pairs = [(gq, in_q), (go, in_o), (ff.at[0], in_up), (ff.at[1], in_dn), (gkv, in_kv), (seq, in_seq), (layer_out, pass_a), (grad_in, pass_b)]
    loads = []
    for n, (source, target) in enumerate(pairs):
        loads.append(pltpu.make_async_copy(source, target, in_sems.at[n]))
        loads[-1].start()
    stores = []

    def put(staged, out):
        copy = pltpu.make_async_copy(staged, out, out_sems.at[len(stores)])
        copy.start()
        stores.append(copy)

    for n, (held, out) in enumerate(((pass_a, o_layer), (pass_b, o_grad))):
        loads[6 + n].wait()
        put(held, out)
    for n, row in enumerate((0, 1, 2, 3, 4, 5, 6, 7, 8)):
        vectors[n][...] = vec[row, :]
    vectors[9][...] = vec[pl.ds(9 + lax.axis_index("tp"), 1), :][0]
    width = gq.shape[0]
    for n, (narrow, wide, out) in enumerate(
        ((in_q, f_q, o_q), (in_o, f_o, o_o), (in_up, f_up, o_up), (in_dn, f_dn, o_dn))
    ):
        loads[n].wait()
        wide[...] = narrow[...].astype(F32)
        put(wide, out)
    loads[4].wait()
    owned = width // tp_size
    for n, (wide, out) in enumerate(((f_k, o_k), (f_v, o_v))):
        for c in range(tp_size):
            turn[c * owned : (c + 1) * owned, :] = in_kv[c, n * owned : (n + 1) * owned, :]
        for c in range(3):
            cols = slice(c * (width // 3), (c + 1) * (width // 3))
            wide[:, cols] = turn[cols, :].astype(F32).T
        put(wide, out)
    loads[5].wait()
    rows = in_seq.shape[2]
    for c in range(tp_size):
        f_seq[:, c * rows : (c + 1) * rows] = in_seq[c].astype(F32)
    put(f_seq, o_seq)
    for copy in stores:
        copy.wait()


def finish(tp_size, ff, gq, go, gkv, seq, vec, layer_out, grad_in):
    width = gq.shape[0]
    _, slots, rows = seq.shape
    square, flat = (width, width), (slots, tp_size * rows)
    vmem = pl.BlockSpec(memory_space=pltpu.VMEM)
    hbm = pl.BlockSpec(memory_space=pltpu.HBM)
    shape = jax.ShapeDtypeStruct
    return pl.pallas_call(
        functools.partial(finish_kernel, tp_size),
        out_shape=tuple([shape(square, F32)] * 6 + [shape(flat, F32)] + [shape(layer_out.shape, BF)] * 2 + [shape((width,), F32)] * 10),
        in_specs=[hbm] * 5 + [vmem] + [hbm] * 2,
        out_specs=tuple([hbm] * 9 + [vmem] * 10),
        scratch_shapes=[pltpu.VMEM(square, BF)] * 4
        + [pltpu.VMEM(gkv.shape, BF), pltpu.VMEM(seq.shape, BF)]
        + [pltpu.VMEM(square, F32)] * 6
        + [pltpu.VMEM(flat, F32), pltpu.VMEM(square, BF)]
        + [pltpu.VMEM(layer_out.shape, BF)] * 2
        + [pltpu.SemaphoreType.DMA((8,)), pltpu.SemaphoreType.DMA((9,))],
        compiler_params=pltpu.CompilerParams(vmem_limit_bytes=VMEM_LIMIT),
        name="finish",
    )(ff, gq, go, gkv, seq, vec, layer_out, grad_in)


def on_device(
    mesh,
    layer_in,
    out_grad,
    lengths,
    w_query,
    b_query,
    w_key,
    b_key,
    w_value,
    b_value,
    w_out,
    b_out,
    seq_proj,
    attn_gain,
    attn_shift,
    w_up,
    b_up,
    w_down,
    b_down,
    ffn_gain,
    ffn_shift,
):
    row_count, width = layer_in.shape
    tp_size = mesh.shape["tp"]
    vectors = (b_query, b_key, b_value, b_out, attn_gain, attn_shift, b_down, ffn_gain, ffn_shift)
    vec, xhat, rstd, bup_all, mixed, queries, probs, kb, vb, folded, ssum, own_proj, ups = front(
        mesh, lengths, layer_in, w_query, seq_proj, w_key, w_value, w_out, w_up, vectors, b_up
    )
    layer_out, d_normed, part_vec, ff_landed, ff_near, ff_far, ff_own = middle(
        mesh, vec, bup_all, xhat, out_grad, w_up, w_down, ups
    )
    grad_in, g_ff, g_o, g_q, g_kv, g_seq, vec_sum = back(
        mesh, lengths, vec, part_vec, xhat, rstd, mixed, w_out, ff_far, ff_own, ff_landed, ff_near, d_normed, probs,
        layer_in, queries, kb, vb, folded, ssum, own_proj, w_query, w_key, w_value
    )
    (
        g_w_up, g_w_down, g_w_query, g_w_out, g_w_key, g_w_value, g_seq_proj, layer_out, grad_in,
        g_b_query, g_b_key, g_b_value, g_b_out, g_attn_gain, g_attn_shift, g_ffn_gain, g_ffn_shift, g_b_down, g_b_up,
    ) = finish(tp_size, g_ff, g_q, g_o, g_kv, g_seq, vec_sum, layer_out, grad_in)
    return (
        layer_out,
        grad_in,
        g_w_query,
        g_b_query,
        g_w_key,
        g_b_key,
        g_w_value,
        g_b_value,
        g_w_out,
        g_b_out,
        g_seq_proj,
        g_attn_gain,
        g_attn_shift,
        g_w_up,
        g_b_up,
        g_w_down,
        g_b_down,
        g_ffn_gain,
        g_ffn_shift,
    )


def solution(mesh):
    in_specs = (
        P(("dp", "tp"), None),
        P(("dp", "tp"), None),
        P("dp"),
        *([P()] * 11),
        P(None, "tp"),
        P("tp"),
        P("tp", None),
        P(),
        P(),
        P(),
    )
    out_specs = (
        P(("dp", "tp"), None),
        P(("dp", "tp"), None),
        *([P()] * 11),
        P(None, "tp"),
        P("tp"),
        P("tp", None),
        P(),
        P(),
        P(),
    )
    return jax.shard_map(
        functools.partial(on_device, mesh), mesh=mesh, in_specs=in_specs, out_specs=out_specs, check_vma=False
    )
```

```python
import functools

import jax
import jax.numpy as jnp
from jax import lax
from jax.experimental import pallas as pl
from jax.experimental.pallas import tpu as pltpu
from jax.sharding import PartitionSpec as P

HEADS = 12
HEAD = 64
PAIRS = HEADS // 2
PAIR = 2 * HEAD
BF = jnp.bfloat16
F32 = jnp.float32
MESH = pl.DeviceIdType.MESH
VMEM_LIMIT = 67_043_328
BLOCK_F, BLOCK_M, BLOCK_B, GRAD_SPLIT = 1024, 512, 1024, 2


def dot(left, right, left_dim, right_dim):
    return lax.dot_general(
        left, right, (((left_dim,), (right_dim,)), ((), ())), preferred_element_type=F32
    )


def place(index, size):
    return pl.ds(pl.multiple_of(index * size, size), size)


def rows_at(first, size, multiple):
    return pl.ds(pl.multiple_of(first, multiple), size)


class Link:
    def __init__(self, dp_size, tp_size, send_sems, recv_sems):
        self.dp_size, self.tp_size = dp_size, tp_size
        self.dp, self.tp = lax.axis_index("dp"), lax.axis_index("tp")
        self.bits = dp_size.bit_length() - 1
        self.low = min(3, self.bits)
        self.send_sems, self.recv_sems = send_sems, recv_sems
        self.used = 0
        self.bit_values = [lax.rem(lax.div(self.dp, 1 << b), 2) for b in range(self.bits)]
        self.partners = [
            (self.dp + (1 - 2 * self.bit_values[b]) * (1 << b), self.tp) for b in range(self.bits)
        ]
        self.aheads = [lax.rem(self.tp + k, tp_size) for k in range(tp_size)]

    def bit(self, b):
        return self.bit_values[b]

    def partner(self, b):
        return self.partners[b]

    def ahead(self, k):
        return self.aheads[k]

    def behind(self, k):
        if isinstance(k, int):
            return self.aheads[(self.tp_size - k) % self.tp_size]
        return lax.rem(self.tp + self.tp_size - k, self.tp_size)

    def greet(self, dp_bits):
        barrier = pltpu.get_barrier_semaphore()
        peers = [(self.dp, self.ahead(k)) for k in range(1, self.tp_size)]
        peers += [self.partner(b) for b in range(dp_bits)]
        for peer in peers:
            pl.semaphore_signal(barrier, inc=1, device_id=peer, device_id_type=MESH)
        pl.semaphore_wait(barrier, len(peers))

    def take(self, count):
        first = self.used
        self.used += count
        assert self.used <= self.send_sems.shape[0]
        return first

    def remote(self, slot, source, target, device):
        return pltpu.make_async_remote_copy(
            src_ref=source,
            dst_ref=target,
            send_sem=self.send_sems.at[slot],
            recv_sem=self.recv_sems.at[slot],
            device_id=device,
            device_id_type=MESH,
        )

    def send(self, source, target, device):
        copy = self.remote(self.take(1), source, target, device)
        copy.start()
        return copy


FRONT_SEMS = 64
VECTORS = 16


def half_orders(low):
    return [[b for b in order if b < low] for order in ((1, 2, 0), (2, 1, 0))]


class WeightCollect:
    def __init__(self, link, part, whole):
        self.link, self.whole, self.part = link, whole, part
        self.orders = half_orders(link.low)
        self.piece = self.part >> link.low
        self.stages = link.low
        self.slot = link.take(2 * (link.tp_size - 1) * link.low)
        self.firsts = []
        for h in range(2):
            first, size, starts = h * part, self.piece, []
            for b in self.orders[h]:
                starts.append(size * link.bit(b))
                size *= 2
            self.firsts.append([sum(starts[i:], first) for i in range(self.stages)])

    def rows(self, h, i):
        return rows_at(self.firsts[h][i], self.piece << i, 16)

    def copies(self, k, i):
        for h in range(2):
            region = self.whole(k).at[self.rows(h, i), :]
            slot = self.slot + ((k - 1) * self.stages + i) * 2 + h
            yield self.link.remote(slot, region, region, self.link.partner(self.orders[h][i]))

    def step(self, k, j):
        if j > 0:
            for copy in self.copies(k, j - 1):
                copy.wait()
        if j < self.stages:
            for copy in self.copies(k, j):
                copy.start()


class Cross:
    def __init__(self, link, collect, shard, target):
        self.link, self.collect, self.shard, self.target = link, collect, shard, target
        self.slot = link.take(2 * (link.tp_size - 1))

    def copies(self, k):
        for h in range(2):
            rows = self.collect.rows(h, 0)
            yield self.link.remote(
                self.slot + 2 * (k - 1) + h,
                self.shard.at[rows, :],
                self.target(k, h, rows),
                (self.link.dp, self.link.ahead(k)),
            )

    def start(self, k):
        for copy in self.copies(k):
            copy.start()

    def wait(self, k):
        for copy in self.copies(k):
            copy.wait()


FRONT_TICKS = (
    ((3, 0),),
    (),
    ((3, 1),),
    (),
    ((3, 2),),
    (),
    ((3, 3),),
)


def front_kernel(dp_size, tp_size, n_vectors, len_ref, x_hbm, wq_hbm, e, wk_hbm, wv_hbm, wo_hbm, wup, wdn, *rest):
    vectors, b_up, rest = rest[:n_vectors], rest[n_vectors], rest[n_vectors + 1 :]
    outs, scratch = rest[:14], rest[14:]
    (vec, bup_all, xhat_out, rstd_out, mixed_out, q_out, probs_out, kb_out, vb_out, yb_out, ssum_out, em_out, ups, pieces) = outs
    (x, wq, wk, wv, wo, e_all, xhat, rstd, mixed, q, probs, kb, vb, yb, ssum, em, bup, ysend, yrecv, send_sems, recv_sems, local_sems) = scratch
    link = Link(dp_size, tp_size, send_sems, recv_sems)
    rows, width = x.shape
    slots, total = e_all.shape
    quarter = slots // tp_size
    others = range(1, tp_size)
    used = [0]

    def local(source, target):
        copy = pltpu.make_async_copy(source, target, local_sems.at[used[0]])
        used[0] += 1
        copy.start()
        return copy

    own_first = link.tp * rows
    e_own = local(e.at[:, rows_at(own_first, rows, rows)], em)
    early = [local(x_hbm, x), local(wq_hbm, wq)]
    late = [local(e, e_all), local(wk_hbm, wk), local(wv_hbm, wv), local(wo_hbm, wo)]
    link.greet(link.low)

    collect = WeightCollect(link, wup.shape[0] // 2, lambda k: ups.at[k - 1])
    cross = Cross(link, collect, wup, lambda k, h, rows: ups.at[k - 1, rows, :])
    cross_down = Cross(link, collect, wdn, lambda k, h, rows: pieces.at[k - 1, h])
    cross.start(1)
    vec[...] = jnp.zeros_like(vec)
    for n, vector in enumerate(vectors):
        vec[n : n + 1, :] = vector[...].astype(F32).reshape(1, width)
    bup[...] = jnp.broadcast_to(b_up[...].astype(F32).reshape(1, width), bup.shape)
    bup_all[link.tp] = bup[...]
    length = len_ref[0]
    position = lax.broadcasted_iota(jnp.int32, (1, rows), 1) + own_first
    live = (position < length).astype(F32)
    e_own.wait()
    early[0].wait()
    em[...] = (em[...].astype(F32) * live).astype(BF)
    ysend[...] = dot(em[...], x[...], 1, 0).astype(ysend.dtype)
    reduce = [
        link.send(ysend.at[place(link.ahead(k), quarter), :], yrecv.at[k - 1], (link.dp, link.ahead(k)))
        for k in others
    ]
    biases = [link.send(bup, bup_all.at[link.tp], (link.dp, link.ahead(k))) for k in others]
    cross.wait(1)
    collect.step(1, 0)
    early[1].wait()
    q[...] = (dot(x[...], wq[...], 1, 0) + vec[0:1, :]).astype(BF)
    collect.step(1, 1)
    own_slots = place(link.tp, quarter)
    for copy in reduce:
        copy.wait()
    own_y = ysend[own_slots, :].astype(F32)
    for k in others:
        own_y = own_y + yrecv[k - 1].astype(F32)
    yb[own_slots, :] = own_y.astype(BF)
    share = [
        link.send(yb.at[own_slots, :], yb.at[own_slots, :], (link.dp, link.ahead(k))) for k in others
    ]
    for k in (3, 2):
        cross.start(k)
    for k in (1, 3, 2):
        cross_down.start(k)
    collect.step(1, 2)
    stores = [local(q, q_out), local(em, em_out)]
    row_live = (lax.broadcasted_iota(jnp.int32, (total, 128), 0) < length).astype(F32).astype(BF)
    for load in late:
        load.wait()
    ssum[...] = dot(e_all[...], row_live, 1, 0)
    for copy in share:
        copy.wait()
    for copy in biases:
        copy.wait()
    collect.step(1, 3)
    stores += [local(yb, yb_out), local(ssum, ssum_out)]

    lane = lax.broadcasted_iota(jnp.int32, (1, PAIR), 1)
    first_half = (lane < HEAD).astype(F32)

    def project(weight, bias_row, blocks):
        full = dot(yb[...], weight[...], 1, 0)
        for p in range(PAIRS):
            cols = slice(p * PAIR, (p + 1) * PAIR)
            both = full[:, cols] + ssum[...] * vec[bias_row : bias_row + 1, cols]
            blocks[p, 0:slots, :] = (both * first_half).astype(BF)
            blocks[p, slots : 2 * slots, :] = (both * (1.0 - first_half)).astype(BF)

    project(wk, 1, kb)
    project(wv, 2, vb)
    stores += [local(kb, kb_out), local(vb, vb_out)]

    block = min(BLOCK_F, rows)
    per_pair = rows // block
    probs_sem = used[0]

    def tick(ticks):
        for k, j in ticks:
            if j == 0:
                cross.wait(k)
            collect.step(k, j)

    def attend(p, carry):
        cols = place(p, PAIR)

        def one(step, carry):
            here = place(step, block)
            logits = dot(q[here, cols], kb[p], 1, 1) * 0.125
            halves = []
            for half in range(2):
                part = logits[:, half * slots : (half + 1) * slots]
                peak = jnp.max(part, axis=-1, keepdims=True)
                raised = jnp.exp(part - peak)
                halves.append((raised * (1.0 / jnp.sum(raised, axis=-1, keepdims=True))).astype(BF))
            both = jnp.concatenate(halves, axis=1)
            probs[p, here, :] = both
            mixed[here, cols] = dot(both, vb[p], 1, 0).astype(BF)
            return carry

        lax.fori_loop(0, per_pair, one, 0)
        pltpu.make_async_copy(probs.at[p], probs_out.at[p], local_sems.at[probs_sem + p]).start()
        for n, ticks in enumerate(FRONT_TICKS[:-1]):

            @pl.when(p == n)
            def _():
                tick(ticks)

        return carry

    lax.fori_loop(0, PAIRS, attend, 0)
    used[0] += PAIRS
    stores.append(local(mixed, mixed_out))

    def finish(step, carry):
        here = place(step, block)
        res = x[here, :].astype(F32) + dot(mixed[here, :], wo[...], 1, 0) + vec[3:4, :]
        center = res - jnp.mean(res, axis=-1, keepdims=True)
        inverse = lax.rsqrt(jnp.mean(center * center, axis=-1, keepdims=True) + 1e-05)
        xhat[here, :] = center * inverse
        rstd[here, :] = jnp.broadcast_to(inverse, (block, 128))
        return carry

    lax.fori_loop(0, per_pair, finish, 0)
    stores += [local(xhat, xhat_out), local(rstd, rstd_out)]
    tick(FRONT_TICKS[-1])
    cross.wait(2)
    for k in others:
        cross_down.wait(k)
    for copy in stores:
        copy.wait()
    for p in range(PAIRS):
        pltpu.make_async_copy(probs.at[p], probs_out.at[p], local_sems.at[probs_sem + p]).wait()


def front(mesh, lengths, x, wq, e, wk, wv, wo, wup, wdn, vectors, b_up):
    dp_size, tp_size = mesh.shape["dp"], mesh.shape["tp"]
    low = min(3, dp_size.bit_length() - 1)
    rows, width = x.shape
    slots = e.shape[0]
    vmem = pl.BlockSpec(memory_space=pltpu.VMEM)
    hbm = pl.BlockSpec(memory_space=pltpu.HBM)
    shape = jax.ShapeDtypeStruct
    moved = (
        ((rows, width), F32),
        ((rows, 128), F32),
        ((rows, width), BF),
        ((rows, width), BF),
        ((PAIRS, rows, 2 * slots), BF),
        ((PAIRS, 2 * slots, PAIR), BF),
        ((PAIRS, 2 * slots, PAIR), BF),
        ((slots, width), BF),
        ((slots, 128), F32),
        ((slots, rows), BF),
    )
    kept = (
        ((VECTORS, width), F32),
        ((tp_size, 8, width), F32),
    )
    return pl.pallas_call(
        functools.partial(front_kernel, dp_size, tp_size, len(vectors)),
        out_shape=tuple(shape(*s) for s in kept + moved)
        + (
            shape((tp_size - 1, *wup.shape), BF),
            shape((tp_size - 1, 2, wup.shape[0] >> (low + 1), width), BF),
        ),
        in_specs=[pl.BlockSpec(memory_space=pltpu.SMEM)]
        + [hbm] * 8
        + [vmem] * (len(vectors) + 1),
        out_specs=tuple([vmem] * len(kept) + [hbm] * (len(moved) + 2)),
        scratch_shapes=[pltpu.VMEM(w.shape, BF) for w in (x, wq, wk, wv, wo, e)]
        + [pltpu.VMEM(*s) for s in moved]
        + [
            pltpu.VMEM((8, width), F32),
            pltpu.VMEM((slots, width), BF),
            pltpu.VMEM((tp_size - 1, slots // tp_size, width), BF),
            pltpu.SemaphoreType.DMA((FRONT_SEMS,)),
            pltpu.SemaphoreType.DMA((FRONT_SEMS,)),
            pltpu.SemaphoreType.DMA((32,)),
        ],
        compiler_params=pltpu.CompilerParams(
            collective_id=0, has_side_effects=True, vmem_limit_bytes=VMEM_LIMIT
        ),
        name="front",
    )(lengths, x, wq, e, wk, wv, wo, wup, wdn, *vectors, b_up)


BACK_SEMS = 128
VECTORS = 16


def add_rows(target, first, left, left_first, right, count):
    block = 96 if count % 96 == 0 else (48 if count % 48 == 0 else (32 if count % 32 == 0 else count))

    def step(i, carry):
        at = i * block
        total = (
            left[rows_at(left_first + at, block, 16), :].astype(F32)
            + right[rows_at(at, block, 16), :].astype(F32)
        )
        target[rows_at(first + at, block, 16), :] = total.astype(target.dtype)
        return carry

    lax.fori_loop(0, count // block, step, 0)


class Spread:
    def __init__(self, link, order, rows, source, acc, landing):
        self.link, self.rows, self.source, self.acc, self.landing = link, rows, source, acc, landing
        self.order = [b for b in order if b < link.low]
        self.stages = len(self.order)
        self.slot = link.take(self.stages)
        self.piece = rows >> self.stages
        self.insides, self.others, first = [0], [(1 - link.bit(self.order[0])) * (rows >> 1)], 0
        for j in range(1, self.stages):
            size = rows >> (j + 1)
            self.others.append(first + (1 - link.bit(self.order[j])) * size)
            first = first + link.bit(self.order[j]) * size
            self.insides.append(first)
        self.at = link.bit(self.order[0]) * (rows >> 1) + first

    def inside(self, i):
        return self.insides[i]

    def kept(self):
        return rows_at(self.inside(self.stages - 1), self.piece, 16)

    def offset(self):
        return self.at

    def landed(self, i):
        first = sum(self.rows >> (j + 1) for j in range(i))
        return self.landing.at[pl.ds(first, self.rows >> (i + 1)), :]

    def copy(self, i):
        link, size = self.link, self.rows >> (i + 1)
        where, other = self.source if i == 0 else self.acc, self.others[i]
        return link.remote(
            self.slot + i, where.at[rows_at(other, size, 16), :], self.landed(i), link.partner(self.order[i])
        )

    def start(self, i):
        self.copy(i).start()

    def finish(self, i):
        size = self.rows >> (i + 1)
        self.copy(i).wait()
        if i == 0:
            add_rows(self.acc, 0, self.source, self.link.bit(self.order[0]) * size, self.landed(0), size)
        else:
            at = self.inside(i)
            add_rows(self.acc, at, self.acc, at, self.landed(i), size)

    def steps(self):
        yield lambda: self.start(0)
        for i in range(1, self.stages):

            def step(i=i):
                self.finish(i - 1)
                self.start(i)

            yield step


class Collect:
    def __init__(self, link, order, offset, piece, region):
        self.link, self.offset, self.piece, self.region = link, offset, piece, region
        self.order = [b for b in order if b < link.low][::-1]
        self.slot = link.take(len(self.order))
        starts, size = [], piece
        for b in self.order:
            starts.append(link.bit(b) * size)
            size *= 2
        self.firsts = [sum(starts[i:], 0) for i in range(len(self.order))]

    def copy(self, i):
        size, first = self.piece << i, self.firsts[i]
        ref = self.region(first, size)
        return self.link.remote(self.slot + i, ref, ref, self.link.partner(self.order[i]))

    def steps(self):
        yield lambda: self.copy(0).start()
        for i in range(1, len(self.order)):

            def step(i=i):
                self.copy(i - 1).wait()
                self.copy(i).start()

            yield step
        yield lambda: self.copy(len(self.order) - 1).wait()


class Widen:
    def __init__(self, link, landing):
        self.link, self.landing = link, landing
        self.slot = link.take(max(0, link.bits - link.low))

    def run(self, piece):
        link = self.link
        for i, b in enumerate(range(link.low, link.bits)):
            copy = link.remote(self.slot + i, piece, self.landing.at[i], link.partner(b))
            copy.start()
            copy.wait()
            piece[...] = (piece[...].astype(F32) + self.landing[i].astype(F32)).astype(piece.dtype)


class Fan:
    def __init__(self, link, ends):
        self.link, self.ends = link, ends
        self.slot = link.take(link.tp_size - 1)

    def copy(self, k):
        source, target = self.ends(k)
        return self.link.remote(self.slot + k - 1, source, target, (self.link.dp, self.link.ahead(k)))

    def start(self):
        for k in range(1, self.link.tp_size):
            self.copy(k).start()

    def wait(self):
        for k in range(1, self.link.tp_size):
            self.copy(k).wait()


def then(*actions):
    def both():
        for action in actions:
            action()

    return both


class Track:
    def __init__(self):
        self.todo = []

    def add(self, steps, join=False):
        steps = list(steps)
        if join and self.todo:
            steps[0] = then(self.todo.pop(), steps[0])
        self.todo += steps

    def advance(self):
        if self.todo:
            self.todo.pop(0)()


def back_kernel(
    dp_size,
    tp_size,
    len_ref,
    vec,
    part_vec,
    ff_near,
    dnorm,
    probs,
    far_hbm,
    own_hbm,
    xhat_hbm,
    rstd_hbm,
    mixed_hbm,
    wo_hbm,
    landed_hbm,
    x_hbm,
    q_hbm,
    kb_hbm,
    vb_hbm,
    yb_hbm,
    ssum_hbm,
    em_hbm,
    wq_hbm,
    wk_hbm,
    wv_hbm,
    grad_hbm,
    ff_hbm,
    go_hbm,
    gq_out,
    gkv_out,
    seq_out,
    vec_out,
    grad_in,
    ff_out,
    go_out,
    ff_far,
    ff_own,
    xhat,
    rstd,
    mixed,
    wo,
    ff_landed,
    x,
    q,
    kb,
    vb,
    yb,
    ssum,
    em,
    wq,
    wk,
    wv,
    dres,
    dmix,
    dq,
    dl,
    prob_slots,
    dpart,
    dland,
    dfull,
    ff_zland,
    far_acc,
    far_land,
    own_acc,
    own_land,
    o_acc,
    o_land,
    q_acc,
    q_land,
    o_zland,
    q_zland,
    kv_send,
    kv_acc,
    kv_land,
    s_send,
    s_acc,
    s_land,
    vec_acc,
    vec_land,
    vec_z,
    wide_ff,
    wide_q,
    wide_kv,
    wide_s,
    send_sems,
    recv_sems,
    local_sems,
):
    link = Link(dp_size, tp_size, send_sems, recv_sems)
    rows, width = x.shape
    slots = yb.shape[0]
    low = link.low
    others = range(1, tp_size)
    first_load = pltpu.make_async_copy(dnorm, dres, local_sems.at[0])
    first_load.start()
    late = []
    for n, (source, target) in enumerate(
        (
            (far_hbm, ff_far), (own_hbm, ff_own), (xhat_hbm, xhat), (rstd_hbm, rstd), (mixed_hbm, mixed),
            (wo_hbm, wo), (landed_hbm, ff_landed), (q_hbm, q), (kb_hbm, kb), (vb_hbm, vb), (x_hbm, x), (yb_hbm, yb),
            (wq_hbm, wq), (wk_hbm, wk), (wv_hbm, wv), (ssum_hbm, ssum), (em_hbm, em),
        )
    ):
        late.append(pltpu.make_async_copy(source, target, local_sems.at[3 + n]))
        late[-1].start()
    link.greet(link.bits)

    lanes = 2
    deep = tp_size // lanes
    third = width // GRAD_SPLIT
    owned = width // tp_size

    ff_track, ff_orders = Track(), ((0, 1, 2), (0, 2, 1))
    ff_rows = width >> 3
    ff_parts = []
    for m in range(2):
        first, second, third_bit = ff_orders[m]
        far = Spread(link, (third_bit,), width >> 2, ff_far.at[m], far_acc.at[m], far_land.at[m])
        own = Spread(link, (second, third_bit), width >> 1, ff_own.at[m], own_acc.at[m], own_land.at[m])
        slot = link.take(2)

        def piece_copy(n, m=m, slot=slot):
            source, k = ((far_acc, 3), (ff_near, 2))[n]
            return link.remote(slot + n, source.at[m], ff_zland.at[m, n], (link.dp, link.behind(k)))

        at = link.bit(ff_orders[m][0]) * (width >> 1) + own.offset()

        def offset(at=at):
            return at

        widen = Widen(link, wide_ff.at[m])

        def join(m=m, own=own, piece_copy=piece_copy, offset=offset, widen=widen):
            total = own_acc[m, own.kept(), :].astype(F32) + ff_landed[m].astype(F32)
            for n in range(2):
                piece_copy(n).wait()
                total = total + ff_zland[m, n].astype(F32)
            mine = rows_at(offset(), ff_rows, 16)
            ff_out[m, mine, :] = total.astype(BF)
            widen.run(ff_out.at[m, mine, :])

        collect = Collect(
            link, ff_orders[m], offset, ff_rows,
            lambda first, size, m=m: ff_out.at[m, rows_at(first, size, 16), :],
        )
        ff_parts.append((far, own, piece_copy, join, list(collect.steps())))

    def ff_begin():
        for far, own, piece_copy, _, _ in ff_parts:
            far.start(0)
            own.start(0)
            piece_copy(1).start()

    def ff_second():
        for far, own, piece_copy, _, _ in ff_parts:
            far.finish(0)
            piece_copy(0).start()

    def ff_second_own():
        for far, own, piece_copy, _, _ in ff_parts:
            own.finish(0)
            own.start(1)

    def ff_third():
        for _, own, _, join, collects in ff_parts:
            own.finish(1)

    def ff_join():
        for _, _, _, join, collects in ff_parts:
            join()
            collects[0]()

    stores = []

    def store(n, source, target):
        copy = pltpu.make_async_copy(source, target, local_sems.at[20 + n])
        stores.append(copy)
        return copy

    ff_store, go_store, grad_store = store(0, ff_out, ff_hbm), store(1, go_out, go_hbm), store(2, grad_in, grad_hbm)
    late[0].wait()
    late[1].wait()
    ff_begin()
    ff_track.add([ff_second, ff_second_own, then(ff_third, ff_join)])
    ff_track.add([then(*pair) for pair in zip(ff_parts[0][4][1:], ff_parts[1][4][1:])])
    ff_track.add([ff_store.start], join=True)

    def square_track(order, out, acc, landing, zland, wide):
        track, spread = Track(), Spread(link, order, width, out, acc, landing)
        q_rows, q_cols = spread.piece // deep, width // lanes
        row_of = [lax.div(t, lanes) * q_rows for t in link.aheads]
        col_of = [lax.rem(t, lanes) * q_cols for t in link.aheads]

        def quarter(first, k):
            return (
                rows_at(first + row_of[k], q_rows, 16),
                pl.ds(pl.multiple_of(col_of[k], 128), q_cols),
            )

        def there(k):
            return acc.at[quarter(spread.inside(spread.stages - 1), k)], zland.at[k - 1]

        def again(k):
            region = out.at[quarter(spread.offset(), 0)]
            return region, region

        fan, share, widen = Fan(link, there), Fan(link, again), Widen(link, wide)

        def join():
            fan.wait()
            total = acc[quarter(spread.inside(spread.stages - 1), 0)].astype(F32)
            for k in others:
                total = total + zland[k - 1].astype(F32)
            mine = quarter(spread.offset(), 0)
            out[mine] = total.astype(BF)
            widen.run(out.at[mine])
            share.start()

        collect = Collect(
            link, order, spread.offset, spread.piece, lambda first, size: out.at[rows_at(first, size, 16), :]
        )
        track.add(spread.steps())
        track.add([then(lambda: spread.finish(spread.stages - 1), fan.start), join, share.wait])
        track.add(collect.steps(), join=True)
        return track

    def owned_track(order, total_rows, cols, source, acc, landing, out, wide):
        source, acc, landing = source.at[:, cols], acc.at[:, cols], landing.at[:, cols]
        track, spread = Track(), Spread(link, order, total_rows, source, acc, landing)

        def region(k):
            ref = out.at[link.tp, rows_at(spread.offset(), spread.piece, 16), cols]
            return ref, ref

        share, widen = Fan(link, region), Widen(link, wide)

        def last():
            spread.finish(spread.stages - 1)
            ref = region(0)[0]
            ref[...] = acc[spread.kept(), :]
            widen.run(ref)
            share.start()

        collect = Collect(
            link, order, spread.offset, spread.piece, lambda first, size: out.at[:, rows_at(first, size, 16), cols]
        )
        track.add(spread.steps())
        track.add([last, share.wait])
        track.add(collect.steps(), join=True)
        return track

    o_track = square_track((0, 1, 2), go_out, o_acc, o_land, o_zland, wide_q.at[0])
    o_track.add([go_store.start], join=True)
    q_track = square_track((0, 2, 1), gq_out, q_acc, q_land, q_zland, wide_q.at[1])
    def halves(total_rows, source, acc, landing, out, wide):
        tracks = []
        for h, order in enumerate(((0, 1, 2), (0, 2, 1))):
            cols = slice(h * source.shape[1] // 2, (h + 1) * source.shape[1] // 2)
            tracks.append(owned_track(order, total_rows, cols, source, acc, landing, out, wide.at[h]))
        both = Track()
        both.add([then(*pair) for pair in zip(tracks[0].todo, tracks[1].todo)])
        return both

    kv_track = halves(2 * owned, kv_send, kv_acc, kv_land, gkv_out, wide_kv)
    s_track = halves(slots, s_send, s_acc, s_land, seq_out, wide_s)

    vec_track, vec_slot = Track(), link.take(link.bits)
    vec_fan = Fan(link, lambda k: (vec_z.at[link.tp], vec_z.at[link.tp]))

    def vec_copy(b):
        return link.remote(vec_slot + b, vec_acc.at[b], vec_land.at[b], link.partner(b))

    vec_track.add([lambda: vec_copy(0).start()])
    for b in range(link.bits):

        def vec_step(b=b):
            vec_copy(b).wait()
            total = vec_acc[b] + vec_land[b]
            if b + 1 < link.bits:
                vec_acc[b + 1] = total
                vec_copy(b + 1).start()
            else:
                vec_z[link.tp] = total
                vec_fan.start()

        vec_track.add([vec_step])

    def vec_last():
        vec_fan.wait()
        total = vec_z[0]
        for t in range(1, tp_size):
            total = total + vec_z[t]
        vec_out[...] = total

    vec_track.add([vec_last])

    block = min(BLOCK_B, rows)
    count = rows // block
    gain = vec[4:5, :]

    def norm_back(step, carry):
        g_gain, g_shift, g_out = carry
        here = place(step, block)
        grad, hat = dres[here, :], xhat[here, :]
        g_gain = g_gain + jnp.sum(grad * hat, axis=0, keepdims=True)
        g_shift = g_shift + jnp.sum(grad, axis=0, keepdims=True)
        scaled = grad * gain
        d_res = rstd[here, 0:1] * (
            scaled
            - jnp.mean(scaled, axis=-1, keepdims=True)
            - hat * jnp.mean(scaled * hat, axis=-1, keepdims=True)
        )
        dres[here, :] = d_res
        d_attn = d_res.astype(BF)
        dq[here, :] = d_attn
        g_out = g_out + jnp.sum(d_attn.astype(F32), axis=0, keepdims=True)
        return g_gain, g_shift, g_out

    zero = jnp.zeros((1, width), F32)
    first_load.wait()
    late[2].wait()
    late[3].wait()
    g_gain, g_shift, g_out = lax.fori_loop(0, count, norm_back, (zero, zero, zero))
    vec_acc[0] = part_vec[...]
    vec_acc[0, 3:4, :] = g_out
    vec_acc[0, 4:5, :] = g_gain
    vec_acc[0, 5:6, :] = g_shift
    d_attn = dq

    def weight_grad(left, right, target):
        for m in range(GRAD_SPLIT):
            cols = slice(m * third, (m + 1) * third)
            target[cols, :] = dot(left[:, cols], right[...], 0, 0).astype(BF)

    for load in late[4:7]:
        load.wait()
    weight_grad(mixed, d_attn, go_out)
    o_track.advance()
    ff_track.advance()
    dmix[...] = dot(d_attn[...], wo[...], 1, 1).astype(BF)
    o_track.advance()
    for load in late[7:]:
        load.wait()

    own_half = lax.div(link.tp, 2)
    parity = lax.rem(link.tp, 2)
    three = PAIRS // 2

    def pair_at(n):
        second = lax.div(n, three)
        which = (1 - own_half) * (1 - second) + own_half * second
        along = lax.rem(n, three)
        return which * three + along * parity + (three - 1 - along) * (1 - parity)

    def fetch(n):
        slot = lax.rem(n, 2)
        return pltpu.make_async_copy(probs.at[pair_at(n)], prob_slots.at[slot], local_sems.at[1 + slot])

    fetch(0).start()

    def attend_back(n):
        p = pair_at(n)
        cols = place(p, PAIR)

        @pl.when(n + 1 < PAIRS)
        def _():
            fetch(n + 1).start()

        fetch(n).wait()
        held = prob_slots.at[lax.rem(n, 2)]

        def part(step, carry):
            here = place(step, block)
            d_probs = dot(dmix[here, cols], vb[p], 1, 1)
            weights = held[here, :].astype(F32)
            halves = []
            for h in range(2):
                w = weights[:, h * slots : (h + 1) * slots]
                d = d_probs[:, h * slots : (h + 1) * slots]
                halves.append((w * (d - jnp.sum(w * d, axis=-1, keepdims=True))).astype(BF))
            both = jnp.concatenate(halves, axis=1)
            dl[here, :] = both
            dq[here, cols] = (dot(both, kb[p], 1, 0) * 0.125).astype(BF)
            return carry

        lax.fori_loop(0, count, part, 0)
        top, under = rows_at(p * PAIR, HEAD, HEAD), rows_at(p * PAIR + HEAD, HEAD, HEAD)
        for n, total in enumerate(
            (dot(q[:, cols], dl[...], 0, 0) * 0.125, dot(dmix[:, cols], held[...], 0, 0))
        ):
            dpart[n, top, :] = total[:HEAD, :slots].astype(BF)
            dpart[n, under, :] = total[HEAD:, slots:].astype(BF)

    d_slot = link.take(tp_size - 1)
    d_peers = [2 * (1 - own_half) + parity, 2 * (1 - own_half) + (1 - parity), 2 * own_half + (1 - parity)]

    def d_copy(j):
        peer = d_peers[j]
        block_of = dpart.at[:, rows_at(peer * owned, owned, 64), :]
        return link.remote(d_slot + j, block_of, dland.at[j], (link.dp, peer))

    events = [
        then(),
        then(lambda: d_copy(1).start(), ff_track.advance),
        lambda: d_copy(0).start(),
        o_track.advance,
        then(lambda: d_copy(2).start(), ff_track.advance),
        then(),
    ]

    def one(n, carry):
        attend_back(n)
        for i, event in enumerate(events):
            pl.when(n == i)(event)
        return carry

    lax.fori_loop(0, PAIRS, one, 0)

    weight_grad(x, dq, gq_out)
    q_track.advance()
    ff_track.advance()

    def input_grad(step, carry):
        here = place(step, block)
        dres[here, :] += dot(dq[here, :], wq[...], 1, 1)
        return carry

    lax.fori_loop(0, count, input_grad, 0)
    q_track.advance()
    vec_acc[0, 0:1, :] = jnp.sum(dq[...].astype(F32), axis=0, keepdims=True)

    for j in range(tp_size - 1):
        d_copy(j).wait()
    own_block = rows_at(link.tp * owned, owned, 64)
    for n in range(2):
        total = dpart[n, own_block, :].astype(F32)
        for j in range(tp_size - 1):
            total = total + dland[j, n].astype(F32)
        dfull[n, own_block, :] = total.astype(BF)
    d_share = Fan(link, lambda k: (dfull.at[:, own_block, :], dfull.at[:, own_block, :]))
    d_share.start()
    ff_track.advance()
    for n in range(2):
        kv_send[n * owned : (n + 1) * owned, :] = dot(dfull[n, own_block, :], yb[...], 1, 0).astype(BF)
    kv_track.advance()
    q_track.advance()
    ff_track.advance()
    kv_track.advance()
    o_track.advance()
    kv_track.advance()
    q_track.advance()
    kv_track.advance()
    o_track.advance()
    d_share.wait()
    backs = dot(wk[...], dfull[0], 1, 0) + dot(wv[...], dfull[1], 1, 0)
    back = backs.T.astype(BF)
    small = vec[0:8, :].astype(BF)
    bias_row = dot(small, dfull[0], 1, 0)[1:2, :] + dot(small, dfull[1], 1, 0)[2:3, :]
    bias_column = jnp.broadcast_to(bias_row, (128, slots)).T[:, 0:1]
    position = lax.broadcasted_iota(jnp.int32, (1, rows), 1) + link.tp * rows
    live = (position < len_ref[0]).astype(F32)
    s_send[...] = ((dot(back, x[...], 1, 1) + bias_column) * live).astype(BF)
    s_track.advance()
    column = ssum[...].T[0:8, :]
    column_b = column.astype(BF)
    column_low = (column - column_b.astype(F32)).astype(BF)
    for n in range(2):
        total = dot(column_b, dfull[n], 1, 1) + dot(column_low, dfull[n], 1, 1)
        vec_acc[0, 1 + n : 2 + n, :] = total[0:1, :] * (1.0 / tp_size)
    vec_track.advance()
    s_track.advance()

    def input_grad_last(step, carry):
        here = place(step, block)
        grad_in[here, :] = (dres[here, :] + dot(em[:, here], back, 0, 0)).astype(BF)
        return carry

    lax.fori_loop(0, count, input_grad_last, 0)
    grad_store.start()
    tracks = [s_track, kv_track, q_track, o_track, vec_track, ff_track]
    while any(track.todo for track in tracks):
        for track in tracks:
            track.advance()
    for copy in stores:
        copy.wait()


def back(mesh, lengths, vec, part_vec, ff_near, dnorm, probs, *late):
    dp_size, tp_size = mesh.shape["dp"], mesh.shape["tp"]
    bits = dp_size.bit_length() - 1
    low = min(3, bits)
    wide = max(1, bits - low)
    rows, width = dnorm.shape
    slots = late[11].shape[0]
    owned = width // tp_size
    others = tp_size - 1
    vmem = pl.BlockSpec(memory_space=pltpu.VMEM)
    hbm = pl.BlockSpec(memory_space=pltpu.HBM)
    shape = jax.ShapeDtypeStruct

    def landing(total):
        return sum(total >> (i + 1) for i in range(low))

    def buf(*dims, dtype=BF):
        return pltpu.VMEM(dims, dtype)

    ff_piece, kv_piece, s_piece = width >> low, 2 * owned >> low, slots >> low
    quarter = (ff_piece // (tp_size // 2), width // 2)
    return pl.pallas_call(
        functools.partial(back_kernel, dp_size, tp_size),
        out_shape=(
            shape((rows, width), BF),
            shape((2, width, width), BF),
            shape((width, width), BF),
            shape((width, width), BF),
            shape((tp_size, 2 * owned, width), BF),
            shape((tp_size, slots, rows), BF),
            shape((VECTORS, width), F32),
        ),
        in_specs=[pl.BlockSpec(memory_space=pltpu.SMEM)] + [vmem] * 2 + [hbm] * (3 + len(late)),
        out_specs=tuple([hbm] * 3 + [vmem] * 4),
        scratch_shapes=[buf(rows, width), buf(2, width, width), buf(width, width)]
        + [pltpu.VMEM(array.shape, array.dtype) for array in late]
        + [
            buf(rows, width, dtype=F32),
            buf(rows, width),
            buf(rows, width),
            buf(rows, 2 * slots),
            buf(2, rows, 2 * slots),
            buf(2, width, slots),
            buf(others, 2, owned, slots),
            buf(2, width, slots),
            buf(2, 2, ff_piece, width),
            buf(2, width >> 3, width),
            buf(2, width >> 3, width),
            buf(2, width >> 2, width),
            buf(2, (width >> 2) + (width >> 3), width),
            buf(width // 2, width),
            buf(landing(width), width),
            buf(width // 2, width),
            buf(landing(width), width),
            buf(others, *quarter),
            buf(others, *quarter),
            buf(2 * owned, width),
            buf(owned, width),
            buf(landing(2 * owned), width),
            buf(slots, rows),
            buf(slots // 2, rows),
            buf(landing(slots), rows),
            buf(bits, VECTORS, width, dtype=F32),
            buf(bits, VECTORS, width, dtype=F32),
            buf(tp_size, VECTORS, width, dtype=F32),
            buf(2, wide, ff_piece, width),
            buf(2, wide, *quarter),
            buf(2, wide, kv_piece, width // 2),
            buf(2, wide, s_piece, rows // 2),
            pltpu.SemaphoreType.DMA((BACK_SEMS,)),
            pltpu.SemaphoreType.DMA((BACK_SEMS,)),
            pltpu.SemaphoreType.DMA((6 + len(late),)),
        ],
        compiler_params=pltpu.CompilerParams(
            collective_id=1, has_side_effects=True, vmem_limit_bytes=VMEM_LIMIT
        ),
        name="back",
    )(lengths, vec, part_vec, ff_near, dnorm, probs, *late)


class ChunkSpread:
    def __init__(self, link, rows, sent, acc, landing):
        self.link, self.rows, self.sent, self.acc, self.landing = link, rows, sent, acc, landing
        self.orders = [[b for b in order if b < link.low] for order in ((0, 1, 2), (0, 2, 1))]
        self.stages = link.low
        self.slot = link.take(2 * link.low * acc.shape[1])
        self.insides, self.others = [], []
        for order in self.orders:
            inside, other, first = [0], [(1 - link.bit(order[0])) * (rows >> 1)], 0
            for j in range(1, self.stages):
                size = rows >> (j + 1)
                other.append(first + (1 - link.bit(order[j])) * size)
                first = first + link.bit(order[j]) * size
                inside.append(first)
            self.insides.append(inside)
            self.others.append(other)

    def inside(self, m, i):
        return self.insides[m][i]

    def copy(self, c, m, i):
        link, size = self.link, self.rows >> (i + 1)
        bit = self.orders[m][i]
        if i == 0:
            source = self.sent.at[m, lax.rem(c, 2), rows_at(self.others[m][i], size, 16), :]
        else:
            source = self.acc.at[m, c, rows_at(self.others[m][i], size, 16), :]
        first = sum(self.rows >> (j + 1) for j in range(i))
        slot = self.slot + (i * 2 + m) * self.acc.shape[1] + c
        return link.remote(slot, source, self.landing.at[m, c, pl.ds(first, size), :], link.partner(bit))

    def start(self, c, m, i):
        self.copy(c, m, i).start()

    def finish(self, c, m, i):
        size = self.rows >> (i + 1)
        self.copy(c, m, i).wait()
        first = sum(self.rows >> (j + 1) for j in range(i))
        landed = self.landing.at[m, c, pl.ds(first, size), :]
        acc = self.acc.at[m, c]
        if i == 0:
            mine = self.link.bit(self.orders[m][0]) * size
            add_rows(acc, 0, self.sent.at[m, lax.rem(c, 2)], mine, landed, size)
        else:
            at = self.inside(m, i)
            add_rows(acc, at, acc, at, landed, size)


MIDDLE_SEMS = 96
MIDDLE_TICKS = (
    ((0, 2, 1),),
    ((1, 1, 1), (1, 3, 0)),
    ((0, 2, 2),),
    ((1, 1, 2), (1, 3, 1), (1, 2, 0)),
    ((0, 2, 3),),
    ((1, 3, 2), (1, 2, 1)),
    ((1, 1, 3),),
    ((1, 2, 2), (1, 3, 3), (1, 2, 3)),
)


def middle_kernel(
    dp_size,
    tp_size,
    vec,
    bup_all,
    xhat_hbm,
    out_grad_hbm,
    own_up,
    own_dn,
    ups,
    pieces,
    layer_hbm,
    dnorm,
    part_vec,
    ff_landed,
    ff_near,
    ff_far,
    ff_own,
    whole,
    xhat,
    layer_out,
    out_grad,
    nb,
    act,
    slope,
    d_branch,
    d_acc,
    sent,
    acc,
    landing,
    send_sems,
    recv_sems,
    local_sems,
):
    link = Link(dp_size, tp_size, send_sems, recv_sems)
    rows, width = xhat.shape
    used = [0]

    def local(source, target):
        copy = pltpu.make_async_copy(source, target, local_sems.at[used[0]])
        used[0] += 1
        copy.start()
        return copy

    collect = WeightCollect(link, width // 2, lambda k: whole.at[1, k])
    xhat_load = local(xhat_hbm, xhat)
    up_last = WeightCollect(link, width // 2, lambda k: whole.at[0, 2])
    placed = [
        local(ups.at[1, up_last.rows(h, 0), :], whole.at[0, 2, up_last.rows(h, 0), :]) for h in range(2)
    ]
    placed += [
        local(pieces.at[k - 1, h], whole.at[1, k, collect.rows(h, 0), :]) for k in (1, 3, 2) for h in range(2)
    ]
    owns = [local(own_up, whole.at[0, 0])]
    owns += [local(ups.at[k - 1], whole.at[0, k]) for k in (1, 3)]
    owns += [local(own_dn, whole.at[1, 0]), local(out_grad_hbm, out_grad)]
    link.greet(link.low)
    for copy in placed:
        copy.wait()
    up_last.step(2, 0)
    collect.step(1, 0)
    xhat_load.wait()
    gain, shift, b_down, f_gain, f_shift = (vec[n : n + 1, :] for n in (4, 5, 6, 7, 8))
    block = min(BLOCK_M, rows)
    count = rows // block
    big = rows // 2

    def norm(step, carry):
        here = place(step, block)
        nb[here, :] = (xhat[here, :] * gain + shift).astype(BF)
        return carry

    lax.fori_loop(0, count, norm, 0)
    for copy in owns[:3]:
        copy.wait()

    def forward(step, carry):
        n = lax.div(step, 2)
        k = n + lax.div(n, 2) * (7 - 2 * n - 2)
        here, cols = place(lax.rem(step, 2), big), place(k, width)
        pre = dot(nb[here, :], whole[0, k], 1, 0) + bup_all[link.behind(k), 0:1, :]
        cdf = 0.5 * (1.0 + lax.erf(pre * 0.7071067811865476))
        act[here, cols] = (pre * cdf).astype(BF)
        slope[here, cols] = (cdf + pre * (jnp.exp(pre * pre * -0.5) * 0.3989422804014327)).astype(BF)
        for n, ticks in enumerate(MIDDLE_TICKS):

            @pl.when(step == n)
            def _():
                for m, shard, j in ticks:
                    (up_last, collect)[m].step(shard, j)

        return carry

    lax.fori_loop(0, 2 * tp_size, forward, 0)
    for copy in owns[3:]:
        copy.wait()

    def second_norm(step, carry):
        g_gain, g_shift, g_down = carry
        here = place(step, block)
        branch = dot(act[here, 0:width], whole[1, 0], 1, 0)
        for k in range(1, tp_size):
            branch = branch + dot(act[here, k * width : (k + 1) * width], whole[1, k], 1, 0)
        res = xhat[here, :] * gain + shift + (branch + b_down)
        center = res - jnp.mean(res, axis=-1, keepdims=True)
        inverse = lax.rsqrt(jnp.mean(center * center, axis=-1, keepdims=True) + 1e-05)
        hat = center * inverse
        layer_out[here, :] = (hat * f_gain + f_shift).astype(BF)
        grad = out_grad[here, :].astype(F32)
        g_gain = g_gain + jnp.sum(grad * hat, axis=0, keepdims=True)
        g_shift = g_shift + jnp.sum(grad, axis=0, keepdims=True)
        scaled = grad * f_gain
        d_res = inverse * (
            scaled
            - jnp.mean(scaled, axis=-1, keepdims=True)
            - hat * jnp.mean(scaled * hat, axis=-1, keepdims=True)
        )
        d_acc[here, :] = d_res
        rounded = d_res.astype(BF)
        d_branch[here, :] = rounded
        g_down = g_down + jnp.sum(rounded.astype(F32), axis=0, keepdims=True)
        return g_gain, g_shift, g_down

    zero = jnp.zeros((1, width), F32)
    g_gain, g_shift, g_down = lax.fori_loop(0, count, second_norm, (zero, zero, zero))
    layer_store = local(layer_out, layer_hbm)
    part_vec[...] = jnp.zeros_like(part_vec)
    part_vec[6:7, :] = g_gain
    part_vec[7:8, :] = g_shift
    part_vec[8:9, :] = g_down

    spread = ChunkSpread(link, width, sent, acc, landing)
    third = width // GRAD_SPLIT

    def weight_grad(left, first, right, cols, target):
        for m in range(GRAD_SPLIT):
            mine = pl.ds(pl.multiple_of(first + m * third, third), third)
            target[m * third : (m + 1) * third, :] = dot(left[:, mine], right[:, cols], 0, 0).astype(BF)

    def settle(n, steps):
        for m, late, stage in steps:

            @pl.when(n >= late)
            def _():
                spread.finish(n - late, m, stage)

            if stage < 2:

                @pl.when(jnp.logical_and(n >= late, n - late < 3 - stage))
                def _():
                    spread.start(n - late, m, stage + 1)

    def backward(n, carry):
        k = lax.rem(n + 1, tp_size)
        cols = place(k, width)
        slot = lax.rem(n, 2)
        weight_grad(act, k * width, d_branch, slice(0, width), sent.at[1, slot])
        spread.start(n, 1, 0)
        settle(n, ((0, 1, 0), (1, 2, 1)))

        def through(step, total):
            here = place(step, big)
            grad = (dot(d_branch[here, :], whole[1, k], 1, 1) * slope[here, cols].astype(F32)).astype(BF)
            slope[here, cols] = grad
            return total + jnp.sum(grad.astype(F32), axis=0, keepdims=True)

        part_vec[pl.ds(9 + link.behind(k), 1), :] = lax.fori_loop(0, 2, through, zero)
        settle(n, ((1, 0, 0), (0, 2, 1)))
        weight_grad(nb, 0, slope, cols, sent.at[0, slot])
        spread.start(n, 0, 0)
        return carry

    lax.fori_loop(0, tp_size, backward, 0)

    def input_grad(step, carry):
        here = place(step, big)
        total = d_acc[here, :]
        for k in range(tp_size):
            total = total + dot(slope[here, k * width : (k + 1) * width], whole[0, k], 1, 1)
        d_acc[here, :] = total
        return carry

    slot = link.take(2)
    crossing = []
    lax.fori_loop(0, 1, input_grad, 0)
    for m in (1, 0):
        spread.finish(0, m, 2)
        at = rows_at(spread.inside(m, 2), width >> 3, 16)
        crossing.append(
            link.remote(slot + m, acc.at[m, 0, at, :], ff_landed.at[m], (link.dp, link.behind(1)))
        )
        crossing[-1].start()
    spread.finish(3, 0, 0)
    spread.finish(2, 1, 1)
    stores = [local(acc.at[m, 3], ff_own.at[m]) for m in range(2)]
    lax.fori_loop(1, 2, input_grad, 0)
    stores.append(local(d_acc, dnorm))
    spread.finish(2, 0, 1)
    for m in (1, 0):
        spread.finish(1, m, 2)
    for m in range(2):
        at = rows_at(spread.inside(m, 2), width >> 3, 16)
        stores.append(local(acc.at[m, 1, at, :], ff_near.at[m]))
        at = rows_at(spread.inside(m, 1), width >> 2, 16)
        stores.append(local(acc.at[m, 2, at, :], ff_far.at[m]))
    for copy in crossing + stores + [layer_store]:
        copy.wait()


def middle(mesh, vec, bup_all, xhat, out_grad, w_up, w_dn, ups, pieces):
    dp_size, tp_size = mesh.shape["dp"], mesh.shape["tp"]
    low = min(3, dp_size.bit_length() - 1)
    assert low == 3 and tp_size == 4
    rows, width = xhat.shape
    hidden = tp_size * width
    vmem = pl.BlockSpec(memory_space=pltpu.VMEM)
    hbm = pl.BlockSpec(memory_space=pltpu.HBM)
    shape = jax.ShapeDtypeStruct

    def buf(*dims, dtype=BF):
        return pltpu.VMEM(dims, dtype)

    return pl.pallas_call(
        functools.partial(middle_kernel, dp_size, tp_size),
        out_shape=(
            shape((rows, width), BF),
            shape((rows, width), F32),
            shape((VECTORS, width), F32),
            shape((2, width >> 3, width), BF),
            shape((2, width >> 3, width), BF),
            shape((2, width >> 2, width), BF),
            shape((2, width >> 1, width), BF),
        ),
        in_specs=[vmem] * 2 + [hbm] * 6,
        out_specs=(hbm, hbm, vmem, hbm, hbm, hbm, hbm),
        scratch_shapes=[
            buf(2, tp_size, width, width),
            buf(rows, width, dtype=F32),
            buf(rows, width),
            buf(rows, width),
            buf(rows, width),
            buf(rows, hidden),
            buf(rows, hidden),
            buf(rows, width),
            buf(rows, width, dtype=F32),
            buf(2, 2, width, width),
            buf(2, tp_size, width // 2, width),
            buf(2, tp_size, sum(width >> (i + 1) for i in range(low)), width),
            pltpu.SemaphoreType.DMA((MIDDLE_SEMS,)),
            pltpu.SemaphoreType.DMA((MIDDLE_SEMS,)),
            pltpu.SemaphoreType.DMA((32,)),
        ],
        compiler_params=pltpu.CompilerParams(
            collective_id=2, has_side_effects=True, vmem_limit_bytes=VMEM_LIMIT
        ),
        name="middle",
    )(vec, bup_all, xhat, out_grad, w_up, w_dn, ups, pieces)


def finish_kernel(
    tp_size, ff, gq, go, gkv, seq, vec, layer_out, grad_in,
    o_up, o_dn, o_q, o_o, o_k, o_v, o_seq, o_layer, o_grad, *rest,
):
    vectors, (in_up, in_dn, in_q, in_o, in_kv, in_seq, f_up, f_dn, f_q, f_o, f_k, f_v, f_seq, turn, pass_a, pass_b, in_sems, out_sems) = rest[:10], rest[10:]
    pairs = [(gq, in_q), (go, in_o), (ff.at[0], in_up), (ff.at[1], in_dn), (gkv, in_kv), (seq, in_seq), (layer_out, pass_a), (grad_in, pass_b)]
    loads = []
    for n, (source, target) in enumerate(pairs):
        loads.append(pltpu.make_async_copy(source, target, in_sems.at[n]))
        loads[-1].start()
    stores = []

    def put(staged, out):
        copy = pltpu.make_async_copy(staged, out, out_sems.at[len(stores)])
        copy.start()
        stores.append(copy)

    for n, (held, out) in enumerate(((pass_a, o_layer), (pass_b, o_grad))):
        loads[6 + n].wait()
        put(held, out)
    for n, row in enumerate((0, 1, 2, 3, 4, 5, 6, 7, 8)):
        vectors[n][...] = vec[row, :]
    vectors[9][...] = vec[pl.ds(9 + lax.axis_index("tp"), 1), :][0]
    width = gq.shape[0]
    for n, (narrow, wide, out) in enumerate(
        ((in_q, f_q, o_q), (in_o, f_o, o_o), (in_up, f_up, o_up), (in_dn, f_dn, o_dn))
    ):
        loads[n].wait()
        wide[...] = narrow[...].astype(F32)
        put(wide, out)
    loads[4].wait()
    owned = width // tp_size
    for n, (wide, out) in enumerate(((f_k, o_k), (f_v, o_v))):
        for c in range(tp_size):
            turn[c * owned : (c + 1) * owned, :] = in_kv[c, n * owned : (n + 1) * owned, :]
        for c in range(3):
            cols = slice(c * (width // 3), (c + 1) * (width // 3))
            wide[:, cols] = turn[cols, :].astype(F32).T
        put(wide, out)
    loads[5].wait()
    rows = in_seq.shape[2]
    for c in range(tp_size):
        f_seq[:, c * rows : (c + 1) * rows] = in_seq[c].astype(F32)
    put(f_seq, o_seq)
    for copy in stores:
        copy.wait()


def finish(tp_size, ff, gq, go, gkv, seq, vec, layer_out, grad_in):
    width = gq.shape[0]
    _, slots, rows = seq.shape
    square, flat = (width, width), (slots, tp_size * rows)
    vmem = pl.BlockSpec(memory_space=pltpu.VMEM)
    hbm = pl.BlockSpec(memory_space=pltpu.HBM)
    shape = jax.ShapeDtypeStruct
    return pl.pallas_call(
        functools.partial(finish_kernel, tp_size),
        out_shape=tuple([shape(square, F32)] * 6 + [shape(flat, F32)] + [shape(layer_out.shape, BF)] * 2 + [shape((width,), F32)] * 10),
        in_specs=[hbm] * 5 + [vmem] + [hbm] * 2,
        out_specs=tuple([hbm] * 9 + [vmem] * 10),
        scratch_shapes=[pltpu.VMEM(square, BF)] * 4
        + [pltpu.VMEM(gkv.shape, BF), pltpu.VMEM(seq.shape, BF)]
        + [pltpu.VMEM(square, F32)] * 6
        + [pltpu.VMEM(flat, F32), pltpu.VMEM(square, BF)]
        + [pltpu.VMEM(layer_out.shape, BF)] * 2
        + [pltpu.SemaphoreType.DMA((8,)), pltpu.SemaphoreType.DMA((9,))],
        compiler_params=pltpu.CompilerParams(vmem_limit_bytes=VMEM_LIMIT),
        name="finish",
    )(ff, gq, go, gkv, seq, vec, layer_out, grad_in)


def on_device(
    mesh,
    layer_in,
    out_grad,
    lengths,
    w_query,
    b_query,
    w_key,
    b_key,
    w_value,
    b_value,
    w_out,
    b_out,
    seq_proj,
    attn_gain,
    attn_shift,
    w_up,
    b_up,
    w_down,
    b_down,
    ffn_gain,
    ffn_shift,
):
    row_count, width = layer_in.shape
    tp_size = mesh.shape["tp"]
    vectors = (b_query, b_key, b_value, b_out, attn_gain, attn_shift, b_down, ffn_gain, ffn_shift)
    vec, bup_all, xhat, rstd, mixed, queries, probs, kb, vb, folded, ssum, own_proj, ups, pieces = front(
        mesh, lengths, layer_in, w_query, seq_proj, w_key, w_value, w_out, w_up, w_down, vectors, b_up
    )
    layer_out, d_normed, part_vec, ff_landed, ff_near, ff_far, ff_own = middle(
        mesh, vec, bup_all, xhat, out_grad, w_up, w_down, ups, pieces
    )
    grad_in, g_ff, g_o, g_q, g_kv, g_seq, vec_sum = back(
        mesh, lengths, vec, part_vec, ff_near, d_normed, probs, ff_far, ff_own, xhat, rstd, mixed, w_out, ff_landed,
        layer_in, queries, kb, vb, folded, ssum, own_proj, w_query, w_key, w_value
    )
    (
        g_w_up, g_w_down, g_w_query, g_w_out, g_w_key, g_w_value, g_seq_proj, layer_out, grad_in,
        g_b_query, g_b_key, g_b_value, g_b_out, g_attn_gain, g_attn_shift, g_ffn_gain, g_ffn_shift, g_b_down, g_b_up,
    ) = finish(tp_size, g_ff, g_q, g_o, g_kv, g_seq, vec_sum, layer_out, grad_in)
    return (
        layer_out,
        grad_in,
        g_w_query,
        g_b_query,
        g_w_key,
        g_b_key,
        g_w_value,
        g_b_value,
        g_w_out,
        g_b_out,
        g_seq_proj,
        g_attn_gain,
        g_attn_shift,
        g_w_up,
        g_b_up,
        g_w_down,
        g_b_down,
        g_ffn_gain,
        g_ffn_shift,
    )


def solution(mesh):
    in_specs = (
        P(("dp", "tp"), None),
        P(("dp", "tp"), None),
        P("dp"),
        *([P()] * 11),
        P(None, "tp"),
        P("tp"),
        P("tp", None),
        P(),
        P(),
        P(),
    )
    out_specs = (
        P(("dp", "tp"), None),
        P(("dp", "tp"), None),
        *([P()] * 11),
        P(None, "tp"),
        P("tp"),
        P("tp", None),
        P(),
        P(),
        P(),
    )
    return jax.shard_map(
        functools.partial(on_device, mesh), mesh=mesh, in_specs=in_specs, out_specs=out_specs, check_vma=False
    )
```

```python
import functools

import jax
import jax.numpy as jnp
from jax import lax
from jax.experimental import pallas as pl
from jax.experimental.pallas import tpu as pltpu
from jax.sharding import PartitionSpec as P

HEADS = 12
HEAD = 64
PAIRS = HEADS // 2
PAIR = 2 * HEAD
BF = jnp.bfloat16
F32 = jnp.float32
MESH = pl.DeviceIdType.MESH
VMEM_LIMIT = 67_043_328
BLOCK_F, BLOCK_M, BLOCK_B, GRAD_SPLIT = 1024, 512, 1024, 2


def dot(left, right, left_dim, right_dim):
    return lax.dot_general(
        left, right, (((left_dim,), (right_dim,)), ((), ())), preferred_element_type=F32
    )


def place(index, size):
    return pl.ds(pl.multiple_of(index * size, size), size)


def rows_at(first, size, multiple):
    return pl.ds(pl.multiple_of(first, multiple), size)


class Link:
    def __init__(self, dp_size, tp_size, send_sems, recv_sems):
        self.dp_size, self.tp_size = dp_size, tp_size
        self.dp, self.tp = lax.axis_index("dp"), lax.axis_index("tp")
        self.bits = dp_size.bit_length() - 1
        self.low = min(3, self.bits)
        self.send_sems, self.recv_sems = send_sems, recv_sems
        self.used = 0
        self.bit_values = [lax.rem(lax.div(self.dp, 1 << b), 2) for b in range(self.bits)]
        self.partners = [
            (self.dp + (1 - 2 * self.bit_values[b]) * (1 << b), self.tp) for b in range(self.bits)
        ]
        self.aheads = [lax.rem(self.tp + k, tp_size) for k in range(tp_size)]

    def bit(self, b):
        return self.bit_values[b]

    def partner(self, b):
        return self.partners[b]

    def ahead(self, k):
        return self.aheads[k]

    def behind(self, k):
        if isinstance(k, int):
            return self.aheads[(self.tp_size - k) % self.tp_size]
        return lax.rem(self.tp + self.tp_size - k, self.tp_size)

    def greet(self, dp_bits):
        barrier = pltpu.get_barrier_semaphore()
        peers = [(self.dp, self.ahead(k)) for k in range(1, self.tp_size)]
        peers += [self.partner(b) for b in range(dp_bits)]
        for peer in peers:
            pl.semaphore_signal(barrier, inc=1, device_id=peer, device_id_type=MESH)
        pl.semaphore_wait(barrier, len(peers))

    def take(self, count):
        first = self.used
        self.used += count
        assert self.used <= self.send_sems.shape[0]
        return first

    def remote(self, slot, source, target, device):
        return pltpu.make_async_remote_copy(
            src_ref=source,
            dst_ref=target,
            send_sem=self.send_sems.at[slot],
            recv_sem=self.recv_sems.at[slot],
            device_id=device,
            device_id_type=MESH,
        )

    def send(self, source, target, device):
        copy = self.remote(self.take(1), source, target, device)
        copy.start()
        return copy


FRONT_SEMS = 64
VECTORS = 16


def half_orders(low):
    return [[b for b in order if b < low] for order in ((1, 2, 0), (2, 1, 0))]


class WeightCollect:
    def __init__(self, link, part, whole):
        self.link, self.whole, self.part = link, whole, part
        self.orders = half_orders(link.low)
        self.piece = self.part >> link.low
        self.stages = link.low
        self.slot = link.take(2 * (link.tp_size - 1) * link.low)
        self.firsts = []
        for h in range(2):
            first, size, starts = h * part, self.piece, []
            for b in self.orders[h]:
                starts.append(size * link.bit(b))
                size *= 2
            self.firsts.append([sum(starts[i:], first) for i in range(self.stages)])

    def rows(self, h, i):
        return rows_at(self.firsts[h][i], self.piece << i, 16)

    def copies(self, k, i):
        for h in range(2):
            region = self.whole(k).at[self.rows(h, i), :]
            slot = self.slot + ((k - 1) * self.stages + i) * 2 + h
            yield self.link.remote(slot, region, region, self.link.partner(self.orders[h][i]))

    def step(self, k, j):
        if j > 0:
            for copy in self.copies(k, j - 1):
                copy.wait()
        if j < self.stages:
            for copy in self.copies(k, j):
                copy.start()


class Cross:
    def __init__(self, link, collect, shard, target):
        self.link, self.collect, self.shard, self.target = link, collect, shard, target
        self.slot = link.take(2 * (link.tp_size - 1))

    def copies(self, k):
        for h in range(2):
            rows = self.collect.rows(h, 0)
            yield self.link.remote(
                self.slot + 2 * (k - 1) + h,
                self.shard.at[rows, :],
                self.target(k, h, rows),
                (self.link.dp, self.link.ahead(k)),
            )

    def start(self, k):
        for copy in self.copies(k):
            copy.start()

    def wait(self, k):
        for copy in self.copies(k):
            copy.wait()


EARLY_TICKS = ((0, 1, 0), (1, 1, 0), (0, 1, 1), (1, 3, 0), (1, 1, 1), (0, 1, 2), (1, 3, 1), (1, 1, 2))
SHARE_TICKS = ((0, 1, 3), (1, 3, 2), (1, 1, 3), (1, 3, 3))
PAIR_TICKS = {1: ((0, 3, 0),), 3: ((0, 3, 1),), 5: ((0, 3, 2), (0, 2, 0))}
LAST_TICKS = ((0, 3, 3), (0, 2, -2), (1, 2, -1))


def front_kernel(dp_size, tp_size, n_vectors, len_ref, x_hbm, wq_hbm, e, wk_hbm, wv_hbm, wo_hbm, wup, wdn, *rest):
    vectors, b_up, rest = rest[:n_vectors], rest[n_vectors], rest[n_vectors + 1 :]
    outs, scratch = rest[:14], rest[14:]
    (vec, bup_all, xhat_out, rstd_out, mixed_out, q_out, probs_out, kb_out, vb_out, yb_out, ssum_out, em_out, ups, downs) = outs
    (x, wq, wk, wv, wo, e_all, xhat, rstd, mixed, q, probs, kb, vb, yb, ssum, em, bup, ysend, yrecv, send_sems, recv_sems, local_sems) = scratch
    link = Link(dp_size, tp_size, send_sems, recv_sems)
    rows, width = x.shape
    slots, total = e_all.shape
    quarter = slots // tp_size
    others = range(1, tp_size)
    used = [0]

    def local(source, target):
        copy = pltpu.make_async_copy(source, target, local_sems.at[used[0]])
        used[0] += 1
        copy.start()
        return copy

    own_first = link.tp * rows
    e_own = local(e.at[:, rows_at(own_first, rows, rows)], em)
    early = [local(x_hbm, x), local(wq_hbm, wq)]
    late = [local(e, e_all), local(wk_hbm, wk), local(wv_hbm, wv), local(wo_hbm, wo)]
    link.greet(link.low)

    collect = WeightCollect(link, wup.shape[0] // 2, lambda k: ups.at[k - 1])
    cross = Cross(link, collect, wup, lambda k, h, rows: ups.at[k - 1, rows, :])
    cross_down = Cross(link, collect, wdn, lambda k, h, rows: downs.at[k - 1, rows, :])
    collect_down = WeightCollect(link, wdn.shape[0] // 2, lambda k: downs.at[k - 1])
    def tick(ticks):
        for m, k, j in ticks:
            if -1 <= j <= 0:
                (cross, cross_down)[m].wait(k)
            if j == -2:
                for copy in (collect, collect_down)[m].copies(k, 0):
                    copy.wait()
            elif j >= 0:
                (collect, collect_down)[m].step(k, j)

    cross.start(1)
    cross_down.start(1)
    cross_down.start(3)
    vec[...] = jnp.zeros_like(vec)
    for n, vector in enumerate(vectors):
        vec[n : n + 1, :] = vector[...].astype(F32).reshape(1, width)
    bup[...] = jnp.broadcast_to(b_up[...].astype(F32).reshape(1, width), bup.shape)
    bup_all[link.tp] = bup[...]
    length = len_ref[0]
    position = lax.broadcasted_iota(jnp.int32, (1, rows), 1) + own_first
    live = (position < length).astype(F32)
    e_own.wait()
    early[0].wait()
    em[...] = (em[...].astype(F32) * live).astype(BF)
    ysend[...] = dot(em[...], x[...], 1, 0).astype(ysend.dtype)
    reduce = [
        link.send(ysend.at[place(link.ahead(k), quarter), :], yrecv.at[k - 1], (link.dp, link.ahead(k)))
        for k in others
    ]
    biases = [link.send(bup, bup_all.at[link.tp], (link.dp, link.ahead(k))) for k in others]
    early[1].wait()
    q[...] = (dot(x[...], wq[...], 1, 0) + vec[0:1, :]).astype(BF)
    tick(EARLY_TICKS)
    own_slots = place(link.tp, quarter)
    for copy in reduce:
        copy.wait()
    own_y = ysend[own_slots, :].astype(F32)
    for k in others:
        own_y = own_y + yrecv[k - 1].astype(F32)
    yb[own_slots, :] = own_y.astype(BF)
    share = [
        link.send(yb.at[own_slots, :], yb.at[own_slots, :], (link.dp, link.ahead(k))) for k in others
    ]
    for k in (3, 2):
        cross.start(k)
    cross_down.start(2)
    tick(SHARE_TICKS)
    stores = [local(q, q_out), local(em, em_out)]
    row_live = (lax.broadcasted_iota(jnp.int32, (total, 128), 0) < length).astype(F32).astype(BF)
    for load in late:
        load.wait()
    ssum[...] = dot(e_all[...], row_live, 1, 0)
    for copy in share:
        copy.wait()
    for copy in biases:
        copy.wait()
    stores += [local(yb, yb_out), local(ssum, ssum_out)]

    lane = lax.broadcasted_iota(jnp.int32, (1, PAIR), 1)
    first_half = (lane < HEAD).astype(F32)

    def project(weight, bias_row, blocks):
        full = dot(yb[...], weight[...], 1, 0)
        for p in range(PAIRS):
            cols = slice(p * PAIR, (p + 1) * PAIR)
            both = full[:, cols] + ssum[...] * vec[bias_row : bias_row + 1, cols]
            blocks[p, 0:slots, :] = (both * first_half).astype(BF)
            blocks[p, slots : 2 * slots, :] = (both * (1.0 - first_half)).astype(BF)

    project(wk, 1, kb)
    project(wv, 2, vb)
    stores += [local(kb, kb_out), local(vb, vb_out)]

    block = min(BLOCK_F, rows)
    per_pair = rows // block
    probs_sem = used[0]

    def attend(p, carry):
        cols = place(p, PAIR)

        def one(step, carry):
            here = place(step, block)
            logits = dot(q[here, cols], kb[p], 1, 1) * 0.125
            halves = []
            for half in range(2):
                part = logits[:, half * slots : (half + 1) * slots]
                peak = jnp.max(part, axis=-1, keepdims=True)
                raised = jnp.exp(part - peak)
                halves.append((raised * (1.0 / jnp.sum(raised, axis=-1, keepdims=True))).astype(BF))
            both = jnp.concatenate(halves, axis=1)
            probs[p, here, :] = both
            mixed[here, cols] = dot(both, vb[p], 1, 0).astype(BF)
            return carry

        lax.fori_loop(0, per_pair, one, 0)
        pltpu.make_async_copy(probs.at[p], probs_out.at[p], local_sems.at[probs_sem + p]).start()
        for n, ticks in PAIR_TICKS.items():

            @pl.when(p == n)
            def _():
                tick(ticks)

        return carry

    lax.fori_loop(0, PAIRS, attend, 0)
    used[0] += PAIRS
    stores.append(local(mixed, mixed_out))

    def finish(step, carry):
        here = place(step, block)
        res = x[here, :].astype(F32) + dot(mixed[here, :], wo[...], 1, 0) + vec[3:4, :]
        center = res - jnp.mean(res, axis=-1, keepdims=True)
        inverse = lax.rsqrt(jnp.mean(center * center, axis=-1, keepdims=True) + 1e-05)
        xhat[here, :] = center * inverse
        rstd[here, :] = jnp.broadcast_to(inverse, (block, 128))
        return carry

    lax.fori_loop(0, per_pair, finish, 0)
    stores += [local(xhat, xhat_out), local(rstd, rstd_out)]
    tick(LAST_TICKS)
    for copy in stores:
        copy.wait()
    for p in range(PAIRS):
        pltpu.make_async_copy(probs.at[p], probs_out.at[p], local_sems.at[probs_sem + p]).wait()


def front(mesh, lengths, x, wq, e, wk, wv, wo, wup, wdn, vectors, b_up):
    dp_size, tp_size = mesh.shape["dp"], mesh.shape["tp"]
    low = min(3, dp_size.bit_length() - 1)
    rows, width = x.shape
    slots = e.shape[0]
    vmem = pl.BlockSpec(memory_space=pltpu.VMEM)
    hbm = pl.BlockSpec(memory_space=pltpu.HBM)
    shape = jax.ShapeDtypeStruct
    moved = (
        ((rows, width), F32),
        ((rows, 128), F32),
        ((rows, width), BF),
        ((rows, width), BF),
        ((PAIRS, rows, 2 * slots), BF),
        ((PAIRS, 2 * slots, PAIR), BF),
        ((PAIRS, 2 * slots, PAIR), BF),
        ((slots, width), BF),
        ((slots, 128), F32),
        ((slots, rows), BF),
    )
    kept = (
        ((VECTORS, width), F32),
        ((tp_size, 8, width), F32),
    )
    return pl.pallas_call(
        functools.partial(front_kernel, dp_size, tp_size, len(vectors)),
        out_shape=tuple(shape(*s) for s in kept + moved)
        + (
            shape((tp_size - 1, *wup.shape), BF),
            shape((tp_size - 1, *wdn.shape), BF),
        ),
        in_specs=[pl.BlockSpec(memory_space=pltpu.SMEM)]
        + [hbm] * 8
        + [vmem] * (len(vectors) + 1),
        out_specs=tuple([vmem] * len(kept) + [hbm] * (len(moved) + 2)),
        scratch_shapes=[pltpu.VMEM(w.shape, BF) for w in (x, wq, wk, wv, wo, e)]
        + [pltpu.VMEM(*s) for s in moved]
        + [
            pltpu.VMEM((8, width), F32),
            pltpu.VMEM((slots, width), BF),
            pltpu.VMEM((tp_size - 1, slots // tp_size, width), BF),
            pltpu.SemaphoreType.DMA((FRONT_SEMS,)),
            pltpu.SemaphoreType.DMA((FRONT_SEMS,)),
            pltpu.SemaphoreType.DMA((32,)),
        ],
        compiler_params=pltpu.CompilerParams(
            collective_id=0, has_side_effects=True, vmem_limit_bytes=VMEM_LIMIT
        ),
        name="front",
    )(lengths, x, wq, e, wk, wv, wo, wup, wdn, *vectors, b_up)


BACK_SEMS = 128
VECTORS = 16


def add_rows(target, first, left, left_first, right, count):
    block = 96 if count % 96 == 0 else (48 if count % 48 == 0 else (32 if count % 32 == 0 else count))

    def step(i, carry):
        at = i * block
        total = (
            left[rows_at(left_first + at, block, 16), :].astype(F32)
            + right[rows_at(at, block, 16), :].astype(F32)
        )
        target[rows_at(first + at, block, 16), :] = total.astype(target.dtype)
        return carry

    lax.fori_loop(0, count // block, step, 0)


class Spread:
    def __init__(self, link, order, rows, source, acc, landing):
        self.link, self.rows, self.source, self.acc, self.landing = link, rows, source, acc, landing
        self.order = [b for b in order if b < link.low]
        self.stages = len(self.order)
        self.slot = link.take(self.stages)
        self.piece = rows >> self.stages
        self.insides, self.others, first = [0], [(1 - link.bit(self.order[0])) * (rows >> 1)], 0
        for j in range(1, self.stages):
            size = rows >> (j + 1)
            self.others.append(first + (1 - link.bit(self.order[j])) * size)
            first = first + link.bit(self.order[j]) * size
            self.insides.append(first)
        self.at = link.bit(self.order[0]) * (rows >> 1) + first

    def inside(self, i):
        return self.insides[i]

    def kept(self):
        return rows_at(self.inside(self.stages - 1), self.piece, 16)

    def offset(self):
        return self.at

    def landed(self, i):
        first = sum(self.rows >> (j + 1) for j in range(i))
        return self.landing.at[pl.ds(first, self.rows >> (i + 1)), :]

    def copy(self, i):
        link, size = self.link, self.rows >> (i + 1)
        where, other = self.source if i == 0 else self.acc, self.others[i]
        return link.remote(
            self.slot + i, where.at[rows_at(other, size, 16), :], self.landed(i), link.partner(self.order[i])
        )

    def start(self, i):
        self.copy(i).start()

    def finish(self, i):
        size = self.rows >> (i + 1)
        self.copy(i).wait()
        if i == 0:
            add_rows(self.acc, 0, self.source, self.link.bit(self.order[0]) * size, self.landed(0), size)
        else:
            at = self.inside(i)
            add_rows(self.acc, at, self.acc, at, self.landed(i), size)

    def steps(self):
        yield lambda: self.start(0)
        for i in range(1, self.stages):

            def step(i=i):
                self.finish(i - 1)
                self.start(i)

            yield step


class Collect:
    def __init__(self, link, order, offset, piece, region):
        self.link, self.offset, self.piece, self.region = link, offset, piece, region
        self.order = [b for b in order if b < link.low][::-1]
        self.slot = link.take(len(self.order))
        starts, size = [], piece
        for b in self.order:
            starts.append(link.bit(b) * size)
            size *= 2
        self.firsts = [sum(starts[i:], 0) for i in range(len(self.order))]

    def copy(self, i):
        size, first = self.piece << i, self.firsts[i]
        ref = self.region(first, size)
        return self.link.remote(self.slot + i, ref, ref, self.link.partner(self.order[i]))

    def steps(self):
        yield lambda: self.copy(0).start()
        for i in range(1, len(self.order)):

            def step(i=i):
                self.copy(i - 1).wait()
                self.copy(i).start()

            yield step
        yield lambda: self.copy(len(self.order) - 1).wait()


class Widen:
    def __init__(self, link, landing):
        self.link, self.landing = link, landing
        self.slot = link.take(max(0, link.bits - link.low))

    def run(self, piece):
        link = self.link
        for i, b in enumerate(range(link.low, link.bits)):
            copy = link.remote(self.slot + i, piece, self.landing.at[i], link.partner(b))
            copy.start()
            copy.wait()
            piece[...] = (piece[...].astype(F32) + self.landing[i].astype(F32)).astype(piece.dtype)


class Fan:
    def __init__(self, link, ends):
        self.link, self.ends = link, ends
        self.slot = link.take(link.tp_size - 1)

    def copy(self, k):
        source, target = self.ends(k)
        return self.link.remote(self.slot + k - 1, source, target, (self.link.dp, self.link.ahead(k)))

    def start(self):
        for k in range(1, self.link.tp_size):
            self.copy(k).start()

    def wait(self):
        for k in range(1, self.link.tp_size):
            self.copy(k).wait()


def then(*actions):
    def both():
        for action in actions:
            action()

    return both


class Track:
    def __init__(self):
        self.todo = []

    def add(self, steps, join=False):
        steps = list(steps)
        if join and self.todo:
            steps[0] = then(self.todo.pop(), steps[0])
        self.todo += steps

    def advance(self):
        if self.todo:
            self.todo.pop(0)()


def back_kernel(
    dp_size,
    tp_size,
    len_ref,
    vec,
    part_vec,
    ff_near,
    dnorm,
    probs,
    far_hbm,
    own_hbm,
    xhat_hbm,
    rstd_hbm,
    mixed_hbm,
    wo_hbm,
    landed_hbm,
    x_hbm,
    q_hbm,
    kb_hbm,
    vb_hbm,
    yb_hbm,
    ssum_hbm,
    em_hbm,
    wq_hbm,
    wk_hbm,
    wv_hbm,
    grad_hbm,
    ff_hbm,
    go_hbm,
    gq_out,
    gkv_out,
    seq_out,
    vec_out,
    grad_in,
    ff_out,
    go_out,
    ff_far,
    ff_own,
    xhat,
    rstd,
    mixed,
    wo,
    ff_landed,
    x,
    q,
    kb,
    vb,
    yb,
    ssum,
    em,
    wq,
    wk,
    wv,
    dres,
    dmix,
    dq,
    dl,
    prob_slots,
    dpart,
    dland,
    dfull,
    ff_zland,
    far_acc,
    far_land,
    own_acc,
    own_land,
    o_acc,
    o_land,
    q_acc,
    q_land,
    o_zland,
    q_zland,
    kv_send,
    kv_acc,
    kv_land,
    s_send,
    s_acc,
    s_land,
    vec_acc,
    vec_land,
    vec_z,
    wide_ff,
    wide_q,
    wide_kv,
    wide_s,
    send_sems,
    recv_sems,
    local_sems,
):
    link = Link(dp_size, tp_size, send_sems, recv_sems)
    rows, width = x.shape
    slots = yb.shape[0]
    low = link.low
    others = range(1, tp_size)
    first_load = pltpu.make_async_copy(dnorm, dres, local_sems.at[0])
    first_load.start()
    late = []
    for n, (source, target) in enumerate(
        (
            (far_hbm, ff_far), (own_hbm, ff_own), (xhat_hbm, xhat), (rstd_hbm, rstd), (mixed_hbm, mixed),
            (wo_hbm, wo), (landed_hbm, ff_landed), (q_hbm, q), (kb_hbm, kb), (vb_hbm, vb), (x_hbm, x), (yb_hbm, yb),
            (wq_hbm, wq), (wk_hbm, wk), (wv_hbm, wv), (ssum_hbm, ssum), (em_hbm, em),
        )
    ):
        late.append(pltpu.make_async_copy(source, target, local_sems.at[3 + n]))
        late[-1].start()
    link.greet(link.bits)

    lanes = 2
    deep = tp_size // lanes
    third = width // GRAD_SPLIT
    owned = width // tp_size

    ff_track, ff_orders = Track(), ((0, 1, 2), (0, 2, 1))
    ff_rows = width >> 3
    ff_parts = []
    for m in range(2):
        first, second, third_bit = ff_orders[m]
        far = Spread(link, (third_bit,), width >> 2, ff_far.at[m], far_acc.at[m], far_land.at[m])
        own = Spread(link, (second, third_bit), width >> 1, ff_own.at[m], own_acc.at[m], own_land.at[m])
        slot = link.take(2)

        def piece_copy(n, m=m, slot=slot):
            source, k = ((far_acc, 3), (ff_near, 2))[n]
            return link.remote(slot + n, source.at[m], ff_zland.at[m, n], (link.dp, link.behind(k)))

        at = link.bit(ff_orders[m][0]) * (width >> 1) + own.offset()

        def offset(at=at):
            return at

        widen = Widen(link, wide_ff.at[m])

        def join(m=m, own=own, piece_copy=piece_copy, offset=offset, widen=widen):
            total = own_acc[m, own.kept(), :].astype(F32) + ff_landed[m].astype(F32)
            for n in range(2):
                piece_copy(n).wait()
                total = total + ff_zland[m, n].astype(F32)
            mine = rows_at(offset(), ff_rows, 16)
            ff_out[m, mine, :] = total.astype(BF)
            widen.run(ff_out.at[m, mine, :])

        collect = Collect(
            link, ff_orders[m], offset, ff_rows,
            lambda first, size, m=m: ff_out.at[m, rows_at(first, size, 16), :],
        )
        ff_parts.append((far, own, piece_copy, join, list(collect.steps())))

    def ff_begin():
        for far, own, piece_copy, _, _ in ff_parts:
            far.start(0)
            own.start(0)
            piece_copy(1).start()

    def ff_second():
        for far, own, piece_copy, _, _ in ff_parts:
            far.finish(0)
            piece_copy(0).start()

    def ff_second_own():
        for far, own, piece_copy, _, _ in ff_parts:
            own.finish(0)
            own.start(1)

    def ff_third():
        for _, own, _, join, collects in ff_parts:
            own.finish(1)

    def ff_join():
        for _, _, _, join, collects in ff_parts:
            join()
            collects[0]()

    stores = []

    def store(n, source, target):
        copy = pltpu.make_async_copy(source, target, local_sems.at[20 + n])
        stores.append(copy)
        return copy

    ff_store, go_store, grad_store = store(0, ff_out, ff_hbm), store(1, go_out, go_hbm), store(2, grad_in, grad_hbm)
    late[0].wait()
    late[1].wait()
    ff_begin()
    ff_track.add([ff_second, ff_second_own, then(ff_third, ff_join)])
    ff_track.add([then(*pair) for pair in zip(ff_parts[0][4][1:], ff_parts[1][4][1:])])
    ff_track.add([ff_store.start], join=True)

    def square_track(order, out, acc, landing, zland, wide):
        track, spread = Track(), Spread(link, order, width, out, acc, landing)
        q_rows, q_cols = spread.piece // deep, width // lanes
        row_of = [lax.div(t, lanes) * q_rows for t in link.aheads]
        col_of = [lax.rem(t, lanes) * q_cols for t in link.aheads]

        def quarter(first, k):
            return (
                rows_at(first + row_of[k], q_rows, 16),
                pl.ds(pl.multiple_of(col_of[k], 128), q_cols),
            )

        def there(k):
            return acc.at[quarter(spread.inside(spread.stages - 1), k)], zland.at[k - 1]

        def again(k):
            region = out.at[quarter(spread.offset(), 0)]
            return region, region

        fan, share, widen = Fan(link, there), Fan(link, again), Widen(link, wide)

        def join():
            fan.wait()
            total = acc[quarter(spread.inside(spread.stages - 1), 0)].astype(F32)
            for k in others:
                total = total + zland[k - 1].astype(F32)
            mine = quarter(spread.offset(), 0)
            out[mine] = total.astype(BF)
            widen.run(out.at[mine])
            share.start()

        collect = Collect(
            link, order, spread.offset, spread.piece, lambda first, size: out.at[rows_at(first, size, 16), :]
        )
        track.add(spread.steps())
        track.add([then(lambda: spread.finish(spread.stages - 1), fan.start), join, share.wait])
        track.add(collect.steps(), join=True)
        return track

    def owned_track(order, total_rows, cols, source, acc, landing, out, wide):
        source, acc, landing = source.at[:, cols], acc.at[:, cols], landing.at[:, cols]
        track, spread = Track(), Spread(link, order, total_rows, source, acc, landing)

        def region(k):
            ref = out.at[link.tp, rows_at(spread.offset(), spread.piece, 16), cols]
            return ref, ref

        share, widen = Fan(link, region), Widen(link, wide)

        def last():
            spread.finish(spread.stages - 1)
            ref = region(0)[0]
            ref[...] = acc[spread.kept(), :]
            widen.run(ref)
            share.start()

        collect = Collect(
            link, order, spread.offset, spread.piece, lambda first, size: out.at[:, rows_at(first, size, 16), cols]
        )
        track.add(spread.steps())
        track.add([last, share.wait])
        track.add(collect.steps(), join=True)
        return track

    o_track = square_track((0, 1, 2), go_out, o_acc, o_land, o_zland, wide_q.at[0])
    o_track.add([go_store.start], join=True)
    q_track = square_track((0, 2, 1), gq_out, q_acc, q_land, q_zland, wide_q.at[1])
    def halves(total_rows, source, acc, landing, out, wide):
        tracks = []
        for h, order in enumerate(((0, 1, 2), (0, 2, 1))):
            cols = slice(h * source.shape[1] // 2, (h + 1) * source.shape[1] // 2)
            tracks.append(owned_track(order, total_rows, cols, source, acc, landing, out, wide.at[h]))
        both = Track()
        both.add([then(*pair) for pair in zip(tracks[0].todo, tracks[1].todo)])
        return both

    kv_track = halves(2 * owned, kv_send, kv_acc, kv_land, gkv_out, wide_kv)
    s_track = halves(slots, s_send, s_acc, s_land, seq_out, wide_s)

    vec_track, vec_slot = Track(), link.take(link.bits)
    vec_fan = Fan(link, lambda k: (vec_z.at[link.tp], vec_z.at[link.tp]))

    def vec_copy(b):
        return link.remote(vec_slot + b, vec_acc.at[b], vec_land.at[b], link.partner(b))

    vec_track.add([lambda: vec_copy(0).start()])
    for b in range(link.bits):

        def vec_step(b=b):
            vec_copy(b).wait()
            total = vec_acc[b] + vec_land[b]
            if b + 1 < link.bits:
                vec_acc[b + 1] = total
                vec_copy(b + 1).start()
            else:
                vec_z[link.tp] = total
                vec_fan.start()

        vec_track.add([vec_step])

    def vec_last():
        vec_fan.wait()
        total = vec_z[0]
        for t in range(1, tp_size):
            total = total + vec_z[t]
        vec_out[...] = total

    vec_track.add([vec_last])

    block = min(BLOCK_B, rows)
    count = rows // block
    gain = vec[4:5, :]

    def norm_back(step, carry):
        g_gain, g_shift, g_out = carry
        here = place(step, block)
        grad, hat = dres[here, :], xhat[here, :]
        g_gain = g_gain + jnp.sum(grad * hat, axis=0, keepdims=True)
        g_shift = g_shift + jnp.sum(grad, axis=0, keepdims=True)
        scaled = grad * gain
        d_res = rstd[here, 0:1] * (
            scaled
            - jnp.mean(scaled, axis=-1, keepdims=True)
            - hat * jnp.mean(scaled * hat, axis=-1, keepdims=True)
        )
        dres[here, :] = d_res
        d_attn = d_res.astype(BF)
        dq[here, :] = d_attn
        g_out = g_out + jnp.sum(d_attn.astype(F32), axis=0, keepdims=True)
        return g_gain, g_shift, g_out

    zero = jnp.zeros((1, width), F32)
    first_load.wait()
    late[2].wait()
    late[3].wait()
    g_gain, g_shift, g_out = lax.fori_loop(0, count, norm_back, (zero, zero, zero))
    vec_acc[0] = part_vec[...]
    vec_acc[0, 3:4, :] = g_out
    vec_acc[0, 4:5, :] = g_gain
    vec_acc[0, 5:6, :] = g_shift
    d_attn = dq

    def weight_grad(left, right, target):
        for m in range(GRAD_SPLIT):
            cols = slice(m * third, (m + 1) * third)
            target[cols, :] = dot(left[:, cols], right[...], 0, 0).astype(BF)

    for load in late[4:7]:
        load.wait()
    weight_grad(mixed, d_attn, go_out)
    o_track.advance()
    ff_track.advance()
    dmix[...] = dot(d_attn[...], wo[...], 1, 1).astype(BF)
    o_track.advance()
    for load in late[7:]:
        load.wait()

    own_half = lax.div(link.tp, 2)
    parity = lax.rem(link.tp, 2)
    three = PAIRS // 2

    def pair_at(n):
        second = lax.div(n, three)
        which = (1 - own_half) * (1 - second) + own_half * second
        along = lax.rem(n, three)
        return which * three + along * parity + (three - 1 - along) * (1 - parity)

    def fetch(n):
        slot = lax.rem(n, 2)
        return pltpu.make_async_copy(probs.at[pair_at(n)], prob_slots.at[slot], local_sems.at[1 + slot])

    fetch(0).start()

    def attend_back(n):
        p = pair_at(n)
        cols = place(p, PAIR)

        @pl.when(n + 1 < PAIRS)
        def _():
            fetch(n + 1).start()

        fetch(n).wait()
        held = prob_slots.at[lax.rem(n, 2)]

        def part(step, carry):
            here = place(step, block)
            d_probs = dot(dmix[here, cols], vb[p], 1, 1)
            weights = held[here, :].astype(F32)
            halves = []
            for h in range(2):
                w = weights[:, h * slots : (h + 1) * slots]
                d = d_probs[:, h * slots : (h + 1) * slots]
                halves.append((w * (d - jnp.sum(w * d, axis=-1, keepdims=True))).astype(BF))
            both = jnp.concatenate(halves, axis=1)
            dl[here, :] = both
            dq[here, cols] = (dot(both, kb[p], 1, 0) * 0.125).astype(BF)
            return carry

        lax.fori_loop(0, count, part, 0)
        top, under = rows_at(p * PAIR, HEAD, HEAD), rows_at(p * PAIR + HEAD, HEAD, HEAD)
        for n, total in enumerate(
            (dot(q[:, cols], dl[...], 0, 0) * 0.125, dot(dmix[:, cols], held[...], 0, 0))
        ):
            dpart[n, top, :] = total[:HEAD, :slots].astype(BF)
            dpart[n, under, :] = total[HEAD:, slots:].astype(BF)

    d_slot = link.take(tp_size - 1)
    d_peers = [2 * (1 - own_half) + parity, 2 * (1 - own_half) + (1 - parity), 2 * own_half + (1 - parity)]

    def d_copy(j):
        peer = d_peers[j]
        block_of = dpart.at[:, rows_at(peer * owned, owned, 64), :]
        return link.remote(d_slot + j, block_of, dland.at[j], (link.dp, peer))

    events = [
        then(),
        then(lambda: d_copy(1).start(), ff_track.advance),
        lambda: d_copy(0).start(),
        o_track.advance,
        then(lambda: d_copy(2).start(), ff_track.advance),
        then(),
    ]

    def one(n, carry):
        attend_back(n)
        for i, event in enumerate(events):
            pl.when(n == i)(event)
        return carry

    lax.fori_loop(0, PAIRS, one, 0)

    weight_grad(x, dq, gq_out)
    q_track.advance()
    ff_track.advance()

    def input_grad(step, carry):
        here = place(step, block)
        dres[here, :] += dot(dq[here, :], wq[...], 1, 1)
        return carry

    lax.fori_loop(0, count, input_grad, 0)
    q_track.advance()
    vec_acc[0, 0:1, :] = jnp.sum(dq[...].astype(F32), axis=0, keepdims=True)

    for j in range(tp_size - 1):
        d_copy(j).wait()
    own_block = rows_at(link.tp * owned, owned, 64)
    for n in range(2):
        total = dpart[n, own_block, :].astype(F32)
        for j in range(tp_size - 1):
            total = total + dland[j, n].astype(F32)
        dfull[n, own_block, :] = total.astype(BF)
    d_share = Fan(link, lambda k: (dfull.at[:, own_block, :], dfull.at[:, own_block, :]))
    d_share.start()
    ff_track.advance()
    for n in range(2):
        kv_send[n * owned : (n + 1) * owned, :] = dot(dfull[n, own_block, :], yb[...], 1, 0).astype(BF)
    kv_track.advance()
    q_track.advance()
    ff_track.advance()
    kv_track.advance()
    o_track.advance()
    kv_track.advance()
    q_track.advance()
    kv_track.advance()
    o_track.advance()
    d_share.wait()
    backs = dot(wk[...], dfull[0], 1, 0) + dot(wv[...], dfull[1], 1, 0)
    back = backs.T.astype(BF)
    small = vec[0:8, :].astype(BF)
    bias_row = dot(small, dfull[0], 1, 0)[1:2, :] + dot(small, dfull[1], 1, 0)[2:3, :]
    bias_column = jnp.broadcast_to(bias_row, (128, slots)).T[:, 0:1]
    position = lax.broadcasted_iota(jnp.int32, (1, rows), 1) + link.tp * rows
    live = (position < len_ref[0]).astype(F32)
    s_send[...] = ((dot(back, x[...], 1, 1) + bias_column) * live).astype(BF)
    s_track.advance()
    column = ssum[...].T[0:8, :]
    column_b = column.astype(BF)
    column_low = (column - column_b.astype(F32)).astype(BF)
    for n in range(2):
        total = dot(column_b, dfull[n], 1, 1) + dot(column_low, dfull[n], 1, 1)
        vec_acc[0, 1 + n : 2 + n, :] = total[0:1, :] * (1.0 / tp_size)
    vec_track.advance()
    s_track.advance()

    def input_grad_last(step, carry):
        here = place(step, block)
        grad_in[here, :] = (dres[here, :] + dot(em[:, here], back, 0, 0)).astype(BF)
        return carry

    lax.fori_loop(0, count, input_grad_last, 0)
    grad_store.start()
    tracks = [s_track, kv_track, q_track, o_track, vec_track, ff_track]
    while any(track.todo for track in tracks):
        for track in tracks:
            track.advance()
    for copy in stores:
        copy.wait()


def back(mesh, lengths, vec, part_vec, ff_near, dnorm, probs, *late):
    dp_size, tp_size = mesh.shape["dp"], mesh.shape["tp"]
    bits = dp_size.bit_length() - 1
    low = min(3, bits)
    wide = max(1, bits - low)
    rows, width = dnorm.shape
    slots = late[11].shape[0]
    owned = width // tp_size
    others = tp_size - 1
    vmem = pl.BlockSpec(memory_space=pltpu.VMEM)
    hbm = pl.BlockSpec(memory_space=pltpu.HBM)
    shape = jax.ShapeDtypeStruct

    def landing(total):
        return sum(total >> (i + 1) for i in range(low))

    def buf(*dims, dtype=BF):
        return pltpu.VMEM(dims, dtype)

    ff_piece, kv_piece, s_piece = width >> low, 2 * owned >> low, slots >> low
    quarter = (ff_piece // (tp_size // 2), width // 2)
    return pl.pallas_call(
        functools.partial(back_kernel, dp_size, tp_size),
        out_shape=(
            shape((rows, width), BF),
            shape((2, width, width), BF),
            shape((width, width), BF),
            shape((width, width), BF),
            shape((tp_size, 2 * owned, width), BF),
            shape((tp_size, slots, rows), BF),
            shape((VECTORS, width), F32),
        ),
        in_specs=[pl.BlockSpec(memory_space=pltpu.SMEM)] + [vmem] * 2 + [hbm] * (3 + len(late)),
        out_specs=tuple([hbm] * 3 + [vmem] * 4),
        scratch_shapes=[buf(rows, width), buf(2, width, width), buf(width, width)]
        + [pltpu.VMEM(array.shape, array.dtype) for array in late]
        + [
            buf(rows, width, dtype=F32),
            buf(rows, width),
            buf(rows, width),
            buf(rows, 2 * slots),
            buf(2, rows, 2 * slots),
            buf(2, width, slots),
            buf(others, 2, owned, slots),
            buf(2, width, slots),
            buf(2, 2, ff_piece, width),
            buf(2, width >> 3, width),
            buf(2, width >> 3, width),
            buf(2, width >> 2, width),
            buf(2, (width >> 2) + (width >> 3), width),
            buf(width // 2, width),
            buf(landing(width), width),
            buf(width // 2, width),
            buf(landing(width), width),
            buf(others, *quarter),
            buf(others, *quarter),
            buf(2 * owned, width),
            buf(owned, width),
            buf(landing(2 * owned), width),
            buf(slots, rows),
            buf(slots // 2, rows),
            buf(landing(slots), rows),
            buf(bits, VECTORS, width, dtype=F32),
            buf(bits, VECTORS, width, dtype=F32),
            buf(tp_size, VECTORS, width, dtype=F32),
            buf(2, wide, ff_piece, width),
            buf(2, wide, *quarter),
            buf(2, wide, kv_piece, width // 2),
            buf(2, wide, s_piece, rows // 2),
            pltpu.SemaphoreType.DMA((BACK_SEMS,)),
            pltpu.SemaphoreType.DMA((BACK_SEMS,)),
            pltpu.SemaphoreType.DMA((6 + len(late),)),
        ],
        compiler_params=pltpu.CompilerParams(
            collective_id=1, has_side_effects=True, vmem_limit_bytes=VMEM_LIMIT
        ),
        name="back",
    )(lengths, vec, part_vec, ff_near, dnorm, probs, *late)


class ChunkSpread:
    def __init__(self, link, rows, sent, acc, landing):
        self.link, self.rows, self.sent, self.acc, self.landing = link, rows, sent, acc, landing
        self.orders = [[b for b in order if b < link.low] for order in ((0, 1, 2), (0, 2, 1))]
        self.stages = link.low
        self.slot = link.take(2 * link.low * acc.shape[1])
        self.insides, self.others = [], []
        for order in self.orders:
            inside, other, first = [0], [(1 - link.bit(order[0])) * (rows >> 1)], 0
            for j in range(1, self.stages):
                size = rows >> (j + 1)
                other.append(first + (1 - link.bit(order[j])) * size)
                first = first + link.bit(order[j]) * size
                inside.append(first)
            self.insides.append(inside)
            self.others.append(other)

    def inside(self, m, i):
        return self.insides[m][i]

    def copy(self, c, m, i):
        link, size = self.link, self.rows >> (i + 1)
        bit = self.orders[m][i]
        if i == 0:
            source = self.sent.at[m, lax.rem(c, 2), rows_at(self.others[m][i], size, 16), :]
        else:
            source = self.acc.at[m, c, rows_at(self.others[m][i], size, 16), :]
        first = sum(self.rows >> (j + 1) for j in range(i))
        slot = self.slot + (i * 2 + m) * self.acc.shape[1] + c
        return link.remote(slot, source, self.landing.at[m, c, pl.ds(first, size), :], link.partner(bit))

    def start(self, c, m, i):
        self.copy(c, m, i).start()

    def finish(self, c, m, i):
        size = self.rows >> (i + 1)
        self.copy(c, m, i).wait()
        first = sum(self.rows >> (j + 1) for j in range(i))
        landed = self.landing.at[m, c, pl.ds(first, size), :]
        acc = self.acc.at[m, c]
        if i == 0:
            mine = self.link.bit(self.orders[m][0]) * size
            add_rows(acc, 0, self.sent.at[m, lax.rem(c, 2)], mine, landed, size)
        else:
            at = self.inside(m, i)
            add_rows(acc, at, acc, at, landed, size)


MIDDLE_SEMS = 96
MIDDLE_TICKS = {3: ((1, 1),), 5: ((0, 2), (0, 3)), 7: ((1, 2), (1, 3))}


def middle_kernel(
    dp_size,
    tp_size,
    vec,
    bup_all,
    xhat_hbm,
    out_grad_hbm,
    own_up,
    own_dn,
    ups,
    downs,
    layer_hbm,
    dnorm,
    part_vec,
    ff_landed,
    ff_near,
    ff_far,
    ff_own,
    whole,
    xhat,
    layer_out,
    out_grad,
    nb,
    act,
    slope,
    d_branch,
    d_acc,
    sent,
    acc,
    landing,
    send_sems,
    recv_sems,
    local_sems,
):
    link = Link(dp_size, tp_size, send_sems, recv_sems)
    rows, width = xhat.shape
    used = [0]

    def local(source, target):
        copy = pltpu.make_async_copy(source, target, local_sems.at[used[0]])
        used[0] += 1
        copy.start()
        return copy

    collect = WeightCollect(link, width // 2, lambda k: whole.at[1, k])
    xhat_load = local(xhat_hbm, xhat)
    up_last = WeightCollect(link, width // 2, lambda k: whole.at[0, k])
    placed = [
        local(ups.at[1, up_last.rows(h, 1), :], whole.at[0, 2, up_last.rows(h, 1), :]) for h in range(2)
    ]
    placed += [
        local(downs.at[1, collect.rows(h, 0), :], whole.at[1, 2, collect.rows(h, 0), :]) for h in range(2)
    ]
    owns = [local(own_up, whole.at[0, 0])]
    owns += [local(ups.at[k - 1], whole.at[0, k]) for k in (1, 3)]
    owns += [local(own_dn, whole.at[1, 0])] + [local(downs.at[k - 1], whole.at[1, k]) for k in (1, 3)]
    owns.append(local(out_grad_hbm, out_grad))
    link.greet(link.low)
    for copy in placed:
        copy.wait()
    collect.step(2, 0)
    for copy in up_last.copies(2, 1):
        copy.start()
    xhat_load.wait()
    gain, shift, b_down, f_gain, f_shift = (vec[n : n + 1, :] for n in (4, 5, 6, 7, 8))
    block = min(BLOCK_M, rows)
    count = rows // block
    big = rows // 2

    def norm(step, carry):
        here = place(step, block)
        nb[here, :] = (xhat[here, :] * gain + shift).astype(BF)
        return carry

    lax.fori_loop(0, count, norm, 0)
    for copy in owns[: tp_size - 1]:
        copy.wait()

    def forward(step, carry):
        n = lax.div(step, 2)
        k = n + lax.div(n, 2) * (7 - 2 * n - 2)
        here, cols = place(lax.rem(step, 2), big), place(k, width)
        pre = dot(nb[here, :], whole[0, k], 1, 0) + bup_all[link.behind(k), 0:1, :]
        cdf = 0.5 * (1.0 + lax.erf(pre * 0.7071067811865476))
        act[here, cols] = (pre * cdf).astype(BF)
        slope[here, cols] = (cdf + pre * (jnp.exp(pre * pre * -0.5) * 0.3989422804014327)).astype(BF)
        for n, ticks in MIDDLE_TICKS.items():

            @pl.when(step == n)
            def _():
                for m, j in ticks:
                    (up_last, collect)[m].step(2, j)

        return carry

    lax.fori_loop(0, 2 * tp_size, forward, 0)
    for copy in owns[tp_size - 1 :]:
        copy.wait()

    def second_norm(step, carry):
        g_gain, g_shift, g_down = carry
        here = place(step, block)
        branch = dot(act[here, 0:width], whole[1, 0], 1, 0)
        for k in range(1, tp_size):
            branch = branch + dot(act[here, k * width : (k + 1) * width], whole[1, k], 1, 0)
        res = xhat[here, :] * gain + shift + (branch + b_down)
        center = res - jnp.mean(res, axis=-1, keepdims=True)
        inverse = lax.rsqrt(jnp.mean(center * center, axis=-1, keepdims=True) + 1e-05)
        hat = center * inverse
        layer_out[here, :] = (hat * f_gain + f_shift).astype(BF)
        grad = out_grad[here, :].astype(F32)
        g_gain = g_gain + jnp.sum(grad * hat, axis=0, keepdims=True)
        g_shift = g_shift + jnp.sum(grad, axis=0, keepdims=True)
        scaled = grad * f_gain
        d_res = inverse * (
            scaled
            - jnp.mean(scaled, axis=-1, keepdims=True)
            - hat * jnp.mean(scaled * hat, axis=-1, keepdims=True)
        )
        d_acc[here, :] = d_res
        rounded = d_res.astype(BF)
        d_branch[here, :] = rounded
        g_down = g_down + jnp.sum(rounded.astype(F32), axis=0, keepdims=True)
        return g_gain, g_shift, g_down

    zero = jnp.zeros((1, width), F32)
    g_gain, g_shift, g_down = lax.fori_loop(0, count, second_norm, (zero, zero, zero))
    layer_store = local(layer_out, layer_hbm)
    part_vec[...] = jnp.zeros_like(part_vec)
    part_vec[6:7, :] = g_gain
    part_vec[7:8, :] = g_shift
    part_vec[8:9, :] = g_down

    spread = ChunkSpread(link, width, sent, acc, landing)
    third = width // GRAD_SPLIT

    def weight_grad(left, first, right, cols, target):
        for m in range(GRAD_SPLIT):
            mine = pl.ds(pl.multiple_of(first + m * third, third), third)
            target[m * third : (m + 1) * third, :] = dot(left[:, mine], right[:, cols], 0, 0).astype(BF)

    def settle(n, steps):
        for m, late, stage in steps:

            @pl.when(n >= late)
            def _():
                spread.finish(n - late, m, stage)

            if stage < 2:

                @pl.when(jnp.logical_and(n >= late, n - late < 3 - stage))
                def _():
                    spread.start(n - late, m, stage + 1)

    def backward(n, carry):
        k = lax.rem(n + 1, tp_size)
        cols = place(k, width)
        slot = lax.rem(n, 2)
        weight_grad(act, k * width, d_branch, slice(0, width), sent.at[1, slot])
        spread.start(n, 1, 0)
        settle(n, ((0, 1, 0), (1, 2, 1)))

        def through(step, total):
            here = place(step, big)
            grad = (dot(d_branch[here, :], whole[1, k], 1, 1) * slope[here, cols].astype(F32)).astype(BF)
            slope[here, cols] = grad
            return total + jnp.sum(grad.astype(F32), axis=0, keepdims=True)

        part_vec[pl.ds(9 + link.behind(k), 1), :] = lax.fori_loop(0, 2, through, zero)
        settle(n, ((1, 0, 0), (0, 2, 1)))
        weight_grad(nb, 0, slope, cols, sent.at[0, slot])
        spread.start(n, 0, 0)
        return carry

    lax.fori_loop(0, tp_size, backward, 0)

    def input_grad(step, carry):
        here = place(step, big)
        total = d_acc[here, :]
        for k in range(tp_size):
            total = total + dot(slope[here, k * width : (k + 1) * width], whole[0, k], 1, 1)
        d_acc[here, :] = total
        return carry

    slot = link.take(2)
    crossing = []
    lax.fori_loop(0, 1, input_grad, 0)
    for m in (1, 0):
        spread.finish(0, m, 2)
        at = rows_at(spread.inside(m, 2), width >> 3, 16)
        crossing.append(
            link.remote(slot + m, acc.at[m, 0, at, :], ff_landed.at[m], (link.dp, link.behind(1)))
        )
        crossing[-1].start()
    spread.finish(3, 0, 0)
    spread.finish(2, 1, 1)
    stores = [local(acc.at[m, 3], ff_own.at[m]) for m in range(2)]
    lax.fori_loop(1, 2, input_grad, 0)
    stores.append(local(d_acc, dnorm))
    spread.finish(2, 0, 1)
    for m in (1, 0):
        spread.finish(1, m, 2)
    for m in range(2):
        at = rows_at(spread.inside(m, 2), width >> 3, 16)
        stores.append(local(acc.at[m, 1, at, :], ff_near.at[m]))
        at = rows_at(spread.inside(m, 1), width >> 2, 16)
        stores.append(local(acc.at[m, 2, at, :], ff_far.at[m]))
    for copy in crossing + stores + [layer_store]:
        copy.wait()


def middle(mesh, vec, bup_all, xhat, out_grad, w_up, w_dn, ups, downs):
    dp_size, tp_size = mesh.shape["dp"], mesh.shape["tp"]
    low = min(3, dp_size.bit_length() - 1)
    assert low == 3 and tp_size == 4
    rows, width = xhat.shape
    hidden = tp_size * width
    vmem = pl.BlockSpec(memory_space=pltpu.VMEM)
    hbm = pl.BlockSpec(memory_space=pltpu.HBM)
    shape = jax.ShapeDtypeStruct

    def buf(*dims, dtype=BF):
        return pltpu.VMEM(dims, dtype)

    return pl.pallas_call(
        functools.partial(middle_kernel, dp_size, tp_size),
        out_shape=(
            shape((rows, width), BF),
            shape((rows, width), F32),
            shape((VECTORS, width), F32),
            shape((2, width >> 3, width), BF),
            shape((2, width >> 3, width), BF),
            shape((2, width >> 2, width), BF),
            shape((2, width >> 1, width), BF),
        ),
        in_specs=[vmem] * 2 + [hbm] * 6,
        out_specs=(hbm, hbm, vmem, hbm, hbm, hbm, hbm),
        scratch_shapes=[
            buf(2, tp_size, width, width),
            buf(rows, width, dtype=F32),
            buf(rows, width),
            buf(rows, width),
            buf(rows, width),
            buf(rows, hidden),
            buf(rows, hidden),
            buf(rows, width),
            buf(rows, width, dtype=F32),
            buf(2, 2, width, width),
            buf(2, tp_size, width // 2, width),
            buf(2, tp_size, sum(width >> (i + 1) for i in range(low)), width),
            pltpu.SemaphoreType.DMA((MIDDLE_SEMS,)),
            pltpu.SemaphoreType.DMA((MIDDLE_SEMS,)),
            pltpu.SemaphoreType.DMA((32,)),
        ],
        compiler_params=pltpu.CompilerParams(
            collective_id=2, has_side_effects=True, vmem_limit_bytes=VMEM_LIMIT
        ),
        name="middle",
    )(vec, bup_all, xhat, out_grad, w_up, w_dn, ups, downs)


def finish_kernel(
    tp_size, ff, gq, go, gkv, seq, vec, layer_out, grad_in,
    o_up, o_dn, o_q, o_o, o_k, o_v, o_seq, o_layer, o_grad, *rest,
):
    vectors, (in_up, in_dn, in_q, in_o, in_kv, in_seq, f_up, f_dn, f_q, f_o, f_k, f_v, f_seq, turn, pass_a, pass_b, in_sems, out_sems) = rest[:10], rest[10:]
    pairs = [(gq, in_q), (go, in_o), (ff.at[0], in_up), (ff.at[1], in_dn), (gkv, in_kv), (seq, in_seq), (layer_out, pass_a), (grad_in, pass_b)]
    loads = []
    for n, (source, target) in enumerate(pairs):
        loads.append(pltpu.make_async_copy(source, target, in_sems.at[n]))
        loads[-1].start()
    stores = []

    def put(staged, out):
        copy = pltpu.make_async_copy(staged, out, out_sems.at[len(stores)])
        copy.start()
        stores.append(copy)

    for n, (held, out) in enumerate(((pass_a, o_layer), (pass_b, o_grad))):
        loads[6 + n].wait()
        put(held, out)
    for n, row in enumerate((0, 1, 2, 3, 4, 5, 6, 7, 8)):
        vectors[n][...] = vec[row, :]
    vectors[9][...] = vec[pl.ds(9 + lax.axis_index("tp"), 1), :][0]
    width = gq.shape[0]
    for n, (narrow, wide, out) in enumerate(
        ((in_q, f_q, o_q), (in_o, f_o, o_o), (in_up, f_up, o_up), (in_dn, f_dn, o_dn))
    ):
        loads[n].wait()
        wide[...] = narrow[...].astype(F32)
        put(wide, out)
    loads[4].wait()
    owned = width // tp_size
    for n, (wide, out) in enumerate(((f_k, o_k), (f_v, o_v))):
        for c in range(tp_size):
            turn[c * owned : (c + 1) * owned, :] = in_kv[c, n * owned : (n + 1) * owned, :]
        for c in range(3):
            cols = slice(c * (width // 3), (c + 1) * (width // 3))
            wide[:, cols] = turn[cols, :].astype(F32).T
        put(wide, out)
    loads[5].wait()
    rows = in_seq.shape[2]
    for c in range(tp_size):
        f_seq[:, c * rows : (c + 1) * rows] = in_seq[c].astype(F32)
    put(f_seq, o_seq)
    for copy in stores:
        copy.wait()


def finish(tp_size, ff, gq, go, gkv, seq, vec, layer_out, grad_in):
    width = gq.shape[0]
    _, slots, rows = seq.shape
    square, flat = (width, width), (slots, tp_size * rows)
    vmem = pl.BlockSpec(memory_space=pltpu.VMEM)
    hbm = pl.BlockSpec(memory_space=pltpu.HBM)
    shape = jax.ShapeDtypeStruct
    return pl.pallas_call(
        functools.partial(finish_kernel, tp_size),
        out_shape=tuple([shape(square, F32)] * 6 + [shape(flat, F32)] + [shape(layer_out.shape, BF)] * 2 + [shape((width,), F32)] * 10),
        in_specs=[hbm] * 5 + [vmem] + [hbm] * 2,
        out_specs=tuple([hbm] * 9 + [vmem] * 10),
        scratch_shapes=[pltpu.VMEM(square, BF)] * 4
        + [pltpu.VMEM(gkv.shape, BF), pltpu.VMEM(seq.shape, BF)]
        + [pltpu.VMEM(square, F32)] * 6
        + [pltpu.VMEM(flat, F32), pltpu.VMEM(square, BF)]
        + [pltpu.VMEM(layer_out.shape, BF)] * 2
        + [pltpu.SemaphoreType.DMA((8,)), pltpu.SemaphoreType.DMA((9,))],
        compiler_params=pltpu.CompilerParams(vmem_limit_bytes=VMEM_LIMIT),
        name="finish",
    )(ff, gq, go, gkv, seq, vec, layer_out, grad_in)


def on_device(
    mesh,
    layer_in,
    out_grad,
    lengths,
    w_query,
    b_query,
    w_key,
    b_key,
    w_value,
    b_value,
    w_out,
    b_out,
    seq_proj,
    attn_gain,
    attn_shift,
    w_up,
    b_up,
    w_down,
    b_down,
    ffn_gain,
    ffn_shift,
):
    row_count, width = layer_in.shape
    tp_size = mesh.shape["tp"]
    vectors = (b_query, b_key, b_value, b_out, attn_gain, attn_shift, b_down, ffn_gain, ffn_shift)
    vec, bup_all, xhat, rstd, mixed, queries, probs, kb, vb, folded, ssum, own_proj, ups, downs = front(
        mesh, lengths, layer_in, w_query, seq_proj, w_key, w_value, w_out, w_up, w_down, vectors, b_up
    )
    layer_out, d_normed, part_vec, ff_landed, ff_near, ff_far, ff_own = middle(
        mesh, vec, bup_all, xhat, out_grad, w_up, w_down, ups, downs
    )
    grad_in, g_ff, g_o, g_q, g_kv, g_seq, vec_sum = back(
        mesh, lengths, vec, part_vec, ff_near, d_normed, probs, ff_far, ff_own, xhat, rstd, mixed, w_out, ff_landed,
        layer_in, queries, kb, vb, folded, ssum, own_proj, w_query, w_key, w_value
    )
    (
        g_w_up, g_w_down, g_w_query, g_w_out, g_w_key, g_w_value, g_seq_proj, layer_out, grad_in,
        g_b_query, g_b_key, g_b_value, g_b_out, g_attn_gain, g_attn_shift, g_ffn_gain, g_ffn_shift, g_b_down, g_b_up,
    ) = finish(tp_size, g_ff, g_q, g_o, g_kv, g_seq, vec_sum, layer_out, grad_in)
    return (
        layer_out,
        grad_in,
        g_w_query,
        g_b_query,
        g_w_key,
        g_b_key,
        g_w_value,
        g_b_value,
        g_w_out,
        g_b_out,
        g_seq_proj,
        g_attn_gain,
        g_attn_shift,
        g_w_up,
        g_b_up,
        g_w_down,
        g_b_down,
        g_ffn_gain,
        g_ffn_shift,
    )


def solution(mesh):
    in_specs = (
        P(("dp", "tp"), None),
        P(("dp", "tp"), None),
        P("dp"),
        *([P()] * 11),
        P(None, "tp"),
        P("tp"),
        P("tp", None),
        P(),
        P(),
        P(),
    )
    out_specs = (
        P(("dp", "tp"), None),
        P(("dp", "tp"), None),
        *([P()] * 11),
        P(None, "tp"),
        P("tp"),
        P("tp", None),
        P(),
        P(),
        P(),
    )
    return jax.shard_map(
        functools.partial(on_device, mesh), mesh=mesh, in_specs=in_specs, out_specs=out_specs, check_vma=False
    )
```

```python
import functools

import jax
import jax.numpy as jnp
from jax import lax
from jax.experimental import pallas as pl
from jax.experimental.pallas import tpu as pltpu
from jax.sharding import PartitionSpec as P

HEADS = 12
HEAD = 64
PAIRS = HEADS // 2
PAIR = 2 * HEAD
BF = jnp.bfloat16
F32 = jnp.float32
MESH = pl.DeviceIdType.MESH
VMEM_LIMIT = 67_043_328
BLOCK_F, BLOCK_M, BLOCK_B, GRAD_SPLIT = 1024, 512, 1024, 2


def dot(left, right, left_dim, right_dim):
    return lax.dot_general(
        left, right, (((left_dim,), (right_dim,)), ((), ())), preferred_element_type=F32
    )


def place(index, size):
    return pl.ds(pl.multiple_of(index * size, size), size)


def rows_at(first, size, multiple):
    return pl.ds(pl.multiple_of(first, multiple), size)


class Link:
    def __init__(self, dp_size, tp_size, send_sems, recv_sems):
        self.dp_size, self.tp_size = dp_size, tp_size
        self.dp, self.tp = lax.axis_index("dp"), lax.axis_index("tp")
        self.bits = dp_size.bit_length() - 1
        self.low = min(3, self.bits)
        self.send_sems, self.recv_sems = send_sems, recv_sems
        self.used = 0
        self.bit_values = [lax.rem(lax.div(self.dp, 1 << b), 2) for b in range(self.bits)]
        self.partners = [
            (self.dp + (1 - 2 * self.bit_values[b]) * (1 << b), self.tp) for b in range(self.bits)
        ]
        self.aheads = [lax.rem(self.tp + k, tp_size) for k in range(tp_size)]

    def bit(self, b):
        return self.bit_values[b]

    def partner(self, b):
        return self.partners[b]

    def ahead(self, k):
        return self.aheads[k]

    def behind(self, k):
        if isinstance(k, int):
            return self.aheads[(self.tp_size - k) % self.tp_size]
        return lax.rem(self.tp + self.tp_size - k, self.tp_size)

    def greet(self, dp_bits):
        barrier = pltpu.get_barrier_semaphore()
        peers = [(self.dp, self.ahead(k)) for k in range(1, self.tp_size)]
        peers += [self.partner(b) for b in range(dp_bits)]
        for peer in peers:
            pl.semaphore_signal(barrier, inc=1, device_id=peer, device_id_type=MESH)
        pl.semaphore_wait(barrier, len(peers))

    def take(self, count):
        first = self.used
        self.used += count
        assert self.used <= self.send_sems.shape[0]
        return first

    def remote(self, slot, source, target, device):
        return pltpu.make_async_remote_copy(
            src_ref=source,
            dst_ref=target,
            send_sem=self.send_sems.at[slot],
            recv_sem=self.recv_sems.at[slot],
            device_id=device,
            device_id_type=MESH,
        )

    def send(self, source, target, device):
        copy = self.remote(self.take(1), source, target, device)
        copy.start()
        return copy


FRONT_SEMS = 64
VECTORS = 16


def half_orders(low):
    return [[b for b in order if b < low] for order in ((1, 2, 0), (2, 1, 0))]


class WeightCollect:
    def __init__(self, link, part, whole):
        self.link, self.whole, self.part = link, whole, part
        self.orders = half_orders(link.low)
        self.piece = self.part >> link.low
        self.stages = link.low
        self.slot = link.take(2 * (link.tp_size - 1) * link.low)
        self.firsts = []
        for h in range(2):
            first, size, starts = h * part, self.piece, []
            for b in self.orders[h]:
                starts.append(size * link.bit(b))
                size *= 2
            self.firsts.append([sum(starts[i:], first) for i in range(self.stages)])

    def rows(self, h, i):
        return rows_at(self.firsts[h][i], self.piece << i, 16)

    def copies(self, k, i):
        for h in range(2):
            region = self.whole(k).at[self.rows(h, i), :]
            slot = self.slot + ((k - 1) * self.stages + i) * 2 + h
            yield self.link.remote(slot, region, region, self.link.partner(self.orders[h][i]))

    def step(self, k, j):
        if j > 0:
            for copy in self.copies(k, j - 1):
                copy.wait()
        if j < self.stages:
            for copy in self.copies(k, j):
                copy.start()


class Cross:
    def __init__(self, link, collect, shard, target):
        self.link, self.collect, self.shard, self.target = link, collect, shard, target
        self.slot = link.take(2 * (link.tp_size - 1))

    def copies(self, k):
        for h in range(2):
            rows = self.collect.rows(h, 0)
            yield self.link.remote(
                self.slot + 2 * (k - 1) + h,
                self.shard.at[rows, :],
                self.target(k, h, rows),
                (self.link.dp, self.link.ahead(k)),
            )

    def start(self, k):
        for copy in self.copies(k):
            copy.start()

    def wait(self, k):
        for copy in self.copies(k):
            copy.wait()


EARLY_TICKS = ((0, 1, 0), (1, 1, 0), (0, 1, 1), (1, 3, 0), (1, 1, 1), (0, 1, 2), (1, 3, 1), (1, 1, 2))
SHARE_TICKS = ((0, 1, 3), (1, 3, 2), (1, 1, 3), (1, 3, 3))
PAIR_TICKS = {1: ((0, 3, 0),), 3: ((0, 3, 1),), 5: ((0, 3, 2), (0, 2, 0))}
LAST_TICKS = ((0, 3, 3), (0, 2, -2), (1, 2, -1))


def front_kernel(dp_size, tp_size, n_vectors, len_ref, x_hbm, wq_hbm, e, wk_hbm, wv_hbm, wo_hbm, wup, wdn, *rest):
    vectors, b_up, rest = rest[:n_vectors], rest[n_vectors], rest[n_vectors + 1 :]
    outs, scratch = rest[:14], rest[14:]
    (vec, bup_all, xhat_out, rstd_out, mixed_out, q_out, probs_out, kb_out, vb_out, yb_out, ssum_out, em_out, ups, downs) = outs
    (x, wq, wk, wv, wo, e_all, xhat, rstd, mixed, q, probs, kb, vb, yb, ssum, em, bup, ysend, yrecv, send_sems, recv_sems, local_sems) = scratch
    link = Link(dp_size, tp_size, send_sems, recv_sems)
    rows, width = x.shape
    slots, total = e_all.shape
    quarter = slots // tp_size
    others = range(1, tp_size)
    used = [0]

    def local(source, target):
        copy = pltpu.make_async_copy(source, target, local_sems.at[used[0]])
        used[0] += 1
        copy.start()
        return copy

    own_first = link.tp * rows
    e_own = local(e.at[:, rows_at(own_first, rows, rows)], em)
    early = [local(x_hbm, x), local(wq_hbm, wq)]
    late = [local(e, e_all), local(wk_hbm, wk), local(wv_hbm, wv), local(wo_hbm, wo)]
    link.greet(link.low)

    collect = WeightCollect(link, wup.shape[0] // 2, lambda k: ups.at[k - 1])
    cross = Cross(link, collect, wup, lambda k, h, rows: ups.at[k - 1, rows, :])
    cross_down = Cross(link, collect, wdn, lambda k, h, rows: downs.at[k - 1, rows, :])
    collect_down = WeightCollect(link, wdn.shape[0] // 2, lambda k: downs.at[k - 1])
    def tick(ticks):
        for m, k, j in ticks:
            if -1 <= j <= 0:
                (cross, cross_down)[m].wait(k)
            if j == -2:
                for copy in (collect, collect_down)[m].copies(k, 0):
                    copy.wait()
            elif j >= 0:
                (collect, collect_down)[m].step(k, j)

    cross.start(1)
    cross_down.start(1)
    cross_down.start(3)
    vec[...] = jnp.zeros_like(vec)
    for n, vector in enumerate(vectors):
        vec[n : n + 1, :] = vector[...].astype(F32).reshape(1, width)
    bup[...] = jnp.broadcast_to(b_up[...].astype(F32).reshape(1, width), bup.shape)
    bup_all[link.tp] = bup[...]
    length = len_ref[0]
    position = lax.broadcasted_iota(jnp.int32, (1, rows), 1) + own_first
    live = (position < length).astype(F32)
    e_own.wait()
    early[0].wait()
    em[...] = (em[...].astype(F32) * live).astype(BF)
    ysend[...] = dot(em[...], x[...], 1, 0).astype(ysend.dtype)
    reduce = [
        link.send(ysend.at[place(link.ahead(k), quarter), :], yrecv.at[k - 1], (link.dp, link.ahead(k)))
        for k in others
    ]
    biases = [link.send(bup, bup_all.at[link.tp], (link.dp, link.ahead(k))) for k in others]
    early[1].wait()
    q[...] = (dot(x[...], wq[...], 1, 0) + vec[0:1, :]).astype(BF)
    tick(EARLY_TICKS)
    own_slots = place(link.tp, quarter)
    for copy in reduce:
        copy.wait()
    own_y = ysend[own_slots, :].astype(F32)
    for k in others:
        own_y = own_y + yrecv[k - 1].astype(F32)
    yb[own_slots, :] = own_y.astype(BF)
    share = [
        link.send(yb.at[own_slots, :], yb.at[own_slots, :], (link.dp, link.ahead(k))) for k in others
    ]
    for k in (3, 2):
        cross.start(k)
    cross_down.start(2)
    tick(SHARE_TICKS)
    stores = [local(q, q_out), local(em, em_out)]
    row_live = (lax.broadcasted_iota(jnp.int32, (total, 128), 0) < length).astype(F32).astype(BF)
    for load in late:
        load.wait()
    ssum[...] = dot(e_all[...], row_live, 1, 0)
    for copy in share:
        copy.wait()
    for copy in biases:
        copy.wait()
    stores += [local(yb, yb_out), local(ssum, ssum_out)]

    lane = lax.broadcasted_iota(jnp.int32, (1, PAIR), 1)
    first_half = (lane < HEAD).astype(F32)

    def project(weight, bias_row, blocks):
        full = dot(yb[...], weight[...], 1, 0)
        for p in range(PAIRS):
            cols = slice(p * PAIR, (p + 1) * PAIR)
            both = full[:, cols] + ssum[...] * vec[bias_row : bias_row + 1, cols]
            blocks[p, 0:slots, :] = (both * first_half).astype(BF)
            blocks[p, slots : 2 * slots, :] = (both * (1.0 - first_half)).astype(BF)

    project(wk, 1, kb)
    project(wv, 2, vb)
    stores += [local(kb, kb_out), local(vb, vb_out)]

    block = min(BLOCK_F, rows)
    per_pair = rows // block
    probs_sem = used[0]

    def attend(p, carry):
        cols = place(p, PAIR)

        def one(step, carry):
            here = place(step, block)
            logits = dot(q[here, cols], kb[p], 1, 1) * 0.125
            halves = []
            for half in range(2):
                part = logits[:, half * slots : (half + 1) * slots]
                peak = jnp.max(part, axis=-1, keepdims=True)
                raised = jnp.exp(part - peak)
                halves.append((raised * (1.0 / jnp.sum(raised, axis=-1, keepdims=True))).astype(BF))
            both = jnp.concatenate(halves, axis=1)
            probs[p, here, :] = both
            mixed[here, cols] = dot(both, vb[p], 1, 0).astype(BF)
            return carry

        lax.fori_loop(0, per_pair, one, 0)
        pltpu.make_async_copy(probs.at[p], probs_out.at[p], local_sems.at[probs_sem + p]).start()
        for n, ticks in PAIR_TICKS.items():

            @pl.when(p == n)
            def _():
                tick(ticks)

        return carry

    lax.fori_loop(0, PAIRS, attend, 0)
    used[0] += PAIRS
    stores.append(local(mixed, mixed_out))

    def finish(step, carry):
        here = place(step, block)
        res = x[here, :].astype(F32) + dot(mixed[here, :], wo[...], 1, 0) + vec[3:4, :]
        center = res - jnp.mean(res, axis=-1, keepdims=True)
        inverse = lax.rsqrt(jnp.mean(center * center, axis=-1, keepdims=True) + 1e-05)
        xhat[here, :] = center * inverse
        rstd[here, :] = jnp.broadcast_to(inverse, (block, 128))
        return carry

    lax.fori_loop(0, per_pair, finish, 0)
    stores += [local(xhat, xhat_out), local(rstd, rstd_out)]
    tick(LAST_TICKS)
    for copy in stores:
        copy.wait()
    for p in range(PAIRS):
        pltpu.make_async_copy(probs.at[p], probs_out.at[p], local_sems.at[probs_sem + p]).wait()


def front(mesh, lengths, x, wq, e, wk, wv, wo, wup, wdn, vectors, b_up):
    dp_size, tp_size = mesh.shape["dp"], mesh.shape["tp"]
    low = min(3, dp_size.bit_length() - 1)
    rows, width = x.shape
    slots = e.shape[0]
    vmem = pl.BlockSpec(memory_space=pltpu.VMEM)
    hbm = pl.BlockSpec(memory_space=pltpu.HBM)
    shape = jax.ShapeDtypeStruct
    moved = (
        ((rows, width), F32),
        ((rows, 128), F32),
        ((rows, width), BF),
        ((rows, width), BF),
        ((PAIRS, rows, 2 * slots), BF),
        ((PAIRS, 2 * slots, PAIR), BF),
        ((PAIRS, 2 * slots, PAIR), BF),
        ((slots, width), BF),
        ((slots, 128), F32),
        ((slots, rows), BF),
    )
    kept = (
        ((VECTORS, width), F32),
        ((tp_size, 8, width), F32),
    )
    return pl.pallas_call(
        functools.partial(front_kernel, dp_size, tp_size, len(vectors)),
        out_shape=tuple(shape(*s) for s in kept + moved)
        + (
            shape((tp_size - 1, *wup.shape), BF),
            shape((tp_size - 1, *wdn.shape), BF),
        ),
        in_specs=[pl.BlockSpec(memory_space=pltpu.SMEM)]
        + [hbm] * 8
        + [vmem] * (len(vectors) + 1),
        out_specs=tuple([vmem] * len(kept) + [hbm] * (len(moved) + 2)),
        scratch_shapes=[pltpu.VMEM(w.shape, BF) for w in (x, wq, wk, wv, wo, e)]
        + [pltpu.VMEM(*s) for s in moved]
        + [
            pltpu.VMEM((8, width), F32),
            pltpu.VMEM((slots, width), BF),
            pltpu.VMEM((tp_size - 1, slots // tp_size, width), BF),
            pltpu.SemaphoreType.DMA((FRONT_SEMS,)),
            pltpu.SemaphoreType.DMA((FRONT_SEMS,)),
            pltpu.SemaphoreType.DMA((32,)),
        ],
        compiler_params=pltpu.CompilerParams(
            collective_id=0, has_side_effects=True, vmem_limit_bytes=VMEM_LIMIT
        ),
        name="front",
    )(lengths, x, wq, e, wk, wv, wo, wup, wdn, *vectors, b_up)


BACK_SEMS = 128
VECTORS = 16


def add_rows(target, first, left, left_first, right, count):
    block = 96 if count % 96 == 0 else (48 if count % 48 == 0 else (32 if count % 32 == 0 else count))

    def step(i, carry):
        at = i * block
        total = (
            left[rows_at(left_first + at, block, 16), :].astype(F32)
            + right[rows_at(at, block, 16), :].astype(F32)
        )
        target[rows_at(first + at, block, 16), :] = total.astype(target.dtype)
        return carry

    lax.fori_loop(0, count // block, step, 0)


class Spread:
    def __init__(self, link, order, rows, source, acc, landing):
        self.link, self.rows, self.source, self.acc, self.landing = link, rows, source, acc, landing
        self.order = [b for b in order if b < link.low]
        self.stages = len(self.order)
        self.slot = link.take(self.stages)
        self.piece = rows >> self.stages
        self.insides, self.others, first = [0], [(1 - link.bit(self.order[0])) * (rows >> 1)], 0
        for j in range(1, self.stages):
            size = rows >> (j + 1)
            self.others.append(first + (1 - link.bit(self.order[j])) * size)
            first = first + link.bit(self.order[j]) * size
            self.insides.append(first)
        self.at = link.bit(self.order[0]) * (rows >> 1) + first

    def inside(self, i):
        return self.insides[i]

    def kept(self):
        return rows_at(self.inside(self.stages - 1), self.piece, 16)

    def offset(self):
        return self.at

    def landed(self, i):
        first = sum(self.rows >> (j + 1) for j in range(i))
        return self.landing.at[pl.ds(first, self.rows >> (i + 1)), :]

    def copy(self, i):
        link, size = self.link, self.rows >> (i + 1)
        where, other = self.source if i == 0 else self.acc, self.others[i]
        return link.remote(
            self.slot + i, where.at[rows_at(other, size, 16), :], self.landed(i), link.partner(self.order[i])
        )

    def start(self, i):
        self.copy(i).start()

    def finish(self, i):
        size = self.rows >> (i + 1)
        self.copy(i).wait()
        if i == 0:
            add_rows(self.acc, 0, self.source, self.link.bit(self.order[0]) * size, self.landed(0), size)
        else:
            at = self.inside(i)
            add_rows(self.acc, at, self.acc, at, self.landed(i), size)

    def steps(self):
        yield lambda: self.start(0)
        for i in range(1, self.stages):

            def step(i=i):
                self.finish(i - 1)
                self.start(i)

            yield step


class Collect:
    def __init__(self, link, order, offset, piece, region):
        self.link, self.offset, self.piece, self.region = link, offset, piece, region
        self.order = [b for b in order if b < link.low][::-1]
        self.slot = link.take(len(self.order))
        starts, size = [], piece
        for b in self.order:
            starts.append(link.bit(b) * size)
            size *= 2
        self.firsts = [sum(starts[i:], 0) for i in range(len(self.order))]

    def copy(self, i):
        size, first = self.piece << i, self.firsts[i]
        ref = self.region(first, size)
        return self.link.remote(self.slot + i, ref, ref, self.link.partner(self.order[i]))

    def steps(self):
        yield lambda: self.copy(0).start()
        for i in range(1, len(self.order)):

            def step(i=i):
                self.copy(i - 1).wait()
                self.copy(i).start()

            yield step
        yield lambda: self.copy(len(self.order) - 1).wait()


class Widen:
    def __init__(self, link, landing):
        self.link, self.landing = link, landing
        self.slot = link.take(max(0, link.bits - link.low))

    def run(self, piece):
        link = self.link
        for i, b in enumerate(range(link.low, link.bits)):
            copy = link.remote(self.slot + i, piece, self.landing.at[i], link.partner(b))
            copy.start()
            copy.wait()
            piece[...] = (piece[...].astype(F32) + self.landing[i].astype(F32)).astype(piece.dtype)


class Fan:
    def __init__(self, link, ends):
        self.link, self.ends = link, ends
        self.slot = link.take(link.tp_size - 1)

    def copy(self, k):
        source, target = self.ends(k)
        return self.link.remote(self.slot + k - 1, source, target, (self.link.dp, self.link.ahead(k)))

    def start(self):
        for k in range(1, self.link.tp_size):
            self.copy(k).start()

    def wait(self):
        for k in range(1, self.link.tp_size):
            self.copy(k).wait()


def then(*actions):
    def both():
        for action in actions:
            action()

    return both


class Track:
    def __init__(self):
        self.todo = []

    def add(self, steps, join=False):
        steps = list(steps)
        if join and self.todo:
            steps[0] = then(self.todo.pop(), steps[0])
        self.todo += steps

    def advance(self):
        if self.todo:
            self.todo.pop(0)()


def back_kernel(
    dp_size,
    tp_size,
    len_ref,
    vec,
    part_vec,
    ff_near,
    dnorm,
    probs,
    far_hbm,
    own_hbm,
    xhat_hbm,
    rstd_hbm,
    mixed_hbm,
    wo_hbm,
    landed_hbm,
    x_hbm,
    q_hbm,
    kb_hbm,
    vb_hbm,
    yb_hbm,
    ssum_hbm,
    em_hbm,
    wq_hbm,
    wk_hbm,
    wv_hbm,
    grad_hbm,
    ff_hbm,
    go_hbm,
    gq_out,
    gkv_out,
    seq_out,
    vec_out,
    grad_in,
    ff_out,
    go_out,
    ff_far,
    ff_own,
    xhat,
    rstd,
    mixed,
    wo,
    ff_landed,
    x,
    q,
    kb,
    vb,
    yb,
    ssum,
    em,
    wq,
    wk,
    wv,
    dres,
    dmix,
    dq,
    dl,
    prob_slots,
    dpart,
    dland,
    dcross,
    dfull,
    ff_zland,
    far_acc,
    far_land,
    own_acc,
    own_land,
    o_acc,
    o_land,
    q_acc,
    q_land,
    o_zland,
    q_zland,
    kv_send,
    kv_acc,
    kv_land,
    s_send,
    s_acc,
    s_land,
    vec_acc,
    vec_land,
    vec_z,
    wide_ff,
    wide_q,
    wide_kv,
    wide_s,
    send_sems,
    recv_sems,
    local_sems,
):
    link = Link(dp_size, tp_size, send_sems, recv_sems)
    rows, width = x.shape
    slots = yb.shape[0]
    low = link.low
    others = range(1, tp_size)
    first_load = pltpu.make_async_copy(dnorm, dres, local_sems.at[0])
    first_load.start()
    late = []
    for n, (source, target) in enumerate(
        (
            (far_hbm, ff_far), (own_hbm, ff_own), (xhat_hbm, xhat), (rstd_hbm, rstd), (mixed_hbm, mixed),
            (wo_hbm, wo), (landed_hbm, ff_landed), (q_hbm, q), (kb_hbm, kb), (vb_hbm, vb), (x_hbm, x), (yb_hbm, yb),
            (wq_hbm, wq), (wk_hbm, wk), (wv_hbm, wv), (ssum_hbm, ssum), (em_hbm, em),
        )
    ):
        late.append(pltpu.make_async_copy(source, target, local_sems.at[3 + n]))
        late[-1].start()
    link.greet(link.bits)

    lanes = 2
    deep = tp_size // lanes
    third = width // GRAD_SPLIT
    owned = width // tp_size

    ff_track, ff_orders = Track(), ((0, 1, 2), (0, 2, 1))
    ff_rows = width >> 3
    ff_parts = []
    for m in range(2):
        first, second, third_bit = ff_orders[m]
        far = Spread(link, (third_bit,), width >> 2, ff_far.at[m], far_acc.at[m], far_land.at[m])
        own = Spread(link, (second, third_bit), width >> 1, ff_own.at[m], own_acc.at[m], own_land.at[m])
        slot = link.take(2)

        def piece_copy(n, m=m, slot=slot):
            source, k = ((far_acc, 3), (ff_near, 2))[n]
            return link.remote(slot + n, source.at[m], ff_zland.at[m, n], (link.dp, link.behind(k)))

        at = link.bit(ff_orders[m][0]) * (width >> 1) + own.offset()

        def offset(at=at):
            return at

        widen = Widen(link, wide_ff.at[m])

        def join(m=m, own=own, piece_copy=piece_copy, offset=offset, widen=widen):
            total = own_acc[m, own.kept(), :].astype(F32) + ff_landed[m].astype(F32)
            for n in range(2):
                piece_copy(n).wait()
                total = total + ff_zland[m, n].astype(F32)
            mine = rows_at(offset(), ff_rows, 16)
            ff_out[m, mine, :] = total.astype(BF)
            widen.run(ff_out.at[m, mine, :])

        collect = Collect(
            link, ff_orders[m], offset, ff_rows,
            lambda first, size, m=m: ff_out.at[m, rows_at(first, size, 16), :],
        )
        ff_parts.append((far, own, piece_copy, join, list(collect.steps())))

    def ff_begin():
        for far, own, piece_copy, _, _ in ff_parts:
            far.start(0)
            own.start(0)
            piece_copy(1).start()

    def ff_second():
        for far, own, piece_copy, _, _ in ff_parts:
            far.finish(0)
            piece_copy(0).start()

    def ff_second_own():
        for far, own, piece_copy, _, _ in ff_parts:
            own.finish(0)
            own.start(1)

    def ff_third():
        for _, own, _, join, collects in ff_parts:
            own.finish(1)

    def ff_join():
        for _, _, _, join, collects in ff_parts:
            join()
            collects[0]()

    stores = []

    def store(n, source, target):
        copy = pltpu.make_async_copy(source, target, local_sems.at[20 + n])
        stores.append(copy)
        return copy

    ff_store, go_store, grad_store = store(0, ff_out, ff_hbm), store(1, go_out, go_hbm), store(2, grad_in, grad_hbm)
    late[0].wait()
    late[1].wait()
    ff_begin()
    ff_track.add([ff_second, ff_second_own, then(ff_third, ff_join)])
    ff_track.add([then(*pair) for pair in zip(ff_parts[0][4][1:], ff_parts[1][4][1:])])
    ff_track.add([ff_store.start], join=True)

    def square_track(out, acc, landing, zland, wide):
        track, spreads, collects = Track(), [], []
        q_cols = width // lanes
        for h, order in enumerate(((0, 1, 2), (0, 2, 1))):
            cols = slice(h * q_cols, (h + 1) * q_cols)
            spread = Spread(link, order, width, out.at[:, cols], acc.at[:, cols], landing.at[:, cols])
            spreads.append(spread)
            collects.append(
                Collect(
                    link, order, spread.offset, spread.piece,
                    lambda first, size, cols=cols: out.at[rows_at(first, size, 16), cols],
                )
            )
        q_rows = spreads[0].piece // deep
        halves = [lax.rem(t, lanes) for t in link.aheads]

        def quarter(firsts, k):
            first = firsts[0] + halves[k] * (firsts[1] - firsts[0]) + lax.div(link.aheads[k], lanes) * q_rows
            return rows_at(first, q_rows, 16), pl.ds(pl.multiple_of(halves[k] * q_cols, 128), q_cols)

        inner = [quarter([spread.inside(spread.stages - 1) for spread in spreads], k) for k in range(tp_size)]
        mine = quarter([spread.offset() for spread in spreads], 0)
        fan = Fan(link, lambda k: (acc.at[inner[k]], zland.at[k - 1]))
        share, widen = Fan(link, lambda k: (out.at[mine], out.at[mine])), Widen(link, wide)

        def join():
            fan.wait()
            total = acc[inner[0]].astype(F32)
            for k in others:
                total = total + zland[k - 1].astype(F32)
            out[mine] = total.astype(BF)
            widen.run(out.at[mine])
            share.start()

        def summed():
            for spread in spreads:
                spread.finish(spread.stages - 1)
            fan.start()

        track.add([then(*pair) for pair in zip(spreads[0].steps(), spreads[1].steps())])
        track.add([summed, join, share.wait])
        track.add([then(*pair) for pair in zip(collects[0].steps(), collects[1].steps())], join=True)
        return track

    def owned_track(order, total_rows, cols, source, acc, landing, out, wide):
        source, acc, landing = source.at[:, cols], acc.at[:, cols], landing.at[:, cols]
        track, spread = Track(), Spread(link, order, total_rows, source, acc, landing)

        def region(k):
            ref = out.at[link.tp, rows_at(spread.offset(), spread.piece, 16), cols]
            return ref, ref

        share, widen = Fan(link, region), Widen(link, wide)

        def last():
            spread.finish(spread.stages - 1)
            ref = region(0)[0]
            ref[...] = acc[spread.kept(), :]
            widen.run(ref)
            share.start()

        collect = Collect(
            link, order, spread.offset, spread.piece, lambda first, size: out.at[:, rows_at(first, size, 16), cols]
        )
        track.add(spread.steps())
        track.add([last, share.wait])
        track.add(collect.steps(), join=True)
        return track

    o_track = square_track(go_out, o_acc, o_land, o_zland, wide_q.at[0])
    o_track.add([go_store.start], join=True)
    q_track = square_track(gq_out, q_acc, q_land, q_zland, wide_q.at[1])
    def halves(total_rows, source, acc, landing, out, wide):
        tracks = []
        for h, order in enumerate(((0, 1, 2), (0, 2, 1))):
            cols = slice(h * source.shape[1] // 2, (h + 1) * source.shape[1] // 2)
            tracks.append(owned_track(order, total_rows, cols, source, acc, landing, out, wide.at[h]))
        both = Track()
        both.add([then(*pair) for pair in zip(tracks[0].todo, tracks[1].todo)])
        return both

    kv_track = halves(2 * owned, kv_send, kv_acc, kv_land, gkv_out, wide_kv)
    s_track = halves(slots, s_send, s_acc, s_land, seq_out, wide_s)

    vec_track, vec_slot = Track(), link.take(link.bits)
    vec_fan = Fan(link, lambda k: (vec_z.at[link.tp], vec_z.at[link.tp]))

    def vec_copy(b):
        return link.remote(vec_slot + b, vec_acc.at[b], vec_land.at[b], link.partner(b))

    vec_track.add([lambda: vec_copy(0).start()])
    for b in range(link.bits):

        def vec_step(b=b):
            vec_copy(b).wait()
            total = vec_acc[b] + vec_land[b]
            if b + 1 < link.bits:
                vec_acc[b + 1] = total
                vec_copy(b + 1).start()
            else:
                vec_z[link.tp] = total
                vec_fan.start()

        vec_track.add([vec_step])

    def vec_last():
        vec_fan.wait()
        total = vec_z[0]
        for t in range(1, tp_size):
            total = total + vec_z[t]
        vec_out[...] = total

    vec_track.add([vec_last])

    block = min(BLOCK_B, rows)
    count = rows // block
    gain = vec[4:5, :]

    def norm_back(step, carry):
        g_gain, g_shift, g_out = carry
        here = place(step, block)
        grad, hat = dres[here, :], xhat[here, :]
        g_gain = g_gain + jnp.sum(grad * hat, axis=0, keepdims=True)
        g_shift = g_shift + jnp.sum(grad, axis=0, keepdims=True)
        scaled = grad * gain
        d_res = rstd[here, 0:1] * (
            scaled
            - jnp.mean(scaled, axis=-1, keepdims=True)
            - hat * jnp.mean(scaled * hat, axis=-1, keepdims=True)
        )
        dres[here, :] = d_res
        d_attn = d_res.astype(BF)
        dq[here, :] = d_attn
        g_out = g_out + jnp.sum(d_attn.astype(F32), axis=0, keepdims=True)
        return g_gain, g_shift, g_out

    zero = jnp.zeros((1, width), F32)
    first_load.wait()
    late[2].wait()
    late[3].wait()
    g_gain, g_shift, g_out = lax.fori_loop(0, count, norm_back, (zero, zero, zero))
    vec_acc[0] = part_vec[...]
    vec_acc[0, 3:4, :] = g_out
    vec_acc[0, 4:5, :] = g_gain
    vec_acc[0, 5:6, :] = g_shift
    d_attn = dq

    def weight_grad(left, right, target):
        for m in range(GRAD_SPLIT):
            cols = slice(m * third, (m + 1) * third)
            target[cols, :] = dot(left[:, cols], right[...], 0, 0).astype(BF)

    for load in late[4:7]:
        load.wait()
    weight_grad(mixed, d_attn, go_out)
    o_track.advance()
    ff_track.advance()
    dmix[...] = dot(d_attn[...], wo[...], 1, 1).astype(BF)
    o_track.advance()
    for load in late[7:]:
        load.wait()

    own_half = lax.div(link.tp, 2)
    parity = lax.rem(link.tp, 2)
    three = PAIRS // 2

    def pair_at(n):
        second = lax.div(n, three)
        which = (1 - own_half) * (1 - second) + own_half * second
        along = lax.rem(n, three)
        return which * three + along * parity + (three - 1 - along) * (1 - parity)

    def fetch(n):
        slot = lax.rem(n, 2)
        return pltpu.make_async_copy(probs.at[pair_at(n)], prob_slots.at[slot], local_sems.at[1 + slot])

    fetch(0).start()

    def attend_back(n):
        p = pair_at(n)
        cols = place(p, PAIR)

        @pl.when(n + 1 < PAIRS)
        def _():
            fetch(n + 1).start()

        fetch(n).wait()
        held = prob_slots.at[lax.rem(n, 2)]

        def part(step, carry):
            here = place(step, block)
            d_probs = dot(dmix[here, cols], vb[p], 1, 1)
            weights = held[here, :].astype(F32)
            halves = []
            for h in range(2):
                w = weights[:, h * slots : (h + 1) * slots]
                d = d_probs[:, h * slots : (h + 1) * slots]
                halves.append((w * (d - jnp.sum(w * d, axis=-1, keepdims=True))).astype(BF))
            both = jnp.concatenate(halves, axis=1)
            dl[here, :] = both
            dq[here, cols] = (dot(both, kb[p], 1, 0) * 0.125).astype(BF)
            return carry

        lax.fori_loop(0, count, part, 0)
        top, under = rows_at(p * PAIR, HEAD, HEAD), rows_at(p * PAIR + HEAD, HEAD, HEAD)
        for n, total in enumerate(
            (dot(q[:, cols], dl[...], 0, 0) * 0.125, dot(dmix[:, cols], held[...], 0, 0))
        ):
            dpart[n, top, :] = total[:HEAD, :slots].astype(BF)
            dpart[n, under, :] = total[HEAD:, slots:].astype(BF)

    d_slot = link.take(tp_size - 1)
    sibling = 2 * own_half + (1 - parity)
    far_same = rows_at((2 * (1 - own_half) + parity) * owned, owned, 64)
    far_other = rows_at((2 * (1 - own_half) + (1 - parity)) * owned, owned, 64)
    d_peers = [2 * (1 - own_half) + parity, sibling, sibling]
    d_sources = [
        dcross, dpart.at[:, far_other, :], dpart.at[:, rows_at(sibling * owned, owned, 64), :],
    ]

    def d_copy(j):
        return link.remote(d_slot + j, d_sources[j], dland.at[j], (link.dp, d_peers[j]))

    def d_across():
        d_copy(1).wait()
        for n in range(2):
            dcross[n] = (dpart[n, far_same, :].astype(F32) + dland[1, n].astype(F32)).astype(BF)
        d_copy(0).start()

    events = {
        1: lambda: d_copy(1).start(),
        2: ff_track.advance,
        4: lambda: d_copy(2).start(),
        5: then(d_across, o_track.advance),
    }

    def one(n, carry):
        attend_back(n)
        for i, event in events.items():
            pl.when(n == i)(event)
        return carry

    lax.fori_loop(0, PAIRS, one, 0)

    weight_grad(x, dq, gq_out)
    q_track.advance()
    ff_track.advance()

    def input_grad(step, carry):
        here = place(step, block)
        dres[here, :] += dot(dq[here, :], wq[...], 1, 1)
        return carry

    lax.fori_loop(0, count, input_grad, 0)
    q_track.advance()
    vec_acc[0, 0:1, :] = jnp.sum(dq[...].astype(F32), axis=0, keepdims=True)
    o_track.advance()

    for j in (0, 2):
        d_copy(j).wait()
    own_block = rows_at(link.tp * owned, owned, 64)
    for n in range(2):
        total = dpart[n, own_block, :].astype(F32)
        for j in (0, 2):
            total = total + dland[j, n].astype(F32)
        dfull[n, own_block, :] = total.astype(BF)
    share_slot = link.take(3)
    share_plan = ((own_block, d_peers[0]), (own_block, sibling), (far_same, sibling))

    def share_copy(n):
        block_rows, peer = share_plan[n]
        return link.remote(
            share_slot + n, dfull.at[:, block_rows, :], dfull.at[:, block_rows, :], (link.dp, peer)
        )

    share_copy(0).start()
    share_copy(1).start()
    ff_track.advance()
    for n in range(2):
        kv_send[n * owned : (n + 1) * owned, :] = dot(dfull[n, own_block, :], yb[...], 1, 0).astype(BF)
    kv_track.advance()
    o_track.advance()
    q_track.advance()
    kv_track.advance()
    ff_track.advance()
    share_copy(0).wait()
    share_copy(2).start()
    kv_track.advance()
    q_track.advance()
    ff_track.advance()
    kv_track.advance()
    share_copy(1).wait()
    share_copy(2).wait()
    backs = dot(wk[...], dfull[0], 1, 0) + dot(wv[...], dfull[1], 1, 0)
    back = backs.T.astype(BF)
    small = vec[0:8, :].astype(BF)
    bias_row = dot(small, dfull[0], 1, 0)[1:2, :] + dot(small, dfull[1], 1, 0)[2:3, :]
    bias_column = jnp.broadcast_to(bias_row, (128, slots)).T[:, 0:1]
    position = lax.broadcasted_iota(jnp.int32, (1, rows), 1) + link.tp * rows
    live = (position < len_ref[0]).astype(F32)
    s_send[...] = ((dot(back, x[...], 1, 1) + bias_column) * live).astype(BF)
    s_track.advance()
    column = ssum[...].T[0:8, :]
    column_b = column.astype(BF)
    column_low = (column - column_b.astype(F32)).astype(BF)
    for n in range(2):
        total = dot(column_b, dfull[n], 1, 1) + dot(column_low, dfull[n], 1, 1)
        vec_acc[0, 1 + n : 2 + n, :] = total[0:1, :] * (1.0 / tp_size)
    vec_track.advance()
    s_track.advance()

    def input_grad_last(step, carry):
        here = place(step, block)
        grad_in[here, :] = (dres[here, :] + dot(em[:, here], back, 0, 0)).astype(BF)
        return carry

    lax.fori_loop(0, count, input_grad_last, 0)
    grad_store.start()
    tracks = {"s": s_track, "k": kv_track, "q": q_track, "o": o_track, "v": vec_track, "f": ff_track}
    for name in "oqskvosqkvoqskvqsokvsqs":
        tracks[name].advance()
    tracks = list(tracks.values())
    while any(track.todo for track in tracks):
        for track in tracks:
            track.advance()
    for copy in stores:
        copy.wait()


def back(mesh, lengths, vec, part_vec, ff_near, dnorm, probs, *late):
    dp_size, tp_size = mesh.shape["dp"], mesh.shape["tp"]
    bits = dp_size.bit_length() - 1
    low = min(3, bits)
    wide = max(1, bits - low)
    rows, width = dnorm.shape
    slots = late[11].shape[0]
    owned = width // tp_size
    others = tp_size - 1
    vmem = pl.BlockSpec(memory_space=pltpu.VMEM)
    hbm = pl.BlockSpec(memory_space=pltpu.HBM)
    shape = jax.ShapeDtypeStruct

    def landing(total):
        return sum(total >> (i + 1) for i in range(low))

    def buf(*dims, dtype=BF):
        return pltpu.VMEM(dims, dtype)

    ff_piece, kv_piece, s_piece = width >> low, 2 * owned >> low, slots >> low
    quarter = (ff_piece // (tp_size // 2), width // 2)
    return pl.pallas_call(
        functools.partial(back_kernel, dp_size, tp_size),
        out_shape=(
            shape((rows, width), BF),
            shape((2, width, width), BF),
            shape((width, width), BF),
            shape((width, width), BF),
            shape((tp_size, 2 * owned, width), BF),
            shape((tp_size, slots, rows), BF),
            shape((VECTORS, width), F32),
        ),
        in_specs=[pl.BlockSpec(memory_space=pltpu.SMEM)] + [vmem] * 2 + [hbm] * (3 + len(late)),
        out_specs=tuple([hbm] * 3 + [vmem] * 4),
        scratch_shapes=[buf(rows, width), buf(2, width, width), buf(width, width)]
        + [pltpu.VMEM(array.shape, array.dtype) for array in late]
        + [
            buf(rows, width, dtype=F32),
            buf(rows, width),
            buf(rows, width),
            buf(rows, 2 * slots),
            buf(2, rows, 2 * slots),
            buf(2, width, slots),
            buf(others, 2, owned, slots),
            buf(2, owned, slots),
            buf(2, width, slots),
            buf(2, 2, ff_piece, width),
            buf(2, width >> 3, width),
            buf(2, width >> 3, width),
            buf(2, width >> 2, width),
            buf(2, (width >> 2) + (width >> 3), width),
            buf(width // 2, width),
            buf(landing(width), width),
            buf(width // 2, width),
            buf(landing(width), width),
            buf(others, *quarter),
            buf(others, *quarter),
            buf(2 * owned, width),
            buf(owned, width),
            buf(landing(2 * owned), width),
            buf(slots, rows),
            buf(slots // 2, rows),
            buf(landing(slots), rows),
            buf(bits, VECTORS, width, dtype=F32),
            buf(bits, VECTORS, width, dtype=F32),
            buf(tp_size, VECTORS, width, dtype=F32),
            buf(2, wide, ff_piece, width),
            buf(2, wide, *quarter),
            buf(2, wide, kv_piece, width // 2),
            buf(2, wide, s_piece, rows // 2),
            pltpu.SemaphoreType.DMA((BACK_SEMS,)),
            pltpu.SemaphoreType.DMA((BACK_SEMS,)),
            pltpu.SemaphoreType.DMA((6 + len(late),)),
        ],
        compiler_params=pltpu.CompilerParams(
            collective_id=1, has_side_effects=True, vmem_limit_bytes=VMEM_LIMIT
        ),
        name="back",
    )(lengths, vec, part_vec, ff_near, dnorm, probs, *late)


class ChunkSpread:
    def __init__(self, link, rows, sent, acc, landing):
        self.link, self.rows, self.sent, self.acc, self.landing = link, rows, sent, acc, landing
        self.orders = [[b for b in order if b < link.low] for order in ((0, 1, 2), (0, 2, 1))]
        self.stages = link.low
        self.slot = link.take(2 * link.low * acc.shape[1])
        self.insides, self.others = [], []
        for order in self.orders:
            inside, other, first = [0], [(1 - link.bit(order[0])) * (rows >> 1)], 0
            for j in range(1, self.stages):
                size = rows >> (j + 1)
                other.append(first + (1 - link.bit(order[j])) * size)
                first = first + link.bit(order[j]) * size
                inside.append(first)
            self.insides.append(inside)
            self.others.append(other)

    def inside(self, m, i):
        return self.insides[m][i]

    def copy(self, c, m, i):
        link, size = self.link, self.rows >> (i + 1)
        bit = self.orders[m][i]
        if i == 0:
            source = self.sent.at[m, lax.rem(c, 2), rows_at(self.others[m][i], size, 16), :]
        else:
            source = self.acc.at[m, c, rows_at(self.others[m][i], size, 16), :]
        first = sum(self.rows >> (j + 1) for j in range(i))
        slot = self.slot + (i * 2 + m) * self.acc.shape[1] + c
        return link.remote(slot, source, self.landing.at[m, c, pl.ds(first, size), :], link.partner(bit))

    def start(self, c, m, i):
        self.copy(c, m, i).start()

    def finish(self, c, m, i):
        size = self.rows >> (i + 1)
        self.copy(c, m, i).wait()
        first = sum(self.rows >> (j + 1) for j in range(i))
        landed = self.landing.at[m, c, pl.ds(first, size), :]
        acc = self.acc.at[m, c]
        if i == 0:
            mine = self.link.bit(self.orders[m][0]) * size
            add_rows(acc, 0, self.sent.at[m, lax.rem(c, 2)], mine, landed, size)
        else:
            at = self.inside(m, i)
            add_rows(acc, at, acc, at, landed, size)


MIDDLE_SEMS = 96
MIDDLE_TICKS = {3: ((1, 1),), 5: ((0, 2), (0, 3)), 7: ((1, 2), (1, 3))}


def middle_kernel(
    dp_size,
    tp_size,
    vec,
    bup_all,
    xhat_hbm,
    out_grad_hbm,
    own_up,
    own_dn,
    ups,
    downs,
    layer_hbm,
    dnorm,
    part_vec,
    ff_landed,
    ff_near,
    ff_far,
    ff_own,
    whole,
    xhat,
    layer_out,
    out_grad,
    nb,
    act,
    slope,
    d_branch,
    d_acc,
    sent,
    acc,
    landing,
    send_sems,
    recv_sems,
    local_sems,
):
    link = Link(dp_size, tp_size, send_sems, recv_sems)
    rows, width = xhat.shape
    used = [0]

    def local(source, target):
        copy = pltpu.make_async_copy(source, target, local_sems.at[used[0]])
        used[0] += 1
        copy.start()
        return copy

    collect = WeightCollect(link, width // 2, lambda k: whole.at[1, k])
    xhat_load = local(xhat_hbm, xhat)
    up_last = WeightCollect(link, width // 2, lambda k: whole.at[0, k])
    placed = [
        local(ups.at[1, up_last.rows(h, 1), :], whole.at[0, 2, up_last.rows(h, 1), :]) for h in range(2)
    ]
    placed += [
        local(downs.at[1, collect.rows(h, 0), :], whole.at[1, 2, collect.rows(h, 0), :]) for h in range(2)
    ]
    owns = [local(own_up, whole.at[0, 0])]
    owns += [local(ups.at[k - 1], whole.at[0, k]) for k in (1, 3)]
    owns += [local(own_dn, whole.at[1, 0])] + [local(downs.at[k - 1], whole.at[1, k]) for k in (1, 3)]
    owns.append(local(out_grad_hbm, out_grad))
    link.greet(link.low)
    for copy in placed:
        copy.wait()
    collect.step(2, 0)
    for copy in up_last.copies(2, 1):
        copy.start()
    xhat_load.wait()
    gain, shift, b_down, f_gain, f_shift = (vec[n : n + 1, :] for n in (4, 5, 6, 7, 8))
    block = min(BLOCK_M, rows)
    count = rows // block
    big = rows // 2

    def norm(step, carry):
        here = place(step, block)
        nb[here, :] = (xhat[here, :] * gain + shift).astype(BF)
        return carry

    lax.fori_loop(0, count, norm, 0)
    for copy in owns[: tp_size - 1]:
        copy.wait()

    def forward(step, carry):
        n = lax.div(step, 2)
        k = n + lax.div(n, 2) * (7 - 2 * n - 2)
        here, cols = place(lax.rem(step, 2), big), place(k, width)
        pre = dot(nb[here, :], whole[0, k], 1, 0) + bup_all[link.behind(k), 0:1, :]
        cdf = 0.5 * (1.0 + lax.erf(pre * 0.7071067811865476))
        act[here, cols] = (pre * cdf).astype(BF)
        slope[here, cols] = (cdf + pre * (jnp.exp(pre * pre * -0.5) * 0.3989422804014327)).astype(BF)
        for n, ticks in MIDDLE_TICKS.items():

            @pl.when(step == n)
            def _():
                for m, j in ticks:
                    (up_last, collect)[m].step(2, j)

        return carry

    lax.fori_loop(0, 2 * tp_size, forward, 0)
    for copy in owns[tp_size - 1 :]:
        copy.wait()

    def second_norm(step, carry):
        g_gain, g_shift, g_down = carry
        here = place(step, block)
        branch = dot(act[here, 0:width], whole[1, 0], 1, 0)
        for k in range(1, tp_size):
            branch = branch + dot(act[here, k * width : (k + 1) * width], whole[1, k], 1, 0)
        res = xhat[here, :] * gain + shift + (branch + b_down)
        center = res - jnp.mean(res, axis=-1, keepdims=True)
        inverse = lax.rsqrt(jnp.mean(center * center, axis=-1, keepdims=True) + 1e-05)
        hat = center * inverse
        layer_out[here, :] = (hat * f_gain + f_shift).astype(BF)
        grad = out_grad[here, :].astype(F32)
        g_gain = g_gain + jnp.sum(grad * hat, axis=0, keepdims=True)
        g_shift = g_shift + jnp.sum(grad, axis=0, keepdims=True)
        scaled = grad * f_gain
        d_res = inverse * (
            scaled
            - jnp.mean(scaled, axis=-1, keepdims=True)
            - hat * jnp.mean(scaled * hat, axis=-1, keepdims=True)
        )
        d_acc[here, :] = d_res
        rounded = d_res.astype(BF)
        d_branch[here, :] = rounded
        g_down = g_down + jnp.sum(rounded.astype(F32), axis=0, keepdims=True)
        return g_gain, g_shift, g_down

    zero = jnp.zeros((1, width), F32)
    g_gain, g_shift, g_down = lax.fori_loop(0, count, second_norm, (zero, zero, zero))
    layer_store = local(layer_out, layer_hbm)
    part_vec[...] = jnp.zeros_like(part_vec)
    part_vec[6:7, :] = g_gain
    part_vec[7:8, :] = g_shift
    part_vec[8:9, :] = g_down

    spread = ChunkSpread(link, width, sent, acc, landing)
    third = width // GRAD_SPLIT

    def weight_grad(left, first, right, cols, target):
        for m in range(GRAD_SPLIT):
            mine = pl.ds(pl.multiple_of(first + m * third, third), third)
            target[m * third : (m + 1) * third, :] = dot(left[:, mine], right[:, cols], 0, 0).astype(BF)

    def settle(n, steps):
        for m, late, stage in steps:

            @pl.when(n >= late)
            def _():
                spread.finish(n - late, m, stage)

            if stage < 2:

                @pl.when(jnp.logical_and(n >= late, n - late < 3 - stage))
                def _():
                    spread.start(n - late, m, stage + 1)

    def backward(n, carry):
        k = lax.rem(n + 1, tp_size)
        cols = place(k, width)
        slot = lax.rem(n, 2)
        weight_grad(act, k * width, d_branch, slice(0, width), sent.at[1, slot])
        spread.start(n, 1, 0)
        settle(n, ((0, 1, 0), (1, 2, 1)))

        def through(step, total):
            here = place(step, big)
            grad = (dot(d_branch[here, :], whole[1, k], 1, 1) * slope[here, cols].astype(F32)).astype(BF)
            slope[here, cols] = grad
            return total + jnp.sum(grad.astype(F32), axis=0, keepdims=True)

        part_vec[pl.ds(9 + link.behind(k), 1), :] = lax.fori_loop(0, 2, through, zero)
        settle(n, ((1, 0, 0), (0, 2, 1)))
        weight_grad(nb, 0, slope, cols, sent.at[0, slot])
        spread.start(n, 0, 0)
        return carry

    lax.fori_loop(0, tp_size, backward, 0)

    def input_grad(step, carry):
        here = place(step, big)
        total = d_acc[here, :]
        for k in range(tp_size):
            total = total + dot(slope[here, k * width : (k + 1) * width], whole[0, k], 1, 1)
        d_acc[here, :] = total
        return carry

    slot = link.take(2)
    crossing = []
    lax.fori_loop(0, 1, input_grad, 0)
    for m in (1, 0):
        spread.finish(0, m, 2)
        at = rows_at(spread.inside(m, 2), width >> 3, 16)
        crossing.append(
            link.remote(slot + m, acc.at[m, 0, at, :], ff_landed.at[m], (link.dp, link.behind(1)))
        )
        crossing[-1].start()
    spread.finish(3, 0, 0)
    spread.finish(2, 1, 1)
    stores = [local(acc.at[m, 3], ff_own.at[m]) for m in range(2)]
    lax.fori_loop(1, 2, input_grad, 0)
    stores.append(local(d_acc, dnorm))
    spread.finish(2, 0, 1)
    for m in (1, 0):
        spread.finish(1, m, 2)
    for m in range(2):
        at = rows_at(spread.inside(m, 2), width >> 3, 16)
        stores.append(local(acc.at[m, 1, at, :], ff_near.at[m]))
        at = rows_at(spread.inside(m, 1), width >> 2, 16)
        stores.append(local(acc.at[m, 2, at, :], ff_far.at[m]))
    for copy in crossing + stores + [layer_store]:
        copy.wait()


def middle(mesh, vec, bup_all, xhat, out_grad, w_up, w_dn, ups, downs):
    dp_size, tp_size = mesh.shape["dp"], mesh.shape["tp"]
    low = min(3, dp_size.bit_length() - 1)
    assert low == 3 and tp_size == 4
    rows, width = xhat.shape
    hidden = tp_size * width
    vmem = pl.BlockSpec(memory_space=pltpu.VMEM)
    hbm = pl.BlockSpec(memory_space=pltpu.HBM)
    shape = jax.ShapeDtypeStruct

    def buf(*dims, dtype=BF):
        return pltpu.VMEM(dims, dtype)

    return pl.pallas_call(
        functools.partial(middle_kernel, dp_size, tp_size),
        out_shape=(
            shape((rows, width), BF),
            shape((rows, width), F32),
            shape((VECTORS, width), F32),
            shape((2, width >> 3, width), BF),
            shape((2, width >> 3, width), BF),
            shape((2, width >> 2, width), BF),
            shape((2, width >> 1, width), BF),
        ),
        in_specs=[vmem] * 2 + [hbm] * 6,
        out_specs=(hbm, hbm, vmem, hbm, hbm, hbm, hbm),
        scratch_shapes=[
            buf(2, tp_size, width, width),
            buf(rows, width, dtype=F32),
            buf(rows, width),
            buf(rows, width),
            buf(rows, width),
            buf(rows, hidden),
            buf(rows, hidden),
            buf(rows, width),
            buf(rows, width, dtype=F32),
            buf(2, 2, width, width),
            buf(2, tp_size, width // 2, width),
            buf(2, tp_size, sum(width >> (i + 1) for i in range(low)), width),
            pltpu.SemaphoreType.DMA((MIDDLE_SEMS,)),
            pltpu.SemaphoreType.DMA((MIDDLE_SEMS,)),
            pltpu.SemaphoreType.DMA((32,)),
        ],
        compiler_params=pltpu.CompilerParams(
            collective_id=2, has_side_effects=True, vmem_limit_bytes=VMEM_LIMIT
        ),
        name="middle",
    )(vec, bup_all, xhat, out_grad, w_up, w_dn, ups, downs)


def finish_kernel(
    tp_size, ff, gq, go, gkv, seq, vec, layer_out, grad_in,
    o_up, o_dn, o_q, o_o, o_k, o_v, o_seq, o_layer, o_grad, *rest,
):
    vectors, (in_up, in_dn, in_q, in_o, in_kv, in_seq, f_up, f_dn, f_q, f_o, f_k, f_v, f_seq, turn, pass_a, pass_b, in_sems, out_sems) = rest[:10], rest[10:]
    pairs = [(gq, in_q), (go, in_o), (ff.at[0], in_up), (ff.at[1], in_dn), (gkv, in_kv), (seq, in_seq), (layer_out, pass_a), (grad_in, pass_b)]
    loads = []
    for n, (source, target) in enumerate(pairs):
        loads.append(pltpu.make_async_copy(source, target, in_sems.at[n]))
        loads[-1].start()
    stores = []

    def put(staged, out):
        copy = pltpu.make_async_copy(staged, out, out_sems.at[len(stores)])
        copy.start()
        stores.append(copy)

    for n, (held, out) in enumerate(((pass_a, o_layer), (pass_b, o_grad))):
        loads[6 + n].wait()
        put(held, out)
    for n, row in enumerate((0, 1, 2, 3, 4, 5, 6, 7, 8)):
        vectors[n][...] = vec[row, :]
    vectors[9][...] = vec[pl.ds(9 + lax.axis_index("tp"), 1), :][0]
    width = gq.shape[0]
    for n, (narrow, wide, out) in enumerate(
        ((in_q, f_q, o_q), (in_o, f_o, o_o), (in_up, f_up, o_up), (in_dn, f_dn, o_dn))
    ):
        loads[n].wait()
        wide[...] = narrow[...].astype(F32)
        put(wide, out)
    loads[4].wait()
    owned = width // tp_size
    for n, (wide, out) in enumerate(((f_k, o_k), (f_v, o_v))):
        for c in range(tp_size):
            turn[c * owned : (c + 1) * owned, :] = in_kv[c, n * owned : (n + 1) * owned, :]
        for c in range(3):
            cols = slice(c * (width // 3), (c + 1) * (width // 3))
            wide[:, cols] = turn[cols, :].astype(F32).T
        put(wide, out)
    loads[5].wait()
    rows = in_seq.shape[2]
    for c in range(tp_size):
        f_seq[:, c * rows : (c + 1) * rows] = in_seq[c].astype(F32)
    put(f_seq, o_seq)
    for copy in stores:
        copy.wait()


def finish(tp_size, ff, gq, go, gkv, seq, vec, layer_out, grad_in):
    width = gq.shape[0]
    _, slots, rows = seq.shape
    square, flat = (width, width), (slots, tp_size * rows)
    vmem = pl.BlockSpec(memory_space=pltpu.VMEM)
    hbm = pl.BlockSpec(memory_space=pltpu.HBM)
    shape = jax.ShapeDtypeStruct
    return pl.pallas_call(
        functools.partial(finish_kernel, tp_size),
        out_shape=tuple([shape(square, F32)] * 6 + [shape(flat, F32)] + [shape(layer_out.shape, BF)] * 2 + [shape((width,), F32)] * 10),
        in_specs=[hbm] * 5 + [vmem] + [hbm] * 2,
        out_specs=tuple([hbm] * 9 + [vmem] * 10),
        scratch_shapes=[pltpu.VMEM(square, BF)] * 4
        + [pltpu.VMEM(gkv.shape, BF), pltpu.VMEM(seq.shape, BF)]
        + [pltpu.VMEM(square, F32)] * 6
        + [pltpu.VMEM(flat, F32), pltpu.VMEM(square, BF)]
        + [pltpu.VMEM(layer_out.shape, BF)] * 2
        + [pltpu.SemaphoreType.DMA((8,)), pltpu.SemaphoreType.DMA((9,))],
        compiler_params=pltpu.CompilerParams(vmem_limit_bytes=VMEM_LIMIT),
        name="finish",
    )(ff, gq, go, gkv, seq, vec, layer_out, grad_in)


def on_device(
    mesh,
    layer_in,
    out_grad,
    lengths,
    w_query,
    b_query,
    w_key,
    b_key,
    w_value,
    b_value,
    w_out,
    b_out,
    seq_proj,
    attn_gain,
    attn_shift,
    w_up,
    b_up,
    w_down,
    b_down,
    ffn_gain,
    ffn_shift,
):
    row_count, width = layer_in.shape
    tp_size = mesh.shape["tp"]
    vectors = (b_query, b_key, b_value, b_out, attn_gain, attn_shift, b_down, ffn_gain, ffn_shift)
    vec, bup_all, xhat, rstd, mixed, queries, probs, kb, vb, folded, ssum, own_proj, ups, downs = front(
        mesh, lengths, layer_in, w_query, seq_proj, w_key, w_value, w_out, w_up, w_down, vectors, b_up
    )
    layer_out, d_normed, part_vec, ff_landed, ff_near, ff_far, ff_own = middle(
        mesh, vec, bup_all, xhat, out_grad, w_up, w_down, ups, downs
    )
    grad_in, g_ff, g_o, g_q, g_kv, g_seq, vec_sum = back(
        mesh, lengths, vec, part_vec, ff_near, d_normed, probs, ff_far, ff_own, xhat, rstd, mixed, w_out, ff_landed,
        layer_in, queries, kb, vb, folded, ssum, own_proj, w_query, w_key, w_value
    )
    (
        g_w_up, g_w_down, g_w_query, g_w_out, g_w_key, g_w_value, g_seq_proj, layer_out, grad_in,
        g_b_query, g_b_key, g_b_value, g_b_out, g_attn_gain, g_attn_shift, g_ffn_gain, g_ffn_shift, g_b_down, g_b_up,
    ) = finish(tp_size, g_ff, g_q, g_o, g_kv, g_seq, vec_sum, layer_out, grad_in)
    return (
        layer_out,
        grad_in,
        g_w_query,
        g_b_query,
        g_w_key,
        g_b_key,
        g_w_value,
        g_b_value,
        g_w_out,
        g_b_out,
        g_seq_proj,
        g_attn_gain,
        g_attn_shift,
        g_w_up,
        g_b_up,
        g_w_down,
        g_b_down,
        g_ffn_gain,
        g_ffn_shift,
    )


def solution(mesh):
    in_specs = (
        P(("dp", "tp"), None),
        P(("dp", "tp"), None),
        P("dp"),
        *([P()] * 11),
        P(None, "tp"),
        P("tp"),
        P("tp", None),
        P(),
        P(),
        P(),
    )
    out_specs = (
        P(("dp", "tp"), None),
        P(("dp", "tp"), None),
        *([P()] * 11),
        P(None, "tp"),
        P("tp"),
        P("tp", None),
        P(),
        P(),
        P(),
    )
    return jax.shard_map(
        functools.partial(on_device, mesh), mesh=mesh, in_specs=in_specs, out_specs=out_specs, check_vma=False
    )
```

```python
import functools

import jax
import jax.numpy as jnp
from jax import lax
from jax.experimental import pallas as pl
from jax.experimental.pallas import tpu as pltpu
from jax.sharding import PartitionSpec as P

HEADS = 12
HEAD = 64
PAIRS = HEADS // 2
PAIR = 2 * HEAD
BF = jnp.bfloat16
F32 = jnp.float32
MESH = pl.DeviceIdType.MESH
VMEM_LIMIT = 67_043_328
BLOCK_F, BLOCK_M, BLOCK_B, GRAD_SPLIT = 1024, 512, 1024, 2


def dot(left, right, left_dim, right_dim):
    return lax.dot_general(
        left, right, (((left_dim,), (right_dim,)), ((), ())), preferred_element_type=F32
    )


def place(index, size):
    return pl.ds(pl.multiple_of(index * size, size), size)


def rows_at(first, size, multiple):
    return pl.ds(pl.multiple_of(first, multiple), size)


class Link:
    def __init__(self, dp_size, tp_size, send_sems, recv_sems):
        self.dp_size, self.tp_size = dp_size, tp_size
        self.dp, self.tp = lax.axis_index("dp"), lax.axis_index("tp")
        self.bits = dp_size.bit_length() - 1
        self.low = min(3, self.bits)
        self.send_sems, self.recv_sems = send_sems, recv_sems
        self.used = 0
        self.bit_values = [lax.rem(lax.div(self.dp, 1 << b), 2) for b in range(self.bits)]
        self.partners = [
            (self.dp + (1 - 2 * self.bit_values[b]) * (1 << b), self.tp) for b in range(self.bits)
        ]
        self.aheads = [lax.rem(self.tp + k, tp_size) for k in range(tp_size)]

    def bit(self, b):
        return self.bit_values[b]

    def partner(self, b):
        return self.partners[b]

    def ahead(self, k):
        return self.aheads[k]

    def behind(self, k):
        if isinstance(k, int):
            return self.aheads[(self.tp_size - k) % self.tp_size]
        return lax.rem(self.tp + self.tp_size - k, self.tp_size)

    def greet(self, dp_bits):
        barrier = pltpu.get_barrier_semaphore()
        peers = [(self.dp, self.ahead(k)) for k in range(1, self.tp_size)]
        peers += [self.partner(b) for b in range(dp_bits)]
        for peer in peers:
            pl.semaphore_signal(barrier, inc=1, device_id=peer, device_id_type=MESH)
        pl.semaphore_wait(barrier, len(peers))

    def take(self, count):
        first = self.used
        self.used += count
        assert self.used <= self.send_sems.shape[0]
        return first

    def remote(self, slot, source, target, device):
        return pltpu.make_async_remote_copy(
            src_ref=source,
            dst_ref=target,
            send_sem=self.send_sems.at[slot],
            recv_sem=self.recv_sems.at[slot],
            device_id=device,
            device_id_type=MESH,
        )

    def send(self, source, target, device):
        copy = self.remote(self.take(1), source, target, device)
        copy.start()
        return copy


FRONT_SEMS = 64
VECTORS = 16


def half_orders(low):
    return [[b for b in order if b < low] for order in ((1, 2, 0), (2, 1, 0))]


class WeightCollect:
    def __init__(self, link, part, whole):
        self.link, self.whole, self.part = link, whole, part
        self.orders = half_orders(link.low)
        self.piece = self.part >> link.low
        self.stages = link.low
        self.slot = link.take(2 * (link.tp_size - 1) * link.low)
        self.firsts = []
        for h in range(2):
            first, size, starts = h * part, self.piece, []
            for b in self.orders[h]:
                starts.append(size * link.bit(b))
                size *= 2
            self.firsts.append([sum(starts[i:], first) for i in range(self.stages)])

    def rows(self, h, i):
        return rows_at(self.firsts[h][i], self.piece << i, 16)

    def copies(self, k, i):
        for h in range(2):
            region = self.whole(k).at[self.rows(h, i), :]
            slot = self.slot + ((k - 1) * self.stages + i) * 2 + h
            yield self.link.remote(slot, region, region, self.link.partner(self.orders[h][i]))

    def step(self, k, j):
        if j > 0:
            for copy in self.copies(k, j - 1):
                copy.wait()
        if j < self.stages:
            for copy in self.copies(k, j):
                copy.start()


class Cross:
    def __init__(self, link, collect, shard, target):
        self.link, self.collect, self.shard, self.target = link, collect, shard, target
        self.slot = link.take(2 * (link.tp_size - 1))

    def copies(self, k):
        for h in range(2):
            rows = self.collect.rows(h, 0)
            yield self.link.remote(
                self.slot + 2 * (k - 1) + h,
                self.shard.at[rows, :],
                self.target(k, h, rows),
                (self.link.dp, self.link.ahead(k)),
            )

    def start(self, k):
        for copy in self.copies(k):
            copy.start()

    def wait(self, k):
        for copy in self.copies(k):
            copy.wait()


EARLY_TICKS = ((0, 1, 0), (1, 1, 0), (0, 1, 1), (1, 3, 0), (1, 1, 1), (0, 1, 2), (1, 3, 1), (1, 1, 2))
SHARE_TICKS = ((0, 1, 3), (1, 3, 2), (1, 1, 3), (1, 3, 3))
PAIR_TICKS = {1: ((0, 3, 0),), 3: ((0, 3, 1),), 5: ((0, 3, 2), (0, 2, 0))}
LAST_TICKS = ((0, 3, 3), (0, 2, -2), (1, 2, -1))


def front_kernel(dp_size, tp_size, n_vectors, len_ref, x_hbm, wq_hbm, e, wk_hbm, wv_hbm, wo_hbm, wup, wdn, *rest):
    vectors, b_up, rest = rest[:n_vectors], rest[n_vectors], rest[n_vectors + 1 :]
    outs, scratch = rest[:14], rest[14:]
    (vec, bup_all, xhat_out, rstd_out, mixed_out, q_out, probs_out, kb_out, vb_out, yb_out, ssum_out, em_out, ups, downs) = outs
    (x, wq, wk, wv, wo, e_all, xhat, rstd, mixed, q, probs, kb, vb, yb, ssum, em, bup, ysend, yrecv, send_sems, recv_sems, local_sems) = scratch
    link = Link(dp_size, tp_size, send_sems, recv_sems)
    rows, width = x.shape
    slots, total = e_all.shape
    quarter = slots // tp_size
    others = range(1, tp_size)
    used = [0]

    def local(source, target):
        copy = pltpu.make_async_copy(source, target, local_sems.at[used[0]])
        used[0] += 1
        copy.start()
        return copy

    own_first = link.tp * rows
    e_own = local(e.at[:, rows_at(own_first, rows, rows)], em)
    early = [local(x_hbm, x), local(wq_hbm, wq)]
    late = [local(e, e_all), local(wk_hbm, wk), local(wv_hbm, wv), local(wo_hbm, wo)]
    link.greet(link.low)

    collect = WeightCollect(link, wup.shape[0] // 2, lambda k: ups.at[k - 1])
    cross = Cross(link, collect, wup, lambda k, h, rows: ups.at[k - 1, rows, :])
    cross_down = Cross(link, collect, wdn, lambda k, h, rows: downs.at[k - 1, rows, :])
    collect_down = WeightCollect(link, wdn.shape[0] // 2, lambda k: downs.at[k - 1])
    def tick(ticks):
        for m, k, j in ticks:
            if -1 <= j <= 0:
                (cross, cross_down)[m].wait(k)
            if j == -2:
                for copy in (collect, collect_down)[m].copies(k, 0):
                    copy.wait()
            elif j >= 0:
                (collect, collect_down)[m].step(k, j)

    cross.start(1)
    cross_down.start(1)
    cross_down.start(3)
    vec[...] = jnp.zeros_like(vec)
    for n, vector in enumerate(vectors):
        vec[n : n + 1, :] = vector[...].astype(F32).reshape(1, width)
    bup[...] = jnp.broadcast_to(b_up[...].astype(F32).reshape(1, width), bup.shape)
    bup_all[link.tp] = bup[...]
    length = len_ref[0]
    position = lax.broadcasted_iota(jnp.int32, (1, rows), 1) + own_first
    live = (position < length).astype(F32)
    e_own.wait()
    early[0].wait()
    em[...] = (em[...].astype(F32) * live).astype(BF)
    ysend[...] = dot(em[...], x[...], 1, 0).astype(ysend.dtype)
    reduce = [
        link.send(ysend.at[place(link.ahead(k), quarter), :], yrecv.at[k - 1], (link.dp, link.ahead(k)))
        for k in others
    ]
    biases = [link.send(bup, bup_all.at[link.tp], (link.dp, link.ahead(k))) for k in others]
    early[1].wait()
    q[...] = (dot(x[...], wq[...], 1, 0) + vec[0:1, :]).astype(BF)
    tick(EARLY_TICKS)
    own_slots = place(link.tp, quarter)
    for copy in reduce:
        copy.wait()
    own_y = ysend[own_slots, :].astype(F32)
    for k in others:
        own_y = own_y + yrecv[k - 1].astype(F32)
    yb[own_slots, :] = own_y.astype(BF)
    share = [
        link.send(yb.at[own_slots, :], yb.at[own_slots, :], (link.dp, link.ahead(k))) for k in others
    ]
    for k in (3, 2):
        cross.start(k)
    cross_down.start(2)
    tick(SHARE_TICKS)
    stores = [local(q, q_out), local(em, em_out)]
    row_live = (lax.broadcasted_iota(jnp.int32, (total, 128), 0) < length).astype(F32).astype(BF)
    for load in late:
        load.wait()
    ssum[...] = dot(e_all[...], row_live, 1, 0)
    for copy in share:
        copy.wait()
    for copy in biases:
        copy.wait()
    stores += [local(yb, yb_out), local(ssum, ssum_out)]

    lane = lax.broadcasted_iota(jnp.int32, (1, PAIR), 1)
    first_half = (lane < HEAD).astype(F32)

    def project(weight, bias_row, blocks):
        full = dot(yb[...], weight[...], 1, 0)
        for p in range(PAIRS):
            cols = slice(p * PAIR, (p + 1) * PAIR)
            both = full[:, cols] + ssum[...] * vec[bias_row : bias_row + 1, cols]
            blocks[p, 0:slots, :] = (both * first_half).astype(BF)
            blocks[p, slots : 2 * slots, :] = (both * (1.0 - first_half)).astype(BF)

    project(wk, 1, kb)
    project(wv, 2, vb)
    stores += [local(kb, kb_out), local(vb, vb_out)]

    block = min(BLOCK_F, rows)
    per_pair = rows // block
    probs_sem = used[0]

    def attend(p, carry):
        cols = place(p, PAIR)

        def one(step, carry):
            here = place(step, block)
            logits = dot(q[here, cols], kb[p], 1, 1) * 0.125
            halves = []
            for half in range(2):
                part = logits[:, half * slots : (half + 1) * slots]
                peak = jnp.max(part, axis=-1, keepdims=True)
                raised = jnp.exp(part - peak)
                halves.append((raised * (1.0 / jnp.sum(raised, axis=-1, keepdims=True))).astype(BF))
            both = jnp.concatenate(halves, axis=1)
            probs[p, here, :] = both
            mixed[here, cols] = dot(both, vb[p], 1, 0).astype(BF)
            return carry

        lax.fori_loop(0, per_pair, one, 0)
        pltpu.make_async_copy(probs.at[p], probs_out.at[p], local_sems.at[probs_sem + p]).start()
        for n, ticks in PAIR_TICKS.items():

            @pl.when(p == n)
            def _():
                tick(ticks)

        return carry

    lax.fori_loop(0, PAIRS, attend, 0)
    used[0] += PAIRS
    stores.append(local(mixed, mixed_out))

    def finish(step, carry):
        here = place(step, block)
        res = x[here, :].astype(F32) + dot(mixed[here, :], wo[...], 1, 0) + vec[3:4, :]
        center = res - jnp.mean(res, axis=-1, keepdims=True)
        inverse = lax.rsqrt(jnp.mean(center * center, axis=-1, keepdims=True) + 1e-05)
        xhat[here, :] = center * inverse
        rstd[here, :] = jnp.broadcast_to(inverse, (block, 128))
        return carry

    lax.fori_loop(0, per_pair, finish, 0)
    stores += [local(xhat, xhat_out), local(rstd, rstd_out)]
    tick(LAST_TICKS)
    for copy in stores:
        copy.wait()
    for p in range(PAIRS):
        pltpu.make_async_copy(probs.at[p], probs_out.at[p], local_sems.at[probs_sem + p]).wait()


def front(mesh, lengths, x, wq, e, wk, wv, wo, wup, wdn, vectors, b_up):
    dp_size, tp_size = mesh.shape["dp"], mesh.shape["tp"]
    low = min(3, dp_size.bit_length() - 1)
    rows, width = x.shape
    slots = e.shape[0]
    vmem = pl.BlockSpec(memory_space=pltpu.VMEM)
    hbm = pl.BlockSpec(memory_space=pltpu.HBM)
    shape = jax.ShapeDtypeStruct
    moved = (
        ((rows, width), F32),
        ((rows, 128), F32),
        ((rows, width), BF),
        ((rows, width), BF),
        ((PAIRS, rows, 2 * slots), BF),
        ((PAIRS, 2 * slots, PAIR), BF),
        ((PAIRS, 2 * slots, PAIR), BF),
        ((slots, width), BF),
        ((slots, 128), F32),
        ((slots, rows), BF),
    )
    kept = (
        ((VECTORS, width), F32),
        ((tp_size, 8, width), F32),
    )
    return pl.pallas_call(
        functools.partial(front_kernel, dp_size, tp_size, len(vectors)),
        out_shape=tuple(shape(*s) for s in kept + moved)
        + (
            shape((tp_size - 1, *wup.shape), BF),
            shape((tp_size - 1, *wdn.shape), BF),
        ),
        in_specs=[pl.BlockSpec(memory_space=pltpu.SMEM)]
        + [hbm] * 8
        + [vmem] * (len(vectors) + 1),
        out_specs=tuple([vmem] * len(kept) + [hbm] * (len(moved) + 2)),
        scratch_shapes=[pltpu.VMEM(w.shape, BF) for w in (x, wq, wk, wv, wo, e)]
        + [pltpu.VMEM(*s) for s in moved]
        + [
            pltpu.VMEM((8, width), F32),
            pltpu.VMEM((slots, width), BF),
            pltpu.VMEM((tp_size - 1, slots // tp_size, width), BF),
            pltpu.SemaphoreType.DMA((FRONT_SEMS,)),
            pltpu.SemaphoreType.DMA((FRONT_SEMS,)),
            pltpu.SemaphoreType.DMA((32,)),
        ],
        compiler_params=pltpu.CompilerParams(
            collective_id=0, has_side_effects=True, vmem_limit_bytes=VMEM_LIMIT
        ),
        name="front",
    )(lengths, x, wq, e, wk, wv, wo, wup, wdn, *vectors, b_up)


BACK_SEMS = 128
VECTORS = 16


def add_rows(target, first, left, left_first, right, count):
    block = 96 if count % 96 == 0 else (48 if count % 48 == 0 else (32 if count % 32 == 0 else count))

    def step(i, carry):
        at = i * block
        total = (
            left[rows_at(left_first + at, block, 16), :].astype(F32)
            + right[rows_at(at, block, 16), :].astype(F32)
        )
        target[rows_at(first + at, block, 16), :] = total.astype(target.dtype)
        return carry

    lax.fori_loop(0, count // block, step, 0)


class Spread:
    def __init__(self, link, order, rows, source, acc, landing):
        self.link, self.rows, self.source, self.acc, self.landing = link, rows, source, acc, landing
        self.order = [b for b in order if b < link.low]
        self.stages = len(self.order)
        self.slot = link.take(self.stages)
        self.piece = rows >> self.stages
        self.insides, self.others, first = [0], [(1 - link.bit(self.order[0])) * (rows >> 1)], 0
        for j in range(1, self.stages):
            size = rows >> (j + 1)
            self.others.append(first + (1 - link.bit(self.order[j])) * size)
            first = first + link.bit(self.order[j]) * size
            self.insides.append(first)
        self.at = link.bit(self.order[0]) * (rows >> 1) + first

    def inside(self, i):
        return self.insides[i]

    def kept(self):
        return rows_at(self.inside(self.stages - 1), self.piece, 16)

    def offset(self):
        return self.at

    def landed(self, i):
        first = sum(self.rows >> (j + 1) for j in range(i))
        return self.landing.at[pl.ds(first, self.rows >> (i + 1)), :]

    def copy(self, i):
        link, size = self.link, self.rows >> (i + 1)
        where, other = self.source if i == 0 else self.acc, self.others[i]
        return link.remote(
            self.slot + i, where.at[rows_at(other, size, 16), :], self.landed(i), link.partner(self.order[i])
        )

    def start(self, i):
        self.copy(i).start()

    def finish(self, i):
        size = self.rows >> (i + 1)
        self.copy(i).wait()
        if i == 0:
            add_rows(self.acc, 0, self.source, self.link.bit(self.order[0]) * size, self.landed(0), size)
        else:
            at = self.inside(i)
            add_rows(self.acc, at, self.acc, at, self.landed(i), size)

    def steps(self):
        yield lambda: self.start(0)
        for i in range(1, self.stages):

            def step(i=i):
                self.finish(i - 1)
                self.start(i)

            yield step


class Collect:
    def __init__(self, link, order, offset, piece, region):
        self.link, self.offset, self.piece, self.region = link, offset, piece, region
        self.order = [b for b in order if b < link.low][::-1]
        self.slot = link.take(len(self.order))
        starts, size = [], piece
        for b in self.order:
            starts.append(link.bit(b) * size)
            size *= 2
        self.firsts = [sum(starts[i:], 0) for i in range(len(self.order))]

    def copy(self, i):
        size, first = self.piece << i, self.firsts[i]
        ref = self.region(first, size)
        return self.link.remote(self.slot + i, ref, ref, self.link.partner(self.order[i]))

    def steps(self):
        yield lambda: self.copy(0).start()
        for i in range(1, len(self.order)):

            def step(i=i):
                self.copy(i - 1).wait()
                self.copy(i).start()

            yield step
        yield lambda: self.copy(len(self.order) - 1).wait()


class Widen:
    def __init__(self, link, landing):
        self.link, self.landing = link, landing
        self.slot = link.take(max(0, link.bits - link.low))

    def run(self, piece):
        link = self.link
        for i, b in enumerate(range(link.low, link.bits)):
            copy = link.remote(self.slot + i, piece, self.landing.at[i], link.partner(b))
            copy.start()
            copy.wait()
            piece[...] = (piece[...].astype(F32) + self.landing[i].astype(F32)).astype(piece.dtype)


class Fan:
    def __init__(self, link, ends):
        self.link, self.ends = link, ends
        self.slot = link.take(link.tp_size - 1)

    def copy(self, k):
        source, target = self.ends(k)
        return self.link.remote(self.slot + k - 1, source, target, (self.link.dp, self.link.ahead(k)))

    def start(self):
        for k in range(1, self.link.tp_size):
            self.copy(k).start()

    def wait(self):
        for k in range(1, self.link.tp_size):
            self.copy(k).wait()


def then(*actions):
    def both():
        for action in actions:
            action()

    return both


class Track:
    def __init__(self):
        self.todo = []

    def add(self, steps, join=False):
        steps = list(steps)
        if join and self.todo:
            steps[0] = then(self.todo.pop(), steps[0])
        self.todo += steps

    def advance(self):
        if self.todo:
            self.todo.pop(0)()


def back_kernel(
    dp_size,
    tp_size,
    len_ref,
    vec,
    part_vec,
    ff_near,
    dnorm,
    probs,
    far_hbm,
    own_hbm,
    xhat_hbm,
    rstd_hbm,
    mixed_hbm,
    wo_hbm,
    landed_hbm,
    x_hbm,
    q_hbm,
    kb_hbm,
    vb_hbm,
    yb_hbm,
    ssum_hbm,
    em_hbm,
    wq_hbm,
    wk_hbm,
    wv_hbm,
    grad_hbm,
    ff_hbm,
    go_hbm,
    gq_out,
    gkv_out,
    seq_out,
    vec_out,
    grad_in,
    ff_out,
    go_out,
    ff_far,
    ff_own,
    xhat,
    rstd,
    mixed,
    wo,
    ff_landed,
    x,
    q,
    kb,
    vb,
    yb,
    ssum,
    em,
    wq,
    wk,
    wv,
    dres,
    dmix,
    dq,
    dl,
    prob_slots,
    dpart,
    dland,
    dcross,
    dfull,
    ff_zland,
    far_acc,
    far_land,
    own_acc,
    own_land,
    o_acc,
    o_land,
    q_acc,
    q_land,
    o_zland,
    q_zland,
    kv_send,
    kv_acc,
    kv_land,
    s_send,
    s_acc,
    s_land,
    vec_acc,
    vec_land,
    vec_z,
    wide_ff,
    wide_q,
    wide_kv,
    wide_s,
    send_sems,
    recv_sems,
    local_sems,
):
    link = Link(dp_size, tp_size, send_sems, recv_sems)
    rows, width = x.shape
    slots = yb.shape[0]
    low = link.low
    others = range(1, tp_size)
    first_load = pltpu.make_async_copy(dnorm, dres, local_sems.at[0])
    first_load.start()
    late = []
    for n, (source, target) in enumerate(
        (
            (far_hbm, ff_far), (own_hbm, ff_own), (xhat_hbm, xhat), (rstd_hbm, rstd), (mixed_hbm, mixed),
            (wo_hbm, wo), (landed_hbm, ff_landed), (q_hbm, q), (kb_hbm, kb), (vb_hbm, vb), (x_hbm, x), (yb_hbm, yb),
            (wq_hbm, wq), (wk_hbm, wk), (wv_hbm, wv), (ssum_hbm, ssum), (em_hbm, em),
        )
    ):
        late.append(pltpu.make_async_copy(source, target, local_sems.at[3 + n]))
        late[-1].start()
    link.greet(link.bits)

    lanes = 2
    deep = tp_size // lanes
    third = width // GRAD_SPLIT
    owned = width // tp_size

    ff_track, ff_orders = Track(), ((0, 1, 2), (0, 2, 1))
    ff_rows = width >> 3
    ff_parts = []
    for m in range(2):
        first, second, third_bit = ff_orders[m]
        far = Spread(link, (third_bit,), width >> 2, ff_far.at[m], far_acc.at[m], far_land.at[m])
        own = Spread(link, (second, third_bit), width >> 1, ff_own.at[m], own_acc.at[m], own_land.at[m])
        slot = link.take(2)

        def piece_copy(n, m=m, slot=slot):
            source, k = ((far_acc, 3), (ff_near, 1))[n]
            return link.remote(slot + n, source.at[m], ff_zland.at[m, n], (link.dp, link.behind(k)))

        at = link.bit(ff_orders[m][0]) * (width >> 1) + own.offset()

        def offset(at=at):
            return at

        widen = Widen(link, wide_ff.at[m])

        def join(m=m, own=own, piece_copy=piece_copy, offset=offset, widen=widen):
            total = own_acc[m, own.kept(), :].astype(F32) + ff_landed[m].astype(F32)
            for n in range(2):
                piece_copy(n).wait()
                total = total + ff_zland[m, n].astype(F32)
            mine = rows_at(offset(), ff_rows, 16)
            ff_out[m, mine, :] = total.astype(BF)
            widen.run(ff_out.at[m, mine, :])

        collect = Collect(
            link, ff_orders[m], offset, ff_rows,
            lambda first, size, m=m: ff_out.at[m, rows_at(first, size, 16), :],
        )
        ff_parts.append((far, own, piece_copy, join, list(collect.steps())))

    def ff_begin():
        for far, own, piece_copy, _, _ in ff_parts:
            far.start(0)
            own.start(0)
            piece_copy(1).start()

    def ff_second():
        for far, own, piece_copy, _, _ in ff_parts:
            far.finish(0)
            piece_copy(0).start()

    def ff_second_own():
        for far, own, piece_copy, _, _ in ff_parts:
            own.finish(0)
            own.start(1)

    def ff_third():
        for _, own, _, join, collects in ff_parts:
            own.finish(1)

    def ff_join():
        for _, _, _, join, collects in ff_parts:
            join()
            collects[0]()

    stores = []

    def store(n, source, target):
        copy = pltpu.make_async_copy(source, target, local_sems.at[20 + n])
        stores.append(copy)
        return copy

    ff_store, go_store, grad_store = store(0, ff_out, ff_hbm), store(1, go_out, go_hbm), store(2, grad_in, grad_hbm)
    late[0].wait()
    late[1].wait()
    ff_begin()
    ff_track.add([ff_second, ff_second_own, then(ff_third, ff_join)])
    ff_track.add([then(*pair) for pair in zip(ff_parts[0][4][1:], ff_parts[1][4][1:])])
    ff_track.add([ff_store.start], join=True)

    def square_track(out, acc, landing, zland, wide):
        track, spreads, collects = Track(), [], []
        q_cols = width // lanes
        for h, order in enumerate(((0, 1, 2), (0, 2, 1))):
            cols = slice(h * q_cols, (h + 1) * q_cols)
            spread = Spread(link, order, width, out.at[:, cols], acc.at[:, cols], landing.at[:, cols])
            spreads.append(spread)
            collects.append(
                Collect(
                    link, order, spread.offset, spread.piece,
                    lambda first, size, cols=cols: out.at[rows_at(first, size, 16), cols],
                )
            )
        q_rows = spreads[0].piece // deep
        halves = [lax.rem(t, lanes) for t in link.aheads]

        def quarter(firsts, k):
            first = firsts[0] + halves[k] * (firsts[1] - firsts[0]) + lax.div(link.aheads[k], lanes) * q_rows
            return rows_at(first, q_rows, 16), pl.ds(pl.multiple_of(halves[k] * q_cols, 128), q_cols)

        inner = [quarter([spread.inside(spread.stages - 1) for spread in spreads], k) for k in range(tp_size)]
        mine = quarter([spread.offset() for spread in spreads], 0)
        fan = Fan(link, lambda k: (acc.at[inner[k]], zland.at[k - 1]))
        share, widen = Fan(link, lambda k: (out.at[mine], out.at[mine])), Widen(link, wide)

        def join():
            fan.wait()
            total = acc[inner[0]].astype(F32)
            for k in others:
                total = total + zland[k - 1].astype(F32)
            out[mine] = total.astype(BF)
            widen.run(out.at[mine])
            share.start()

        def summed():
            for spread in spreads:
                spread.finish(spread.stages - 1)
            fan.start()

        track.add([then(*pair) for pair in zip(spreads[0].steps(), spreads[1].steps())])
        track.add([summed, join, share.wait])
        track.add([then(*pair) for pair in zip(collects[0].steps(), collects[1].steps())], join=True)
        return track

    def owned_track(order, total_rows, cols, source, acc, landing, out, wide):
        source, acc, landing = source.at[:, cols], acc.at[:, cols], landing.at[:, cols]
        track, spread = Track(), Spread(link, order, total_rows, source, acc, landing)

        def region(k):
            ref = out.at[link.tp, rows_at(spread.offset(), spread.piece, 16), cols]
            return ref, ref

        share, widen = Fan(link, region), Widen(link, wide)

        def last():
            spread.finish(spread.stages - 1)
            ref = region(0)[0]
            ref[...] = acc[spread.kept(), :]
            widen.run(ref)
            share.start()

        collect = Collect(
            link, order, spread.offset, spread.piece, lambda first, size: out.at[:, rows_at(first, size, 16), cols]
        )
        track.add(spread.steps())
        track.add([last, share.wait])
        track.add(collect.steps(), join=True)
        return track

    o_track = square_track(go_out, o_acc, o_land, o_zland, wide_q.at[0])
    o_track.add([go_store.start], join=True)
    q_track = square_track(gq_out, q_acc, q_land, q_zland, wide_q.at[1])
    def halves(total_rows, source, acc, landing, out, wide):
        tracks = []
        for h, order in enumerate(((0, 1, 2), (0, 2, 1))):
            cols = slice(h * source.shape[1] // 2, (h + 1) * source.shape[1] // 2)
            tracks.append(owned_track(order, total_rows, cols, source, acc, landing, out, wide.at[h]))
        both = Track()
        both.add([then(*pair) for pair in zip(tracks[0].todo, tracks[1].todo)])
        return both

    kv_track = halves(2 * owned, kv_send, kv_acc, kv_land, gkv_out, wide_kv)
    s_track = halves(slots, s_send, s_acc, s_land, seq_out, wide_s)

    vec_track, vec_slot = Track(), link.take(link.bits)
    vec_fan = Fan(link, lambda k: (vec_z.at[link.tp], vec_z.at[link.tp]))

    def vec_copy(b):
        return link.remote(vec_slot + b, vec_acc.at[b], vec_land.at[b], link.partner(b))

    vec_track.add([lambda: vec_copy(0).start()])
    for b in range(link.bits):

        def vec_step(b=b):
            vec_copy(b).wait()
            total = vec_acc[b] + vec_land[b]
            if b + 1 < link.bits:
                vec_acc[b + 1] = total
                vec_copy(b + 1).start()
            else:
                vec_z[link.tp] = total
                vec_fan.start()

        vec_track.add([vec_step])

    def vec_last():
        vec_fan.wait()
        total = vec_z[0]
        for t in range(1, tp_size):
            total = total + vec_z[t]
        vec_out[...] = total

    vec_track.add([vec_last])

    block = min(BLOCK_B, rows)
    count = rows // block
    gain = vec[4:5, :]

    def norm_back(step, carry):
        g_gain, g_shift, g_out = carry
        here = place(step, block)
        grad, hat = dres[here, :], xhat[here, :]
        g_gain = g_gain + jnp.sum(grad * hat, axis=0, keepdims=True)
        g_shift = g_shift + jnp.sum(grad, axis=0, keepdims=True)
        scaled = grad * gain
        d_res = rstd[here, 0:1] * (
            scaled
            - jnp.mean(scaled, axis=-1, keepdims=True)
            - hat * jnp.mean(scaled * hat, axis=-1, keepdims=True)
        )
        dres[here, :] = d_res
        d_attn = d_res.astype(BF)
        dq[here, :] = d_attn
        g_out = g_out + jnp.sum(d_attn.astype(F32), axis=0, keepdims=True)
        return g_gain, g_shift, g_out

    zero = jnp.zeros((1, width), F32)
    first_load.wait()
    late[2].wait()
    late[3].wait()
    g_gain, g_shift, g_out = lax.fori_loop(0, count, norm_back, (zero, zero, zero))
    vec_acc[0] = part_vec[...]
    vec_acc[0, 3:4, :] = g_out
    vec_acc[0, 4:5, :] = g_gain
    vec_acc[0, 5:6, :] = g_shift
    d_attn = dq

    def weight_grad(left, right, target):
        for m in range(GRAD_SPLIT):
            cols = slice(m * third, (m + 1) * third)
            target[cols, :] = dot(left[:, cols], right[...], 0, 0).astype(BF)

    for load in late[4:7]:
        load.wait()
    weight_grad(mixed, d_attn, go_out)
    o_track.advance()
    ff_track.advance()
    dmix[...] = dot(d_attn[...], wo[...], 1, 1).astype(BF)
    o_track.advance()
    for load in late[7:]:
        load.wait()

    own_half = lax.div(link.tp, 2)
    parity = lax.rem(link.tp, 2)
    three = PAIRS // 2

    def pair_at(n):
        second = lax.div(n, three)
        which = (1 - own_half) * (1 - second) + own_half * second
        along = lax.rem(n, three)
        return which * three + along * parity + (three - 1 - along) * (1 - parity)

    def fetch(n):
        slot = lax.rem(n, 2)
        return pltpu.make_async_copy(probs.at[pair_at(n)], prob_slots.at[slot], local_sems.at[1 + slot])

    fetch(0).start()

    def attend_back(n):
        p = pair_at(n)
        cols = place(p, PAIR)

        @pl.when(n + 1 < PAIRS)
        def _():
            fetch(n + 1).start()

        fetch(n).wait()
        held = prob_slots.at[lax.rem(n, 2)]

        def part(step, carry):
            here = place(step, block)
            d_probs = dot(dmix[here, cols], vb[p], 1, 1)
            weights = held[here, :].astype(F32)
            halves = []
            for h in range(2):
                w = weights[:, h * slots : (h + 1) * slots]
                d = d_probs[:, h * slots : (h + 1) * slots]
                halves.append((w * (d - jnp.sum(w * d, axis=-1, keepdims=True))).astype(BF))
            both = jnp.concatenate(halves, axis=1)
            dl[here, :] = both
            dq[here, cols] = (dot(both, kb[p], 1, 0) * 0.125).astype(BF)
            return carry

        lax.fori_loop(0, count, part, 0)
        top, under = rows_at(p * PAIR, HEAD, HEAD), rows_at(p * PAIR + HEAD, HEAD, HEAD)
        for n, total in enumerate(
            (dot(q[:, cols], dl[...], 0, 0) * 0.125, dot(dmix[:, cols], held[...], 0, 0))
        ):
            dpart[n, top, :] = total[:HEAD, :slots].astype(BF)
            dpart[n, under, :] = total[HEAD:, slots:].astype(BF)

    d_slot = link.take(tp_size - 1)
    sibling = 2 * own_half + (1 - parity)
    far_same = rows_at((2 * (1 - own_half) + parity) * owned, owned, 64)
    far_other = rows_at((2 * (1 - own_half) + (1 - parity)) * owned, owned, 64)
    d_peers = [2 * (1 - own_half) + parity, sibling, sibling]
    d_sources = [
        dcross, dpart.at[:, far_other, :], dpart.at[:, rows_at(sibling * owned, owned, 64), :],
    ]

    def d_copy(j):
        return link.remote(d_slot + j, d_sources[j], dland.at[j], (link.dp, d_peers[j]))

    def d_across():
        d_copy(1).wait()
        for n in range(2):
            dcross[n] = (dpart[n, far_same, :].astype(F32) + dland[1, n].astype(F32)).astype(BF)
        d_copy(0).start()

    events = {
        1: lambda: d_copy(1).start(),
        2: ff_track.advance,
        4: lambda: d_copy(2).start(),
        5: then(d_across, o_track.advance),
    }

    def one(n, carry):
        attend_back(n)
        for i, event in events.items():
            pl.when(n == i)(event)
        return carry

    lax.fori_loop(0, PAIRS, one, 0)

    weight_grad(x, dq, gq_out)
    q_track.advance()
    ff_track.advance()

    def input_grad(step, carry):
        here = place(step, block)
        dres[here, :] += dot(dq[here, :], wq[...], 1, 1)
        return carry

    lax.fori_loop(0, count, input_grad, 0)
    q_track.advance()
    vec_acc[0, 0:1, :] = jnp.sum(dq[...].astype(F32), axis=0, keepdims=True)
    o_track.advance()

    for j in (0, 2):
        d_copy(j).wait()
    own_block = rows_at(link.tp * owned, owned, 64)
    for n in range(2):
        total = dpart[n, own_block, :].astype(F32)
        for j in (0, 2):
            total = total + dland[j, n].astype(F32)
        dfull[n, own_block, :] = total.astype(BF)
    share_slot = link.take(3)
    share_plan = ((own_block, d_peers[0]), (own_block, sibling), (far_same, sibling))

    def share_copy(n):
        block_rows, peer = share_plan[n]
        return link.remote(
            share_slot + n, dfull.at[:, block_rows, :], dfull.at[:, block_rows, :], (link.dp, peer)
        )

    share_copy(0).start()
    share_copy(1).start()
    ff_track.advance()
    for n in range(2):
        kv_send[n * owned : (n + 1) * owned, :] = dot(dfull[n, own_block, :], yb[...], 1, 0).astype(BF)
    kv_track.advance()
    o_track.advance()
    q_track.advance()
    kv_track.advance()
    ff_track.advance()
    share_copy(0).wait()
    share_copy(2).start()
    kv_track.advance()
    q_track.advance()
    ff_track.advance()
    kv_track.advance()
    share_copy(1).wait()
    share_copy(2).wait()
    backs = dot(wk[...], dfull[0], 1, 0) + dot(wv[...], dfull[1], 1, 0)
    back = backs.T.astype(BF)
    small = vec[0:8, :].astype(BF)
    bias_row = dot(small, dfull[0], 1, 0)[1:2, :] + dot(small, dfull[1], 1, 0)[2:3, :]
    bias_column = jnp.broadcast_to(bias_row, (128, slots)).T[:, 0:1]
    position = lax.broadcasted_iota(jnp.int32, (1, rows), 1) + link.tp * rows
    live = (position < len_ref[0]).astype(F32)
    s_send[...] = ((dot(back, x[...], 1, 1) + bias_column) * live).astype(BF)
    s_track.advance()
    column = ssum[...].T[0:8, :]
    column_b = column.astype(BF)
    column_low = (column - column_b.astype(F32)).astype(BF)
    for n in range(2):
        total = dot(column_b, dfull[n], 1, 1) + dot(column_low, dfull[n], 1, 1)
        vec_acc[0, 1 + n : 2 + n, :] = total[0:1, :] * (1.0 / tp_size)
    vec_track.advance()
    s_track.advance()

    def input_grad_last(step, carry):
        here = place(step, block)
        grad_in[here, :] = (dres[here, :] + dot(em[:, here], back, 0, 0)).astype(BF)
        return carry

    lax.fori_loop(0, count, input_grad_last, 0)
    grad_store.start()
    tracks = {"s": s_track, "k": kv_track, "q": q_track, "o": o_track, "v": vec_track, "f": ff_track}
    for name in "oqskvosqkvoqskvqsokvsqs":
        tracks[name].advance()
    tracks = list(tracks.values())
    while any(track.todo for track in tracks):
        for track in tracks:
            track.advance()
    for copy in stores:
        copy.wait()


def back(mesh, lengths, vec, part_vec, ff_near, dnorm, probs, *late):
    dp_size, tp_size = mesh.shape["dp"], mesh.shape["tp"]
    bits = dp_size.bit_length() - 1
    low = min(3, bits)
    wide = max(1, bits - low)
    rows, width = dnorm.shape
    slots = late[11].shape[0]
    owned = width // tp_size
    others = tp_size - 1
    vmem = pl.BlockSpec(memory_space=pltpu.VMEM)
    hbm = pl.BlockSpec(memory_space=pltpu.HBM)
    shape = jax.ShapeDtypeStruct

    def landing(total):
        return sum(total >> (i + 1) for i in range(low))

    def buf(*dims, dtype=BF):
        return pltpu.VMEM(dims, dtype)

    ff_piece, kv_piece, s_piece = width >> low, 2 * owned >> low, slots >> low
    quarter = (ff_piece // (tp_size // 2), width // 2)
    return pl.pallas_call(
        functools.partial(back_kernel, dp_size, tp_size),
        out_shape=(
            shape((rows, width), BF),
            shape((2, width, width), BF),
            shape((width, width), BF),
            shape((width, width), BF),
            shape((tp_size, 2 * owned, width), BF),
            shape((tp_size, slots, rows), BF),
            shape((VECTORS, width), F32),
        ),
        in_specs=[pl.BlockSpec(memory_space=pltpu.SMEM)] + [vmem] * 2 + [hbm] * (3 + len(late)),
        out_specs=tuple([hbm] * 3 + [vmem] * 4),
        scratch_shapes=[buf(rows, width), buf(2, width, width), buf(width, width)]
        + [pltpu.VMEM(array.shape, array.dtype) for array in late]
        + [
            buf(rows, width, dtype=F32),
            buf(rows, width),
            buf(rows, width),
            buf(rows, 2 * slots),
            buf(2, rows, 2 * slots),
            buf(2, width, slots),
            buf(others, 2, owned, slots),
            buf(2, owned, slots),
            buf(2, width, slots),
            buf(2, 2, ff_piece, width),
            buf(2, width >> 3, width),
            buf(2, width >> 3, width),
            buf(2, width >> 2, width),
            buf(2, (width >> 2) + (width >> 3), width),
            buf(width // 2, width),
            buf(landing(width), width),
            buf(width // 2, width),
            buf(landing(width), width),
            buf(others, *quarter),
            buf(others, *quarter),
            buf(2 * owned, width),
            buf(owned, width),
            buf(landing(2 * owned), width),
            buf(slots, rows),
            buf(slots // 2, rows),
            buf(landing(slots), rows),
            buf(bits, VECTORS, width, dtype=F32),
            buf(bits, VECTORS, width, dtype=F32),
            buf(tp_size, VECTORS, width, dtype=F32),
            buf(2, wide, ff_piece, width),
            buf(2, wide, *quarter),
            buf(2, wide, kv_piece, width // 2),
            buf(2, wide, s_piece, rows // 2),
            pltpu.SemaphoreType.DMA((BACK_SEMS,)),
            pltpu.SemaphoreType.DMA((BACK_SEMS,)),
            pltpu.SemaphoreType.DMA((6 + len(late),)),
        ],
        compiler_params=pltpu.CompilerParams(
            collective_id=1, has_side_effects=True, vmem_limit_bytes=VMEM_LIMIT
        ),
        name="back",
    )(lengths, vec, part_vec, ff_near, dnorm, probs, *late)


class ChunkSpread:
    def __init__(self, link, rows, sent, acc, landing):
        self.link, self.rows, self.sent, self.acc, self.landing = link, rows, sent, acc, landing
        self.orders = [[b for b in order if b < link.low] for order in ((0, 1, 2), (0, 2, 1))]
        self.stages = link.low
        self.slot = link.take(2 * link.low * acc.shape[1])
        self.insides, self.others = [], []
        for order in self.orders:
            inside, other, first = [0], [(1 - link.bit(order[0])) * (rows >> 1)], 0
            for j in range(1, self.stages):
                size = rows >> (j + 1)
                other.append(first + (1 - link.bit(order[j])) * size)
                first = first + link.bit(order[j]) * size
                inside.append(first)
            self.insides.append(inside)
            self.others.append(other)

    def inside(self, m, i):
        return self.insides[m][i]

    def copy(self, c, m, i):
        link, size = self.link, self.rows >> (i + 1)
        bit = self.orders[m][i]
        if i == 0:
            source = self.sent.at[m, lax.rem(c, 2), rows_at(self.others[m][i], size, 16), :]
        else:
            source = self.acc.at[m, c, rows_at(self.others[m][i], size, 16), :]
        first = sum(self.rows >> (j + 1) for j in range(i))
        slot = self.slot + (i * 2 + m) * self.acc.shape[1] + c
        return link.remote(slot, source, self.landing.at[m, c, pl.ds(first, size), :], link.partner(bit))

    def start(self, c, m, i):
        self.copy(c, m, i).start()

    def finish(self, c, m, i):
        size = self.rows >> (i + 1)
        self.copy(c, m, i).wait()
        first = sum(self.rows >> (j + 1) for j in range(i))
        landed = self.landing.at[m, c, pl.ds(first, size), :]
        acc = self.acc.at[m, c]
        if i == 0:
            mine = self.link.bit(self.orders[m][0]) * size
            add_rows(acc, 0, self.sent.at[m, lax.rem(c, 2)], mine, landed, size)
        else:
            at = self.inside(m, i)
            add_rows(acc, at, acc, at, landed, size)


MIDDLE_SEMS = 96
MIDDLE_TICKS = {3: ((1, 1),), 5: ((0, 2), (0, 3)), 7: ((1, 2), (1, 3))}


def middle_kernel(
    dp_size,
    tp_size,
    vec,
    bup_all,
    xhat_hbm,
    out_grad_hbm,
    own_up,
    own_dn,
    ups,
    downs,
    layer_hbm,
    dnorm,
    part_vec,
    ff_landed,
    ff_near,
    ff_far,
    ff_own,
    whole,
    xhat,
    layer_out,
    out_grad,
    nb,
    act,
    slope,
    d_branch,
    d_acc,
    sent,
    acc,
    landing,
    send_sems,
    recv_sems,
    local_sems,
):
    link = Link(dp_size, tp_size, send_sems, recv_sems)
    rows, width = xhat.shape
    used = [0]

    def local(source, target):
        copy = pltpu.make_async_copy(source, target, local_sems.at[used[0]])
        used[0] += 1
        copy.start()
        return copy

    collect = WeightCollect(link, width // 2, lambda k: whole.at[1, k])
    xhat_load = local(xhat_hbm, xhat)
    up_last = WeightCollect(link, width // 2, lambda k: whole.at[0, k])
    placed = [
        local(ups.at[1, up_last.rows(h, 1), :], whole.at[0, 2, up_last.rows(h, 1), :]) for h in range(2)
    ]
    placed += [
        local(downs.at[1, collect.rows(h, 0), :], whole.at[1, 2, collect.rows(h, 0), :]) for h in range(2)
    ]
    owns = [local(own_up, whole.at[0, 0])]
    owns += [local(ups.at[k - 1], whole.at[0, k]) for k in (1, 3)]
    owns += [local(own_dn, whole.at[1, 0])] + [local(downs.at[k - 1], whole.at[1, k]) for k in (1, 3)]
    owns.append(local(out_grad_hbm, out_grad))
    link.greet(link.low)
    for copy in placed:
        copy.wait()
    collect.step(2, 0)
    for copy in up_last.copies(2, 1):
        copy.start()
    xhat_load.wait()
    gain, shift, b_down, f_gain, f_shift = (vec[n : n + 1, :] for n in (4, 5, 6, 7, 8))
    block = min(BLOCK_M, rows)
    count = rows // block
    big = rows // 2

    def norm(step, carry):
        here = place(step, block)
        nb[here, :] = (xhat[here, :] * gain + shift).astype(BF)
        return carry

    lax.fori_loop(0, count, norm, 0)
    for copy in owns[: tp_size - 1]:
        copy.wait()

    def forward(step, carry):
        n = lax.div(step, 2)
        k = n + lax.div(n, 2) * (7 - 2 * n - 2)
        here, cols = place(lax.rem(step, 2), big), place(k, width)
        pre = dot(nb[here, :], whole[0, k], 1, 0) + bup_all[link.behind(k), 0:1, :]
        cdf = 0.5 * (1.0 + lax.erf(pre * 0.7071067811865476))
        act[here, cols] = (pre * cdf).astype(BF)
        slope[here, cols] = (cdf + pre * (jnp.exp(pre * pre * -0.5) * 0.3989422804014327)).astype(BF)
        for n, ticks in MIDDLE_TICKS.items():

            @pl.when(step == n)
            def _():
                for m, j in ticks:
                    (up_last, collect)[m].step(2, j)

        return carry

    lax.fori_loop(0, 2 * tp_size, forward, 0)
    for copy in owns[tp_size - 1 :]:
        copy.wait()

    def second_norm(step, carry):
        g_gain, g_shift, g_down = carry
        here = place(step, block)
        branch = dot(act[here, 0:width], whole[1, 0], 1, 0)
        for k in range(1, tp_size):
            branch = branch + dot(act[here, k * width : (k + 1) * width], whole[1, k], 1, 0)
        res = xhat[here, :] * gain + shift + (branch + b_down)
        center = res - jnp.mean(res, axis=-1, keepdims=True)
        inverse = lax.rsqrt(jnp.mean(center * center, axis=-1, keepdims=True) + 1e-05)
        hat = center * inverse
        layer_out[here, :] = (hat * f_gain + f_shift).astype(BF)
        grad = out_grad[here, :].astype(F32)
        g_gain = g_gain + jnp.sum(grad * hat, axis=0, keepdims=True)
        g_shift = g_shift + jnp.sum(grad, axis=0, keepdims=True)
        scaled = grad * f_gain
        d_res = inverse * (
            scaled
            - jnp.mean(scaled, axis=-1, keepdims=True)
            - hat * jnp.mean(scaled * hat, axis=-1, keepdims=True)
        )
        d_acc[here, :] = d_res
        rounded = d_res.astype(BF)
        d_branch[here, :] = rounded
        g_down = g_down + jnp.sum(rounded.astype(F32), axis=0, keepdims=True)
        return g_gain, g_shift, g_down

    zero = jnp.zeros((1, width), F32)
    g_gain, g_shift, g_down = lax.fori_loop(0, count, second_norm, (zero, zero, zero))
    layer_store = local(layer_out, layer_hbm)
    part_vec[...] = jnp.zeros_like(part_vec)
    part_vec[6:7, :] = g_gain
    part_vec[7:8, :] = g_shift
    part_vec[8:9, :] = g_down

    spread = ChunkSpread(link, width, sent, acc, landing)
    third = width // GRAD_SPLIT

    def weight_grad(left, first, right, cols, target):
        for m in range(GRAD_SPLIT):
            mine = pl.ds(pl.multiple_of(first + m * third, third), third)
            target[m * third : (m + 1) * third, :] = dot(left[:, mine], right[:, cols], 0, 0).astype(BF)

    def settle(n, steps):
        for m, late, stage in steps:

            @pl.when(n >= late)
            def _():
                spread.finish(n - late, m, stage)

            if stage < 2:

                @pl.when(jnp.logical_and(n >= late, n - late < 3 - stage))
                def _():
                    spread.start(n - late, m, stage + 1)

    def backward(n, carry):
        k = 2 - n + lax.div(n, 2) * (7 - 2 * n)
        cols = place(k, width)
        slot = lax.rem(n, 2)
        weight_grad(act, k * width, d_branch, slice(0, width), sent.at[1, slot])
        spread.start(n, 1, 0)
        settle(n, ((0, 1, 0), (1, 2, 1)))

        def through(step, total):
            here = place(step, big)
            grad = (dot(d_branch[here, :], whole[1, k], 1, 1) * slope[here, cols].astype(F32)).astype(BF)
            slope[here, cols] = grad
            return total + jnp.sum(grad.astype(F32), axis=0, keepdims=True)

        part_vec[pl.ds(9 + link.behind(k), 1), :] = lax.fori_loop(0, 2, through, zero)
        settle(n, ((1, 0, 0), (0, 2, 1)))
        weight_grad(nb, 0, slope, cols, sent.at[0, slot])
        spread.start(n, 0, 0)
        return carry

    lax.fori_loop(0, tp_size, backward, 0)

    def input_grad(step, carry):
        here = place(step, big)
        total = d_acc[here, :]
        for k in range(tp_size):
            total = total + dot(slope[here, k * width : (k + 1) * width], whole[0, k], 1, 1)
        d_acc[here, :] = total
        return carry

    slot = link.take(2)
    crossing = []
    lax.fori_loop(0, 1, input_grad, 0)
    for m in (1, 0):
        spread.finish(0, m, 2)
        at = rows_at(spread.inside(m, 2), width >> 3, 16)
        crossing.append(
            link.remote(slot + m, acc.at[m, 0, at, :], ff_landed.at[m], (link.dp, link.behind(2)))
        )
        crossing[-1].start()
    spread.finish(3, 0, 0)
    spread.finish(2, 1, 1)
    stores = [local(acc.at[m, 3], ff_own.at[m]) for m in range(2)]
    lax.fori_loop(1, 2, input_grad, 0)
    stores.append(local(d_acc, dnorm))
    spread.finish(2, 0, 1)
    for m in (1, 0):
        spread.finish(1, m, 2)
    for m in range(2):
        at = rows_at(spread.inside(m, 2), width >> 3, 16)
        stores.append(local(acc.at[m, 1, at, :], ff_near.at[m]))
        at = rows_at(spread.inside(m, 1), width >> 2, 16)
        stores.append(local(acc.at[m, 2, at, :], ff_far.at[m]))
    for copy in crossing + stores + [layer_store]:
        copy.wait()


def middle(mesh, vec, bup_all, xhat, out_grad, w_up, w_dn, ups, downs):
    dp_size, tp_size = mesh.shape["dp"], mesh.shape["tp"]
    low = min(3, dp_size.bit_length() - 1)
    assert low == 3 and tp_size == 4
    rows, width = xhat.shape
    hidden = tp_size * width
    vmem = pl.BlockSpec(memory_space=pltpu.VMEM)
    hbm = pl.BlockSpec(memory_space=pltpu.HBM)
    shape = jax.ShapeDtypeStruct

    def buf(*dims, dtype=BF):
        return pltpu.VMEM(dims, dtype)

    return pl.pallas_call(
        functools.partial(middle_kernel, dp_size, tp_size),
        out_shape=(
            shape((rows, width), BF),
            shape((rows, width), F32),
            shape((VECTORS, width), F32),
            shape((2, width >> 3, width), BF),
            shape((2, width >> 3, width), BF),
            shape((2, width >> 2, width), BF),
            shape((2, width >> 1, width), BF),
        ),
        in_specs=[vmem] * 2 + [hbm] * 6,
        out_specs=(hbm, hbm, vmem, hbm, hbm, hbm, hbm),
        scratch_shapes=[
            buf(2, tp_size, width, width),
            buf(rows, width, dtype=F32),
            buf(rows, width),
            buf(rows, width),
            buf(rows, width),
            buf(rows, hidden),
            buf(rows, hidden),
            buf(rows, width),
            buf(rows, width, dtype=F32),
            buf(2, 2, width, width),
            buf(2, tp_size, width // 2, width),
            buf(2, tp_size, sum(width >> (i + 1) for i in range(low)), width),
            pltpu.SemaphoreType.DMA((MIDDLE_SEMS,)),
            pltpu.SemaphoreType.DMA((MIDDLE_SEMS,)),
            pltpu.SemaphoreType.DMA((32,)),
        ],
        compiler_params=pltpu.CompilerParams(
            collective_id=2, has_side_effects=True, vmem_limit_bytes=VMEM_LIMIT
        ),
        name="middle",
    )(vec, bup_all, xhat, out_grad, w_up, w_dn, ups, downs)


def finish_kernel(
    tp_size, ff, gq, go, gkv, seq, vec, layer_out, grad_in,
    o_up, o_dn, o_q, o_o, o_k, o_v, o_seq, o_layer, o_grad, *rest,
):
    vectors, (in_up, in_dn, in_q, in_o, in_kv, in_seq, f_up, f_dn, f_q, f_o, f_k, f_v, f_seq, turn, pass_a, pass_b, in_sems, out_sems) = rest[:10], rest[10:]
    pairs = [(gq, in_q), (go, in_o), (ff.at[0], in_up), (ff.at[1], in_dn), (gkv, in_kv), (seq, in_seq), (layer_out, pass_a), (grad_in, pass_b)]
    loads = []
    for n, (source, target) in enumerate(pairs):
        loads.append(pltpu.make_async_copy(source, target, in_sems.at[n]))
        loads[-1].start()
    stores = []

    def put(staged, out):
        copy = pltpu.make_async_copy(staged, out, out_sems.at[len(stores)])
        copy.start()
        stores.append(copy)

    for n, (held, out) in enumerate(((pass_a, o_layer), (pass_b, o_grad))):
        loads[6 + n].wait()
        put(held, out)
    for n, row in enumerate((0, 1, 2, 3, 4, 5, 6, 7, 8)):
        vectors[n][...] = vec[row, :]
    vectors[9][...] = vec[pl.ds(9 + lax.axis_index("tp"), 1), :][0]
    width = gq.shape[0]
    for n, (narrow, wide, out) in enumerate(
        ((in_q, f_q, o_q), (in_o, f_o, o_o), (in_up, f_up, o_up), (in_dn, f_dn, o_dn))
    ):
        loads[n].wait()
        wide[...] = narrow[...].astype(F32)
        put(wide, out)
    loads[4].wait()
    owned = width // tp_size
    for n, (wide, out) in enumerate(((f_k, o_k), (f_v, o_v))):
        for c in range(tp_size):
            turn[c * owned : (c + 1) * owned, :] = in_kv[c, n * owned : (n + 1) * owned, :]
        for c in range(3):
            cols = slice(c * (width // 3), (c + 1) * (width // 3))
            wide[:, cols] = turn[cols, :].astype(F32).T
        put(wide, out)
    loads[5].wait()
    rows = in_seq.shape[2]
    for c in range(tp_size):
        f_seq[:, c * rows : (c + 1) * rows] = in_seq[c].astype(F32)
    put(f_seq, o_seq)
    for copy in stores:
        copy.wait()


def finish(tp_size, ff, gq, go, gkv, seq, vec, layer_out, grad_in):
    width = gq.shape[0]
    _, slots, rows = seq.shape
    square, flat = (width, width), (slots, tp_size * rows)
    vmem = pl.BlockSpec(memory_space=pltpu.VMEM)
    hbm = pl.BlockSpec(memory_space=pltpu.HBM)
    shape = jax.ShapeDtypeStruct
    return pl.pallas_call(
        functools.partial(finish_kernel, tp_size),
        out_shape=tuple([shape(square, F32)] * 6 + [shape(flat, F32)] + [shape(layer_out.shape, BF)] * 2 + [shape((width,), F32)] * 10),
        in_specs=[hbm] * 5 + [vmem] + [hbm] * 2,
        out_specs=tuple([hbm] * 9 + [vmem] * 10),
        scratch_shapes=[pltpu.VMEM(square, BF)] * 4
        + [pltpu.VMEM(gkv.shape, BF), pltpu.VMEM(seq.shape, BF)]
        + [pltpu.VMEM(square, F32)] * 6
        + [pltpu.VMEM(flat, F32), pltpu.VMEM(square, BF)]
        + [pltpu.VMEM(layer_out.shape, BF)] * 2
        + [pltpu.SemaphoreType.DMA((8,)), pltpu.SemaphoreType.DMA((9,))],
        compiler_params=pltpu.CompilerParams(vmem_limit_bytes=VMEM_LIMIT),
        name="finish",
    )(ff, gq, go, gkv, seq, vec, layer_out, grad_in)


def on_device(
    mesh,
    layer_in,
    out_grad,
    lengths,
    w_query,
    b_query,
    w_key,
    b_key,
    w_value,
    b_value,
    w_out,
    b_out,
    seq_proj,
    attn_gain,
    attn_shift,
    w_up,
    b_up,
    w_down,
    b_down,
    ffn_gain,
    ffn_shift,
):
    row_count, width = layer_in.shape
    tp_size = mesh.shape["tp"]
    vectors = (b_query, b_key, b_value, b_out, attn_gain, attn_shift, b_down, ffn_gain, ffn_shift)
    vec, bup_all, xhat, rstd, mixed, queries, probs, kb, vb, folded, ssum, own_proj, ups, downs = front(
        mesh, lengths, layer_in, w_query, seq_proj, w_key, w_value, w_out, w_up, w_down, vectors, b_up
    )
    layer_out, d_normed, part_vec, ff_landed, ff_near, ff_far, ff_own = middle(
        mesh, vec, bup_all, xhat, out_grad, w_up, w_down, ups, downs
    )
    grad_in, g_ff, g_o, g_q, g_kv, g_seq, vec_sum = back(
        mesh, lengths, vec, part_vec, ff_near, d_normed, probs, ff_far, ff_own, xhat, rstd, mixed, w_out, ff_landed,
        layer_in, queries, kb, vb, folded, ssum, own_proj, w_query, w_key, w_value
    )
    (
        g_w_up, g_w_down, g_w_query, g_w_out, g_w_key, g_w_value, g_seq_proj, layer_out, grad_in,
        g_b_query, g_b_key, g_b_value, g_b_out, g_attn_gain, g_attn_shift, g_ffn_gain, g_ffn_shift, g_b_down, g_b_up,
    ) = finish(tp_size, g_ff, g_q, g_o, g_kv, g_seq, vec_sum, layer_out, grad_in)
    return (
        layer_out,
        grad_in,
        g_w_query,
        g_b_query,
        g_w_key,
        g_b_key,
        g_w_value,
        g_b_value,
        g_w_out,
        g_b_out,
        g_seq_proj,
        g_attn_gain,
        g_attn_shift,
        g_w_up,
        g_b_up,
        g_w_down,
        g_b_down,
        g_ffn_gain,
        g_ffn_shift,
    )


def solution(mesh):
    in_specs = (
        P(("dp", "tp"), None),
        P(("dp", "tp"), None),
        P("dp"),
        *([P()] * 11),
        P(None, "tp"),
        P("tp"),
        P("tp", None),
        P(),
        P(),
        P(),
    )
    out_specs = (
        P(("dp", "tp"), None),
        P(("dp", "tp"), None),
        *([P()] * 11),
        P(None, "tp"),
        P("tp"),
        P("tp", None),
        P(),
        P(),
        P(),
    )
    return jax.shard_map(
        functools.partial(on_device, mesh), mesh=mesh, in_specs=in_specs, out_specs=out_specs, check_vma=False
    )
```

```python
import functools

import jax
import jax.numpy as jnp
from jax import lax
from jax.experimental import pallas as pl
from jax.experimental.pallas import tpu as pltpu
from jax.sharding import PartitionSpec as P

HEADS = 12
HEAD = 64
PAIRS = HEADS // 2
PAIR = 2 * HEAD
BF = jnp.bfloat16
F32 = jnp.float32
MESH = pl.DeviceIdType.MESH
VMEM_LIMIT = 67_043_328
BLOCK_F, BLOCK_M, BLOCK_B, GRAD_SPLIT = 1024, 512, 1024, 2


def dot(left, right, left_dim, right_dim):
    return lax.dot_general(
        left, right, (((left_dim,), (right_dim,)), ((), ())), preferred_element_type=F32
    )


def place(index, size):
    return pl.ds(pl.multiple_of(index * size, size), size)


def rows_at(first, size, multiple):
    return pl.ds(pl.multiple_of(first, multiple), size)


class Link:
    def __init__(self, dp_size, tp_size, send_sems, recv_sems):
        self.dp_size, self.tp_size = dp_size, tp_size
        self.dp, self.tp = lax.axis_index("dp"), lax.axis_index("tp")
        self.bits = dp_size.bit_length() - 1
        self.low = min(3, self.bits)
        self.send_sems, self.recv_sems = send_sems, recv_sems
        self.used = 0
        self.bit_values = [lax.rem(lax.div(self.dp, 1 << b), 2) for b in range(self.bits)]
        self.partners = [
            (self.dp + (1 - 2 * self.bit_values[b]) * (1 << b), self.tp) for b in range(self.bits)
        ]
        self.aheads = [lax.rem(self.tp + k, tp_size) for k in range(tp_size)]

    def bit(self, b):
        return self.bit_values[b]

    def partner(self, b):
        return self.partners[b]

    def ahead(self, k):
        return self.aheads[k]

    def behind(self, k):
        if isinstance(k, int):
            return self.aheads[(self.tp_size - k) % self.tp_size]
        return lax.rem(self.tp + self.tp_size - k, self.tp_size)

    def greet(self, dp_bits):
        barrier = pltpu.get_barrier_semaphore()
        peers = [(self.dp, self.ahead(k)) for k in range(1, self.tp_size)]
        peers += [self.partner(b) for b in range(dp_bits)]
        for peer in peers:
            pl.semaphore_signal(barrier, inc=1, device_id=peer, device_id_type=MESH)
        pl.semaphore_wait(barrier, len(peers))

    def take(self, count):
        first = self.used
        self.used += count
        assert self.used <= self.send_sems.shape[0]
        return first

    def remote(self, slot, source, target, device):
        return pltpu.make_async_remote_copy(
            src_ref=source,
            dst_ref=target,
            send_sem=self.send_sems.at[slot],
            recv_sem=self.recv_sems.at[slot],
            device_id=device,
            device_id_type=MESH,
        )

    def send(self, source, target, device):
        copy = self.remote(self.take(1), source, target, device)
        copy.start()
        return copy


FRONT_SEMS = 64
VECTORS = 16


def half_orders(low):
    return [[b for b in order if b < low] for order in ((1, 2, 0), (2, 1, 0))]


class WeightCollect:
    def __init__(self, link, part, whole):
        self.link, self.whole, self.part = link, whole, part
        self.orders = half_orders(link.low)
        self.piece = self.part >> link.low
        self.stages = link.low
        self.slot = link.take(2 * (link.tp_size - 1) * link.low)
        self.firsts = []
        for h in range(2):
            first, size, starts = h * part, self.piece, []
            for b in self.orders[h]:
                starts.append(size * link.bit(b))
                size *= 2
            self.firsts.append([sum(starts[i:], first) for i in range(self.stages)])

    def rows(self, h, i):
        return rows_at(self.firsts[h][i], self.piece << i, 16)

    def copies(self, k, i):
        for h in range(2):
            region = self.whole(k).at[self.rows(h, i), :]
            slot = self.slot + ((k - 1) * self.stages + i) * 2 + h
            yield self.link.remote(slot, region, region, self.link.partner(self.orders[h][i]))

    def step(self, k, j):
        if j > 0:
            for copy in self.copies(k, j - 1):
                copy.wait()
        if j < self.stages:
            for copy in self.copies(k, j):
                copy.start()


class Cross:
    def __init__(self, link, collect, shard, target):
        self.link, self.collect, self.shard, self.target = link, collect, shard, target
        self.slot = link.take(2 * (link.tp_size - 1))

    def copies(self, k):
        for h in range(2):
            rows = self.collect.rows(h, 0)
            yield self.link.remote(
                self.slot + 2 * (k - 1) + h,
                self.shard.at[rows, :],
                self.target(k, h, rows),
                (self.link.dp, self.link.ahead(k)),
            )

    def start(self, k):
        for copy in self.copies(k):
            copy.start()

    def wait(self, k):
        for copy in self.copies(k):
            copy.wait()


EARLY_TICKS = ((0, 1, 0), (1, 1, 0), (0, 1, 1), (1, 3, 0), (1, 1, 1), (0, 1, 2), (1, 3, 1), (1, 1, 2))
SHARE_TICKS = ((0, 1, 3), (1, 3, 2), (1, 1, 3), (1, 3, 3))
PAIR_TICKS = {1: ((0, 3, 0),), 3: ((0, 3, 1),), 5: ((0, 3, 2), (0, 2, 0))}
LAST_TICKS = ((0, 3, 3), (0, 2, -2), (1, 2, -1))


def front_kernel(dp_size, tp_size, n_vectors, len_ref, x_hbm, wq_hbm, e, wk_hbm, wv_hbm, wo_hbm, wup, wdn, *rest):
    vectors, b_up, rest = rest[:n_vectors], rest[n_vectors], rest[n_vectors + 1 :]
    outs, scratch = rest[:14], rest[14:]
    (vec, bup_all, xhat_out, rstd_out, mixed_out, q_out, probs_out, kb_out, vb_out, yb_out, ssum_out, em_out, ups, downs) = outs
    (x, wq, wk, wv, wo, e_all, xhat, rstd, mixed, q, probs, kb, vb, yb, ssum, em, bup, ysend, yrecv, send_sems, recv_sems, local_sems) = scratch
    link = Link(dp_size, tp_size, send_sems, recv_sems)
    rows, width = x.shape
    slots, total = e_all.shape
    quarter = slots // tp_size
    others = range(1, tp_size)
    used = [0]

    def local(source, target):
        copy = pltpu.make_async_copy(source, target, local_sems.at[used[0]])
        used[0] += 1
        copy.start()
        return copy

    own_first = link.tp * rows
    e_own = local(e.at[:, rows_at(own_first, rows, rows)], em)
    early = [local(x_hbm, x), local(wq_hbm, wq)]
    late = [local(e, e_all), local(wk_hbm, wk), local(wv_hbm, wv), local(wo_hbm, wo)]
    link.greet(link.low)

    collect = WeightCollect(link, wup.shape[0] // 2, lambda k: ups.at[k - 1])
    cross = Cross(link, collect, wup, lambda k, h, rows: ups.at[k - 1, rows, :])
    cross_down = Cross(link, collect, wdn, lambda k, h, rows: downs.at[k - 1, rows, :])
    collect_down = WeightCollect(link, wdn.shape[0] // 2, lambda k: downs.at[k - 1])
    def tick(ticks):
        for m, k, j in ticks:
            if -1 <= j <= 0:
                (cross, cross_down)[m].wait(k)
            if j == -2:
                for copy in (collect, collect_down)[m].copies(k, 0):
                    copy.wait()
            elif j >= 0:
                (collect, collect_down)[m].step(k, j)

    cross.start(1)
    cross_down.start(1)
    cross_down.start(3)
    vec[...] = jnp.zeros_like(vec)
    for n, vector in enumerate(vectors):
        vec[n : n + 1, :] = vector[...].astype(F32).reshape(1, width)
    bup[...] = jnp.broadcast_to(b_up[...].astype(F32).reshape(1, width), bup.shape)
    bup_all[link.tp] = bup[...]
    length = len_ref[0]
    position = lax.broadcasted_iota(jnp.int32, (1, rows), 1) + own_first
    live = (position < length).astype(F32)
    e_own.wait()
    early[0].wait()
    em[...] = (em[...].astype(F32) * live).astype(BF)
    ysend[...] = dot(em[...], x[...], 1, 0).astype(ysend.dtype)
    reduce = [
        link.send(ysend.at[place(link.ahead(k), quarter), :], yrecv.at[k - 1], (link.dp, link.ahead(k)))
        for k in others
    ]
    biases = [link.send(bup, bup_all.at[link.tp], (link.dp, link.ahead(k))) for k in others]
    early[1].wait()
    q[...] = (dot(x[...], wq[...], 1, 0) + vec[0:1, :]).astype(BF)
    tick(EARLY_TICKS)
    own_slots = place(link.tp, quarter)
    for copy in reduce:
        copy.wait()
    own_y = ysend[own_slots, :].astype(F32)
    for k in others:
        own_y = own_y + yrecv[k - 1].astype(F32)
    yb[own_slots, :] = own_y.astype(BF)
    share = [
        link.send(yb.at[own_slots, :], yb.at[own_slots, :], (link.dp, link.ahead(k))) for k in others
    ]
    for k in (3, 2):
        cross.start(k)
    cross_down.start(2)
    tick(SHARE_TICKS)
    stores = [local(q, q_out), local(em, em_out)]
    row_live = (lax.broadcasted_iota(jnp.int32, (total, 128), 0) < length).astype(F32).astype(BF)
    for load in late:
        load.wait()
    ssum[...] = dot(e_all[...], row_live, 1, 0)
    for copy in share:
        copy.wait()
    for copy in biases:
        copy.wait()
    stores += [local(yb, yb_out), local(ssum, ssum_out)]

    lane = lax.broadcasted_iota(jnp.int32, (1, PAIR), 1)
    first_half = (lane < HEAD).astype(F32)

    def project(weight, bias_row, blocks):
        full = dot(yb[...], weight[...], 1, 0)
        for p in range(PAIRS):
            cols = slice(p * PAIR, (p + 1) * PAIR)
            both = full[:, cols] + ssum[...] * vec[bias_row : bias_row + 1, cols]
            blocks[p, 0:slots, :] = (both * first_half).astype(BF)
            blocks[p, slots : 2 * slots, :] = (both * (1.0 - first_half)).astype(BF)

    project(wk, 1, kb)
    project(wv, 2, vb)
    stores += [local(kb, kb_out), local(vb, vb_out)]

    block = min(BLOCK_F, rows)
    per_pair = rows // block
    probs_sem = used[0]

    def attend(p, carry):
        cols = place(p, PAIR)

        def one(step, carry):
            here = place(step, block)
            logits = dot(q[here, cols], kb[p], 1, 1) * 0.125
            halves = []
            for half in range(2):
                part = logits[:, half * slots : (half + 1) * slots]
                peak = jnp.max(part, axis=-1, keepdims=True)
                raised = jnp.exp(part - peak)
                halves.append((raised * (1.0 / jnp.sum(raised, axis=-1, keepdims=True))).astype(BF))
            both = jnp.concatenate(halves, axis=1)
            probs[p, here, :] = both
            mixed[here, cols] = dot(both, vb[p], 1, 0).astype(BF)
            return carry

        lax.fori_loop(0, per_pair, one, 0)
        pltpu.make_async_copy(probs.at[p], probs_out.at[p], local_sems.at[probs_sem + p]).start()
        for n, ticks in PAIR_TICKS.items():

            @pl.when(p == n)
            def _():
                tick(ticks)

        return carry

    lax.fori_loop(0, PAIRS, attend, 0)
    used[0] += PAIRS
    stores.append(local(mixed, mixed_out))

    def finish(step, carry):
        here = place(step, block)
        res = x[here, :].astype(F32) + dot(mixed[here, :], wo[...], 1, 0) + vec[3:4, :]
        center = res - jnp.mean(res, axis=-1, keepdims=True)
        inverse = lax.rsqrt(jnp.mean(center * center, axis=-1, keepdims=True) + 1e-05)
        xhat[here, :] = center * inverse
        rstd[here, :] = jnp.broadcast_to(inverse, (block, 128))
        return carry

    lax.fori_loop(0, per_pair, finish, 0)
    stores += [local(xhat, xhat_out), local(rstd, rstd_out)]
    tick(LAST_TICKS)
    for copy in stores:
        copy.wait()
    for p in range(PAIRS):
        pltpu.make_async_copy(probs.at[p], probs_out.at[p], local_sems.at[probs_sem + p]).wait()


def front(mesh, lengths, x, wq, e, wk, wv, wo, wup, wdn, vectors, b_up):
    dp_size, tp_size = mesh.shape["dp"], mesh.shape["tp"]
    low = min(3, dp_size.bit_length() - 1)
    rows, width = x.shape
    slots = e.shape[0]
    vmem = pl.BlockSpec(memory_space=pltpu.VMEM)
    hbm = pl.BlockSpec(memory_space=pltpu.HBM)
    shape = jax.ShapeDtypeStruct
    moved = (
        ((rows, width), F32),
        ((rows, 128), F32),
        ((rows, width), BF),
        ((rows, width), BF),
        ((PAIRS, rows, 2 * slots), BF),
        ((PAIRS, 2 * slots, PAIR), BF),
        ((PAIRS, 2 * slots, PAIR), BF),
        ((slots, width), BF),
        ((slots, 128), F32),
        ((slots, rows), BF),
    )
    kept = (
        ((VECTORS, width), F32),
        ((tp_size, 8, width), F32),
    )
    return pl.pallas_call(
        functools.partial(front_kernel, dp_size, tp_size, len(vectors)),
        out_shape=tuple(shape(*s) for s in kept + moved)
        + (
            shape((tp_size - 1, *wup.shape), BF),
            shape((tp_size - 1, *wdn.shape), BF),
        ),
        in_specs=[pl.BlockSpec(memory_space=pltpu.SMEM)]
        + [hbm] * 8
        + [vmem] * (len(vectors) + 1),
        out_specs=tuple([vmem] * len(kept) + [hbm] * (len(moved) + 2)),
        scratch_shapes=[pltpu.VMEM(w.shape, BF) for w in (x, wq, wk, wv, wo, e)]
        + [pltpu.VMEM(*s) for s in moved]
        + [
            pltpu.VMEM((8, width), F32),
            pltpu.VMEM((slots, width), BF),
            pltpu.VMEM((tp_size - 1, slots // tp_size, width), BF),
            pltpu.SemaphoreType.DMA((FRONT_SEMS,)),
            pltpu.SemaphoreType.DMA((FRONT_SEMS,)),
            pltpu.SemaphoreType.DMA((32,)),
        ],
        compiler_params=pltpu.CompilerParams(
            collective_id=0, has_side_effects=True, vmem_limit_bytes=VMEM_LIMIT
        ),
        name="front",
    )(lengths, x, wq, e, wk, wv, wo, wup, wdn, *vectors, b_up)


BACK_SEMS = 128
VECTORS = 16


def add_rows(target, first, left, left_first, right, count):
    block = 96 if count % 96 == 0 else (48 if count % 48 == 0 else (32 if count % 32 == 0 else count))

    def step(i, carry):
        at = i * block
        total = (
            left[rows_at(left_first + at, block, 16), :].astype(F32)
            + right[rows_at(at, block, 16), :].astype(F32)
        )
        target[rows_at(first + at, block, 16), :] = total.astype(target.dtype)
        return carry

    lax.fori_loop(0, count // block, step, 0)


class Spread:
    def __init__(self, link, order, rows, source, acc, landing):
        self.link, self.rows, self.source, self.acc, self.landing = link, rows, source, acc, landing
        self.order = [b for b in order if b < link.low]
        self.stages = len(self.order)
        self.slot = link.take(self.stages)
        self.piece = rows >> self.stages
        self.insides, self.others, first = [0], [(1 - link.bit(self.order[0])) * (rows >> 1)], 0
        for j in range(1, self.stages):
            size = rows >> (j + 1)
            self.others.append(first + (1 - link.bit(self.order[j])) * size)
            first = first + link.bit(self.order[j]) * size
            self.insides.append(first)
        self.at = link.bit(self.order[0]) * (rows >> 1) + first

    def inside(self, i):
        return self.insides[i]

    def kept(self):
        return rows_at(self.inside(self.stages - 1), self.piece, 16)

    def offset(self):
        return self.at

    def landed(self, i):
        first = sum(self.rows >> (j + 1) for j in range(i))
        return self.landing.at[pl.ds(first, self.rows >> (i + 1)), :]

    def copy(self, i):
        link, size = self.link, self.rows >> (i + 1)
        where, other = self.source if i == 0 else self.acc, self.others[i]
        return link.remote(
            self.slot + i, where.at[rows_at(other, size, 16), :], self.landed(i), link.partner(self.order[i])
        )

    def start(self, i):
        self.copy(i).start()

    def finish(self, i):
        size = self.rows >> (i + 1)
        self.copy(i).wait()
        if i == 0:
            add_rows(self.acc, 0, self.source, self.link.bit(self.order[0]) * size, self.landed(0), size)
        else:
            at = self.inside(i)
            add_rows(self.acc, at, self.acc, at, self.landed(i), size)

    def steps(self):
        yield lambda: self.start(0)
        for i in range(1, self.stages):

            def step(i=i):
                self.finish(i - 1)
                self.start(i)

            yield step


class Collect:
    def __init__(self, link, order, offset, piece, region):
        self.link, self.offset, self.piece, self.region = link, offset, piece, region
        self.order = [b for b in order if b < link.low][::-1]
        self.slot = link.take(len(self.order))
        starts, size = [], piece
        for b in self.order:
            starts.append(link.bit(b) * size)
            size *= 2
        self.firsts = [sum(starts[i:], 0) for i in range(len(self.order))]

    def copy(self, i):
        size, first = self.piece << i, self.firsts[i]
        ref = self.region(first, size)
        return self.link.remote(self.slot + i, ref, ref, self.link.partner(self.order[i]))

    def steps(self):
        yield lambda: self.copy(0).start()
        for i in range(1, len(self.order)):

            def step(i=i):
                self.copy(i - 1).wait()
                self.copy(i).start()

            yield step
        yield lambda: self.copy(len(self.order) - 1).wait()


class Widen:
    def __init__(self, link, landing):
        self.link, self.landing = link, landing
        self.slot = link.take(max(0, link.bits - link.low))

    def run(self, piece):
        link = self.link
        for i, b in enumerate(range(link.low, link.bits)):
            copy = link.remote(self.slot + i, piece, self.landing.at[i], link.partner(b))
            copy.start()
            copy.wait()
            piece[...] = (piece[...].astype(F32) + self.landing[i].astype(F32)).astype(piece.dtype)


class Fan:
    def __init__(self, link, ends):
        self.link, self.ends = link, ends
        self.slot = link.take(link.tp_size - 1)

    def copy(self, k):
        source, target = self.ends(k)
        return self.link.remote(self.slot + k - 1, source, target, (self.link.dp, self.link.ahead(k)))

    def start(self):
        for k in range(1, self.link.tp_size):
            self.copy(k).start()

    def wait(self):
        for k in range(1, self.link.tp_size):
            self.copy(k).wait()


def then(*actions):
    def both():
        for action in actions:
            action()

    return both


class Track:
    def __init__(self):
        self.todo = []

    def add(self, steps, join=False):
        steps = list(steps)
        if join and self.todo:
            steps[0] = then(self.todo.pop(), steps[0])
        self.todo += steps

    def advance(self):
        if self.todo:
            self.todo.pop(0)()


def back_kernel(
    dp_size,
    tp_size,
    len_ref,
    vec,
    part_vec,
    ff_near,
    dnorm,
    probs,
    far_hbm,
    own_hbm,
    xhat_hbm,
    rstd_hbm,
    mixed_hbm,
    wo_hbm,
    landed_hbm,
    x_hbm,
    q_hbm,
    kb_hbm,
    vb_hbm,
    yb_hbm,
    ssum_hbm,
    em_hbm,
    wq_hbm,
    wk_hbm,
    wv_hbm,
    grad_hbm,
    ff_hbm,
    go_hbm,
    gq_out,
    gkv_out,
    seq_out,
    vec_out,
    grad_in,
    ff_out,
    go_out,
    ff_far,
    ff_own,
    xhat,
    rstd,
    mixed,
    wo,
    ff_landed,
    x,
    q,
    kb,
    vb,
    yb,
    ssum,
    em,
    wq,
    wk,
    wv,
    dres,
    dmix,
    dq,
    dl,
    prob_slots,
    dpart,
    dland,
    dcross,
    dfull,
    ff_zland,
    far_acc,
    far_land,
    own_acc,
    own_land,
    o_acc,
    o_land,
    q_acc,
    q_land,
    o_zland,
    q_zland,
    kv_send,
    kv_acc,
    kv_land,
    s_send,
    s_acc,
    s_land,
    vec_acc,
    vec_land,
    vec_z,
    wide_ff,
    wide_q,
    wide_kv,
    wide_s,
    send_sems,
    recv_sems,
    local_sems,
):
    link = Link(dp_size, tp_size, send_sems, recv_sems)
    rows, width = x.shape
    slots = yb.shape[0]
    low = link.low
    others = range(1, tp_size)
    first_load = pltpu.make_async_copy(dnorm, dres, local_sems.at[0])
    first_load.start()
    late = []
    for n, (source, target) in enumerate(
        (
            (far_hbm, ff_far), (own_hbm, ff_own), (xhat_hbm, xhat), (rstd_hbm, rstd), (mixed_hbm, mixed),
            (wo_hbm, wo), (landed_hbm, ff_landed), (q_hbm, q), (kb_hbm, kb), (vb_hbm, vb), (x_hbm, x), (yb_hbm, yb),
            (wq_hbm, wq), (wk_hbm, wk), (wv_hbm, wv), (ssum_hbm, ssum), (em_hbm, em),
        )
    ):
        late.append(pltpu.make_async_copy(source, target, local_sems.at[3 + n]))
        late[-1].start()
    link.greet(link.bits)

    lanes = 2
    deep = tp_size // lanes
    third = width // GRAD_SPLIT
    owned = width // tp_size

    ff_track, ff_orders = Track(), ((0, 1, 2), (0, 2, 1))
    ff_rows = width >> 3
    ff_parts = []
    for m in range(2):
        first, second, third_bit = ff_orders[m]
        far = Spread(link, (third_bit,), width >> 2, ff_far.at[m], far_acc.at[m], far_land.at[m])
        own = Spread(link, (second, third_bit), width >> 1, ff_own.at[m], own_acc.at[m], own_land.at[m])
        slot = link.take(2)

        def piece_copy(n, m=m, slot=slot):
            source, k = ((far_acc, 3), (ff_near, 1))[n]
            return link.remote(slot + n, source.at[m], ff_zland.at[m, n], (link.dp, link.behind(k)))

        at = link.bit(ff_orders[m][0]) * (width >> 1) + own.offset()

        def offset(at=at):
            return at

        widen = Widen(link, wide_ff.at[m])

        def join(m=m, own=own, piece_copy=piece_copy, offset=offset, widen=widen):
            total = own_acc[m, own.kept(), :].astype(F32) + ff_landed[m].astype(F32)
            for n in range(2):
                piece_copy(n).wait()
                total = total + ff_zland[m, n].astype(F32)
            mine = rows_at(offset(), ff_rows, 16)
            ff_out[m, mine, :] = total.astype(BF)
            widen.run(ff_out.at[m, mine, :])

        collect = Collect(
            link, ff_orders[m], offset, ff_rows,
            lambda first, size, m=m: ff_out.at[m, rows_at(first, size, 16), :],
        )
        ff_parts.append((far, own, piece_copy, join, list(collect.steps())))

    def ff_begin():
        for far, own, piece_copy, _, _ in ff_parts:
            far.start(0)
            own.start(0)
            piece_copy(1).start()

    def ff_second():
        for far, own, piece_copy, _, _ in ff_parts:
            far.finish(0)
            piece_copy(0).start()

    def ff_second_own():
        for far, own, piece_copy, _, _ in ff_parts:
            own.finish(0)
            own.start(1)

    def ff_third():
        for _, own, _, join, collects in ff_parts:
            own.finish(1)

    def ff_join():
        for _, _, _, join, collects in ff_parts:
            join()
            collects[0]()

    stores = []

    def store(n, source, target):
        copy = pltpu.make_async_copy(source, target, local_sems.at[20 + n])
        stores.append(copy)
        return copy

    ff_store, go_store, grad_store = store(0, ff_out, ff_hbm), store(1, go_out, go_hbm), store(2, grad_in, grad_hbm)
    late[0].wait()
    late[1].wait()
    ff_begin()
    ff_track.add([ff_second, ff_second_own, then(ff_third, ff_join)])
    ff_track.add([then(*pair) for pair in zip(ff_parts[0][4][1:], ff_parts[1][4][1:])])
    ff_track.add([ff_store.start], join=True)

    def square_track(out, acc, landing, zland, wide):
        track, spreads, collects = Track(), [], []
        q_cols = width // lanes
        for h, order in enumerate(((0, 1, 2), (0, 2, 1))):
            cols = slice(h * q_cols, (h + 1) * q_cols)
            spread = Spread(link, order, width, out.at[:, cols], acc.at[:, cols], landing.at[:, cols])
            spreads.append(spread)
            collects.append(
                Collect(
                    link, order, spread.offset, spread.piece,
                    lambda first, size, cols=cols: out.at[rows_at(first, size, 16), cols],
                )
            )
        q_rows = spreads[0].piece // deep
        halves = [lax.rem(t, lanes) for t in link.aheads]

        def quarter(firsts, k):
            first = firsts[0] + halves[k] * (firsts[1] - firsts[0]) + lax.div(link.aheads[k], lanes) * q_rows
            return rows_at(first, q_rows, 16), pl.ds(pl.multiple_of(halves[k] * q_cols, 128), q_cols)

        inner = [quarter([spread.inside(spread.stages - 1) for spread in spreads], k) for k in range(tp_size)]
        mine = quarter([spread.offset() for spread in spreads], 0)
        fan = Fan(link, lambda k: (acc.at[inner[k]], zland.at[k - 1]))
        share, widen = Fan(link, lambda k: (out.at[mine], out.at[mine])), Widen(link, wide)

        def join():
            fan.wait()
            total = acc[inner[0]].astype(F32)
            for k in others:
                total = total + zland[k - 1].astype(F32)
            out[mine] = total.astype(BF)
            widen.run(out.at[mine])
            share.start()

        def summed():
            for spread in spreads:
                spread.finish(spread.stages - 1)
            fan.start()

        track.add([then(*pair) for pair in zip(spreads[0].steps(), spreads[1].steps())])
        track.add([summed, join, share.wait])
        track.add([then(*pair) for pair in zip(collects[0].steps(), collects[1].steps())], join=True)
        return track

    def owned_track(order, total_rows, cols, source, acc, landing, out, wide):
        source, acc, landing = source.at[:, cols], acc.at[:, cols], landing.at[:, cols]
        track, spread = Track(), Spread(link, order, total_rows, source, acc, landing)

        def region(k):
            ref = out.at[link.tp, rows_at(spread.offset(), spread.piece, 16), cols]
            return ref, ref

        share, widen = Fan(link, region), Widen(link, wide)

        def last():
            spread.finish(spread.stages - 1)
            ref = region(0)[0]
            ref[...] = acc[spread.kept(), :]
            widen.run(ref)
            share.start()

        collect = Collect(
            link, order, spread.offset, spread.piece, lambda first, size: out.at[:, rows_at(first, size, 16), cols]
        )
        track.add(spread.steps())
        track.add([last, share.wait])
        track.add(collect.steps(), join=True)
        return track

    o_track = square_track(go_out, o_acc, o_land, o_zland, wide_q.at[0])
    o_track.add([go_store.start], join=True)
    q_track = square_track(gq_out, q_acc, q_land, q_zland, wide_q.at[1])
    def halves(total_rows, source, acc, landing, out, wide):
        tracks = []
        for h, order in enumerate(((0, 1, 2), (0, 2, 1))):
            cols = slice(h * source.shape[1] // 2, (h + 1) * source.shape[1] // 2)
            tracks.append(owned_track(order, total_rows, cols, source, acc, landing, out, wide.at[h]))
        both = Track()
        both.add([then(*pair) for pair in zip(tracks[0].todo, tracks[1].todo)])
        return both

    kv_track = halves(2 * owned, kv_send, kv_acc, kv_land, gkv_out, wide_kv)
    s_track = halves(slots, s_send, s_acc, s_land, seq_out, wide_s)

    vec_track, vec_slot = Track(), link.take(link.bits)
    vec_fan = Fan(link, lambda k: (vec_z.at[link.tp], vec_z.at[link.tp]))

    def vec_copy(b):
        return link.remote(vec_slot + b, vec_acc.at[b], vec_land.at[b], link.partner(b))

    vec_track.add([lambda: vec_copy(0).start()])
    for b in range(link.bits):

        def vec_step(b=b):
            vec_copy(b).wait()
            total = vec_acc[b] + vec_land[b]
            if b + 1 < link.bits:
                vec_acc[b + 1] = total
                vec_copy(b + 1).start()
            else:
                vec_z[link.tp] = total
                vec_fan.start()

        vec_track.add([vec_step])

    def vec_last():
        vec_fan.wait()
        total = vec_z[0]
        for t in range(1, tp_size):
            total = total + vec_z[t]
        vec_out[...] = total

    vec_track.add([vec_last])

    block = min(BLOCK_B, rows)
    count = rows // block
    gain = vec[4:5, :]

    def norm_back(step, carry):
        g_gain, g_shift, g_out = carry
        here = place(step, block)
        grad, hat = dres[here, :], xhat[here, :]
        g_gain = g_gain + jnp.sum(grad * hat, axis=0, keepdims=True)
        g_shift = g_shift + jnp.sum(grad, axis=0, keepdims=True)
        scaled = grad * gain
        d_res = rstd[here, 0:1] * (
            scaled
            - jnp.mean(scaled, axis=-1, keepdims=True)
            - hat * jnp.mean(scaled * hat, axis=-1, keepdims=True)
        )
        dres[here, :] = d_res
        d_attn = d_res.astype(BF)
        dq[here, :] = d_attn
        g_out = g_out + jnp.sum(d_attn.astype(F32), axis=0, keepdims=True)
        return g_gain, g_shift, g_out

    zero = jnp.zeros((1, width), F32)
    first_load.wait()
    late[2].wait()
    late[3].wait()
    g_gain, g_shift, g_out = lax.fori_loop(0, count, norm_back, (zero, zero, zero))
    vec_acc[0] = part_vec[...]
    vec_acc[0, 3:4, :] = g_out
    vec_acc[0, 4:5, :] = g_gain
    vec_acc[0, 5:6, :] = g_shift
    d_attn = dq

    def weight_grad(left, right, target):
        for m in range(GRAD_SPLIT):
            cols = slice(m * third, (m + 1) * third)
            target[cols, :] = dot(left[:, cols], right[...], 0, 0).astype(BF)

    for load in late[4:7]:
        load.wait()
    weight_grad(mixed, d_attn, go_out)
    o_track.advance()
    ff_track.advance()
    dmix[...] = dot(d_attn[...], wo[...], 1, 1).astype(BF)
    o_track.advance()
    for load in late[7:]:
        load.wait()

    own_half = lax.div(link.tp, 2)
    parity = lax.rem(link.tp, 2)
    three = PAIRS // 2

    def pair_at(n):
        second = lax.div(n, three)
        which = (1 - own_half) * (1 - second) + own_half * second
        along = lax.rem(n, three)
        return which * three + along * parity + (three - 1 - along) * (1 - parity)

    def fetch(n):
        slot = lax.rem(n, 2)
        return pltpu.make_async_copy(probs.at[pair_at(n)], prob_slots.at[slot], local_sems.at[1 + slot])

    fetch(0).start()

    def attend_back(n):
        p = pair_at(n)
        cols = place(p, PAIR)

        @pl.when(n + 1 < PAIRS)
        def _():
            fetch(n + 1).start()

        fetch(n).wait()
        held = prob_slots.at[lax.rem(n, 2)]

        def part(step, carry):
            here = place(step, block)
            d_probs = dot(dmix[here, cols], vb[p], 1, 1)
            weights = held[here, :].astype(F32)
            halves = []
            for h in range(2):
                w = weights[:, h * slots : (h + 1) * slots]
                d = d_probs[:, h * slots : (h + 1) * slots]
                halves.append((w * (d - jnp.sum(w * d, axis=-1, keepdims=True))).astype(BF))
            both = jnp.concatenate(halves, axis=1)
            dl[here, :] = both
            dq[here, cols] = (dot(both, kb[p], 1, 0) * 0.125).astype(BF)
            return carry

        lax.fori_loop(0, count, part, 0)
        top, under = rows_at(p * PAIR, HEAD, HEAD), rows_at(p * PAIR + HEAD, HEAD, HEAD)
        for n, total in enumerate(
            (dot(q[:, cols], dl[...], 0, 0) * 0.125, dot(dmix[:, cols], held[...], 0, 0))
        ):
            dpart[n, top, :] = total[:HEAD, :slots].astype(BF)
            dpart[n, under, :] = total[HEAD:, slots:].astype(BF)

    d_slot = link.take(tp_size - 1)
    sibling = 2 * own_half + (1 - parity)
    far_same = rows_at((2 * (1 - own_half) + parity) * owned, owned, 64)
    far_other = rows_at((2 * (1 - own_half) + (1 - parity)) * owned, owned, 64)
    d_peers = [2 * (1 - own_half) + parity, sibling, sibling]
    d_sources = [
        dcross, dpart.at[:, far_other, :], dpart.at[:, rows_at(sibling * owned, owned, 64), :],
    ]

    def d_copy(j):
        return link.remote(d_slot + j, d_sources[j], dland.at[j], (link.dp, d_peers[j]))

    def d_across():
        d_copy(1).wait()
        for n in range(2):
            dcross[n] = (dpart[n, far_same, :].astype(F32) + dland[1, n].astype(F32)).astype(BF)
        d_copy(0).start()

    events = {
        1: lambda: d_copy(1).start(),
        2: ff_track.advance,
        4: lambda: d_copy(2).start(),
        5: then(d_across, o_track.advance),
    }

    def one(n, carry):
        attend_back(n)
        for i, event in events.items():
            pl.when(n == i)(event)
        return carry

    lax.fori_loop(0, PAIRS, one, 0)

    weight_grad(x, dq, gq_out)
    q_track.advance()
    ff_track.advance()

    def input_grad(step, carry):
        here = place(step, block)
        dres[here, :] += dot(dq[here, :], wq[...], 1, 1)
        return carry

    lax.fori_loop(0, count, input_grad, 0)
    q_track.advance()
    vec_acc[0, 0:1, :] = jnp.sum(dq[...].astype(F32), axis=0, keepdims=True)
    o_track.advance()

    for j in (0, 2):
        d_copy(j).wait()
    own_block = rows_at(link.tp * owned, owned, 64)
    for n in range(2):
        total = dpart[n, own_block, :].astype(F32)
        for j in (0, 2):
            total = total + dland[j, n].astype(F32)
        dfull[n, own_block, :] = total.astype(BF)
    share_slot = link.take(3)
    share_plan = ((own_block, d_peers[0]), (own_block, sibling), (far_same, sibling))

    def share_copy(n):
        block_rows, peer = share_plan[n]
        return link.remote(
            share_slot + n, dfull.at[:, block_rows, :], dfull.at[:, block_rows, :], (link.dp, peer)
        )

    share_copy(0).start()
    share_copy(1).start()
    ff_track.advance()
    for n in range(2):
        kv_send[n * owned : (n + 1) * owned, :] = dot(dfull[n, own_block, :], yb[...], 1, 0).astype(BF)
    kv_track.advance()
    o_track.advance()
    q_track.advance()
    kv_track.advance()
    ff_track.advance()
    share_copy(0).wait()
    share_copy(2).start()
    kv_track.advance()
    q_track.advance()
    ff_track.advance()
    kv_track.advance()
    share_copy(1).wait()
    share_copy(2).wait()
    backs = dot(wk[...], dfull[0], 1, 0) + dot(wv[...], dfull[1], 1, 0)
    back = backs.T.astype(BF)
    small = vec[0:8, :].astype(BF)
    bias_row = dot(small, dfull[0], 1, 0)[1:2, :] + dot(small, dfull[1], 1, 0)[2:3, :]
    bias_column = jnp.broadcast_to(bias_row, (128, slots)).T[:, 0:1]
    position = lax.broadcasted_iota(jnp.int32, (1, rows), 1) + link.tp * rows
    live = (position < len_ref[0]).astype(F32)
    s_send[...] = ((dot(back, x[...], 1, 1) + bias_column) * live).astype(BF)
    s_track.advance()
    column = ssum[...].T[0:8, :]
    column_b = column.astype(BF)
    column_low = (column - column_b.astype(F32)).astype(BF)
    for n in range(2):
        total = dot(column_b, dfull[n], 1, 1) + dot(column_low, dfull[n], 1, 1)
        vec_acc[0, 1 + n : 2 + n, :] = total[0:1, :] * (1.0 / tp_size)
    vec_track.advance()
    s_track.advance()

    def input_grad_last(step, carry):
        here = place(step, block)
        grad_in[here, :] = (dres[here, :] + dot(em[:, here], back, 0, 0)).astype(BF)
        return carry

    lax.fori_loop(0, count, input_grad_last, 0)
    grad_store.start()
    tracks = {"s": s_track, "k": kv_track, "q": q_track, "o": o_track, "v": vec_track, "f": ff_track}
    for name in "oqskvosqkvoqskvqsokvsqs":
        tracks[name].advance()
    tracks = list(tracks.values())
    while any(track.todo for track in tracks):
        for track in tracks:
            track.advance()
    for copy in stores:
        copy.wait()


def back(mesh, lengths, vec, part_vec, ff_near, dnorm, probs, *late):
    dp_size, tp_size = mesh.shape["dp"], mesh.shape["tp"]
    bits = dp_size.bit_length() - 1
    low = min(3, bits)
    wide = max(1, bits - low)
    rows, width = dnorm.shape
    slots = late[11].shape[0]
    owned = width // tp_size
    others = tp_size - 1
    vmem = pl.BlockSpec(memory_space=pltpu.VMEM)
    hbm = pl.BlockSpec(memory_space=pltpu.HBM)
    shape = jax.ShapeDtypeStruct

    def landing(total):
        return sum(total >> (i + 1) for i in range(low))

    def buf(*dims, dtype=BF):
        return pltpu.VMEM(dims, dtype)

    ff_piece, kv_piece, s_piece = width >> low, 2 * owned >> low, slots >> low
    quarter = (ff_piece // (tp_size // 2), width // 2)
    return pl.pallas_call(
        functools.partial(back_kernel, dp_size, tp_size),
        out_shape=(
            shape((rows, width), BF),
            shape((2, width, width), BF),
            shape((width, width), BF),
            shape((width, width), BF),
            shape((tp_size, 2 * owned, width), BF),
            shape((tp_size, slots, rows), BF),
            shape((VECTORS, width), F32),
        ),
        in_specs=[pl.BlockSpec(memory_space=pltpu.SMEM)] + [vmem] * 2 + [hbm] * (3 + len(late)),
        out_specs=tuple([hbm] * 3 + [vmem] * 4),
        scratch_shapes=[buf(rows, width), buf(2, width, width), buf(width, width)]
        + [pltpu.VMEM(array.shape, array.dtype) for array in late]
        + [
            buf(rows, width, dtype=F32),
            buf(rows, width),
            buf(rows, width),
            buf(rows, 2 * slots),
            buf(2, rows, 2 * slots),
            buf(2, width, slots),
            buf(others, 2, owned, slots),
            buf(2, owned, slots),
            buf(2, width, slots),
            buf(2, 2, ff_piece, width),
            buf(2, width >> 3, width),
            buf(2, width >> 3, width),
            buf(2, width >> 2, width),
            buf(2, (width >> 2) + (width >> 3), width),
            buf(width // 2, width),
            buf(landing(width), width),
            buf(width // 2, width),
            buf(landing(width), width),
            buf(others, *quarter),
            buf(others, *quarter),
            buf(2 * owned, width),
            buf(owned, width),
            buf(landing(2 * owned), width),
            buf(slots, rows),
            buf(slots // 2, rows),
            buf(landing(slots), rows),
            buf(bits, VECTORS, width, dtype=F32),
            buf(bits, VECTORS, width, dtype=F32),
            buf(tp_size, VECTORS, width, dtype=F32),
            buf(2, wide, ff_piece, width),
            buf(2, wide, *quarter),
            buf(2, wide, kv_piece, width // 2),
            buf(2, wide, s_piece, rows // 2),
            pltpu.SemaphoreType.DMA((BACK_SEMS,)),
            pltpu.SemaphoreType.DMA((BACK_SEMS,)),
            pltpu.SemaphoreType.DMA((6 + len(late),)),
        ],
        compiler_params=pltpu.CompilerParams(
            collective_id=1, has_side_effects=True, vmem_limit_bytes=VMEM_LIMIT
        ),
        name="back",
    )(lengths, vec, part_vec, ff_near, dnorm, probs, *late)


class ChunkSpread:
    def __init__(self, link, rows, sent, acc, landing):
        self.link, self.rows, self.sent, self.acc, self.landing = link, rows, sent, acc, landing
        self.orders = [[b for b in order if b < link.low] for order in ((0, 1, 2), (0, 2, 1))]
        self.stages = link.low
        self.slot = link.take(2 * link.low * acc.shape[1])
        self.insides, self.others = [], []
        for order in self.orders:
            inside, other, first = [0], [(1 - link.bit(order[0])) * (rows >> 1)], 0
            for j in range(1, self.stages):
                size = rows >> (j + 1)
                other.append(first + (1 - link.bit(order[j])) * size)
                first = first + link.bit(order[j]) * size
                inside.append(first)
            self.insides.append(inside)
            self.others.append(other)

    def inside(self, m, i):
        return self.insides[m][i]

    def copy(self, c, m, i):
        link, size = self.link, self.rows >> (i + 1)
        bit = self.orders[m][i]
        if i == 0:
            source = self.sent.at[m, lax.rem(c, 2), rows_at(self.others[m][i], size, 16), :]
        else:
            source = self.acc.at[m, c, rows_at(self.others[m][i], size, 16), :]
        first = sum(self.rows >> (j + 1) for j in range(i))
        slot = self.slot + (i * 2 + m) * self.acc.shape[1] + c
        return link.remote(slot, source, self.landing.at[m, c, pl.ds(first, size), :], link.partner(bit))

    def start(self, c, m, i):
        self.copy(c, m, i).start()

    def finish(self, c, m, i):
        size = self.rows >> (i + 1)
        self.copy(c, m, i).wait()
        first = sum(self.rows >> (j + 1) for j in range(i))
        landed = self.landing.at[m, c, pl.ds(first, size), :]
        acc = self.acc.at[m, c]
        if i == 0:
            mine = self.link.bit(self.orders[m][0]) * size
            add_rows(acc, 0, self.sent.at[m, lax.rem(c, 2)], mine, landed, size)
        else:
            at = self.inside(m, i)
            add_rows(acc, at, acc, at, landed, size)


MIDDLE_SEMS = 96
MIDDLE_TICKS = {3: ((1, 1),), 5: ((0, 2), (0, 3)), 7: ((1, 2), (1, 3))}


def middle_kernel(
    dp_size,
    tp_size,
    vec,
    bup_all,
    xhat_hbm,
    out_grad_hbm,
    own_up,
    own_dn,
    ups,
    downs,
    layer_hbm,
    dnorm,
    part_vec,
    ff_landed,
    ff_near,
    ff_far,
    ff_own,
    whole,
    xhat,
    layer_out,
    out_grad,
    nb,
    act,
    slope,
    d_branch,
    d_acc,
    sent,
    acc,
    landing,
    send_sems,
    recv_sems,
    local_sems,
):
    link = Link(dp_size, tp_size, send_sems, recv_sems)
    rows, width = xhat.shape
    used = [0]

    def local(source, target):
        copy = pltpu.make_async_copy(source, target, local_sems.at[used[0]])
        used[0] += 1
        copy.start()
        return copy

    collect = WeightCollect(link, width // 2, lambda k: whole.at[1, k])
    xhat_load = local(xhat_hbm, xhat)
    up_last = WeightCollect(link, width // 2, lambda k: whole.at[0, k])
    placed = [
        local(ups.at[1, up_last.rows(h, 1), :], whole.at[0, 2, up_last.rows(h, 1), :]) for h in range(2)
    ]
    placed += [
        local(downs.at[1, collect.rows(h, 0), :], whole.at[1, 2, collect.rows(h, 0), :]) for h in range(2)
    ]
    owns = [local(own_up, whole.at[0, 0])]
    owns += [local(ups.at[k - 1], whole.at[0, k]) for k in (1, 3)]
    owns += [local(own_dn, whole.at[1, 0])] + [local(downs.at[k - 1], whole.at[1, k]) for k in (1, 3)]
    owns.append(local(out_grad_hbm, out_grad))
    link.greet(link.low)
    for copy in placed:
        copy.wait()
    collect.step(2, 0)
    for copy in up_last.copies(2, 1):
        copy.start()
    xhat_load.wait()
    gain, shift, b_down, f_gain, f_shift = (vec[n : n + 1, :] for n in (4, 5, 6, 7, 8))
    block = min(BLOCK_M, rows)
    count = rows // block
    big = rows // 2

    def norm(step, carry):
        here = place(step, block)
        nb[here, :] = (xhat[here, :] * gain + shift).astype(BF)
        return carry

    lax.fori_loop(0, count, norm, 0)
    for copy in owns[: tp_size - 1]:
        copy.wait()

    def forward(step, carry):
        n = lax.div(step, 2)
        k = n + lax.div(n, 2) * (7 - 2 * n - 2)
        here, cols = place(lax.rem(step, 2), big), place(k, width)
        pre = dot(nb[here, :], whole[0, k], 1, 0) + bup_all[link.behind(k), 0:1, :]
        cdf = 0.5 * (1.0 + lax.erf(pre * 0.7071067811865476))
        act[here, cols] = (pre * cdf).astype(BF)
        slope[here, cols] = (cdf + pre * (jnp.exp(pre * pre * -0.5) * 0.3989422804014327)).astype(BF)
        for n, ticks in MIDDLE_TICKS.items():

            @pl.when(step == n)
            def _():
                for m, j in ticks:
                    (up_last, collect)[m].step(2, j)

        return carry

    lax.fori_loop(0, 2 * tp_size, forward, 0)
    for copy in owns[tp_size - 1 :]:
        copy.wait()

    def second_norm(step, carry):
        g_gain, g_shift, g_down = carry
        here = place(step, block)
        branch = dot(act[here, 0:width], whole[1, 0], 1, 0)
        for k in range(1, tp_size):
            branch = branch + dot(act[here, k * width : (k + 1) * width], whole[1, k], 1, 0)
        res = xhat[here, :] * gain + shift + (branch + b_down)
        center = res - jnp.mean(res, axis=-1, keepdims=True)
        inverse = lax.rsqrt(jnp.mean(center * center, axis=-1, keepdims=True) + 1e-05)
        hat = center * inverse
        layer_out[here, :] = (hat * f_gain + f_shift).astype(BF)
        grad = out_grad[here, :].astype(F32)
        g_gain = g_gain + jnp.sum(grad * hat, axis=0, keepdims=True)
        g_shift = g_shift + jnp.sum(grad, axis=0, keepdims=True)
        scaled = grad * f_gain
        d_res = inverse * (
            scaled
            - jnp.mean(scaled, axis=-1, keepdims=True)
            - hat * jnp.mean(scaled * hat, axis=-1, keepdims=True)
        )
        d_acc[here, :] = d_res
        rounded = d_res.astype(BF)
        d_branch[here, :] = rounded
        g_down = g_down + jnp.sum(rounded.astype(F32), axis=0, keepdims=True)
        return g_gain, g_shift, g_down

    zero = jnp.zeros((1, width), F32)
    g_gain, g_shift, g_down = lax.fori_loop(0, count, second_norm, (zero, zero, zero))
    layer_store = local(layer_out, layer_hbm)
    part_vec[...] = jnp.zeros_like(part_vec)
    part_vec[6:7, :] = g_gain
    part_vec[7:8, :] = g_shift
    part_vec[8:9, :] = g_down

    spread = ChunkSpread(link, width, sent, acc, landing)
    third = width // GRAD_SPLIT

    def weight_grad(left, first, right, cols, target):
        for m in range(GRAD_SPLIT):
            mine = pl.ds(pl.multiple_of(first + m * third, third), third)
            target[m * third : (m + 1) * third, :] = dot(left[:, mine], right[:, cols], 0, 0).astype(BF)

    def settle(n, steps):
        for m, late, stage in steps:

            @pl.when(n >= late)
            def _():
                spread.finish(n - late, m, stage)

            if stage < 2:

                @pl.when(jnp.logical_and(n >= late, n - late < 3 - stage))
                def _():
                    spread.start(n - late, m, stage + 1)

    def backward(n, carry):
        k = 2 - n + lax.div(n, 2) * (7 - 2 * n)
        cols = place(k, width)
        slot = lax.rem(n, 2)
        weight_grad(act, k * width, d_branch, slice(0, width), sent.at[1, slot])
        spread.start(n, 1, 0)
        settle(n, ((0, 1, 0), (1, 2, 1)))

        def through(step, total):
            here = place(step, big)
            grad = (dot(d_branch[here, :], whole[1, k], 1, 1) * slope[here, cols].astype(F32)).astype(BF)
            slope[here, cols] = grad
            return total + jnp.sum(grad.astype(F32), axis=0, keepdims=True)

        part_vec[pl.ds(9 + link.behind(k), 1), :] = lax.fori_loop(0, 2, through, zero)
        settle(n, ((1, 0, 0), (0, 2, 1)))
        weight_grad(nb, 0, slope, cols, sent.at[0, slot])
        spread.start(n, 0, 0)
        return carry

    lax.fori_loop(0, tp_size, backward, 0)

    def input_grad(step, carry):
        here = place(step, big)
        total = d_acc[here, :]
        for k in range(tp_size):
            total = total + dot(slope[here, k * width : (k + 1) * width], whole[0, k], 1, 1)
        d_acc[here, :] = total
        return carry

    slot = link.take(2)
    crossing = []
    for m in (1, 0):
        spread.finish(0, m, 2)
        at = rows_at(spread.inside(m, 2), width >> 3, 16)
        crossing.append(
            link.remote(slot + m, acc.at[m, 0, at, :], ff_landed.at[m], (link.dp, link.behind(2)))
        )
        crossing[-1].start()
    lax.fori_loop(0, 1, input_grad, 0)
    spread.finish(3, 0, 0)
    spread.finish(2, 1, 1)
    stores = [local(acc.at[m, 3], ff_own.at[m]) for m in range(2)]
    lax.fori_loop(1, 2, input_grad, 0)
    stores.append(local(d_acc, dnorm))
    spread.finish(2, 0, 1)
    for m in (1, 0):
        spread.finish(1, m, 2)
    for m in range(2):
        at = rows_at(spread.inside(m, 2), width >> 3, 16)
        stores.append(local(acc.at[m, 1, at, :], ff_near.at[m]))
        at = rows_at(spread.inside(m, 1), width >> 2, 16)
        stores.append(local(acc.at[m, 2, at, :], ff_far.at[m]))
    for copy in crossing + stores + [layer_store]:
        copy.wait()


def middle(mesh, vec, bup_all, xhat, out_grad, w_up, w_dn, ups, downs):
    dp_size, tp_size = mesh.shape["dp"], mesh.shape["tp"]
    low = min(3, dp_size.bit_length() - 1)
    assert low == 3 and tp_size == 4
    rows, width = xhat.shape
    hidden = tp_size * width
    vmem = pl.BlockSpec(memory_space=pltpu.VMEM)
    hbm = pl.BlockSpec(memory_space=pltpu.HBM)
    shape = jax.ShapeDtypeStruct

    def buf(*dims, dtype=BF):
        return pltpu.VMEM(dims, dtype)

    return pl.pallas_call(
        functools.partial(middle_kernel, dp_size, tp_size),
        out_shape=(
            shape((rows, width), BF),
            shape((rows, width), F32),
            shape((VECTORS, width), F32),
            shape((2, width >> 3, width), BF),
            shape((2, width >> 3, width), BF),
            shape((2, width >> 2, width), BF),
            shape((2, width >> 1, width), BF),
        ),
        in_specs=[vmem] * 2 + [hbm] * 6,
        out_specs=(hbm, hbm, vmem, hbm, hbm, hbm, hbm),
        scratch_shapes=[
            buf(2, tp_size, width, width),
            buf(rows, width, dtype=F32),
            buf(rows, width),
            buf(rows, width),
            buf(rows, width),
            buf(rows, hidden),
            buf(rows, hidden),
            buf(rows, width),
            buf(rows, width, dtype=F32),
            buf(2, 2, width, width),
            buf(2, tp_size, width // 2, width),
            buf(2, tp_size, sum(width >> (i + 1) for i in range(low)), width),
            pltpu.SemaphoreType.DMA((MIDDLE_SEMS,)),
            pltpu.SemaphoreType.DMA((MIDDLE_SEMS,)),
            pltpu.SemaphoreType.DMA((32,)),
        ],
        compiler_params=pltpu.CompilerParams(
            collective_id=2, has_side_effects=True, vmem_limit_bytes=VMEM_LIMIT
        ),
        name="middle",
    )(vec, bup_all, xhat, out_grad, w_up, w_dn, ups, downs)


def finish_kernel(
    tp_size, ff, gq, go, gkv, seq, vec, layer_out, grad_in,
    o_up, o_dn, o_q, o_o, o_k, o_v, o_seq, o_layer, o_grad, *rest,
):
    vectors, (in_up, in_dn, in_q, in_o, in_kv, in_seq, f_up, f_dn, f_q, f_o, f_k, f_v, f_seq, turn, pass_a, pass_b, in_sems, out_sems) = rest[:10], rest[10:]
    pairs = [(gq, in_q), (go, in_o), (ff.at[0], in_up), (ff.at[1], in_dn), (gkv, in_kv), (seq, in_seq), (layer_out, pass_a), (grad_in, pass_b)]
    loads = []
    for n, (source, target) in enumerate(pairs):
        loads.append(pltpu.make_async_copy(source, target, in_sems.at[n]))
        loads[-1].start()
    stores = []

    def put(staged, out):
        copy = pltpu.make_async_copy(staged, out, out_sems.at[len(stores)])
        copy.start()
        stores.append(copy)

    for n, (held, out) in enumerate(((pass_a, o_layer), (pass_b, o_grad))):
        loads[6 + n].wait()
        put(held, out)
    for n, row in enumerate((0, 1, 2, 3, 4, 5, 6, 7, 8)):
        vectors[n][...] = vec[row, :]
    vectors[9][...] = vec[pl.ds(9 + lax.axis_index("tp"), 1), :][0]
    width = gq.shape[0]
    for n, (narrow, wide, out) in enumerate(
        ((in_q, f_q, o_q), (in_o, f_o, o_o), (in_up, f_up, o_up), (in_dn, f_dn, o_dn))
    ):
        loads[n].wait()
        wide[...] = narrow[...].astype(F32)
        put(wide, out)
    loads[4].wait()
    owned = width // tp_size
    for n, (wide, out) in enumerate(((f_k, o_k), (f_v, o_v))):
        for c in range(tp_size):
            turn[c * owned : (c + 1) * owned, :] = in_kv[c, n * owned : (n + 1) * owned, :]
        for c in range(3):
            cols = slice(c * (width // 3), (c + 1) * (width // 3))
            wide[:, cols] = turn[cols, :].astype(F32).T
        put(wide, out)
    loads[5].wait()
    rows = in_seq.shape[2]
    for c in range(tp_size):
        f_seq[:, c * rows : (c + 1) * rows] = in_seq[c].astype(F32)
    put(f_seq, o_seq)
    for copy in stores:
        copy.wait()


def finish(tp_size, ff, gq, go, gkv, seq, vec, layer_out, grad_in):
    width = gq.shape[0]
    _, slots, rows = seq.shape
    square, flat = (width, width), (slots, tp_size * rows)
    vmem = pl.BlockSpec(memory_space=pltpu.VMEM)
    hbm = pl.BlockSpec(memory_space=pltpu.HBM)
    shape = jax.ShapeDtypeStruct
    return pl.pallas_call(
        functools.partial(finish_kernel, tp_size),
        out_shape=tuple([shape(square, F32)] * 6 + [shape(flat, F32)] + [shape(layer_out.shape, BF)] * 2 + [shape((width,), F32)] * 10),
        in_specs=[hbm] * 5 + [vmem] + [hbm] * 2,
        out_specs=tuple([hbm] * 9 + [vmem] * 10),
        scratch_shapes=[pltpu.VMEM(square, BF)] * 4
        + [pltpu.VMEM(gkv.shape, BF), pltpu.VMEM(seq.shape, BF)]
        + [pltpu.VMEM(square, F32)] * 6
        + [pltpu.VMEM(flat, F32), pltpu.VMEM(square, BF)]
        + [pltpu.VMEM(layer_out.shape, BF)] * 2
        + [pltpu.SemaphoreType.DMA((8,)), pltpu.SemaphoreType.DMA((9,))],
        compiler_params=pltpu.CompilerParams(vmem_limit_bytes=VMEM_LIMIT),
        name="finish",
    )(ff, gq, go, gkv, seq, vec, layer_out, grad_in)


def on_device(
    mesh,
    layer_in,
    out_grad,
    lengths,
    w_query,
    b_query,
    w_key,
    b_key,
    w_value,
    b_value,
    w_out,
    b_out,
    seq_proj,
    attn_gain,
    attn_shift,
    w_up,
    b_up,
    w_down,
    b_down,
    ffn_gain,
    ffn_shift,
):
    row_count, width = layer_in.shape
    tp_size = mesh.shape["tp"]
    vectors = (b_query, b_key, b_value, b_out, attn_gain, attn_shift, b_down, ffn_gain, ffn_shift)
    vec, bup_all, xhat, rstd, mixed, queries, probs, kb, vb, folded, ssum, own_proj, ups, downs = front(
        mesh, lengths, layer_in, w_query, seq_proj, w_key, w_value, w_out, w_up, w_down, vectors, b_up
    )
    layer_out, d_normed, part_vec, ff_landed, ff_near, ff_far, ff_own = middle(
        mesh, vec, bup_all, xhat, out_grad, w_up, w_down, ups, downs
    )
    grad_in, g_ff, g_o, g_q, g_kv, g_seq, vec_sum = back(
        mesh, lengths, vec, part_vec, ff_near, d_normed, probs, ff_far, ff_own, xhat, rstd, mixed, w_out, ff_landed,
        layer_in, queries, kb, vb, folded, ssum, own_proj, w_query, w_key, w_value
    )
    (
        g_w_up, g_w_down, g_w_query, g_w_out, g_w_key, g_w_value, g_seq_proj, layer_out, grad_in,
        g_b_query, g_b_key, g_b_value, g_b_out, g_attn_gain, g_attn_shift, g_ffn_gain, g_ffn_shift, g_b_down, g_b_up,
    ) = finish(tp_size, g_ff, g_q, g_o, g_kv, g_seq, vec_sum, layer_out, grad_in)
    return (
        layer_out,
        grad_in,
        g_w_query,
        g_b_query,
        g_w_key,
        g_b_key,
        g_w_value,
        g_b_value,
        g_w_out,
        g_b_out,
        g_seq_proj,
        g_attn_gain,
        g_attn_shift,
        g_w_up,
        g_b_up,
        g_w_down,
        g_b_down,
        g_ffn_gain,
        g_ffn_shift,
    )


def solution(mesh):
    in_specs = (
        P(("dp", "tp"), None),
        P(("dp", "tp"), None),
        P("dp"),
        *([P()] * 11),
        P(None, "tp"),
        P("tp"),
        P("tp", None),
        P(),
        P(),
        P(),
    )
    out_specs = (
        P(("dp", "tp"), None),
        P(("dp", "tp"), None),
        *([P()] * 11),
        P(None, "tp"),
        P("tp"),
        P("tp", None),
        P(),
        P(),
        P(),
    )
    return jax.shard_map(
        functools.partial(on_device, mesh), mesh=mesh, in_specs=in_specs, out_specs=out_specs, check_vma=False
    )
```
